32 devices in a mesh: row: 4 (over y, x), col: 8 (over z, core).
Axes of the slice: x: 2, y: 2, z: 4, core: 2. Of those that a mesh axis runs over, the one named last changes fastest.
Arguments:
- currents: float32 [2, 64, 16384], P(None, None, ('row', 'col')), may hold values from -6 to 6
- projection: bfloat16 [64, 64, 16384], P(None, None, ('row', 'col')), may hold values from -0.75 to 0.75
- near_blocks: bfloat16 [4, 64, 64, 16384], P(None, None, None, ('row', 'col')), may hold values from -0.375 to 0.375
- partners: int32 [4, 16384], P(None, ('row', 'col')), may hold values from 0 to 8, as said below
- shifts: int32 [2, 16384], P(None, ('row', 'col')), may hold values from -2 to 2, as said below
- green: float32 [2048, 2048], P(('row', 'col')), may hold values from 0.5 to 2.5, as said below
Outputs:
- product: float32 [2, 64, 16384], P(None, None, ('row', 'col'))
The draws below stay inside these ranges and needn't reach their ends.
Inputs may be any that keep to these rules, and one draw needn't show every extreme that they name: shifts[0, n] is 0 or more for elements of the first element row and 0 or less for those of the last; shifts[1, n] likewise for the first and last element columns, so that every stencil lies inside the grid. partners[0, n] is 4, the element itself; for k of 1 or more the codes of one element are distinct, each 3 (dr + 1) + (dc + 1) for offsets dr, dc in -1, 0, 1, not both 0, of an element that lies inside the array. green is the spectrum of a real even kernel: green[ky, kx] = green[(2048 - ky) % 2048, kx] = green[ky, (2048 - kx) % 2048].
All inputs are finite; a program needn't handle non-finite values.
Results may differ from the reference program's by a relative error of at most 0.0038.
Values may be sent and summed in bfloat16 or wider, within the bound.
No kernel may reach another device: no remote copies, remote signals or barrier semaphores. Data moves between devices by JAX's collectives and lax.ppermute only.
A program may use at most 192 MiB of HBM per device.

```python
import jax
import jax.numpy as jnp
from jax import lax

BASIS = 64
STEN = 8
PITCH = 8
HALO = 2
NEIGH = 4
RHS = 2
ER = 32
EC = 16
EX = 128
EY = 128
ELEMS = 16384
NGR = 1024
NGC = 1024
LR = 2048
LC = 2048


def element_place_drawn():
    number = jnp.arange(EX * EY, dtype=jnp.int32)
    block_index = number // (ER * EC)
    inside = number % (ER * EC)
    elem_row = block_index // (EY // EC) * ER + inside // EC
    elem_col = block_index % (EY // EC) * EC + inside % EC
    return (elem_row, elem_col)


def draw_shifts(key, part):
    elem_row, elem_col = element_place_drawn()
    row_key = jax.random.fold_in(key, 17)
    col_key = jax.random.fold_in(key, 29)
    row_shift = jax.random.randint(row_key, elem_row.shape, -HALO, HALO + 1, dtype=jnp.int32)
    col_shift = jax.random.randint(col_key, elem_col.shape, -HALO, HALO + 1, dtype=jnp.int32)
    first_mark = (elem_row == 1) & (elem_col == 1)
    second_mark = (elem_row == 2) & (elem_col == 2)
    row_shift = jnp.where(first_mark, -HALO, row_shift)
    row_shift = jnp.where(second_mark, HALO, row_shift)
    col_shift = jnp.where(first_mark, HALO, col_shift)
    col_shift = jnp.where(second_mark, -HALO, col_shift)
    row_shift = jnp.where(elem_row == 0, jnp.maximum(row_shift, 0), row_shift)
    row_shift = jnp.where(elem_row == EX - 1, jnp.minimum(row_shift, 0), row_shift)
    col_shift = jnp.where(elem_col == 0, jnp.maximum(col_shift, 0), col_shift)
    col_shift = jnp.where(elem_col == EY - 1, jnp.minimum(col_shift, 0), col_shift)
    return jnp.stack([row_shift, col_shift]).astype(jnp.int32)


def draw_partners(key, part):
    elem_row, elem_col = element_place_drawn()
    symbols = jnp.arange(9, dtype=jnp.int32)
    near_row = elem_row[None, :] + symbols[:, None] // 3 - 1
    near_col = elem_col[None, :] + symbols[:, None] % 3 - 1
    inside = (near_row >= 0) & (near_row < EX) & (near_col >= 0) & (near_col < EY) & (symbols[:, None] != 4)
    scores = jax.random.randint(jax.random.fold_in(key, 41), near_row.shape, 0, 1 << 20, dtype=jnp.int32) * 16 + symbols[:, None]
    scores = jnp.where(inside, scores, -1 - symbols[:, None])
    chosen = lax.top_k(jnp.transpose(scores), NEIGH - 1)[1]
    itself = jnp.full((1, EX * EY), 4, jnp.int32)
    return jnp.concatenate([itself, jnp.transpose(chosen).astype(jnp.int32)], axis=0)


def draw_green(key, part):
    quarter = jax.random.uniform(jax.random.fold_in(key, 53), (LC // 2 + 1, LR // 2 + 1), jnp.float32, 0.5, 2.5)
    col_freq = jnp.arange(LC, dtype=jnp.int32)
    row_freq = jnp.arange(LR, dtype=jnp.int32)
    col_fold = jnp.minimum(col_freq, LC - col_freq)
    row_fold = jnp.minimum(row_freq, LR - row_freq)
    return quarter[col_fold[:, None], row_fold[None, :]].astype(jnp.float32)


def block_levels(stream_key, dims, pieces, low, top_value):
    loudness, own = 1.0, jax.random.fold_in(stream_key, 6)
    for dim, blocks in pieces:
        draws = jnp.exp(jax.random.uniform(jax.random.fold_in(own, dim), (blocks,), jnp.float32, low / len(pieces), top_value / len(pieces)))
        loudness = loudness * jnp.repeat(draws, dims[dim] // blocks).reshape([-1 if axis == dim else 1 for axis in range(len(dims))])
    return loudness


def bell_draw(key, dims, deviation, bound, shards=(), kind=jnp.bfloat16):
    array = deviation * jax.random.normal(key, dims, jnp.float32)
    if shards:
        array = array * block_levels(key, dims, shards, -0.22, 0.18)
    return jnp.clip(array, -bound, bound).astype(kind)


def setup_inputs(seed: int = 0) -> dict:
    splits = jax.random.split(jax.random.key(seed), 7)
    currents = bell_draw(splits[0], (RHS, BASIS, ELEMS), 1.0, 6.0, ((2, 32),), jnp.float32)
    projection = bell_draw(splits[1], (STEN * STEN, BASIS, ELEMS), BASIS ** -0.5, 0.75, ((2, 32),))
    near_blocks = bell_draw(splits[2], (NEIGH, BASIS, BASIS, ELEMS), (BASIS * NEIGH) ** -0.5, 0.375, ((3, 32),))
    partners = draw_partners(jax.random.fold_in(splits[6], 71), 0)
    shifts = draw_shifts(jax.random.fold_in(splits[6], 71), 0)
    green = draw_green(jax.random.fold_in(splits[6], 71), 0)
    return dict(currents=currents, projection=projection, near_blocks=near_blocks, partners=partners, shifts=shifts, green=green)


def element_place():
    number = jnp.arange(EX * EY, dtype=jnp.int32)
    block_index = number // (ER * EC)
    inside = number % (ER * EC)
    elem_row = (block_index // (EY // EC)) * ER + inside // EC
    elem_col = (block_index % (EY // EC)) * EC + inside % EC
    return elem_row, elem_col


def element_number(elem_row, elem_col):
    block_index = (elem_row // ER) * (EY // EC) + elem_col // EC
    return (block_index * (ER * EC) + (elem_row % ER) * EC + elem_col % EC).astype(jnp.int32)


def reference(currents, projection, near_blocks, partners, shifts, green):
    highest = lax.Precision.HIGHEST
    elem_row, elem_col = element_place()
    cur_half = currents.astype(jnp.bfloat16)
    widened = cur_half.astype(jnp.float32)
    block_size = ER * EC
    starts = (jnp.arange(EX * EY // block_size, dtype=jnp.int32) * block_size).astype(jnp.int32)

    def stencil_block(start):
        weights = lax.dynamic_slice_in_dim(projection, start, block_size, 2).astype(jnp.float32)
        values = lax.dynamic_slice_in_dim(widened, start, block_size, 2)
        return jnp.einsum("sbn,qbn->qsn", weights, values, precision=highest)

    stencil = jnp.transpose(lax.map(stencil_block, starts), (1, 2, 0, 3)).reshape(RHS, STEN * STEN, EX * EY)
    offsets = jnp.arange(STEN * STEN, dtype=jnp.int32)
    cell_row = (PITCH * elem_row + shifts[0])[None, :] + (offsets // STEN)[:, None]
    cell_col = (PITCH * elem_col + shifts[1])[None, :] + (offsets % STEN)[:, None]
    charges = jnp.zeros((RHS, NGR, NGC), jnp.float32).at[:, cell_row, cell_col].add(stencil)
    padded = jnp.zeros((RHS, LR, LC), jnp.float32).at[:, :NGR, :NGC].set(charges)
    spectrum = jnp.fft.fft2(padded) * jnp.transpose(green)[None, :, :]
    potential = jnp.real(jnp.fft.ifft2(spectrum))[:, :NGR, :NGC]
    samples = potential[:, cell_row, cell_col]

    def far_block(start):
        weights = lax.dynamic_slice_in_dim(projection, start, block_size, 2).astype(jnp.float32)
        values = lax.dynamic_slice_in_dim(samples, start, block_size, 2)
        return jnp.einsum("sbn,qsn->qbn", weights, values, precision=highest)

    far_term = jnp.transpose(lax.map(far_block, starts), (1, 2, 0, 3)).reshape(RHS, BASIS, EX * EY)
    partner_row = elem_row[None, :] + partners // 3 - 1
    partner_col = elem_col[None, :] + partners % 3 - 1
    partner = element_number(partner_row, partner_col)
    picked = widened[:, :, partner]

    def near_block(start):
        blocks = lax.dynamic_slice_in_dim(near_blocks, start, block_size, 3).astype(jnp.float32)
        values = lax.dynamic_slice_in_dim(picked, start, block_size, 3)
        return jnp.einsum("kabn,qbkn->qan", blocks, values, precision=highest)

    near_term = jnp.transpose(lax.map(near_block, starts), (1, 2, 0, 3)).reshape(RHS, BASIS, EX * EY)
    return far_term + near_term
```

```python
import functools
import math

import jax
import jax.numpy as jnp
import numpy as np
from jax import lax
from jax.experimental import pallas as pl
from jax.experimental.pallas import tpu as pltpu
from jax.sharding import PartitionSpec as P

BASIS = 64
STEN = 8
PITCH = 8
HALO = 2
NEIGH = 4
RHS = 2
ER = 32
EC = 16


def extended_2(block, sides, width):
    for axis, dim in sides:
        count = lax.axis_size(axis)
        forward = [(i, i + 1) for i in range(count - 1)]
        backward = [(target, source) for source, target in forward]
        low = lax.ppermute(
            lax.slice_in_dim(block, block.shape[dim] - width, None, axis=dim), axis, forward
        )
        high = lax.ppermute(lax.slice_in_dim(block, 0, width, axis=dim), axis, backward)
        block = jnp.concatenate([low, block, high], axis=dim)
    return block


def angle_table(first_size, second_size, modulus, direction):
    left_index = jnp.arange(first_size, dtype=jnp.int32)
    right_index = jnp.arange(second_size, dtype=jnp.int32)
    turn_count = left_index[:, None] * right_index[None, :] % modulus
    angles = turn_count.astype(jnp.float32) * (2.0 * math.pi / modulus)
    return (jnp.cos(angles), direction * jnp.sin(angles))


def complex_apply(real_part, imag_part, cosine, sine_table, pattern):
    highest = lax.Precision.HIGHEST
    out_real = jnp.einsum(pattern, real_part, cosine, precision=highest)
    out_imag = jnp.einsum(pattern, real_part, sine_table, precision=highest)
    if imag_part is not None:
        out_real = out_real - jnp.einsum(pattern, imag_part, sine_table, precision=highest)
        out_imag = out_imag + jnp.einsum(pattern, imag_part, cosine, precision=highest)
    return (out_real, out_imag)


def transform_last(real_part, imag_part, length, count_in, count_out, direction):
    leading = real_part.shape[:-1]
    inner_size = 128
    outer_size = length // inner_size
    rows_in = count_in // inner_size
    kept_count = count_out // outer_size
    shaped_real = real_part.reshape(leading + (rows_in, inner_size))
    shaped_imag = None
    if imag_part is not None:
        shaped_imag = imag_part.reshape(leading + (rows_in, inner_size))
    cosine, sine_table = angle_table(rows_in, outer_size, outer_size, direction)
    first_real, first_imag = complex_apply(
        shaped_real, shaped_imag, cosine, sine_table, "...ab,ak->...kb"
    )
    twist_cos, twist_sin = angle_table(outer_size, inner_size, length, direction)
    turned_real = first_real * twist_cos - first_imag * twist_sin
    turned_imag = first_real * twist_sin + first_imag * twist_cos
    cosine, sine_table = angle_table(inner_size, kept_count, inner_size, direction)
    last_real, last_imag = complex_apply(
        turned_real, turned_imag, cosine, sine_table, "...kb,bj->...jk"
    )
    out_shape = leading + (kept_count * outer_size,)
    return (last_real.reshape(out_shape), last_imag.reshape(out_shape))


def place_shifted(blocks, amount, dim_index):
    new_shape = list(blocks.shape)
    new_shape[dim_index] = new_shape[dim_index] + 2 * HALO
    result = jnp.zeros(tuple(new_shape), blocks.dtype)
    for offset in range(-HALO, HALO + 1):
        widths = [(0, 0)] * blocks.ndim
        widths[dim_index] = (HALO + offset, HALO - offset)
        result = jnp.where(amount == offset, jnp.pad(blocks, widths), result)
    return result


def pick_shifted(windows, amount, dim_index):
    new_shape = list(windows.shape)
    new_shape[dim_index] = STEN
    result = jnp.zeros(tuple(new_shape), windows.dtype)
    for offset in range(-HALO, HALO + 1):
        piece = lax.slice_in_dim(windows, HALO + offset, HALO + offset + STEN, axis=dim_index)
        result = jnp.where(amount == offset, piece, result)
    return result


def intersection_add(framed, dim_index):
    element_count = framed.shape[dim_index]
    window_size = framed.shape[dim_index + 1]
    head_part = lax.slice_in_dim(framed, 0, PITCH, axis=dim_index + 1)
    tail_part = lax.slice_in_dim(framed, PITCH, window_size, axis=dim_index + 1)
    widths = [(0, 0)] * framed.ndim
    widths[dim_index + 1] = (0, 2 * PITCH - window_size)
    tail_part = jnp.pad(tail_part, widths)
    merged = framed.shape[:dim_index] + (element_count * PITCH,) + framed.shape[dim_index + 2 :]
    head_part = head_part.reshape(merged)
    tail_part = tail_part.reshape(merged)
    front_pad = [(0, 0)] * len(merged)
    front_pad[dim_index] = (0, PITCH)
    back_pad = [(0, 0)] * len(merged)
    back_pad[dim_index] = (PITCH, 0)
    summed = jnp.pad(head_part, front_pad) + jnp.pad(tail_part, back_pad)
    return lax.slice_in_dim(summed, 0, element_count * PITCH + 2 * HALO, axis=dim_index)


def cut_windows(field, dim_index):
    element_count = (field.shape[dim_index] - 2 * HALO) // PITCH
    widths = [(0, 0)] * field.ndim
    widths[dim_index] = (0, PITCH - 2 * HALO)
    extended = jnp.pad(field, widths)
    split_shape = field.shape[:dim_index] + (element_count, PITCH) + field.shape[dim_index + 1 :]
    head_part = lax.slice_in_dim(extended, 0, element_count * PITCH, axis=dim_index).reshape(
        split_shape
    )
    tail_part = lax.slice_in_dim(
        extended, PITCH, PITCH + element_count * PITCH, axis=dim_index
    ).reshape(split_shape)
    tail_part = lax.slice_in_dim(tail_part, 0, 2 * HALO, axis=dim_index + 1)
    return jnp.concatenate([head_part, tail_part], axis=dim_index + 1)


def fold_margin(padded, dim_index):
    full_size = padded.shape[dim_index]
    inner_size = full_size - 4 * HALO
    core_part = lax.slice_in_dim(padded, 2 * HALO, 2 * HALO + inner_size, axis=dim_index)
    upper_part = lax.slice_in_dim(padded, 0, HALO, axis=dim_index)
    lower_part = lax.slice_in_dim(padded, full_size - HALO, full_size, axis=dim_index)
    upper_pad = [(0, 0)] * padded.ndim
    upper_pad[dim_index] = (0, inner_size - HALO)
    lower_pad = [(0, 0)] * padded.ndim
    lower_pad[dim_index] = (inner_size - HALO, 0)
    return core_part + jnp.pad(upper_part, upper_pad) + jnp.pad(lower_part, lower_pad)


def shards_general(currents, projection, near_blocks, partners, shifts, green):
    row_count = lax.axis_size("row")
    col_count = lax.axis_size("col")
    device_count = row_count * col_count
    elements = ER * EC
    cur_half = currents.astype(jnp.bfloat16)
    spread = extended_2(cur_half.reshape(RHS, BASIS, ER, EC), (("row", 2), ("col", 3)), 1)
    views = []
    for symbol in range(9):
        row_start = symbol // 3
        col_start = symbol % 3
        views.append(
            spread[:, :, row_start : row_start + ER, col_start : col_start + EC].reshape(
                RHS, BASIS, elements
            )
        )
    picked = []
    for neighbour_slot in range(NEIGH):
        chosen = jnp.zeros((RHS, BASIS, elements), jnp.bfloat16)
        for symbol in range(9):
            chosen = jnp.where(partners[neighbour_slot] == symbol, views[symbol], chosen)
        picked.append(chosen)
    near_term = jnp.einsum(
        "kabn,kqbn->qan", near_blocks, jnp.stack(picked), preferred_element_type=jnp.float32
    )
    stencil = jnp.einsum("sbn,qbn->qsn", projection, cur_half, preferred_element_type=jnp.float32)
    blocks = stencil.reshape(RHS, STEN, STEN, elements)
    framed = place_shifted(place_shifted(blocks, shifts[0], 1), shifts[1], 2)
    window_size = STEN + 2 * HALO
    framed = framed.reshape(RHS, window_size, window_size, ER, EC).transpose(0, 3, 1, 4, 2)
    extended = intersection_add(intersection_add(framed, 1), 2)
    padded = extended_2(extended, (("row", 1), ("col", 2)), HALO)
    charges = fold_margin(fold_margin(padded, 1), 2)
    slab = lax.all_to_all(charges, "col", split_axis=1, concat_axis=2, tiled=True)
    slab_rows = slab.shape[1]
    width_cols = slab.shape[2]
    length_cols = 2 * width_cols
    block_cols = length_cols // device_count
    grid_rows = slab_rows * device_count
    length_rows = 2 * grid_rows
    fwd_real, fwd_imag = transform_last(slab, None, length_cols, width_cols, length_cols, -1.0)
    out_real = fwd_real.reshape(RHS, slab_rows, device_count, block_cols)
    out_imag = fwd_imag.reshape(RHS, slab_rows, device_count, block_cols)
    arrived = (
        lax.all_to_all(out_real, ("row", "col"), split_axis=2, concat_axis=2, tiled=True),
        lax.all_to_all(out_imag, ("row", "col"), split_axis=2, concat_axis=2, tiled=True),
    )
    col_real = arrived[0].transpose(0, 3, 2, 1).reshape(RHS, block_cols, grid_rows)
    col_imag = arrived[1].transpose(0, 3, 2, 1).reshape(RHS, block_cols, grid_rows)
    spec_real, spec_imag = transform_last(
        col_real, col_imag, length_rows, grid_rows, length_rows, -1.0
    )
    spec_real = spec_real * green
    spec_imag = spec_imag * green
    back_real, back_imag = transform_last(
        spec_real, spec_imag, length_rows, length_rows, grid_rows, 1.0
    )
    send_real = back_real.reshape(RHS, block_cols, device_count, slab_rows)
    send_imag = back_imag.reshape(RHS, block_cols, device_count, slab_rows)
    returned = (
        lax.all_to_all(send_real, ("row", "col"), split_axis=2, concat_axis=2, tiled=True),
        lax.all_to_all(send_imag, ("row", "col"), split_axis=2, concat_axis=2, tiled=True),
    )
    rows_real = returned[0].transpose(0, 3, 2, 1).reshape(RHS, slab_rows, length_cols)
    rows_imag = returned[1].transpose(0, 3, 2, 1).reshape(RHS, slab_rows, length_cols)
    final_real, final_imag = transform_last(
        rows_real, rows_imag, length_cols, length_cols, width_cols, 1.0
    )
    potential_slab = final_real * (1.0 / (length_rows * length_cols))
    potential = lax.all_to_all(potential_slab, "col", split_axis=2, concat_axis=1, tiled=True)
    rimmed = extended_2(potential, (("row", 1), ("col", 2)), HALO)
    windows = cut_windows(cut_windows(rimmed, 1), 3)
    windows = windows.transpose(0, 2, 4, 1, 3).reshape(RHS, window_size, window_size, elements)
    samples = pick_shifted(pick_shifted(windows, shifts[0], 1), shifts[1], 2).reshape(
        RHS, STEN * STEN, elements
    )
    sample_high = samples.astype(jnp.bfloat16)
    sample_low = (samples - sample_high.astype(jnp.float32)).astype(jnp.bfloat16)
    far_term = jnp.einsum(
        "sbn,qsn->qbn", projection, sample_high, preferred_element_type=jnp.float32
    )
    far_term = far_term + jnp.einsum(
        "sbn,qsn->qbn", projection, sample_low, preferred_element_type=jnp.float32
    )
    return far_term + near_term


LANES = 128
SUB = 8
TILES = 4
GROUPS = 9
PARITY_ORDER = (0, 2, 4, 6, 1, 3, 5, 7)


def roll(value, amount, dim):
    return pltpu.roll(value, amount % value.shape[dim], dim)


def lane_index(shape):
    return lax.broadcasted_iota(jnp.int32, shape, len(shape) - 1)


def sub_index(shape):
    return lax.broadcasted_iota(jnp.int32, shape, len(shape) - 2)


def sum_rows(parts):
    sub = sub_index(parts[0].shape)
    top = sub < 4
    level = []
    for i in range(4):
        a, b = parts[i], parts[i + 4]
        level.append(jnp.where(top, a, b) + roll(jnp.where(top, b, a), 4, 0))
    mask = (sub & 2) == 0
    level = [
        jnp.where(mask, level[i], level[i + 2])
        + jnp.where(mask, roll(level[i], -2, 0), roll(level[i + 2], 2, 0))
        for i in range(2)
    ]
    mask = (sub & 1) == 0
    a, b = level
    return jnp.where(mask, a, b) + jnp.where(mask, roll(a, -1, 0), roll(b, 1, 0))


def next_row(value):
    lane = lane_index(value.shape)
    sub = sub_index(value.shape)
    turned = roll(value, EC, 1)
    carried = jnp.where((sub & 3) == 0, 0.0, roll(turned, 1, 0))
    return jnp.where(lane < EC, carried, turned)


def previous_row(value):
    lane = lane_index(value.shape)
    sub = sub_index(value.shape)
    turned = roll(value, -EC, 1)
    carried = jnp.where((sub & 3) == 3, 0.0, roll(turned, -1, 0))
    return jnp.where(lane >= LANES - EC, carried, turned)


def place_charges(stencil, row_shift, col_shift):
    shape = row_shift.shape
    lane = lane_index(shape)
    sub = sub_index(shape)
    window = STEN + 2 * HALO
    row_mask = {o: row_shift == o for o in range(-HALO, HALO + 1)}
    col_mask = {o: col_shift == o for o in range(-HALO, HALO + 1)}
    first = []
    for rr in range(window):
        line = []
        for c in range(STEN):
            value = jnp.zeros(shape, jnp.float32)
            for o in range(-HALO, HALO + 1):
                source = rr - HALO - o
                if 0 <= source < STEN:
                    value = jnp.where(row_mask[o], stencil(source * STEN + c), value)
            line.append(value)
        first.append(line)
    framed = []
    for rr in range(window):
        line = []
        for cc in range(window):
            value = jnp.zeros(shape, jnp.float32)
            for o in range(-HALO, HALO + 1):
                source = cc - HALO - o
                if 0 <= source < STEN:
                    value = jnp.where(col_mask[o], first[rr][source], value)
            line.append(value)
        framed.append(line)
    grid = []
    for r in range(PITCH):
        line = []
        for cc in range(window):
            value = framed[r + HALO][cc]
            if r < HALO:
                value = value + next_row(framed[r + HALO + PITCH][cc])
            if r >= PITCH - HALO:
                value = value + previous_row(framed[r + HALO - PITCH][cc])
            line.append(value)
        grid.append(line)
    slot = sub & 3
    low_lanes = lane < EC
    high_lanes = lane >= LANES - EC
    line = []
    for cc in range(window):
        value = jnp.where(low_lanes & (slot == 0), roll(roll(framed[10][cc], EC, 1), -3, 0), 0.0)
        value = jnp.where(low_lanes & (slot == 1), roll(roll(framed[11][cc], EC, 1), -2, 0), value)
        value = jnp.where(high_lanes & (slot == 3), roll(roll(framed[0][cc], -EC, 1), 3, 0), value)
        value = jnp.where(high_lanes & (slot == 2), roll(roll(framed[1][cc], -EC, 1), 2, 0), value)
        line.append(value)
    grid.append(line)
    elem_col = lane & (EC - 1)
    parts = [[] for _ in range(SUB)]
    edges = [jnp.zeros(shape, jnp.float32) for _ in range(SUB)]
    for r in range(GROUPS):
        cells = []
        for c in range(PITCH):
            value = grid[r][c + HALO]
            if c < HALO:
                value = value + jnp.where(elem_col == 0, 0.0, roll(grid[r][c + HALO + PITCH], 1, 1))
            if c >= PITCH - HALO:
                value = value + jnp.where(
                    elem_col == EC - 1, 0.0, roll(grid[r][c + HALO - PITCH], -1, 1)
                )
            cells.append(value)
        turned = transpose_blocks([cells[c] for c in PARITY_ORDER], lane)
        for e in range(SUB):
            parts[e].append(turned[e])
            start = EC * e
            edge = edges[e]
            edge = jnp.where(lane == r, roll(grid[r][10], r - start - (EC - 1), 1), edge)
            edge = jnp.where(lane == 64 + r, roll(grid[r][11], 64 + r - start - (EC - 1), 1), edge)
            edge = jnp.where(lane == 63 - r, roll(grid[r][0], 63 - r - start, 1), edge)
            edge = jnp.where(lane == 127 - r, roll(grid[r][1], 127 - r - start, 1), edge)
            edges[e] = edge
    return [parts[e] + [edges[e]] for e in range(SUB)]


def transpose_blocks(values, lane):
    block = lane // EC
    for step in (4, 2, 1):
        mask = (block & step) == 0
        result = list(values)
        for i in range(SUB):
            if i & step:
                continue
            a, b = values[i], values[i + step]
            result[i] = jnp.where(mask, a, roll(b, EC * step, 1))
            result[i + step] = jnp.where(mask, roll(a, -EC * step, 1), b)
        values = result
    return values


def halves(a, b):
    low = lane_index(a.shape) < 64
    return jnp.where(low, a, roll(b, 64, 1)), jnp.where(low, roll(a, 64, 1), b)


def half_rows(a, b):
    top = sub_index(a.shape) < 4
    return jnp.where(top, a, roll(b, 4, 0)), jnp.where(top, roll(a, 4, 0), b)


def gather_rows(part, edge, count):
    sample = edge(0)
    lane = lane_index(sample.shape)
    from_low = (lane == 0) | (lane == 64)
    from_high = (lane == 63) | (lane == 127)
    rows = []
    for j in range(count):
        groups = []
        for r in range(GROUPS):
            value = part(j, r)
            if j > 0:
                value = value + jnp.where(from_low, roll(edge(j - 1), -r, 1), 0.0)
            if j < count - 1:
                value = value + jnp.where(from_high, roll(edge(j + 1), r, 1), 0.0)
            groups.append(value)
        first, second = [], []
        for parity in range(2):
            for b in range(2):
                low, high = half_rows(groups[parity + 4 * b], groups[parity + 4 * b + 2])
                first.append(low)
                second.append(high)
        low, high = half_rows(groups[8], groups[8])
        first.append(low)
        second.append(high)
        rows.append(jnp.concatenate(first + second, axis=0))
    even, odd = [], []
    for j in range(0, count, 2):
        low, high = halves(rows[j], rows[j + 1])
        even.append(low)
        odd.append(high)
    return jnp.concatenate(even, axis=1), jnp.concatenate(odd, axis=1)


def join_spectrum(even, odd):
    quarter = even.shape[1] // 2
    ec, es = even[:, :quarter], even[:, quarter:]
    oc, os = odd[:, :quarter], odd[:, quarter:]
    return [ec + oc, es - os, ec - oc, es + os]


def split_spectrum(blocks):
    a, b, c, d = blocks
    return (
        jnp.concatenate([a + c, d + b], axis=1),
        jnp.concatenate([a - c, d - b], axis=1),
    )


def scatter_rows(even, odd, count, put):
    rows = []
    for j in range(0, count, 2):
        tile = slice(64 * j, 64 * j + LANES)
        rows.extend(halves(even[:, tile], odd[:, tile]))
    blocks = []
    for j in range(count):
        first = [rows[j][8 * i : 8 * i + 8] for i in range(5)]
        second = [rows[j][40 + 8 * i : 48 + 8 * i] for i in range(5)]
        groups = [None] * GROUPS
        for parity in range(2):
            for b in range(2):
                low, high = half_rows(first[2 * parity + b], second[2 * parity + b])
                groups[parity + 4 * b] = low
                groups[parity + 4 * b + 2] = high
        sub = sub_index(first[4].shape)
        tail = jnp.where(sub < 4, roll(first[4], 4, 0), second[4])
        head = jnp.where(sub < 4, first[4], roll(second[4], 4, 0))
        groups[8] = jnp.where((sub & 2) == 0, head, tail)
        blocks.append(groups)
    lane = lane_index(blocks[0][0].shape)
    for j in range(count):
        edge = jnp.zeros(blocks[0][0].shape, jnp.float32)
        for r in range(GROUPS):
            if j < count - 1:
                edge = jnp.where(
                    (lane == r) | (lane == 64 + r), roll(blocks[j + 1][r], r, 1), edge
                )
            if j > 0:
                edge = jnp.where(
                    (lane == 63 - r) | (lane == 127 - r), roll(blocks[j - 1][r], -r, 1), edge
                )
        put(j, blocks[j] + [edge])


def read_samples(part, edge, row_shift, col_shift, put):
    shape = row_shift.shape
    lane = lane_index(shape)
    sub = sub_index(shape)
    elem_col = lane & (EC - 1)
    window = STEN + 2 * HALO
    grid = []
    for r in range(GROUPS):
        turned = transpose_blocks([part(e, r) for e in range(SUB)], lane)
        cells = [None] * PITCH
        for place, c in enumerate(PARITY_ORDER):
            cells[c] = turned[place]
        line = [None] * window
        for c in range(PITCH):
            line[c + HALO] = cells[c]
        after = [roll(cells[c], -1, 1) for c in range(HALO)]
        before = [roll(cells[PITCH - HALO + c], 1, 1) for c in range(HALO)]
        for e in range(SUB):
            start = EC * e
            last = lane == start + EC - 1
            zero = lane == start
            after[0] = jnp.where(last, roll(edge(e), start + EC - 1 - r, 1), after[0])
            after[1] = jnp.where(last, roll(edge(e), start + EC - 1 - 64 - r, 1), after[1])
            before[0] = jnp.where(zero, roll(edge(e), start - 63 + r, 1), before[0])
            before[1] = jnp.where(zero, roll(edge(e), start - 127 + r, 1), before[1])
        line[0], line[1] = before
        line[10], line[11] = after
        grid.append(line)
    slot = sub & 3
    first_row = (slot == 0) & (lane < EC)
    last_row = (slot == 3) & (lane >= LANES - EC)
    framed = [[None] * window for _ in range(window)]
    for cc in range(window):
        for r in range(PITCH):
            framed[r + HALO][cc] = grid[r][cc]
        outer = grid[8][cc]
        below = roll(outer, -EC, 1)
        above = roll(outer, EC, 1)
        framed[10][cc] = jnp.where(last_row, roll(below, 3, 0), previous_row(grid[0][cc]))
        framed[11][cc] = jnp.where(last_row, roll(below, 2, 0), previous_row(grid[1][cc]))
        framed[0][cc] = jnp.where(first_row, roll(above, -3, 0), next_row(grid[6][cc]))
        framed[1][cc] = jnp.where(first_row, roll(above, -2, 0), next_row(grid[7][cc]))
    for a in range(STEN):
        line = []
        for cc in range(window):
            value = framed[a + HALO][cc]
            for o in range(-HALO, HALO + 1):
                if o:
                    value = jnp.where(row_shift == o, framed[a + HALO + o][cc], value)
            line.append(value)
        for b in range(STEN):
            value = line[b + HALO]
            for o in range(-HALO, HALO + 1):
                if o:
                    value = jnp.where(col_shift == o, line[b + HALO + o], value)
            put(a * STEN + b, value)


def add_outer_rows(chunk, row_count, col_count):
    sub = sub_index((SUB, LANES))
    even, odd = [], []
    for i in range(row_count):
        for j in range(col_count):
            rows = [chunk(i, j)[8 * k : 8 * k + 8] for k in range(4)]
            if j == 0 and i > 0:
                outer = chunk(i - 1, 0)[32:40]
                rows[0] = rows[0] + jnp.where(sub == 0, outer, 0.0)
                rows[2] = rows[2] + jnp.where(sub == 0, roll(outer, -1, 0), 0.0)
            if j == col_count - 1 and i < row_count - 1:
                outer = chunk(i + 1, j)[32:40]
                rows[1] = rows[1] + jnp.where(sub == 7, outer, 0.0)
                rows[3] = rows[3] + jnp.where(sub == 7, roll(outer, 1, 0), 0.0)
            even.extend(rows[:2])
            odd.extend(rows[2:])
    return jnp.concatenate(even, axis=0), jnp.concatenate(odd, axis=0)


def spread_outer_rows(even, odd, row_count, col_count, put):
    sub = sub_index((SUB, LANES))

    def block(i, j):
        start = 16 * (i * col_count + j)
        return [even[start : start + 8], even[start + 8 : start + 16],
                odd[start : start + 8], odd[start + 8 : start + 16]]

    for i in range(row_count):
        for j in range(col_count):
            outer = jnp.zeros((SUB, LANES), jnp.float32)
            if j == 0 and i < row_count - 1:
                rows = block(i + 1, 0)
                outer = jnp.where(sub == 0, rows[0], jnp.where(sub == 1, roll(rows[2], 1, 0), outer))
            if j == col_count - 1 and i > 0:
                rows = block(i - 1, j)
                outer = jnp.where(sub == 7, rows[1], jnp.where(sub == 6, roll(rows[3], -1, 0), outer))
            put(i, j, block(i, j) + [outer])


def two_terms(value):
    high = value.astype(jnp.bfloat16)
    return high, (value - high.astype(jnp.float32)).astype(jnp.bfloat16)


def dot(left, right, dims=((1,), (0,))):
    return lax.dot_general(left, right, (dims, ((), ())), preferred_element_type=jnp.float32)


def even_positions(row_count, col_count):
    j, c, e = np.meshgrid(np.arange(col_count), np.arange(4), np.arange(EC), indexing="ij")
    columns = (LANES * j + PITCH * e + 2 * c).reshape(-1)
    i, j, b, h, t = np.meshgrid(
        np.arange(row_count), np.arange(col_count), np.arange(2), np.arange(2), np.arange(TILES),
        indexing="ij",
    )
    rows = (ER * PITCH * i + SUB * PITCH * t + PITCH * j + 2 * h + 4 * b).reshape(-1)
    return columns, rows


def basis_tables(positions, length, lane_major):
    quarter = length // 4
    outer = np.arange(quarter // LANES) * LANES
    inner = np.arange(LANES)
    tables = []
    for parity in range(2):
        x = positions + parity
        coarse = 2.0 * np.pi * (x[:, None] * outer[None, :] % length) / length
        fine = 2.0 * np.pi * (x[:, None] * inner[None, :] % length) / length
        sign = np.where(positions % 4 == 0, 1.0, -1.0)
        if lane_major:
            shape_c, shape_f, shape_s = (1, 2), (0, 2), (0, 1)
        parts = [np.cos(coarse), np.sin(coarse), np.cos(fine), np.sin(fine)]
        parts = [np.asarray(p, np.float32) for p in parts]
        sign = np.asarray(sign, np.float32)
        if lane_major:
            cc, cs = (jnp.asarray(np.ascontiguousarray(p.T))[:, None, :] for p in parts[:2])
            fc, fs = (jnp.asarray(np.ascontiguousarray(p.T))[None, :, :] for p in parts[2:])
            sg = jnp.asarray(sign)[None, :]
            shape = (quarter, x.shape[0])
            axis, order = 0, lax.broadcasted_iota(jnp.int32, shape, 0)
        else:
            cc, cs = (jnp.asarray(p)[:, :, None] for p in parts[:2])
            fc, fs = (jnp.asarray(p)[:, None, :] for p in parts[2:])
            sg = jnp.asarray(sign)[:, None]
            shape = (x.shape[0], quarter)
            axis, order = 1, lax.broadcasted_iota(jnp.int32, shape, 1)
        cosine = (cc * fc - cs * fs).reshape(shape)
        if parity == 0:
            sine = (cs * fc + cc * fs).reshape(shape)
            second = jnp.where(order == 0, 1.0, -sine) * sg
        else:
            second = cosine * sg
        full = jnp.concatenate([cosine, second], axis=axis)
        high = lax.reduce_precision(full, 8, 7)
        tables.append(high.astype(jnp.bfloat16))
        tables.append((full - high).astype(jnp.bfloat16))
    return tables


def tiled_shifts(shifts_ref, which):
    rows = [shifts_ref[which : which + 1, LANES * t : LANES * (t + 1)] for t in range(TILES)]
    return jnp.concatenate(rows * RHS, axis=0)


def charge_kernel(currents_ref, projection_ref, shifts_ref, out_ref, current, partial, stencil):
    step = pl.program_id(0)

    @pl.when(step == 0)
    def _():
        current[...] = currents_ref[...].astype(jnp.bfloat16).astype(jnp.float32)

    for t in range(TILES):
        lanes = slice(LANES * t, LANES * (t + 1))
        totals = [[None] * RHS for _ in range(STEN)]
        for b in range(0, BASIS, 16):
            values = [
                [current[q, b + 8 * h : b + 8 * h + 8, lanes] for h in range(2)] for q in range(RHS)
            ]
            for s in range(STEN):
                weight = projection_ref[s, b : b + 16, lanes].astype(jnp.float32)
                for q in range(RHS):
                    term = weight[:8] * values[q][0] + weight[8:] * values[q][1]
                    totals[s][q] = term if totals[s][q] is None else totals[s][q] + term
        for s in range(STEN):
            for q in range(RHS):
                partial[s, q * TILES + t] = totals[s][q]
    for s in range(STEN):
        stencil[step * STEN + s] = sum_rows([partial[s, i] for i in range(SUB)])

    @pl.when(step == pl.num_programs(0) - 1)
    def _():
        chunks = place_charges(
            lambda s: stencil[s], tiled_shifts(shifts_ref, 0), tiled_shifts(shifts_ref, 1)
        )
        for e in range(SUB):
            out_ref[e] = jnp.concatenate(chunks[e], axis=0).astype(out_ref.dtype)


def column_kernel(count, rows_ref, eh, el, oh, ol, out_ref):
    def part(j, r):
        return rows_ref[j, 8 * r : 8 * r + 8, :].astype(jnp.float32)

    even, odd = gather_rows(part, lambda j: part(j, GROUPS), count)
    even = even.astype(jnp.bfloat16)
    odd = odd.astype(jnp.bfloat16)
    blocks = join_spectrum(
        dot(even, eh[...]) + dot(even, el[...]), dot(odd, oh[...]) + dot(odd, ol[...])
    )
    half = out_ref.shape[1]
    device = 0
    for block in blocks:
        for t in range(0, block.shape[1], LANES):
            for chunk in halves(block[:half, t : t + LANES], block[half:, t : t + LANES]):
                out_ref[device] = chunk.astype(out_ref.dtype)
                device += 1


def row_kernel(row_count, col_count, in_ref, eh, el, oh, ol, teh, tel, toh, tol, sum_ref, diff_ref, out_ref):
    even, odd = add_outer_rows(
        lambda i, j: in_ref[i * col_count + j].astype(jnp.float32), row_count, col_count
    )
    even = even.astype(jnp.bfloat16)
    odd = odd.astype(jnp.bfloat16)
    a = dot(eh[...], even) + dot(el[...], even)
    b = dot(oh[...], odd) + dot(ol[...], odd)
    plus, minus = sum_ref[...], diff_ref[...]

    def back(value, high_ref, low_ref):
        high, low = two_terms(value)
        both = dot(high_ref[...], jnp.concatenate([high, low], axis=1))
        return both[:, :LANES] + both[:, LANES:] + dot(low_ref[...], high)

    def put(i, j, parts):
        out_ref[i * col_count + j] = jnp.concatenate(parts, axis=0).astype(out_ref.dtype)

    spread_outer_rows(
        back(a * plus + b * minus, teh, tel),
        back(a * minus + b * plus, toh, tol),
        row_count,
        col_count,
        put,
    )


def grid_kernel(count, in_ref, eh, el, oh, ol, out_ref):
    devices = in_ref.shape[0]
    first, second = [], []
    for d in range(0, devices, 2):
        low, high = halves(in_ref[d].astype(jnp.float32), in_ref[d + 1].astype(jnp.float32))
        first.append(low)
        second.append(high)
    per_block = devices // 8
    blocks = []
    for k in range(4):
        span = slice(per_block * k, per_block * (k + 1))
        blocks.append(
            jnp.concatenate(
                [jnp.concatenate(first[span], axis=1), jnp.concatenate(second[span], axis=1)], axis=0
            )
        )
    contract = ((1,), (1,))

    def back(value, high_ref, low_ref):
        high, low = two_terms(value)
        both = dot(jnp.concatenate([high, low], axis=0), high_ref[...], contract)
        half = high.shape[0]
        return both[:half] + both[half:] + dot(high, low_ref[...], contract)

    even, odd = split_spectrum(blocks)

    def put(j, parts):
        out_ref[j] = jnp.concatenate(parts, axis=0).astype(out_ref.dtype)

    scatter_rows(back(even, eh, el), back(odd, oh, ol), count, put)


def far_kernel(grid_ref, projection_ref, shifts_ref, near_ref, out_ref, samples):
    @pl.when(pl.program_id(0) == 0)
    def _():
        def part(e, r):
            return grid_ref[e, 8 * r : 8 * r + 8, :].astype(jnp.float32)

        def put(s, value):
            samples[s] = value

        read_samples(
            part,
            lambda e: part(e, GROUPS),
            tiled_shifts(shifts_ref, 0),
            tiled_shifts(shifts_ref, 1),
            put,
        )

    depth = out_ref.shape[1]

    def add_row(a, totals):
        totals = list(totals)
        for b in range(STEN):
            s = a * STEN + b
            for t in range(TILES):
                weight = projection_ref[s, :, LANES * t : LANES * (t + 1)].astype(jnp.float32)
                for q in range(RHS):
                    index = q * TILES + t
                    totals[index] = totals[index] + weight * samples[s, index : index + 1, :]
        return tuple(totals)

    start = tuple(
        near_ref[q, :, LANES * t : LANES * (t + 1)] for q in range(RHS) for t in range(TILES)
    )
    totals = lax.fori_loop(0, STEN, add_row, start)
    for q in range(RHS):
        for t in range(TILES):
            out_ref[q, :, LANES * t : LANES * (t + 1)] = totals[q * TILES + t]


def near_kernel(own_ref, left_ref, right_ref, above_ref, below_ref, partners_ref, blocks_ref, out_ref, picked):
    @pl.when(pl.program_id(0) == 0)
    def _():
        lane = lane_index((BASIS, LANES))
        elem_col = lane & (EC - 1)

        def three(own, left, right):
            own, left, right = (v.astype(jnp.float32) for v in (own, left, right))
            return (
                jnp.where(elem_col == 0, roll(left, 1 - EC, 1), roll(own, 1, 1)),
                own,
                jnp.where(elem_col == EC - 1, roll(right, EC - 1, 1), roll(own, -1, 1)),
            )

        for q in range(RHS):
            tiles = [three(above_ref[0, q], above_ref[1, q], above_ref[2, q])]
            for t in range(TILES):
                lanes = slice(LANES * t, LANES * (t + 1))
                tiles.append(three(own_ref[q, :, lanes], left_ref[q, :, lanes], right_ref[q, :, lanes]))
            tiles.append(three(below_ref[0, q], below_ref[1, q], below_ref[2, q]))
            for t in range(TILES):
                lanes = slice(LANES * t, LANES * (t + 1))
                before, here, after = tiles[t : t + 3]
                codes = [partners_ref[k : k + 1, lanes] for k in range(NEIGH)]
                chosen = [here[1]] * NEIGH
                for c in range(3):
                    views = (
                        jnp.where(lane < EC, roll(before[c], EC, 1), roll(here[c], EC, 1)),
                        here[c],
                        jnp.where(lane >= LANES - EC, roll(after[c], -EC, 1), roll(here[c], -EC, 1)),
                    )
                    for r in range(3):
                        if r == 1 and c == 1:
                            continue
                        for k in range(1, NEIGH):
                            chosen[k] = jnp.where(codes[k] == 3 * r + c, views[r], chosen[k])
                for k in range(NEIGH):
                    picked[k, q, :, lanes] = chosen[k]

    def one_tile(t, carry):
        lanes = pl.ds(pl.multiple_of(t * LANES, LANES), LANES)
        totals = [[None] * RHS for _ in range(SUB)]
        for k in range(NEIGH):
            for b in range(0, BASIS, 16):
                values = [
                    [picked[k, q, b + 8 * h : b + 8 * h + 8, lanes] for h in range(2)]
                    for q in range(RHS)
                ]
                for a in range(SUB):
                    weight = blocks_ref[k, a, b : b + 16, lanes].astype(jnp.float32)
                    for q in range(RHS):
                        term = weight[:8] * values[q][0] + weight[8:] * values[q][1]
                        totals[a][q] = term if totals[a][q] is None else totals[a][q] + term
        for q in range(RHS):
            out_ref[q, :, lanes] = sum_rows([totals[a][q] for a in range(SUB)])
        return carry

    lax.fori_loop(0, TILES, one_tile, 0)


def neighbours(value, axis):
    count = lax.axis_size(axis)
    forward = [(i, i + 1) for i in range(count - 1)]
    backward = [(i + 1, i) for i in range(count - 1)]
    return forward, backward


def whole(shape):
    return pl.BlockSpec(shape, lambda *_: (0,) * len(shape))


def shards_real(currents, projection, near_blocks, partners, shifts, green):
    row_count = lax.axis_size("row")
    col_count = lax.axis_size("col")
    elements = currents.shape[2]
    width = col_count * LANES
    length = 2 * width
    quarter = length // 4
    f32, b16 = jnp.float32, jnp.bfloat16
    struct = jax.ShapeDtypeStruct
    devices = row_count * col_count

    charges = pl.pallas_call(
        charge_kernel,
        grid=(STEN,),
        in_specs=[
            whole((RHS, BASIS, elements)),
            pl.BlockSpec((STEN, BASIS, elements), lambda i: (i, 0, 0)),
            whole((2, elements)),
        ],
        out_specs=whole((SUB, 80, LANES)),
        out_shape=struct((SUB, 80, LANES), b16),
        scratch_shapes=[
            pltpu.VMEM((RHS, BASIS, elements), f32),
            pltpu.VMEM((STEN, SUB, SUB, LANES), f32),
            pltpu.VMEM((STEN * STEN, SUB, LANES), f32),
        ],
        name="charges",
    )(currents, projection, shifts)
    slab = lax.all_to_all(charges, "col", 0, 0, tiled=True)

    columns, rows = even_positions(row_count, col_count)
    col_tables = basis_tables(columns, length, False)
    row_tables = basis_tables(rows, length, True)
    back_tables = basis_tables(rows, length, False)
    weight_k = jnp.where(jnp.arange(length) % quarter == 0, 1.0, 2.0).astype(f32)
    mine = lax.axis_index("row") * col_count + lax.axis_index("col")
    depth = green.shape[0]
    weight_m = jnp.where((mine * depth + jnp.arange(depth)) % quarter == 0, 1.0, 2.0).astype(f32)
    scaled = green * (weight_m * (1.0 / (length * length)))[:, None] * weight_k[None, :]
    scaled = jnp.concatenate([scaled, scaled], axis=0).T
    upper = jnp.concatenate([scaled[:quarter], scaled[3 * quarter :]], axis=0)
    lower = jnp.concatenate([scaled[2 * quarter : 3 * quarter], scaled[quarter : 2 * quarter]], axis=0)

    spectrum = pl.pallas_call(
        functools.partial(column_kernel, col_count),
        out_shape=struct((devices, 40, LANES), b16),
        name="columns",
    )(slab, *col_tables)
    arrived = lax.all_to_all(spectrum, ("row", "col"), 0, 0, tiled=True)
    rows_back = pl.pallas_call(
        functools.partial(row_kernel, row_count, col_count),
        out_shape=struct((devices, 40, LANES), b16),
        name="rows",
    )(arrived, *row_tables, *back_tables, upper + lower, upper - lower)
    returned = lax.all_to_all(rows_back, ("row", "col"), 0, 0, tiled=True)
    potential = pl.pallas_call(
        functools.partial(grid_kernel, col_count),
        out_shape=struct((SUB, 80, LANES), b16),
        name="grid",
    )(returned, *col_tables)
    pieces = lax.all_to_all(potential, "col", 0, 0, tiled=True)

    half = currents.astype(b16)
    forward, backward = neighbours(half, "col")
    left = lax.ppermute(half, "col", forward)
    right = lax.ppermute(half, "col", backward)
    three = jnp.stack([half, left, right])
    forward, backward = neighbours(half, "row")
    above = lax.ppermute(three[..., elements - LANES :], "row", forward)
    below = lax.ppermute(three[..., :LANES], "row", backward)
    near = pl.pallas_call(
        near_kernel,
        grid=(BASIS // SUB,),
        in_specs=[
            whole((RHS, BASIS, elements)),
            whole((RHS, BASIS, elements)),
            whole((RHS, BASIS, elements)),
            whole((3, RHS, BASIS, LANES)),
            whole((3, RHS, BASIS, LANES)),
            whole((NEIGH, elements)),
            pl.BlockSpec((NEIGH, SUB, BASIS, elements), lambda i: (0, i, 0, 0)),
        ],
        out_specs=pl.BlockSpec((RHS, SUB, elements), lambda i: (0, i, 0)),
        out_shape=struct((RHS, BASIS, elements), f32),
        scratch_shapes=[pltpu.VMEM((NEIGH, RHS, BASIS, elements), f32)],
        name="near",
    )(half, left, right, above, below, partners, near_blocks)

    depth = 16
    return pl.pallas_call(
        far_kernel,
        grid=(BASIS // depth,),
        in_specs=[
            whole((SUB, 80, LANES)),
            pl.BlockSpec((STEN * STEN, depth, elements), lambda i: (0, i, 0)),
            whole((2, elements)),
            pl.BlockSpec((RHS, depth, elements), lambda i: (0, i, 0)),
        ],
        out_specs=pl.BlockSpec((RHS, depth, elements), lambda i: (0, i, 0)),
        out_shape=struct((RHS, BASIS, elements), f32),
        scratch_shapes=[pltpu.VMEM((STEN * STEN, SUB, LANES), f32)],
        name="far",
    )(pieces, projection, shifts, near)


def shards(currents, projection, near_blocks, partners, shifts, green):
    row_count = lax.axis_size("row")
    col_count = lax.axis_size("col")
    fits = col_count == SUB and green.shape[0] == 64 and 2 * row_count * col_count == green.shape[0]
    if fits and currents.shape[2] == TILES * LANES and row_count * ER == col_count * EC:
        return shards_real(currents, projection, near_blocks, partners, shifts, green)
    return shards_general(currents, projection, near_blocks, partners, shifts, green)


def solution(mesh):
    in_specs = (
        P(None, None, ("row", "col")),
        P(None, None, ("row", "col")),
        P(None, None, None, ("row", "col")),
        P(None, ("row", "col")),
        P(None, ("row", "col")),
        P(("row", "col"), None),
    )
    out_specs = P(None, None, ("row", "col"))
    return jax.shard_map(shards, mesh=mesh, in_specs=in_specs, out_specs=out_specs, check_vma=False)
```

```python
import functools
import math

import jax
import jax.numpy as jnp
import numpy as np
from jax import lax
from jax.experimental import pallas as pl
from jax.experimental.pallas import tpu as pltpu
from jax.sharding import PartitionSpec as P

BASIS = 64
STEN = 8
PITCH = 8
HALO = 2
NEIGH = 4
RHS = 2
ER = 32
EC = 16


def extended_2(block, sides, width):
    for axis, dim in sides:
        count = lax.axis_size(axis)
        forward = [(i, i + 1) for i in range(count - 1)]
        backward = [(target, source) for source, target in forward]
        low = lax.ppermute(
            lax.slice_in_dim(block, block.shape[dim] - width, None, axis=dim), axis, forward
        )
        high = lax.ppermute(lax.slice_in_dim(block, 0, width, axis=dim), axis, backward)
        block = jnp.concatenate([low, block, high], axis=dim)
    return block


def angle_table(first_size, second_size, modulus, direction):
    left_index = jnp.arange(first_size, dtype=jnp.int32)
    right_index = jnp.arange(second_size, dtype=jnp.int32)
    turn_count = left_index[:, None] * right_index[None, :] % modulus
    angles = turn_count.astype(jnp.float32) * (2.0 * math.pi / modulus)
    return (jnp.cos(angles), direction * jnp.sin(angles))


def complex_apply(real_part, imag_part, cosine, sine_table, pattern):
    highest = lax.Precision.HIGHEST
    out_real = jnp.einsum(pattern, real_part, cosine, precision=highest)
    out_imag = jnp.einsum(pattern, real_part, sine_table, precision=highest)
    if imag_part is not None:
        out_real = out_real - jnp.einsum(pattern, imag_part, sine_table, precision=highest)
        out_imag = out_imag + jnp.einsum(pattern, imag_part, cosine, precision=highest)
    return (out_real, out_imag)


def transform_last(real_part, imag_part, length, count_in, count_out, direction):
    leading = real_part.shape[:-1]
    inner_size = 128
    outer_size = length // inner_size
    rows_in = count_in // inner_size
    kept_count = count_out // outer_size
    shaped_real = real_part.reshape(leading + (rows_in, inner_size))
    shaped_imag = None
    if imag_part is not None:
        shaped_imag = imag_part.reshape(leading + (rows_in, inner_size))
    cosine, sine_table = angle_table(rows_in, outer_size, outer_size, direction)
    first_real, first_imag = complex_apply(
        shaped_real, shaped_imag, cosine, sine_table, "...ab,ak->...kb"
    )
    twist_cos, twist_sin = angle_table(outer_size, inner_size, length, direction)
    turned_real = first_real * twist_cos - first_imag * twist_sin
    turned_imag = first_real * twist_sin + first_imag * twist_cos
    cosine, sine_table = angle_table(inner_size, kept_count, inner_size, direction)
    last_real, last_imag = complex_apply(
        turned_real, turned_imag, cosine, sine_table, "...kb,bj->...jk"
    )
    out_shape = leading + (kept_count * outer_size,)
    return (last_real.reshape(out_shape), last_imag.reshape(out_shape))


def place_shifted(blocks, amount, dim_index):
    new_shape = list(blocks.shape)
    new_shape[dim_index] = new_shape[dim_index] + 2 * HALO
    result = jnp.zeros(tuple(new_shape), blocks.dtype)
    for offset in range(-HALO, HALO + 1):
        widths = [(0, 0)] * blocks.ndim
        widths[dim_index] = (HALO + offset, HALO - offset)
        result = jnp.where(amount == offset, jnp.pad(blocks, widths), result)
    return result


def pick_shifted(windows, amount, dim_index):
    new_shape = list(windows.shape)
    new_shape[dim_index] = STEN
    result = jnp.zeros(tuple(new_shape), windows.dtype)
    for offset in range(-HALO, HALO + 1):
        piece = lax.slice_in_dim(windows, HALO + offset, HALO + offset + STEN, axis=dim_index)
        result = jnp.where(amount == offset, piece, result)
    return result


def intersection_add(framed, dim_index):
    element_count = framed.shape[dim_index]
    window_size = framed.shape[dim_index + 1]
    head_part = lax.slice_in_dim(framed, 0, PITCH, axis=dim_index + 1)
    tail_part = lax.slice_in_dim(framed, PITCH, window_size, axis=dim_index + 1)
    widths = [(0, 0)] * framed.ndim
    widths[dim_index + 1] = (0, 2 * PITCH - window_size)
    tail_part = jnp.pad(tail_part, widths)
    merged = framed.shape[:dim_index] + (element_count * PITCH,) + framed.shape[dim_index + 2 :]
    head_part = head_part.reshape(merged)
    tail_part = tail_part.reshape(merged)
    front_pad = [(0, 0)] * len(merged)
    front_pad[dim_index] = (0, PITCH)
    back_pad = [(0, 0)] * len(merged)
    back_pad[dim_index] = (PITCH, 0)
    summed = jnp.pad(head_part, front_pad) + jnp.pad(tail_part, back_pad)
    return lax.slice_in_dim(summed, 0, element_count * PITCH + 2 * HALO, axis=dim_index)


def cut_windows(field, dim_index):
    element_count = (field.shape[dim_index] - 2 * HALO) // PITCH
    widths = [(0, 0)] * field.ndim
    widths[dim_index] = (0, PITCH - 2 * HALO)
    extended = jnp.pad(field, widths)
    split_shape = field.shape[:dim_index] + (element_count, PITCH) + field.shape[dim_index + 1 :]
    head_part = lax.slice_in_dim(extended, 0, element_count * PITCH, axis=dim_index).reshape(
        split_shape
    )
    tail_part = lax.slice_in_dim(
        extended, PITCH, PITCH + element_count * PITCH, axis=dim_index
    ).reshape(split_shape)
    tail_part = lax.slice_in_dim(tail_part, 0, 2 * HALO, axis=dim_index + 1)
    return jnp.concatenate([head_part, tail_part], axis=dim_index + 1)


def fold_margin(padded, dim_index):
    full_size = padded.shape[dim_index]
    inner_size = full_size - 4 * HALO
    core_part = lax.slice_in_dim(padded, 2 * HALO, 2 * HALO + inner_size, axis=dim_index)
    upper_part = lax.slice_in_dim(padded, 0, HALO, axis=dim_index)
    lower_part = lax.slice_in_dim(padded, full_size - HALO, full_size, axis=dim_index)
    upper_pad = [(0, 0)] * padded.ndim
    upper_pad[dim_index] = (0, inner_size - HALO)
    lower_pad = [(0, 0)] * padded.ndim
    lower_pad[dim_index] = (inner_size - HALO, 0)
    return core_part + jnp.pad(upper_part, upper_pad) + jnp.pad(lower_part, lower_pad)


def shards_general(currents, projection, near_blocks, partners, shifts, green):
    row_count = lax.axis_size("row")
    col_count = lax.axis_size("col")
    device_count = row_count * col_count
    elements = ER * EC
    cur_half = currents.astype(jnp.bfloat16)
    spread = extended_2(cur_half.reshape(RHS, BASIS, ER, EC), (("row", 2), ("col", 3)), 1)
    views = []
    for symbol in range(9):
        row_start = symbol // 3
        col_start = symbol % 3
        views.append(
            spread[:, :, row_start : row_start + ER, col_start : col_start + EC].reshape(
                RHS, BASIS, elements
            )
        )
    picked = []
    for neighbour_slot in range(NEIGH):
        chosen = jnp.zeros((RHS, BASIS, elements), jnp.bfloat16)
        for symbol in range(9):
            chosen = jnp.where(partners[neighbour_slot] == symbol, views[symbol], chosen)
        picked.append(chosen)
    near_term = jnp.einsum(
        "kabn,kqbn->qan", near_blocks, jnp.stack(picked), preferred_element_type=jnp.float32
    )
    stencil = jnp.einsum("sbn,qbn->qsn", projection, cur_half, preferred_element_type=jnp.float32)
    blocks = stencil.reshape(RHS, STEN, STEN, elements)
    framed = place_shifted(place_shifted(blocks, shifts[0], 1), shifts[1], 2)
    window_size = STEN + 2 * HALO
    framed = framed.reshape(RHS, window_size, window_size, ER, EC).transpose(0, 3, 1, 4, 2)
    extended = intersection_add(intersection_add(framed, 1), 2)
    padded = extended_2(extended, (("row", 1), ("col", 2)), HALO)
    charges = fold_margin(fold_margin(padded, 1), 2)
    slab = lax.all_to_all(charges, "col", split_axis=1, concat_axis=2, tiled=True)
    slab_rows = slab.shape[1]
    width_cols = slab.shape[2]
    length_cols = 2 * width_cols
    block_cols = length_cols // device_count
    grid_rows = slab_rows * device_count
    length_rows = 2 * grid_rows
    fwd_real, fwd_imag = transform_last(slab, None, length_cols, width_cols, length_cols, -1.0)
    out_real = fwd_real.reshape(RHS, slab_rows, device_count, block_cols)
    out_imag = fwd_imag.reshape(RHS, slab_rows, device_count, block_cols)
    arrived = (
        lax.all_to_all(out_real, ("row", "col"), split_axis=2, concat_axis=2, tiled=True),
        lax.all_to_all(out_imag, ("row", "col"), split_axis=2, concat_axis=2, tiled=True),
    )
    col_real = arrived[0].transpose(0, 3, 2, 1).reshape(RHS, block_cols, grid_rows)
    col_imag = arrived[1].transpose(0, 3, 2, 1).reshape(RHS, block_cols, grid_rows)
    spec_real, spec_imag = transform_last(
        col_real, col_imag, length_rows, grid_rows, length_rows, -1.0
    )
    spec_real = spec_real * green
    spec_imag = spec_imag * green
    back_real, back_imag = transform_last(
        spec_real, spec_imag, length_rows, length_rows, grid_rows, 1.0
    )
    send_real = back_real.reshape(RHS, block_cols, device_count, slab_rows)
    send_imag = back_imag.reshape(RHS, block_cols, device_count, slab_rows)
    returned = (
        lax.all_to_all(send_real, ("row", "col"), split_axis=2, concat_axis=2, tiled=True),
        lax.all_to_all(send_imag, ("row", "col"), split_axis=2, concat_axis=2, tiled=True),
    )
    rows_real = returned[0].transpose(0, 3, 2, 1).reshape(RHS, slab_rows, length_cols)
    rows_imag = returned[1].transpose(0, 3, 2, 1).reshape(RHS, slab_rows, length_cols)
    final_real, final_imag = transform_last(
        rows_real, rows_imag, length_cols, length_cols, width_cols, 1.0
    )
    potential_slab = final_real * (1.0 / (length_rows * length_cols))
    potential = lax.all_to_all(potential_slab, "col", split_axis=2, concat_axis=1, tiled=True)
    rimmed = extended_2(potential, (("row", 1), ("col", 2)), HALO)
    windows = cut_windows(cut_windows(rimmed, 1), 3)
    windows = windows.transpose(0, 2, 4, 1, 3).reshape(RHS, window_size, window_size, elements)
    samples = pick_shifted(pick_shifted(windows, shifts[0], 1), shifts[1], 2).reshape(
        RHS, STEN * STEN, elements
    )
    sample_high = samples.astype(jnp.bfloat16)
    sample_low = (samples - sample_high.astype(jnp.float32)).astype(jnp.bfloat16)
    far_term = jnp.einsum(
        "sbn,qsn->qbn", projection, sample_high, preferred_element_type=jnp.float32
    )
    far_term = far_term + jnp.einsum(
        "sbn,qsn->qbn", projection, sample_low, preferred_element_type=jnp.float32
    )
    return far_term + near_term


LANES = 128
SUB = 8
TILES = 4
GROUPS = 9
PARITY_ORDER = (0, 2, 4, 6, 1, 3, 5, 7)


def roll(value, amount, dim):
    return pltpu.roll(value, amount % value.shape[dim], dim)


def lane_index(shape):
    return lax.broadcasted_iota(jnp.int32, shape, len(shape) - 1)


def sub_index(shape):
    return lax.broadcasted_iota(jnp.int32, shape, len(shape) - 2)


def sum_rows(parts):
    sub = sub_index(parts[0].shape)
    top = sub < 4
    level = []
    for i in range(4):
        a, b = parts[i], parts[i + 4]
        level.append(jnp.where(top, a, b) + roll(jnp.where(top, b, a), 4, 0))
    mask = (sub & 2) == 0
    level = [
        jnp.where(mask, level[i], level[i + 2])
        + jnp.where(mask, roll(level[i], -2, 0), roll(level[i + 2], 2, 0))
        for i in range(2)
    ]
    mask = (sub & 1) == 0
    a, b = level
    return jnp.where(mask, a, b) + jnp.where(mask, roll(a, -1, 0), roll(b, 1, 0))


def next_row(value):
    lane = lane_index(value.shape)
    sub = sub_index(value.shape)
    turned = roll(value, EC, 1)
    carried = jnp.where((sub & 3) == 0, 0.0, roll(turned, 1, 0))
    return jnp.where(lane < EC, carried, turned)


def previous_row(value):
    lane = lane_index(value.shape)
    sub = sub_index(value.shape)
    turned = roll(value, -EC, 1)
    carried = jnp.where((sub & 3) == 3, 0.0, roll(turned, -1, 0))
    return jnp.where(lane >= LANES - EC, carried, turned)


def place_charges(stencil, row_shift, col_shift):
    shape = row_shift.shape
    lane = lane_index(shape)
    sub = sub_index(shape)
    window = STEN + 2 * HALO
    row_mask = {o: row_shift == o for o in range(-HALO, HALO + 1)}
    col_mask = {o: col_shift == o for o in range(-HALO, HALO + 1)}
    first = []
    for rr in range(window):
        line = []
        for c in range(STEN):
            value = jnp.zeros(shape, jnp.float32)
            for o in range(-HALO, HALO + 1):
                source = rr - HALO - o
                if 0 <= source < STEN:
                    value = jnp.where(row_mask[o], stencil(source * STEN + c), value)
            line.append(value)
        first.append(line)
    framed = []
    for rr in range(window):
        line = []
        for cc in range(window):
            value = jnp.zeros(shape, jnp.float32)
            for o in range(-HALO, HALO + 1):
                source = cc - HALO - o
                if 0 <= source < STEN:
                    value = jnp.where(col_mask[o], first[rr][source], value)
            line.append(value)
        framed.append(line)
    grid = []
    for r in range(PITCH):
        line = []
        for cc in range(window):
            value = framed[r + HALO][cc]
            if r < HALO:
                value = value + next_row(framed[r + HALO + PITCH][cc])
            if r >= PITCH - HALO:
                value = value + previous_row(framed[r + HALO - PITCH][cc])
            line.append(value)
        grid.append(line)
    slot = sub & 3
    low_lanes = lane < EC
    high_lanes = lane >= LANES - EC
    line = []
    for cc in range(window):
        value = jnp.where(low_lanes & (slot == 0), roll(roll(framed[10][cc], EC, 1), -3, 0), 0.0)
        value = jnp.where(low_lanes & (slot == 1), roll(roll(framed[11][cc], EC, 1), -2, 0), value)
        value = jnp.where(high_lanes & (slot == 3), roll(roll(framed[0][cc], -EC, 1), 3, 0), value)
        value = jnp.where(high_lanes & (slot == 2), roll(roll(framed[1][cc], -EC, 1), 2, 0), value)
        line.append(value)
    grid.append(line)
    elem_col = lane & (EC - 1)
    parts = [[] for _ in range(SUB)]
    edges = [jnp.zeros(shape, jnp.float32) for _ in range(SUB)]
    for r in range(GROUPS):
        cells = []
        for c in range(PITCH):
            value = grid[r][c + HALO]
            if c < HALO:
                value = value + jnp.where(elem_col == 0, 0.0, roll(grid[r][c + HALO + PITCH], 1, 1))
            if c >= PITCH - HALO:
                value = value + jnp.where(
                    elem_col == EC - 1, 0.0, roll(grid[r][c + HALO - PITCH], -1, 1)
                )
            cells.append(value)
        turned = transpose_blocks([cells[c] for c in PARITY_ORDER], lane)
        for e in range(SUB):
            parts[e].append(turned[e])
            start = EC * e
            edge = edges[e]
            edge = jnp.where(lane == r, roll(grid[r][10], r - start - (EC - 1), 1), edge)
            edge = jnp.where(lane == 64 + r, roll(grid[r][11], 64 + r - start - (EC - 1), 1), edge)
            edge = jnp.where(lane == 63 - r, roll(grid[r][0], 63 - r - start, 1), edge)
            edge = jnp.where(lane == 127 - r, roll(grid[r][1], 127 - r - start, 1), edge)
            edges[e] = edge
    return [parts[e] + [edges[e]] for e in range(SUB)]


def transpose_blocks(values, lane):
    block = lane // EC
    for step in (4, 2, 1):
        mask = (block & step) == 0
        result = list(values)
        for i in range(SUB):
            if i & step:
                continue
            a, b = values[i], values[i + step]
            result[i] = jnp.where(mask, a, roll(b, EC * step, 1))
            result[i + step] = jnp.where(mask, roll(a, -EC * step, 1), b)
        values = result
    return values


def halves(a, b):
    low = lane_index(a.shape) < 64
    return jnp.where(low, a, roll(b, 64, 1)), jnp.where(low, roll(a, 64, 1), b)


def half_rows(a, b):
    top = sub_index(a.shape) < 4
    return jnp.where(top, a, roll(b, 4, 0)), jnp.where(top, roll(a, 4, 0), b)


def gather_rows(part, edge, count):
    sample = edge(0)
    lane = lane_index(sample.shape)
    from_low = (lane == 0) | (lane == 64)
    from_high = (lane == 63) | (lane == 127)
    rows = []
    for j in range(count):
        groups = []
        for r in range(GROUPS):
            value = part(j, r)
            if j > 0:
                value = value + jnp.where(from_low, roll(edge(j - 1), -r, 1), 0.0)
            if j < count - 1:
                value = value + jnp.where(from_high, roll(edge(j + 1), r, 1), 0.0)
            groups.append(value)
        first, second = [], []
        for parity in range(2):
            for b in range(2):
                low, high = half_rows(groups[parity + 4 * b], groups[parity + 4 * b + 2])
                first.append(low)
                second.append(high)
        low, high = half_rows(groups[8], groups[8])
        first.append(low)
        second.append(high)
        rows.append(jnp.concatenate(first + second, axis=0))
    even, odd = [], []
    for j in range(0, count, 2):
        low, high = halves(rows[j], rows[j + 1])
        even.append(low)
        odd.append(high)
    return jnp.concatenate(even, axis=1), jnp.concatenate(odd, axis=1)


def scatter_rows(even, odd, count, put):
    rows = []
    for j in range(0, count, 2):
        tile = slice(64 * j, 64 * j + LANES)
        rows.extend(halves(even[:, tile], odd[:, tile]))
    blocks = []
    for j in range(count):
        first = [rows[j][8 * i : 8 * i + 8] for i in range(5)]
        second = [rows[j][40 + 8 * i : 48 + 8 * i] for i in range(5)]
        groups = [None] * GROUPS
        for parity in range(2):
            for b in range(2):
                low, high = half_rows(first[2 * parity + b], second[2 * parity + b])
                groups[parity + 4 * b] = low
                groups[parity + 4 * b + 2] = high
        sub = sub_index(first[4].shape)
        tail = jnp.where(sub < 4, roll(first[4], 4, 0), second[4])
        head = jnp.where(sub < 4, first[4], roll(second[4], 4, 0))
        groups[8] = jnp.where((sub & 2) == 0, head, tail)
        blocks.append(groups)
    lane = lane_index(blocks[0][0].shape)
    for j in range(count):
        edge = jnp.zeros(blocks[0][0].shape, jnp.float32)
        for r in range(GROUPS):
            if j < count - 1:
                edge = jnp.where(
                    (lane == r) | (lane == 64 + r), roll(blocks[j + 1][r], r, 1), edge
                )
            if j > 0:
                edge = jnp.where(
                    (lane == 63 - r) | (lane == 127 - r), roll(blocks[j - 1][r], -r, 1), edge
                )
        put(j, blocks[j] + [edge])


def read_samples(part, edge, row_shift, col_shift, put):
    shape = row_shift.shape
    lane = lane_index(shape)
    sub = sub_index(shape)
    elem_col = lane & (EC - 1)
    window = STEN + 2 * HALO
    grid = []
    for r in range(GROUPS):
        turned = transpose_blocks([part(e, r) for e in range(SUB)], lane)
        cells = [None] * PITCH
        for place, c in enumerate(PARITY_ORDER):
            cells[c] = turned[place]
        line = [None] * window
        for c in range(PITCH):
            line[c + HALO] = cells[c]
        after = [roll(cells[c], -1, 1) for c in range(HALO)]
        before = [roll(cells[PITCH - HALO + c], 1, 1) for c in range(HALO)]
        for e in range(SUB):
            start = EC * e
            last = lane == start + EC - 1
            zero = lane == start
            after[0] = jnp.where(last, roll(edge(e), start + EC - 1 - r, 1), after[0])
            after[1] = jnp.where(last, roll(edge(e), start + EC - 1 - 64 - r, 1), after[1])
            before[0] = jnp.where(zero, roll(edge(e), start - 63 + r, 1), before[0])
            before[1] = jnp.where(zero, roll(edge(e), start - 127 + r, 1), before[1])
        line[0], line[1] = before
        line[10], line[11] = after
        grid.append(line)
    slot = sub & 3
    first_row = (slot == 0) & (lane < EC)
    last_row = (slot == 3) & (lane >= LANES - EC)
    framed = [[None] * window for _ in range(window)]
    for cc in range(window):
        for r in range(PITCH):
            framed[r + HALO][cc] = grid[r][cc]
        outer = grid[8][cc]
        below = roll(outer, -EC, 1)
        above = roll(outer, EC, 1)
        framed[10][cc] = jnp.where(last_row, roll(below, 3, 0), previous_row(grid[0][cc]))
        framed[11][cc] = jnp.where(last_row, roll(below, 2, 0), previous_row(grid[1][cc]))
        framed[0][cc] = jnp.where(first_row, roll(above, -3, 0), next_row(grid[6][cc]))
        framed[1][cc] = jnp.where(first_row, roll(above, -2, 0), next_row(grid[7][cc]))
    for a in range(STEN):
        line = []
        for cc in range(window):
            value = framed[a + HALO][cc]
            for o in range(-HALO, HALO + 1):
                if o:
                    value = jnp.where(row_shift == o, framed[a + HALO + o][cc], value)
            line.append(value)
        for b in range(STEN):
            value = line[b + HALO]
            for o in range(-HALO, HALO + 1):
                if o:
                    value = jnp.where(col_shift == o, line[b + HALO + o], value)
            put(a * STEN + b, value)


def add_outer_rows(chunk, row_count, col_count):
    sub = sub_index((SUB, LANES))
    even, odd = [], []
    for i in range(row_count):
        for j in range(col_count):
            rows = [chunk(i, j)[8 * k : 8 * k + 8] for k in range(4)]
            if j == 0 and i > 0:
                outer = chunk(i - 1, 0)[32:40]
                rows[0] = rows[0] + jnp.where(sub == 0, outer, 0.0)
                rows[2] = rows[2] + jnp.where(sub == 0, roll(outer, -1, 0), 0.0)
            if j == col_count - 1 and i < row_count - 1:
                outer = chunk(i + 1, j)[32:40]
                rows[1] = rows[1] + jnp.where(sub == 7, outer, 0.0)
                rows[3] = rows[3] + jnp.where(sub == 7, roll(outer, 1, 0), 0.0)
            even.extend(rows[:2])
            odd.extend(rows[2:])
    return jnp.concatenate(even, axis=0), jnp.concatenate(odd, axis=0)


def spread_outer_rows(even, odd, row_count, col_count, put):
    sub = sub_index((SUB, LANES))

    def block(i, j):
        start = 16 * (i * col_count + j)
        return [even[start : start + 8], even[start + 8 : start + 16],
                odd[start : start + 8], odd[start + 8 : start + 16]]

    for i in range(row_count):
        for j in range(col_count):
            outer = jnp.zeros((SUB, LANES), jnp.float32)
            if j == 0 and i < row_count - 1:
                rows = block(i + 1, 0)
                outer = jnp.where(sub == 0, rows[0], jnp.where(sub == 1, roll(rows[2], 1, 0), outer))
            if j == col_count - 1 and i > 0:
                rows = block(i - 1, j)
                outer = jnp.where(sub == 7, rows[1], jnp.where(sub == 6, roll(rows[3], -1, 0), outer))
            put(i, j, block(i, j) + [outer])


def two_terms(value):
    high = value.astype(jnp.bfloat16)
    return high, (value - high.astype(jnp.float32)).astype(jnp.bfloat16)


def dot(left, right, dims=((1,), (0,))):
    return lax.dot_general(left, right, (dims, ((), ())), preferred_element_type=jnp.float32)


def even_positions(row_count, col_count):
    j, c, e = np.meshgrid(np.arange(col_count), np.arange(4), np.arange(EC), indexing="ij")
    columns = (LANES * j + PITCH * e + 2 * c).reshape(-1)
    i, j, b, h, t = np.meshgrid(
        np.arange(row_count), np.arange(col_count), np.arange(2), np.arange(2), np.arange(TILES),
        indexing="ij",
    )
    rows = (ER * PITCH * i + SUB * PITCH * t + PITCH * j + 2 * h + 4 * b).reshape(-1)
    return columns, rows


def angle_pair(left, right, length):
    angles = 2.0 * np.pi * (np.asarray(left)[:, None] * np.asarray(right)[None, :] % length) / length
    return np.asarray(np.cos(angles), np.float32), np.asarray(np.sin(angles), np.float32)


def position_bases(positions, length):
    orders = np.arange(length // 4)
    grouped = positions.reshape(-1, SUB)
    offsets = grouped[0] - grouped[0, 0]
    assert (grouped == grouped[:, :1] + offsets[None, :]).all()
    return (
        *angle_pair(grouped[:, 0], orders, length),
        *angle_pair(offsets, orders, length),
        *angle_pair(offsets + 1, orders, length),
    )


def order_bases(positions, length):
    bases = np.arange(0, length // 4, SUB)
    result = []
    for parity in range(2):
        result.extend(angle_pair(bases, positions + parity, length))
        result.extend(angle_pair(np.arange(SUB), positions + parity, length))
    return tuple(result)


def fill_by_position(sign_of, bases, out_refs):
    base_cos, base_sin, even_cos, even_sin, odd_cos, odd_sin = bases
    ec, es, oc, os = (ref[...] for ref in (even_cos, even_sin, odd_cos, odd_sin))
    start = lane_index(ec.shape) == 0

    def pair(i, carry):
        parts = [[], [], []]
        for h in range(2):
            row = 2 * i + h
            bc, bs = base_cos[pl.ds(row, 1), :], base_sin[pl.ds(row, 1), :]
            parts[0].append(bc * ec - bs * es)
            parts[1].append(jnp.where(start, 1.0, -(bs * ec + bc * es)) * sign_of(row))
            parts[2].append(bc * oc - bs * os)
        rows = pl.ds(pl.multiple_of(16 * i, 16), 16)
        for ref, part in zip(out_refs, parts):
            ref[rows, :] = jnp.concatenate(part, axis=0).astype(ref.dtype)
        return carry

    lax.fori_loop(0, base_cos.shape[0] // 2, pair, 0)


def column_table_kernel(*refs):
    fill_by_position(lambda row: (1 - 2 * ((row // 2) & 1)).astype(jnp.float32), refs[:6], refs[6:])


def row_table_kernel(green_ref, *refs):
    position, order, outs = refs[:6], refs[6:14], refs[14:]
    quarter = position[0].shape[1]
    tiles = quarter // LANES
    sub = sub_index((SUB, quarter))
    flip = jnp.where(sub < 4, 1.0, -1.0)
    fill_by_position(lambda row: flip, position, outs[3:6])
    ebc, ebs, ec, es, obc, obs, oc, os = order
    ec, es, oc, os = (ref[...] for ref in (ec, es, oc, os))
    lanes = jnp.where((lane_index((SUB, quarter)) & 4) == 0, 1.0, -1.0)

    def pair(i, carry):
        parts = [[], [], []]
        for h in range(2):
            row = 2 * i + h
            one = (pl.ds(row, 1), slice(None))
            bc, bs = ebc[one], ebs[one]
            parts[0].append(bc * ec - bs * es)
            first = (sub + row) == 0
            parts[1].append(jnp.where(first, 1.0, -(bs * ec + bc * es)) * lanes)
            parts[2].append(obc[one] * oc - obs[one] * os)
        rows = pl.ds(pl.multiple_of(16 * i, 16), 16)
        for ref, part in zip(outs[:3], parts):
            ref[rows, :] = jnp.concatenate(part, axis=0).astype(ref.dtype)
        return carry

    lax.fori_loop(0, ebc.shape[0] // 2, pair, 0)

    depth = green_ref.shape[0]
    device = lax.axis_index("row") * lax.axis_size("col") + lax.axis_index("col")
    number = sub_index((depth, LANES)) + device * depth
    length = 4 * quarter
    weight = jnp.where(number % quarter == 0, 1.0, 2.0) * (1.0 / (length * length))
    lane = lane_index((depth, LANES))

    def scaled(tile):
        value = green_ref[:, LANES * tile : LANES * (tile + 1)] * weight
        if tile % tiles == 0:
            value = value * jnp.where(lane == 0, 1.0, 2.0)
        else:
            value = value * 2.0
        return jnp.concatenate([value, value], axis=0)

    for t in range(tiles):
        cos_plus, cos_minus = scaled(t), scaled(2 * tiles + t)
        sin_minus, sin_plus = scaled(tiles + t), scaled(3 * tiles + t)
        first = slice(LANES * t, LANES * (t + 1))
        second = slice(quarter + LANES * t, quarter + LANES * (t + 1))
        outs[6][first, :] = (cos_plus + cos_minus).T
        outs[7][first, :] = (cos_plus - cos_minus).T
        outs[6][second, :] = (sin_plus + sin_minus).T
        outs[7][second, :] = (sin_plus - sin_minus).T


def tiled_shifts(shifts_ref, which):
    rows = [shifts_ref[which : which + 1, LANES * t : LANES * (t + 1)] for t in range(TILES)]
    return jnp.concatenate(rows * RHS, axis=0)


def charge_kernel(currents_ref, projection_ref, shifts_ref, out_ref, current, partial, stencil):
    step = pl.program_id(0)

    @pl.when(step == 0)
    def _():
        current[...] = currents_ref[...].astype(jnp.bfloat16).astype(jnp.float32)

    for t in range(TILES):
        lanes = slice(LANES * t, LANES * (t + 1))
        totals = [[None] * RHS for _ in range(STEN)]
        for b in range(0, BASIS, 16):
            values = [
                [current[q, b + 8 * h : b + 8 * h + 8, lanes] for h in range(2)] for q in range(RHS)
            ]
            for s in range(STEN):
                weight = projection_ref[s, b : b + 16, lanes].astype(jnp.float32)
                for q in range(RHS):
                    term = weight[:8] * values[q][0] + weight[8:] * values[q][1]
                    totals[s][q] = term if totals[s][q] is None else totals[s][q] + term
        for s in range(STEN):
            for q in range(RHS):
                partial[s, q * TILES + t] = totals[s][q]
    for s in range(STEN):
        stencil[step * STEN + s] = sum_rows([partial[s, i] for i in range(SUB)])

    @pl.when(step == pl.num_programs(0) - 1)
    def _():
        chunks = place_charges(
            lambda s: stencil[s], tiled_shifts(shifts_ref, 0), tiled_shifts(shifts_ref, 1)
        )
        for e in range(SUB):
            out_ref[e] = jnp.concatenate(chunks[e], axis=0).astype(out_ref.dtype)


def column_sign(shape):
    return jnp.where((lane_index(shape) & EC) == 0, 1.0, -1.0)


def column_kernel(count, rows_ref, even_cos, even_sin, odd_cos, out_ref):
    def part(j, r):
        return rows_ref[j, 8 * r : 8 * r + 8, :].astype(jnp.float32)

    even, odd = gather_rows(part, lambda j: part(j, GROUPS), count)
    both = jnp.concatenate([odd, odd * column_sign(odd.shape)], axis=0).astype(jnp.bfloat16)
    even = even.astype(jnp.bfloat16)
    ec, es = dot(even, even_cos[...]), dot(even, even_sin[...])
    both = dot(both, odd_cos[...])
    oc, os = both[: odd.shape[0]], both[odd.shape[0] :]
    half = out_ref.shape[1]
    device = 0
    for block in (ec + oc, es - os, ec - oc, es + os):
        for t in range(0, block.shape[1], LANES):
            for chunk in halves(block[:half, t : t + LANES], block[half:, t : t + LANES]):
                out_ref[device] = chunk.astype(out_ref.dtype)
                device += 1


def row_kernel(row_count, col_count, in_ref, even_cos, even_sin, odd_cos, back_cos, back_sin, back_odd,
               sum_ref, diff_ref, out_ref):
    even, odd = add_outer_rows(
        lambda i, j: in_ref[i * col_count + j].astype(jnp.float32), row_count, col_count
    )
    flip = jnp.where((sub_index(odd.shape) & 4) == 0, 1.0, -1.0)
    both = jnp.concatenate([odd, odd * flip], axis=1).astype(jnp.bfloat16)
    even = even.astype(jnp.bfloat16)
    a = [dot(even_cos[...], even), dot(even_sin[...], even)]
    both = dot(odd_cos[...], both)
    b = [both[:, :LANES], both[:, LANES:]]
    quarter = odd.shape[0]

    def pieces(left, right):
        for k in range(2):
            span = slice(quarter * k, quarter * (k + 1))
            yield two_terms(left[k] * sum_ref[span, :] + right[k] * diff_ref[span, :])

    def fold(value):
        return value[:, :LANES] + value[:, LANES:]

    (ch, cl), (sh, sl) = pieces(a, b)
    even = fold(
        dot(back_cos[...], jnp.concatenate([ch, cl], axis=1))
        + dot(back_sin[...], jnp.concatenate([sh, sl], axis=1))
    )
    (ch, cl), (sh, sl) = pieces(b, a)
    both = dot(back_odd[...], jnp.concatenate([ch, cl, sh, sl], axis=1))
    odd = fold(both[:, : 2 * LANES]) + fold(both[:, 2 * LANES :]) * flip

    def put(i, j, parts):
        out_ref[i * col_count + j] = jnp.concatenate(parts, axis=0).astype(out_ref.dtype)

    spread_outer_rows(even, odd, row_count, col_count, put)


def grid_kernel(count, in_ref, even_cos, even_sin, odd_cos, out_ref):
    devices = in_ref.shape[0]
    first, second = [], []
    for d in range(0, devices, 2):
        low, high = halves(in_ref[d].astype(jnp.float32), in_ref[d + 1].astype(jnp.float32))
        first.append(low)
        second.append(high)
    per_block = devices // 8
    blocks = []
    for k in range(4):
        span = slice(per_block * k, per_block * (k + 1))
        blocks.append(
            jnp.concatenate(
                [jnp.concatenate(first[span], axis=1), jnp.concatenate(second[span], axis=1)], axis=0
            )
        )
    cos_plus, sin_minus, cos_minus, sin_plus = blocks
    half = cos_plus.shape[0]

    def back(values, table):
        terms = [term for value in values for term in two_terms(value)]
        result = dot(jnp.concatenate(terms, axis=0), table[...], ((1,), (1,)))
        return [
            result[2 * half * i : 2 * half * i + half] + result[2 * half * i + half : 2 * half * (i + 1)]
            for i in range(len(values))
        ]

    even = back([cos_plus + cos_minus], even_cos)[0] + back([sin_plus + sin_minus], even_sin)[0]
    odd, turned = back([cos_plus - cos_minus, sin_plus - sin_minus], odd_cos)
    odd = odd + turned * column_sign(odd.shape)

    def put(j, parts):
        out_ref[j] = jnp.concatenate(parts, axis=0).astype(out_ref.dtype)

    scatter_rows(even, odd, count, put)


def far_kernel(grid_ref, projection_ref, shifts_ref, near_ref, out_ref, samples):
    @pl.when(pl.program_id(0) == 0)
    def _():
        def part(e, r):
            return grid_ref[e, 8 * r : 8 * r + 8, :].astype(jnp.float32)

        def put(s, value):
            samples[s] = value

        read_samples(
            part,
            lambda e: part(e, GROUPS),
            tiled_shifts(shifts_ref, 0),
            tiled_shifts(shifts_ref, 1),
            put,
        )

    depth = out_ref.shape[1]

    def add_row(a, totals):
        totals = list(totals)
        for b in range(STEN):
            s = a * STEN + b
            for t in range(TILES):
                weight = projection_ref[s, :, LANES * t : LANES * (t + 1)].astype(jnp.float32)
                for q in range(RHS):
                    index = q * TILES + t
                    totals[index] = totals[index] + weight * samples[s, index : index + 1, :]
        return tuple(totals)

    start = tuple(
        near_ref[q, :, LANES * t : LANES * (t + 1)] for q in range(RHS) for t in range(TILES)
    )
    totals = lax.fori_loop(0, STEN, add_row, start)
    for q in range(RHS):
        for t in range(TILES):
            out_ref[q, :, LANES * t : LANES * (t + 1)] = totals[q * TILES + t]


def near_kernel(own_ref, left_ref, right_ref, above_ref, below_ref, partners_ref, blocks_ref, out_ref, picked):
    @pl.when(pl.program_id(0) == 0)
    def _():
        lane = lane_index((BASIS, LANES))
        elem_col = lane & (EC - 1)

        def three(own, left, right):
            own, left, right = (v.astype(jnp.float32) for v in (own, left, right))
            return (
                jnp.where(elem_col == 0, roll(left, 1 - EC, 1), roll(own, 1, 1)),
                own,
                jnp.where(elem_col == EC - 1, roll(right, EC - 1, 1), roll(own, -1, 1)),
            )

        for q in range(RHS):
            tiles = [three(above_ref[0, q], above_ref[1, q], above_ref[2, q])]
            for t in range(TILES):
                lanes = slice(LANES * t, LANES * (t + 1))
                tiles.append(three(own_ref[q, :, lanes], left_ref[q, :, lanes], right_ref[q, :, lanes]))
            tiles.append(three(below_ref[0, q], below_ref[1, q], below_ref[2, q]))
            for t in range(TILES):
                lanes = slice(LANES * t, LANES * (t + 1))
                before, here, after = tiles[t : t + 3]
                codes = [partners_ref[k : k + 1, lanes] for k in range(NEIGH)]
                chosen = [here[1]] * NEIGH
                for c in range(3):
                    views = (
                        jnp.where(lane < EC, roll(before[c], EC, 1), roll(here[c], EC, 1)),
                        here[c],
                        jnp.where(lane >= LANES - EC, roll(after[c], -EC, 1), roll(here[c], -EC, 1)),
                    )
                    for r in range(3):
                        if r == 1 and c == 1:
                            continue
                        for k in range(1, NEIGH):
                            chosen[k] = jnp.where(codes[k] == 3 * r + c, views[r], chosen[k])
                for k in range(NEIGH):
                    picked[k, q, :, lanes] = chosen[k]

    def one_tile(t, carry):
        lanes = pl.ds(pl.multiple_of(t * LANES, LANES), LANES)
        totals = [[None] * RHS for _ in range(SUB)]
        for k in range(NEIGH):
            for b in range(0, BASIS, 16):
                values = [
                    [picked[k, q, b + 8 * h : b + 8 * h + 8, lanes] for h in range(2)]
                    for q in range(RHS)
                ]
                for a in range(SUB):
                    weight = blocks_ref[k, a, b : b + 16, lanes].astype(jnp.float32)
                    for q in range(RHS):
                        term = weight[:8] * values[q][0] + weight[8:] * values[q][1]
                        totals[a][q] = term if totals[a][q] is None else totals[a][q] + term
        for q in range(RHS):
            out_ref[q, :, lanes] = sum_rows([totals[a][q] for a in range(SUB)])
        return carry

    lax.fori_loop(0, TILES, one_tile, 0)


def neighbours(value, axis):
    count = lax.axis_size(axis)
    forward = [(i, i + 1) for i in range(count - 1)]
    backward = [(i + 1, i) for i in range(count - 1)]
    return forward, backward


def whole(shape):
    return pl.BlockSpec(shape, lambda *_: (0,) * len(shape))


def shards_real(currents, projection, near_blocks, partners, shifts, green):
    row_count = lax.axis_size("row")
    col_count = lax.axis_size("col")
    elements = currents.shape[2]
    width = col_count * LANES
    length = 2 * width
    quarter = length // 4
    f32, b16 = jnp.float32, jnp.bfloat16
    struct = jax.ShapeDtypeStruct
    devices = row_count * col_count

    charges = pl.pallas_call(
        charge_kernel,
        grid=(STEN,),
        in_specs=[
            whole((RHS, BASIS, elements)),
            pl.BlockSpec((STEN, BASIS, elements), lambda i: (i, 0, 0)),
            whole((2, elements)),
        ],
        out_specs=whole((SUB, 80, LANES)),
        out_shape=struct((SUB, 80, LANES), b16),
        scratch_shapes=[
            pltpu.VMEM((RHS, BASIS, elements), f32),
            pltpu.VMEM((STEN, SUB, SUB, LANES), f32),
            pltpu.VMEM((STEN * STEN, SUB, LANES), f32),
        ],
        name="charges",
    )(currents, projection, shifts)
    slab = lax.all_to_all(charges, "col", 0, 0, tiled=True)

    columns, rows = even_positions(row_count, col_count)
    table = struct((quarter, quarter), b16)
    col_tables = pl.pallas_call(column_table_kernel, out_shape=[table] * 3, name="column_tables")(
        *position_bases(columns, length)
    )
    spread = struct((2 * quarter, LANES), f32)
    row_tables = pl.pallas_call(
        row_table_kernel, out_shape=[table] * 6 + [spread] * 2, name="row_tables"
    )(green, *position_bases(rows, length), *order_bases(rows, length))

    spectrum = pl.pallas_call(
        functools.partial(column_kernel, col_count),
        out_shape=struct((devices, 40, LANES), b16),
        name="columns",
    )(slab, *col_tables)
    arrived = lax.all_to_all(spectrum, ("row", "col"), 0, 0, tiled=True)
    rows_back = pl.pallas_call(
        functools.partial(row_kernel, row_count, col_count),
        out_shape=struct((devices, 40, LANES), b16),
        name="rows",
    )(arrived, *row_tables)
    returned = lax.all_to_all(rows_back, ("row", "col"), 0, 0, tiled=True)
    potential = pl.pallas_call(
        functools.partial(grid_kernel, col_count),
        out_shape=struct((SUB, 80, LANES), b16),
        name="grid",
    )(returned, *col_tables)
    pieces = lax.all_to_all(potential, "col", 0, 0, tiled=True)

    half = currents.astype(b16)
    forward, backward = neighbours(half, "col")
    left = lax.ppermute(half, "col", forward)
    right = lax.ppermute(half, "col", backward)
    three = jnp.stack([half, left, right])
    forward, backward = neighbours(half, "row")
    above = lax.ppermute(three[..., elements - LANES :], "row", forward)
    below = lax.ppermute(three[..., :LANES], "row", backward)
    near = pl.pallas_call(
        near_kernel,
        grid=(BASIS // SUB,),
        in_specs=[
            whole((RHS, BASIS, elements)),
            whole((RHS, BASIS, elements)),
            whole((RHS, BASIS, elements)),
            whole((3, RHS, BASIS, LANES)),
            whole((3, RHS, BASIS, LANES)),
            whole((NEIGH, elements)),
            pl.BlockSpec((NEIGH, SUB, BASIS, elements), lambda i: (0, i, 0, 0)),
        ],
        out_specs=pl.BlockSpec((RHS, SUB, elements), lambda i: (0, i, 0)),
        out_shape=struct((RHS, BASIS, elements), f32),
        scratch_shapes=[pltpu.VMEM((NEIGH, RHS, BASIS, elements), f32)],
        name="near",
    )(half, left, right, above, below, partners, near_blocks)

    depth = 16
    return pl.pallas_call(
        far_kernel,
        grid=(BASIS // depth,),
        in_specs=[
            whole((SUB, 80, LANES)),
            pl.BlockSpec((STEN * STEN, depth, elements), lambda i: (0, i, 0)),
            whole((2, elements)),
            pl.BlockSpec((RHS, depth, elements), lambda i: (0, i, 0)),
        ],
        out_specs=pl.BlockSpec((RHS, depth, elements), lambda i: (0, i, 0)),
        out_shape=struct((RHS, BASIS, elements), f32),
        scratch_shapes=[pltpu.VMEM((STEN * STEN, SUB, LANES), f32)],
        name="far",
    )(pieces, projection, shifts, near)


def shards(currents, projection, near_blocks, partners, shifts, green):
    row_count = lax.axis_size("row")
    col_count = lax.axis_size("col")
    fits = col_count == SUB and green.shape[0] == 64 and 2 * row_count * col_count == green.shape[0]
    if fits and currents.shape[2] == TILES * LANES and row_count * ER == col_count * EC:
        return shards_real(currents, projection, near_blocks, partners, shifts, green)
    return shards_general(currents, projection, near_blocks, partners, shifts, green)


def solution(mesh):
    in_specs = (
        P(None, None, ("row", "col")),
        P(None, None, ("row", "col")),
        P(None, None, None, ("row", "col")),
        P(None, ("row", "col")),
        P(None, ("row", "col")),
        P(("row", "col"), None),
    )
    out_specs = P(None, None, ("row", "col"))
    return jax.shard_map(shards, mesh=mesh, in_specs=in_specs, out_specs=out_specs, check_vma=False)
```

```python
import functools
import math

import jax
import jax.numpy as jnp
import numpy as np
from jax import lax
from jax.experimental import pallas as pl
from jax.experimental.pallas import tpu as pltpu
from jax.sharding import PartitionSpec as P

BASIS = 64
STEN = 8
PITCH = 8
HALO = 2
NEIGH = 4
RHS = 2
ER = 32
EC = 16


def extended_2(block, sides, width):
    for axis, dim in sides:
        count = lax.axis_size(axis)
        forward = [(i, i + 1) for i in range(count - 1)]
        backward = [(target, source) for source, target in forward]
        low = lax.ppermute(
            lax.slice_in_dim(block, block.shape[dim] - width, None, axis=dim), axis, forward
        )
        high = lax.ppermute(lax.slice_in_dim(block, 0, width, axis=dim), axis, backward)
        block = jnp.concatenate([low, block, high], axis=dim)
    return block


def angle_table(first_size, second_size, modulus, direction):
    left_index = jnp.arange(first_size, dtype=jnp.int32)
    right_index = jnp.arange(second_size, dtype=jnp.int32)
    turn_count = left_index[:, None] * right_index[None, :] % modulus
    angles = turn_count.astype(jnp.float32) * (2.0 * math.pi / modulus)
    return (jnp.cos(angles), direction * jnp.sin(angles))


def complex_apply(real_part, imag_part, cosine, sine_table, pattern):
    highest = lax.Precision.HIGHEST
    out_real = jnp.einsum(pattern, real_part, cosine, precision=highest)
    out_imag = jnp.einsum(pattern, real_part, sine_table, precision=highest)
    if imag_part is not None:
        out_real = out_real - jnp.einsum(pattern, imag_part, sine_table, precision=highest)
        out_imag = out_imag + jnp.einsum(pattern, imag_part, cosine, precision=highest)
    return (out_real, out_imag)


def transform_last(real_part, imag_part, length, count_in, count_out, direction):
    leading = real_part.shape[:-1]
    inner_size = 128
    outer_size = length // inner_size
    rows_in = count_in // inner_size
    kept_count = count_out // outer_size
    shaped_real = real_part.reshape(leading + (rows_in, inner_size))
    shaped_imag = None
    if imag_part is not None:
        shaped_imag = imag_part.reshape(leading + (rows_in, inner_size))
    cosine, sine_table = angle_table(rows_in, outer_size, outer_size, direction)
    first_real, first_imag = complex_apply(
        shaped_real, shaped_imag, cosine, sine_table, "...ab,ak->...kb"
    )
    twist_cos, twist_sin = angle_table(outer_size, inner_size, length, direction)
    turned_real = first_real * twist_cos - first_imag * twist_sin
    turned_imag = first_real * twist_sin + first_imag * twist_cos
    cosine, sine_table = angle_table(inner_size, kept_count, inner_size, direction)
    last_real, last_imag = complex_apply(
        turned_real, turned_imag, cosine, sine_table, "...kb,bj->...jk"
    )
    out_shape = leading + (kept_count * outer_size,)
    return (last_real.reshape(out_shape), last_imag.reshape(out_shape))


def place_shifted(blocks, amount, dim_index):
    new_shape = list(blocks.shape)
    new_shape[dim_index] = new_shape[dim_index] + 2 * HALO
    result = jnp.zeros(tuple(new_shape), blocks.dtype)
    for offset in range(-HALO, HALO + 1):
        widths = [(0, 0)] * blocks.ndim
        widths[dim_index] = (HALO + offset, HALO - offset)
        result = jnp.where(amount == offset, jnp.pad(blocks, widths), result)
    return result


def pick_shifted(windows, amount, dim_index):
    new_shape = list(windows.shape)
    new_shape[dim_index] = STEN
    result = jnp.zeros(tuple(new_shape), windows.dtype)
    for offset in range(-HALO, HALO + 1):
        piece = lax.slice_in_dim(windows, HALO + offset, HALO + offset + STEN, axis=dim_index)
        result = jnp.where(amount == offset, piece, result)
    return result


def intersection_add(framed, dim_index):
    element_count = framed.shape[dim_index]
    window_size = framed.shape[dim_index + 1]
    head_part = lax.slice_in_dim(framed, 0, PITCH, axis=dim_index + 1)
    tail_part = lax.slice_in_dim(framed, PITCH, window_size, axis=dim_index + 1)
    widths = [(0, 0)] * framed.ndim
    widths[dim_index + 1] = (0, 2 * PITCH - window_size)
    tail_part = jnp.pad(tail_part, widths)
    merged = framed.shape[:dim_index] + (element_count * PITCH,) + framed.shape[dim_index + 2 :]
    head_part = head_part.reshape(merged)
    tail_part = tail_part.reshape(merged)
    front_pad = [(0, 0)] * len(merged)
    front_pad[dim_index] = (0, PITCH)
    back_pad = [(0, 0)] * len(merged)
    back_pad[dim_index] = (PITCH, 0)
    summed = jnp.pad(head_part, front_pad) + jnp.pad(tail_part, back_pad)
    return lax.slice_in_dim(summed, 0, element_count * PITCH + 2 * HALO, axis=dim_index)


def cut_windows(field, dim_index):
    element_count = (field.shape[dim_index] - 2 * HALO) // PITCH
    widths = [(0, 0)] * field.ndim
    widths[dim_index] = (0, PITCH - 2 * HALO)
    extended = jnp.pad(field, widths)
    split_shape = field.shape[:dim_index] + (element_count, PITCH) + field.shape[dim_index + 1 :]
    head_part = lax.slice_in_dim(extended, 0, element_count * PITCH, axis=dim_index).reshape(
        split_shape
    )
    tail_part = lax.slice_in_dim(
        extended, PITCH, PITCH + element_count * PITCH, axis=dim_index
    ).reshape(split_shape)
    tail_part = lax.slice_in_dim(tail_part, 0, 2 * HALO, axis=dim_index + 1)
    return jnp.concatenate([head_part, tail_part], axis=dim_index + 1)


def fold_margin(padded, dim_index):
    full_size = padded.shape[dim_index]
    inner_size = full_size - 4 * HALO
    core_part = lax.slice_in_dim(padded, 2 * HALO, 2 * HALO + inner_size, axis=dim_index)
    upper_part = lax.slice_in_dim(padded, 0, HALO, axis=dim_index)
    lower_part = lax.slice_in_dim(padded, full_size - HALO, full_size, axis=dim_index)
    upper_pad = [(0, 0)] * padded.ndim
    upper_pad[dim_index] = (0, inner_size - HALO)
    lower_pad = [(0, 0)] * padded.ndim
    lower_pad[dim_index] = (inner_size - HALO, 0)
    return core_part + jnp.pad(upper_part, upper_pad) + jnp.pad(lower_part, lower_pad)


def shards_general(currents, projection, near_blocks, partners, shifts, green):
    row_count = lax.axis_size("row")
    col_count = lax.axis_size("col")
    device_count = row_count * col_count
    elements = ER * EC
    cur_half = currents.astype(jnp.bfloat16)
    spread = extended_2(cur_half.reshape(RHS, BASIS, ER, EC), (("row", 2), ("col", 3)), 1)
    views = []
    for symbol in range(9):
        row_start = symbol // 3
        col_start = symbol % 3
        views.append(
            spread[:, :, row_start : row_start + ER, col_start : col_start + EC].reshape(
                RHS, BASIS, elements
            )
        )
    picked = []
    for neighbour_slot in range(NEIGH):
        chosen = jnp.zeros((RHS, BASIS, elements), jnp.bfloat16)
        for symbol in range(9):
            chosen = jnp.where(partners[neighbour_slot] == symbol, views[symbol], chosen)
        picked.append(chosen)
    near_term = jnp.einsum(
        "kabn,kqbn->qan", near_blocks, jnp.stack(picked), preferred_element_type=jnp.float32
    )
    stencil = jnp.einsum("sbn,qbn->qsn", projection, cur_half, preferred_element_type=jnp.float32)
    blocks = stencil.reshape(RHS, STEN, STEN, elements)
    framed = place_shifted(place_shifted(blocks, shifts[0], 1), shifts[1], 2)
    window_size = STEN + 2 * HALO
    framed = framed.reshape(RHS, window_size, window_size, ER, EC).transpose(0, 3, 1, 4, 2)
    extended = intersection_add(intersection_add(framed, 1), 2)
    padded = extended_2(extended, (("row", 1), ("col", 2)), HALO)
    charges = fold_margin(fold_margin(padded, 1), 2)
    slab = lax.all_to_all(charges, "col", split_axis=1, concat_axis=2, tiled=True)
    slab_rows = slab.shape[1]
    width_cols = slab.shape[2]
    length_cols = 2 * width_cols
    block_cols = length_cols // device_count
    grid_rows = slab_rows * device_count
    length_rows = 2 * grid_rows
    fwd_real, fwd_imag = transform_last(slab, None, length_cols, width_cols, length_cols, -1.0)
    out_real = fwd_real.reshape(RHS, slab_rows, device_count, block_cols)
    out_imag = fwd_imag.reshape(RHS, slab_rows, device_count, block_cols)
    arrived = (
        lax.all_to_all(out_real, ("row", "col"), split_axis=2, concat_axis=2, tiled=True),
        lax.all_to_all(out_imag, ("row", "col"), split_axis=2, concat_axis=2, tiled=True),
    )
    col_real = arrived[0].transpose(0, 3, 2, 1).reshape(RHS, block_cols, grid_rows)
    col_imag = arrived[1].transpose(0, 3, 2, 1).reshape(RHS, block_cols, grid_rows)
    spec_real, spec_imag = transform_last(
        col_real, col_imag, length_rows, grid_rows, length_rows, -1.0
    )
    spec_real = spec_real * green
    spec_imag = spec_imag * green
    back_real, back_imag = transform_last(
        spec_real, spec_imag, length_rows, length_rows, grid_rows, 1.0
    )
    send_real = back_real.reshape(RHS, block_cols, device_count, slab_rows)
    send_imag = back_imag.reshape(RHS, block_cols, device_count, slab_rows)
    returned = (
        lax.all_to_all(send_real, ("row", "col"), split_axis=2, concat_axis=2, tiled=True),
        lax.all_to_all(send_imag, ("row", "col"), split_axis=2, concat_axis=2, tiled=True),
    )
    rows_real = returned[0].transpose(0, 3, 2, 1).reshape(RHS, slab_rows, length_cols)
    rows_imag = returned[1].transpose(0, 3, 2, 1).reshape(RHS, slab_rows, length_cols)
    final_real, final_imag = transform_last(
        rows_real, rows_imag, length_cols, length_cols, width_cols, 1.0
    )
    potential_slab = final_real * (1.0 / (length_rows * length_cols))
    potential = lax.all_to_all(potential_slab, "col", split_axis=2, concat_axis=1, tiled=True)
    rimmed = extended_2(potential, (("row", 1), ("col", 2)), HALO)
    windows = cut_windows(cut_windows(rimmed, 1), 3)
    windows = windows.transpose(0, 2, 4, 1, 3).reshape(RHS, window_size, window_size, elements)
    samples = pick_shifted(pick_shifted(windows, shifts[0], 1), shifts[1], 2).reshape(
        RHS, STEN * STEN, elements
    )
    sample_high = samples.astype(jnp.bfloat16)
    sample_low = (samples - sample_high.astype(jnp.float32)).astype(jnp.bfloat16)
    far_term = jnp.einsum(
        "sbn,qsn->qbn", projection, sample_high, preferred_element_type=jnp.float32
    )
    far_term = far_term + jnp.einsum(
        "sbn,qsn->qbn", projection, sample_low, preferred_element_type=jnp.float32
    )
    return far_term + near_term


LANES = 128
SUB = 8
TILES = 4
GROUPS = 9
PARITY_ORDER = (0, 2, 4, 6, 1, 3, 5, 7)


def roll(value, amount, dim):
    return pltpu.roll(value, amount % value.shape[dim], dim)


def lane_index(shape):
    return lax.broadcasted_iota(jnp.int32, shape, len(shape) - 1)


def sub_index(shape):
    return lax.broadcasted_iota(jnp.int32, shape, len(shape) - 2)


def sum_rows(parts):
    sub = sub_index(parts[0].shape)
    top = sub < 4
    level = []
    for i in range(4):
        a, b = parts[i], parts[i + 4]
        level.append(jnp.where(top, a, b) + roll(jnp.where(top, b, a), 4, 0))
    mask = (sub & 2) == 0
    level = [
        jnp.where(mask, level[i], level[i + 2])
        + jnp.where(mask, roll(level[i], -2, 0), roll(level[i + 2], 2, 0))
        for i in range(2)
    ]
    mask = (sub & 1) == 0
    a, b = level
    return jnp.where(mask, a, b) + jnp.where(mask, roll(a, -1, 0), roll(b, 1, 0))


def next_row(value):
    lane = lane_index(value.shape)
    sub = sub_index(value.shape)
    turned = roll(value, EC, 1)
    carried = jnp.where((sub & 3) == 0, 0.0, roll(turned, 1, 0))
    return jnp.where(lane < EC, carried, turned)


def previous_row(value):
    lane = lane_index(value.shape)
    sub = sub_index(value.shape)
    turned = roll(value, -EC, 1)
    carried = jnp.where((sub & 3) == 3, 0.0, roll(turned, -1, 0))
    return jnp.where(lane >= LANES - EC, carried, turned)


def place_charges(stencil, row_shift, col_shift):
    shape = row_shift.shape
    lane = lane_index(shape)
    sub = sub_index(shape)
    window = STEN + 2 * HALO
    row_mask = {o: row_shift == o for o in range(-HALO, HALO + 1)}
    col_mask = {o: col_shift == o for o in range(-HALO, HALO + 1)}
    first = []
    for rr in range(window):
        line = []
        for c in range(STEN):
            value = jnp.zeros(shape, jnp.float32)
            for o in range(-HALO, HALO + 1):
                source = rr - HALO - o
                if 0 <= source < STEN:
                    value = jnp.where(row_mask[o], stencil(source * STEN + c), value)
            line.append(value)
        first.append(line)
    framed = []
    for rr in range(window):
        line = []
        for cc in range(window):
            value = jnp.zeros(shape, jnp.float32)
            for o in range(-HALO, HALO + 1):
                source = cc - HALO - o
                if 0 <= source < STEN:
                    value = jnp.where(col_mask[o], first[rr][source], value)
            line.append(value)
        framed.append(line)
    grid = []
    for r in range(PITCH):
        line = []
        for cc in range(window):
            value = framed[r + HALO][cc]
            if r < HALO:
                value = value + next_row(framed[r + HALO + PITCH][cc])
            if r >= PITCH - HALO:
                value = value + previous_row(framed[r + HALO - PITCH][cc])
            line.append(value)
        grid.append(line)
    slot = sub & 3
    low_lanes = lane < EC
    high_lanes = lane >= LANES - EC
    line = []
    for cc in range(window):
        value = jnp.where(low_lanes & (slot == 0), roll(roll(framed[10][cc], EC, 1), -3, 0), 0.0)
        value = jnp.where(low_lanes & (slot == 1), roll(roll(framed[11][cc], EC, 1), -2, 0), value)
        value = jnp.where(high_lanes & (slot == 3), roll(roll(framed[0][cc], -EC, 1), 3, 0), value)
        value = jnp.where(high_lanes & (slot == 2), roll(roll(framed[1][cc], -EC, 1), 2, 0), value)
        line.append(value)
    grid.append(line)
    elem_col = lane & (EC - 1)
    parts = [[] for _ in range(SUB)]
    edges = [jnp.zeros(shape, jnp.float32) for _ in range(SUB)]
    for r in range(GROUPS):
        cells = []
        for c in range(PITCH):
            value = grid[r][c + HALO]
            if c < HALO:
                value = value + jnp.where(elem_col == 0, 0.0, roll(grid[r][c + HALO + PITCH], 1, 1))
            if c >= PITCH - HALO:
                value = value + jnp.where(
                    elem_col == EC - 1, 0.0, roll(grid[r][c + HALO - PITCH], -1, 1)
                )
            cells.append(value)
        turned = transpose_blocks([cells[c] for c in PARITY_ORDER], lane)
        for e in range(SUB):
            parts[e].append(turned[e])
            start = EC * e
            edge = edges[e]
            edge = jnp.where(lane == r, roll(grid[r][10], r - start - (EC - 1), 1), edge)
            edge = jnp.where(lane == 64 + r, roll(grid[r][11], 64 + r - start - (EC - 1), 1), edge)
            edge = jnp.where(lane == 63 - r, roll(grid[r][0], 63 - r - start, 1), edge)
            edge = jnp.where(lane == 127 - r, roll(grid[r][1], 127 - r - start, 1), edge)
            edges[e] = edge
    return [parts[e] + [edges[e]] for e in range(SUB)]


def transpose_blocks(values, lane):
    block = lane // EC
    for step in (4, 2, 1):
        mask = (block & step) == 0
        result = list(values)
        for i in range(SUB):
            if i & step:
                continue
            a, b = values[i], values[i + step]
            result[i] = jnp.where(mask, a, roll(b, EC * step, 1))
            result[i + step] = jnp.where(mask, roll(a, -EC * step, 1), b)
        values = result
    return values


def halves(a, b):
    low = lane_index(a.shape) < 64
    return jnp.where(low, a, roll(b, 64, 1)), jnp.where(low, roll(a, 64, 1), b)


def half_rows(a, b):
    top = sub_index(a.shape) < 4
    return jnp.where(top, a, roll(b, 4, 0)), jnp.where(top, roll(a, 4, 0), b)


def gather_rows(part, edge, count):
    sample = edge(0)
    lane = lane_index(sample.shape)
    from_low = (lane == 0) | (lane == 64)
    from_high = (lane == 63) | (lane == 127)
    rows = []
    for j in range(count):
        groups = []
        for r in range(GROUPS):
            value = part(j, r)
            if j > 0:
                value = value + jnp.where(from_low, roll(edge(j - 1), -r, 1), 0.0)
            if j < count - 1:
                value = value + jnp.where(from_high, roll(edge(j + 1), r, 1), 0.0)
            groups.append(value)
        first, second = [], []
        for parity in range(2):
            for b in range(2):
                low, high = half_rows(groups[parity + 4 * b], groups[parity + 4 * b + 2])
                first.append(low)
                second.append(high)
        low, high = half_rows(groups[8], groups[8])
        first.append(low)
        second.append(high)
        rows.append(jnp.concatenate(first + second, axis=0))
    even, odd = [], []
    for j in range(0, count, 2):
        low, high = halves(rows[j], rows[j + 1])
        even.append(low)
        odd.append(high)
    return jnp.concatenate(even, axis=1), jnp.concatenate(odd, axis=1)


def scatter_rows(even, odd, count, put):
    rows = []
    for j in range(0, count, 2):
        tile = slice(64 * j, 64 * j + LANES)
        rows.extend(halves(even[:, tile], odd[:, tile]))
    blocks = []
    for j in range(count):
        first = [rows[j][8 * i : 8 * i + 8] for i in range(5)]
        second = [rows[j][40 + 8 * i : 48 + 8 * i] for i in range(5)]
        groups = [None] * GROUPS
        for parity in range(2):
            for b in range(2):
                low, high = half_rows(first[2 * parity + b], second[2 * parity + b])
                groups[parity + 4 * b] = low
                groups[parity + 4 * b + 2] = high
        sub = sub_index(first[4].shape)
        tail = jnp.where(sub < 4, roll(first[4], 4, 0), second[4])
        head = jnp.where(sub < 4, first[4], roll(second[4], 4, 0))
        groups[8] = jnp.where((sub & 2) == 0, head, tail)
        blocks.append(groups)
    lane = lane_index(blocks[0][0].shape)
    for j in range(count):
        edge = jnp.zeros(blocks[0][0].shape, jnp.float32)
        for r in range(GROUPS):
            if j < count - 1:
                edge = jnp.where(
                    (lane == r) | (lane == 64 + r), roll(blocks[j + 1][r], r, 1), edge
                )
            if j > 0:
                edge = jnp.where(
                    (lane == 63 - r) | (lane == 127 - r), roll(blocks[j - 1][r], -r, 1), edge
                )
        put(j, blocks[j] + [edge])


def read_samples(part, edge, row_shift, col_shift, put):
    shape = row_shift.shape
    lane = lane_index(shape)
    sub = sub_index(shape)
    elem_col = lane & (EC - 1)
    window = STEN + 2 * HALO
    grid = []
    for r in range(GROUPS):
        turned = transpose_blocks([part(e, r) for e in range(SUB)], lane)
        cells = [None] * PITCH
        for place, c in enumerate(PARITY_ORDER):
            cells[c] = turned[place]
        line = [None] * window
        for c in range(PITCH):
            line[c + HALO] = cells[c]
        after = [roll(cells[c], -1, 1) for c in range(HALO)]
        before = [roll(cells[PITCH - HALO + c], 1, 1) for c in range(HALO)]
        for e in range(SUB):
            start = EC * e
            last = lane == start + EC - 1
            zero = lane == start
            after[0] = jnp.where(last, roll(edge(e), start + EC - 1 - r, 1), after[0])
            after[1] = jnp.where(last, roll(edge(e), start + EC - 1 - 64 - r, 1), after[1])
            before[0] = jnp.where(zero, roll(edge(e), start - 63 + r, 1), before[0])
            before[1] = jnp.where(zero, roll(edge(e), start - 127 + r, 1), before[1])
        line[0], line[1] = before
        line[10], line[11] = after
        grid.append(line)
    slot = sub & 3
    first_row = (slot == 0) & (lane < EC)
    last_row = (slot == 3) & (lane >= LANES - EC)
    framed = [[None] * window for _ in range(window)]
    for cc in range(window):
        for r in range(PITCH):
            framed[r + HALO][cc] = grid[r][cc]
        outer = grid[8][cc]
        below = roll(outer, -EC, 1)
        above = roll(outer, EC, 1)
        framed[10][cc] = jnp.where(last_row, roll(below, 3, 0), previous_row(grid[0][cc]))
        framed[11][cc] = jnp.where(last_row, roll(below, 2, 0), previous_row(grid[1][cc]))
        framed[0][cc] = jnp.where(first_row, roll(above, -3, 0), next_row(grid[6][cc]))
        framed[1][cc] = jnp.where(first_row, roll(above, -2, 0), next_row(grid[7][cc]))
    for a in range(STEN):
        line = []
        for cc in range(window):
            value = framed[a + HALO][cc]
            for o in range(-HALO, HALO + 1):
                if o:
                    value = jnp.where(row_shift == o, framed[a + HALO + o][cc], value)
            line.append(value)
        for b in range(STEN):
            value = line[b + HALO]
            for o in range(-HALO, HALO + 1):
                if o:
                    value = jnp.where(col_shift == o, line[b + HALO + o], value)
            put(a * STEN + b, value)


def add_outer_rows(chunk, row_count, col_count):
    sub = sub_index((SUB, LANES))
    even, odd = [], []
    for i in range(row_count):
        for j in range(col_count):
            rows = [chunk(i, j)[8 * k : 8 * k + 8] for k in range(4)]
            if j == 0 and i > 0:
                outer = chunk(i - 1, 0)[32:40]
                rows[0] = rows[0] + jnp.where(sub == 0, outer, 0.0)
                rows[2] = rows[2] + jnp.where(sub == 0, roll(outer, -1, 0), 0.0)
            if j == col_count - 1 and i < row_count - 1:
                outer = chunk(i + 1, j)[32:40]
                rows[1] = rows[1] + jnp.where(sub == 7, outer, 0.0)
                rows[3] = rows[3] + jnp.where(sub == 7, roll(outer, 1, 0), 0.0)
            even.extend(rows[:2])
            odd.extend(rows[2:])
    return jnp.concatenate(even, axis=0), jnp.concatenate(odd, axis=0)


def spread_outer_rows(even, odd, row_count, col_count, put):
    sub = sub_index((SUB, LANES))

    def block(i, j):
        start = 16 * (i * col_count + j)
        return [even[start : start + 8], even[start + 8 : start + 16],
                odd[start : start + 8], odd[start + 8 : start + 16]]

    for i in range(row_count):
        for j in range(col_count):
            outer = jnp.zeros((SUB, LANES), jnp.float32)
            if j == 0 and i < row_count - 1:
                rows = block(i + 1, 0)
                outer = jnp.where(sub == 0, rows[0], jnp.where(sub == 1, roll(rows[2], 1, 0), outer))
            if j == col_count - 1 and i > 0:
                rows = block(i - 1, j)
                outer = jnp.where(sub == 7, rows[1], jnp.where(sub == 6, roll(rows[3], -1, 0), outer))
            put(i, j, block(i, j) + [outer])


def two_terms(value):
    high = value.astype(jnp.bfloat16)
    return high, (value - high.astype(jnp.float32)).astype(jnp.bfloat16)


def dot(left, right, dims=((1,), (0,))):
    return lax.dot_general(left, right, (dims, ((), ())), preferred_element_type=jnp.float32)


def even_positions(row_count, col_count):
    j, c, e = np.meshgrid(np.arange(col_count), np.arange(4), np.arange(EC), indexing="ij")
    columns = (LANES * j + PITCH * e + 2 * c).reshape(-1)
    i, j, b, h, t = np.meshgrid(
        np.arange(row_count), np.arange(col_count), np.arange(2), np.arange(2), np.arange(TILES),
        indexing="ij",
    )
    rows = (ER * PITCH * i + SUB * PITCH * t + PITCH * j + 2 * h + 4 * b).reshape(-1)
    return columns, rows


def angle_pair(left, right, length):
    angles = 2.0 * np.pi * (np.asarray(left)[:, None] * np.asarray(right)[None, :] % length) / length
    return np.asarray(np.cos(angles), np.float32), np.asarray(np.sin(angles), np.float32)


def position_bases(positions, length):
    orders = np.arange(length // 4)
    grouped = positions.reshape(-1, SUB)
    offsets = grouped[0] - grouped[0, 0]
    assert (grouped == grouped[:, :1] + offsets[None, :]).all()
    return (
        *angle_pair(grouped[:, 0], orders, length),
        *angle_pair(offsets, orders, length),
        *angle_pair(offsets + 1, orders, length),
    )


def order_bases(positions, length):
    bases = np.arange(0, length // 4, SUB)
    result = []
    for parity in range(2):
        result.extend(angle_pair(bases, positions + parity, length))
        result.extend(angle_pair(np.arange(SUB), positions + parity, length))
    return tuple(result)


def fill_by_position(sign_of, bases, out_refs):
    base_cos, base_sin, even_cos, even_sin, odd_cos, odd_sin = bases
    ec, es, oc, os = (ref[...] for ref in (even_cos, even_sin, odd_cos, odd_sin))
    start = lane_index(ec.shape) == 0

    def pair(i, carry):
        parts = [[], [], []]
        for h in range(2):
            row = 2 * i + h
            bc, bs = base_cos[pl.ds(row, 1), :], base_sin[pl.ds(row, 1), :]
            parts[0].append(bc * ec - bs * es)
            parts[1].append(jnp.where(start, 1.0, -(bs * ec + bc * es)) * sign_of(row))
            parts[2].append(bc * oc - bs * os)
        rows = pl.ds(pl.multiple_of(16 * i, 16), 16)
        for ref, part in zip(out_refs, parts):
            ref[rows, :] = jnp.concatenate(part, axis=0).astype(ref.dtype)
        return carry

    lax.fori_loop(0, base_cos.shape[0] // 2, pair, 0)


def column_table_kernel(*refs):
    fill_by_position(lambda row: (1 - 2 * ((row // 2) & 1)).astype(jnp.float32), refs[:6], refs[6:])


def row_table_kernel(green_ref, *refs):
    position, order, outs = refs[:6], refs[6:14], refs[14:]
    quarter = position[0].shape[1]
    tiles = quarter // LANES
    sub = sub_index((SUB, quarter))
    flip = jnp.where(sub < 4, 1.0, -1.0)
    fill_by_position(lambda row: flip, position, outs[3:6])
    ebc, ebs, ec, es, obc, obs, oc, os = order
    ec, es, oc, os = (ref[...] for ref in (ec, es, oc, os))
    lanes = jnp.where((lane_index((SUB, quarter)) & 4) == 0, 1.0, -1.0)

    def pair(i, carry):
        parts = [[], [], []]
        for h in range(2):
            row = 2 * i + h
            one = (pl.ds(row, 1), slice(None))
            bc, bs = ebc[one], ebs[one]
            parts[0].append(bc * ec - bs * es)
            first = (sub + row) == 0
            parts[1].append(jnp.where(first, 1.0, -(bs * ec + bc * es)) * lanes)
            parts[2].append(obc[one] * oc - obs[one] * os)
        rows = pl.ds(pl.multiple_of(16 * i, 16), 16)
        for ref, part in zip(outs[:3], parts):
            ref[rows, :] = jnp.concatenate(part, axis=0).astype(ref.dtype)
        return carry

    lax.fori_loop(0, ebc.shape[0] // 2, pair, 0)

    depth = green_ref.shape[0]
    device = lax.axis_index("row") * lax.axis_size("col") + lax.axis_index("col")
    number = sub_index((depth, LANES)) + device * depth
    length = 4 * quarter
    weight = jnp.where(number % quarter == 0, 1.0, 2.0) * (1.0 / (length * length))
    lane = lane_index((depth, LANES))

    def scaled(tile):
        value = green_ref[:, LANES * tile : LANES * (tile + 1)] * weight
        if tile % tiles == 0:
            value = value * jnp.where(lane == 0, 1.0, 2.0)
        else:
            value = value * 2.0
        return jnp.concatenate([value, value], axis=0)

    for t in range(tiles):
        cos_plus, cos_minus = scaled(t), scaled(2 * tiles + t)
        sin_minus, sin_plus = scaled(tiles + t), scaled(3 * tiles + t)
        first = slice(LANES * t, LANES * (t + 1))
        second = slice(quarter + LANES * t, quarter + LANES * (t + 1))
        outs[6][first, :] = (cos_plus + cos_minus).T
        outs[7][first, :] = (cos_plus - cos_minus).T
        outs[6][second, :] = (sin_plus + sin_minus).T
        outs[7][second, :] = (sin_plus - sin_minus).T


def tiled_shifts(shifts_ref, which):
    rows = [shifts_ref[which : which + 1, LANES * t : LANES * (t + 1)] for t in range(TILES)]
    return jnp.concatenate(rows * RHS, axis=0)


def charge_kernel(currents_ref, projection_ref, shifts_ref, out_ref, current, partial, stencil):
    step = pl.program_id(0)

    @pl.when(step == 0)
    def _():
        current[...] = currents_ref[...].astype(jnp.bfloat16).astype(jnp.float32)

    for t in range(TILES):
        lanes = slice(LANES * t, LANES * (t + 1))
        totals = [[None] * RHS for _ in range(STEN)]
        for b in range(0, BASIS, 16):
            values = [
                [current[q, b + 8 * h : b + 8 * h + 8, lanes] for h in range(2)] for q in range(RHS)
            ]
            for s in range(STEN):
                weight = projection_ref[s, b : b + 16, lanes].astype(jnp.float32)
                for q in range(RHS):
                    term = weight[:8] * values[q][0] + weight[8:] * values[q][1]
                    totals[s][q] = term if totals[s][q] is None else totals[s][q] + term
        for s in range(STEN):
            for q in range(RHS):
                partial[s, q * TILES + t] = totals[s][q]
    for s in range(STEN):
        stencil[step * STEN + s] = sum_rows([partial[s, i] for i in range(SUB)])

    @pl.when(step == pl.num_programs(0) - 1)
    def _():
        chunks = place_charges(
            lambda s: stencil[s], tiled_shifts(shifts_ref, 0), tiled_shifts(shifts_ref, 1)
        )
        to_next, to_previous, to_rows = pack_currents(
            lambda q, t: current[q, :, LANES * t : LANES * (t + 1)]
        )
        mine = lax.axis_index("col")
        blank = jnp.zeros((SUB, LANES), jnp.float32)
        for e in range(SUB):
            after = (mine == e - 1).astype(jnp.float32)
            before = (mine == e + 1).astype(jnp.float32)
            rows = chunks[e] + [to_next * after + to_previous * before, to_rows[e], blank]
            out_ref[e] = jnp.concatenate(rows, axis=0).astype(out_ref.dtype)


def pack_currents(tile):
    half = BASIS // 2
    lane = lane_index((half, LANES))
    elem_col = lane & (EC - 1)
    to_next = jnp.zeros((half, LANES), jnp.float32)
    to_previous = jnp.zeros((half, LANES), jnp.float32)
    for q in range(RHS):
        for t in range(TILES):
            value = tile(q, t)
            for h in range(2):
                place = q * TILES + t + SUB * h
                part = value[half * h : half * (h + 1)]
                here = elem_col == place
                to_next = jnp.where(here, roll(part, place - (EC - 1), 1), to_next)
                to_previous = jnp.where(here, roll(part, place, 1), to_previous)
    lane = lane_index((SUB, LANES))
    to_rows = []
    for e in range(SUB):
        rows = jnp.zeros((SUB, LANES), jnp.float32)
        for q in range(RHS):
            span = slice(SUB * e, SUB * (e + 1))
            last = roll(tile(q, TILES - 1)[span], EC * q - (LANES - EC), 1)
            first = roll(tile(q, 0)[span], 2 * EC + EC * q, 1)
            rows = jnp.where(lane // EC == q, last, jnp.where(lane // EC == 2 + q, first, rows))
        to_rows.append(rows)
    return to_next, to_previous, to_rows


def forward_rows(edge_row, j, count, which):
    lane = lane_index((SUB, LANES))
    start = 2 * EC * which
    value = roll(edge_row(j), -start, 1)
    for q in range(RHS):
        place = 2 * EC + 2 * q
        if j > 0:
            corner = roll(edge_row(j - 1), place - start - EC * q - (EC - 1), 1)
            value = jnp.where(lane == place, corner, value)
        if j < count - 1:
            corner = roll(edge_row(j + 1), place + 1 - start - EC * q, 1)
            value = jnp.where(lane == place + 1, corner, value)
    return jnp.where(lane < 64, roll(value, 2, 0), roll(roll(value, 64, 1), -2, 0))


def column_sign(shape):
    return jnp.where((lane_index(shape) & EC) == 0, 1.0, -1.0)


def column_kernel(count, rows_ref, even_cos, even_sin, odd_cos, out_ref):
    def part(j, r):
        return rows_ref[j, 8 * r : 8 * r + 8, :].astype(jnp.float32)

    even, odd = gather_rows(part, lambda j: part(j, GROUPS), count)
    both = jnp.concatenate([odd, odd * column_sign(odd.shape)], axis=0).astype(jnp.bfloat16)
    even = even.astype(jnp.bfloat16)
    ec, es = dot(even, even_cos[...]), dot(even, even_sin[...])
    both = dot(both, odd_cos[...])
    oc, os = both[: odd.shape[0]], both[odd.shape[0] :]
    half = out_ref.shape[1]
    mine = lax.axis_index("row")
    ends = [
        [forward_rows(lambda k: part(k, GROUPS + 5), j, count, which) for which in range(2)]
        for j in range(count)
    ]
    sub = sub_index((SUB, LANES))
    middle = (sub >= 2) & (sub < 6)
    device = 0
    for block in (ec + oc, es - os, ec - oc, es + os):
        for t in range(0, block.shape[1], LANES):
            for chunk in halves(block[:half, t : t + LANES], block[half:, t : t + LANES]):
                i, j = device // count, device % count
                below = (mine == i - 1).astype(jnp.float32)
                above = (mine == i + 1).astype(jnp.float32)
                tail = jnp.where(
                    middle, ends[j][0] * below + ends[j][1] * above, chunk[half - SUB :]
                )
                chunk = jnp.concatenate([chunk[: half - SUB], tail], axis=0)
                out_ref[device] = chunk.astype(out_ref.dtype)
                device += 1


def row_kernel(row_count, col_count, in_ref, even_cos, even_sin, odd_cos, back_cos, back_sin, back_odd,
               sum_ref, diff_ref, out_ref):
    even, odd = add_outer_rows(
        lambda i, j: in_ref[i * col_count + j].astype(jnp.float32), row_count, col_count
    )
    flip = jnp.where((sub_index(odd.shape) & 4) == 0, 1.0, -1.0)
    both = jnp.concatenate([odd, odd * flip], axis=1).astype(jnp.bfloat16)
    even = even.astype(jnp.bfloat16)
    a = [dot(even_cos[...], even), dot(even_sin[...], even)]
    both = dot(odd_cos[...], both)
    b = [both[:, :LANES], both[:, LANES:]]
    quarter = odd.shape[0]

    def pieces(left, right):
        for k in range(2):
            span = slice(quarter * k, quarter * (k + 1))
            yield two_terms(left[k] * sum_ref[span, :] + right[k] * diff_ref[span, :])

    def fold(value):
        return value[:, :LANES] + value[:, LANES:]

    (ch, cl), (sh, sl) = pieces(a, b)
    even = fold(
        dot(back_cos[...], jnp.concatenate([ch, cl], axis=1))
        + dot(back_sin[...], jnp.concatenate([sh, sl], axis=1))
    )
    (ch, cl), (sh, sl) = pieces(b, a)
    both = dot(back_odd[...], jnp.concatenate([ch, cl, sh, sl], axis=1))
    odd = fold(both[:, : 2 * LANES]) + fold(both[:, 2 * LANES :]) * flip

    def put(i, j, parts):
        out_ref[i * col_count + j] = jnp.concatenate(parts, axis=0).astype(out_ref.dtype)

    spread_outer_rows(even, odd, row_count, col_count, put)


def grid_kernel(count, in_ref, even_cos, even_sin, odd_cos, out_ref):
    devices = in_ref.shape[0]
    first, second = [], []
    for d in range(0, devices, 2):
        low, high = halves(in_ref[d].astype(jnp.float32), in_ref[d + 1].astype(jnp.float32))
        first.append(low)
        second.append(high)
    per_block = devices // 8
    blocks = []
    for k in range(4):
        span = slice(per_block * k, per_block * (k + 1))
        blocks.append(
            jnp.concatenate(
                [jnp.concatenate(first[span], axis=1), jnp.concatenate(second[span], axis=1)], axis=0
            )
        )
    cos_plus, sin_minus, cos_minus, sin_plus = blocks
    half = cos_plus.shape[0]

    def back(values, table):
        terms = [term for value in values for term in two_terms(value)]
        result = dot(jnp.concatenate(terms, axis=0), table[...], ((1,), (1,)))
        return [
            result[2 * half * i : 2 * half * i + half] + result[2 * half * i + half : 2 * half * (i + 1)]
            for i in range(len(values))
        ]

    even = back([cos_plus + cos_minus], even_cos)[0] + back([sin_plus + sin_minus], even_sin)[0]
    odd, turned = back([cos_plus - cos_minus, sin_plus - sin_minus], odd_cos)
    odd = odd + turned * column_sign(odd.shape)

    def put(j, parts):
        out_ref[j] = jnp.concatenate(parts, axis=0).astype(out_ref.dtype)

    scatter_rows(even, odd, count, put)


def far_kernel(grid_ref, projection_ref, shifts_ref, near_ref, out_ref, samples):
    @pl.when(pl.program_id(0) == 0)
    def _():
        def part(e, r):
            return grid_ref[e, 8 * r : 8 * r + 8, :].astype(jnp.float32)

        def put(s, value):
            samples[s] = value

        read_samples(
            part,
            lambda e: part(e, GROUPS),
            tiled_shifts(shifts_ref, 0),
            tiled_shifts(shifts_ref, 1),
            put,
        )

    depth = out_ref.shape[1]

    def add_row(a, totals):
        totals = list(totals)
        for b in range(STEN):
            s = a * STEN + b
            for t in range(TILES):
                weight = projection_ref[s, :, LANES * t : LANES * (t + 1)].astype(jnp.float32)
                for q in range(RHS):
                    index = q * TILES + t
                    totals[index] = totals[index] + weight * samples[s, index : index + 1, :]
        return tuple(totals)

    start = tuple(
        near_ref[q, :, LANES * t : LANES * (t + 1)] for q in range(RHS) for t in range(TILES)
    )
    totals = lax.fori_loop(0, STEN, add_row, start)
    for q in range(RHS):
        for t in range(TILES):
            out_ref[q, :, LANES * t : LANES * (t + 1)] = totals[q * TILES + t]


def pick_kernel(currents_ref, slab_ref, arrived_ref, partners_ref, out_ref):
    lane = lane_index((BASIS, LANES))
    elem_col = lane & (EC - 1)
    row, col = lax.axis_index("row"), lax.axis_index("col")
    col_count = lax.axis_size("col")
    devices = arrived_ref.shape[0]

    def column_edge(source):
        source = jnp.clip(source, 0, col_count - 1)
        return slab_ref[source, 80:112, :].astype(jnp.float32)

    from_left, from_right = column_edge(col - 1), column_edge(col + 1)

    def beside(edge, q, t, end):
        place = q * TILES + t
        return jnp.concatenate([roll(edge, end - place, 1), roll(edge, end - place - SUB, 1)], axis=0)

    def three(own, left, right):
        return (
            jnp.where(elem_col == 0, left, roll(own, 1, 1)),
            own,
            jnp.where(elem_col == EC - 1, right, roll(own, -1, 1)),
        )

    sub = sub_index((SUB, LANES))

    def outer_row(source):
        parts = []
        for j in range(col_count):
            index = jnp.clip(source * col_count + j, 0, devices - 1)
            value = arrived_ref[index, 32:40, :].astype(jnp.float32)
            parts.append(jnp.where(sub < 4, roll(value, -2, 0), roll(roll(value, 2, 0), -64, 1)))
        return jnp.concatenate(parts, axis=0)

    rows = outer_row(row - 1), outer_row(row + 1)

    def outer_three(value, q, start):
        own = roll(value, start - EC * q, 1)
        left = roll(value, start - 2 * EC - 2 * q, 1)
        right = roll(value, start + EC - 1 - 2 * EC - 2 * q - 1, 1)
        return three(own, left, right)

    for q in range(RHS):
        tiles = []
        for t in range(TILES):
            own = currents_ref[q, :, LANES * t : LANES * (t + 1)]
            own = own.astype(jnp.bfloat16).astype(jnp.float32)
            tiles.append(three(own, beside(from_left, q, t, 0), beside(from_right, q, t, EC - 1)))
        above = outer_three(rows[0], q, 0)
        below = outer_three(rows[1], q, LANES - EC)
        for t in range(TILES):
            lanes = slice(LANES * t, LANES * (t + 1))
            codes = [partners_ref[k : k + 1, lanes] for k in range(1, NEIGH)]
            chosen = [tiles[t][1]] * (NEIGH - 1)
            for c in range(3):
                here = tiles[t][c]
                before = roll(tiles[t - 1][c], EC, 1) if t else above[c]
                after = roll(tiles[t + 1][c], -EC, 1) if t < TILES - 1 else below[c]
                views = (
                    jnp.where(lane < EC, before, roll(here, EC, 1)),
                    here,
                    jnp.where(lane >= LANES - EC, after, roll(here, -EC, 1)),
                )
                for r in range(3):
                    if r == 1 and c == 1:
                        continue
                    for k in range(NEIGH - 1):
                        chosen[k] = jnp.where(codes[k] == 3 * r + c, views[r], chosen[k])
            for k in range(NEIGH - 1):
                out_ref[k, q, :, lanes] = chosen[k].astype(out_ref.dtype)


def near_kernel(has_total, *refs):
    values_ref, refs = refs[0], refs[1:]
    total_ref = None
    if has_total:
        total_ref, refs = refs[0], refs[1:]
    blocks, out_ref, picked = refs[:-2], refs[-2], refs[-1]

    @pl.when(pl.program_id(0) == 0)
    def _():
        picked[...] = values_ref[...].astype(jnp.bfloat16).astype(jnp.float32).reshape(picked.shape)

    def one_tile(t, carry):
        lanes = pl.ds(pl.multiple_of(t * LANES, LANES), LANES)
        totals = [[None] * RHS for _ in range(SUB)]
        for k, blocks_ref in enumerate(blocks):
            for b in range(0, BASIS, 16):
                values = [
                    [picked[k, q, b + 8 * h : b + 8 * h + 8, lanes] for h in range(2)]
                    for q in range(RHS)
                ]
                for a in range(SUB):
                    weight = blocks_ref[0, a, b : b + 16, lanes].astype(jnp.float32)
                    for q in range(RHS):
                        term = weight[:8] * values[q][0] + weight[8:] * values[q][1]
                        totals[a][q] = term if totals[a][q] is None else totals[a][q] + term
        for q in range(RHS):
            value = sum_rows([totals[a][q] for a in range(SUB)])
            if has_total:
                value = value + total_ref[q, :, lanes]
            out_ref[q, :, lanes] = value
        return carry

    lax.fori_loop(0, TILES, one_tile, 0)


def near_call(values, total, near_blocks, slots, start, stop):
    elements = near_blocks.shape[3]
    part = pl.BlockSpec((RHS, SUB, elements), lambda i: (0, i + start, 0))

    def slot_spec(k):
        return pl.BlockSpec((1, SUB, BASIS, elements), lambda i: (k, i + start, 0, 0))

    return pl.pallas_call(
        functools.partial(near_kernel, total is not None),
        grid=(stop - start,),
        in_specs=[whole(values.shape)]
        + ([part] if total is not None else [])
        + [slot_spec(k) for k in slots],
        out_specs=part,
        out_shape=jax.ShapeDtypeStruct((RHS, BASIS, elements), jnp.float32),
        scratch_shapes=[pltpu.VMEM((len(slots), RHS, BASIS, elements), jnp.float32)],
        input_output_aliases={} if total is None else {1: 0},
        name="near",
    )(*([values] if total is None else [values, total]), *([near_blocks] * len(slots)))


def whole(shape):
    return pl.BlockSpec(shape, lambda *_: (0,) * len(shape))


def shards_real(currents, projection, near_blocks, partners, shifts, green):
    row_count = lax.axis_size("row")
    col_count = lax.axis_size("col")
    elements = currents.shape[2]
    width = col_count * LANES
    length = 2 * width
    quarter = length // 4
    f32, b16 = jnp.float32, jnp.bfloat16
    struct = jax.ShapeDtypeStruct
    devices = row_count * col_count

    charges = pl.pallas_call(
        charge_kernel,
        grid=(STEN,),
        in_specs=[
            whole((RHS, BASIS, elements)),
            pl.BlockSpec((STEN, BASIS, elements), lambda i: (i, 0, 0)),
            whole((2, elements)),
        ],
        out_specs=whole((SUB, 128, LANES)),
        out_shape=struct((SUB, 128, LANES), b16),
        scratch_shapes=[
            pltpu.VMEM((RHS, BASIS, elements), f32),
            pltpu.VMEM((STEN, SUB, SUB, LANES), f32),
            pltpu.VMEM((STEN * STEN, SUB, LANES), f32),
        ],
        name="charges",
    )(currents, projection, shifts)
    slab = lax.all_to_all(charges, "col", 0, 0, tiled=True)

    columns, rows = even_positions(row_count, col_count)
    table = struct((quarter, quarter), b16)
    col_tables = pl.pallas_call(column_table_kernel, out_shape=[table] * 3, name="column_tables")(
        *position_bases(columns, length)
    )
    spread = struct((2 * quarter, LANES), f32)
    row_tables = pl.pallas_call(
        row_table_kernel, out_shape=[table] * 6 + [spread] * 2, name="row_tables"
    )(green, *position_bases(rows, length), *order_bases(rows, length))

    spectrum = pl.pallas_call(
        functools.partial(column_kernel, col_count),
        out_shape=struct((devices, 40, LANES), b16),
        name="columns",
    )(slab, *col_tables)
    spectrum, held = lax.optimization_barrier((spectrum, currents))
    arrived = lax.all_to_all(spectrum, ("row", "col"), 0, 0, tiled=True)
    near = near_call(held, None, near_blocks, (0,), 0, BASIS // SUB)
    arrived, near = lax.optimization_barrier((arrived, near))
    rows_back = pl.pallas_call(
        functools.partial(row_kernel, row_count, col_count),
        out_shape=struct((devices, 40, LANES), b16),
        name="rows",
    )(arrived, *row_tables)
    rows_back, ready = lax.optimization_barrier((rows_back, arrived))
    returned = lax.all_to_all(rows_back, ("row", "col"), 0, 0, tiled=True)
    picked = pl.pallas_call(
        pick_kernel, out_shape=struct((NEIGH - 1, RHS, BASIS, elements), b16), name="pick"
    )(held, slab, ready, partners)
    others = tuple(range(1, NEIGH))
    near = near_call(picked, near, near_blocks, others, 0, BASIS // SUB // 2)
    returned, near, picked = lax.optimization_barrier((returned, near, picked))
    potential = pl.pallas_call(
        functools.partial(grid_kernel, col_count),
        out_shape=struct((SUB, 80, LANES), b16),
        name="grid",
    )(returned, *col_tables)
    potential, near, picked = lax.optimization_barrier((potential, near, picked))
    pieces = lax.all_to_all(potential, "col", 0, 0, tiled=True)
    near = near_call(picked, near, near_blocks, others, BASIS // SUB // 2, BASIS // SUB)

    depth = 16
    return pl.pallas_call(
        far_kernel,
        grid=(BASIS // depth,),
        in_specs=[
            whole((SUB, 80, LANES)),
            pl.BlockSpec((STEN * STEN, depth, elements), lambda i: (0, i, 0)),
            whole((2, elements)),
            pl.BlockSpec((RHS, depth, elements), lambda i: (0, i, 0)),
        ],
        out_specs=pl.BlockSpec((RHS, depth, elements), lambda i: (0, i, 0)),
        out_shape=struct((RHS, BASIS, elements), f32),
        scratch_shapes=[pltpu.VMEM((STEN * STEN, SUB, LANES), f32)],
        name="far",
    )(pieces, projection, shifts, near)


def shards(currents, projection, near_blocks, partners, shifts, green):
    row_count = lax.axis_size("row")
    col_count = lax.axis_size("col")
    fits = col_count == SUB and green.shape[0] == 64 and 2 * row_count * col_count == green.shape[0]
    if fits and currents.shape[2] == TILES * LANES and row_count * ER == col_count * EC:
        return shards_real(currents, projection, near_blocks, partners, shifts, green)
    return shards_general(currents, projection, near_blocks, partners, shifts, green)


def solution(mesh):
    in_specs = (
        P(None, None, ("row", "col")),
        P(None, None, ("row", "col")),
        P(None, None, None, ("row", "col")),
        P(None, ("row", "col")),
        P(None, ("row", "col")),
        P(("row", "col"), None),
    )
    out_specs = P(None, None, ("row", "col"))
    return jax.shard_map(shards, mesh=mesh, in_specs=in_specs, out_specs=out_specs, check_vma=False)
```

```python
import functools
import math

import jax
import jax.numpy as jnp
import numpy as np
from jax import lax
from jax.experimental import pallas as pl
from jax.experimental.pallas import tpu as pltpu
from jax.sharding import PartitionSpec as P

BASIS = 64
STEN = 8
PITCH = 8
HALO = 2
NEIGH = 4
RHS = 2
ER = 32
EC = 16


def extended_2(block, sides, width):
    for axis, dim in sides:
        count = lax.axis_size(axis)
        forward = [(i, i + 1) for i in range(count - 1)]
        backward = [(target, source) for source, target in forward]
        low = lax.ppermute(
            lax.slice_in_dim(block, block.shape[dim] - width, None, axis=dim), axis, forward
        )
        high = lax.ppermute(lax.slice_in_dim(block, 0, width, axis=dim), axis, backward)
        block = jnp.concatenate([low, block, high], axis=dim)
    return block


def angle_table(first_size, second_size, modulus, direction):
    left_index = jnp.arange(first_size, dtype=jnp.int32)
    right_index = jnp.arange(second_size, dtype=jnp.int32)
    turn_count = left_index[:, None] * right_index[None, :] % modulus
    angles = turn_count.astype(jnp.float32) * (2.0 * math.pi / modulus)
    return (jnp.cos(angles), direction * jnp.sin(angles))


def complex_apply(real_part, imag_part, cosine, sine_table, pattern):
    highest = lax.Precision.HIGHEST
    out_real = jnp.einsum(pattern, real_part, cosine, precision=highest)
    out_imag = jnp.einsum(pattern, real_part, sine_table, precision=highest)
    if imag_part is not None:
        out_real = out_real - jnp.einsum(pattern, imag_part, sine_table, precision=highest)
        out_imag = out_imag + jnp.einsum(pattern, imag_part, cosine, precision=highest)
    return (out_real, out_imag)


def transform_last(real_part, imag_part, length, count_in, count_out, direction):
    leading = real_part.shape[:-1]
    inner_size = 128
    outer_size = length // inner_size
    rows_in = count_in // inner_size
    kept_count = count_out // outer_size
    shaped_real = real_part.reshape(leading + (rows_in, inner_size))
    shaped_imag = None
    if imag_part is not None:
        shaped_imag = imag_part.reshape(leading + (rows_in, inner_size))
    cosine, sine_table = angle_table(rows_in, outer_size, outer_size, direction)
    first_real, first_imag = complex_apply(
        shaped_real, shaped_imag, cosine, sine_table, "...ab,ak->...kb"
    )
    twist_cos, twist_sin = angle_table(outer_size, inner_size, length, direction)
    turned_real = first_real * twist_cos - first_imag * twist_sin
    turned_imag = first_real * twist_sin + first_imag * twist_cos
    cosine, sine_table = angle_table(inner_size, kept_count, inner_size, direction)
    last_real, last_imag = complex_apply(
        turned_real, turned_imag, cosine, sine_table, "...kb,bj->...jk"
    )
    out_shape = leading + (kept_count * outer_size,)
    return (last_real.reshape(out_shape), last_imag.reshape(out_shape))


def place_shifted(blocks, amount, dim_index):
    new_shape = list(blocks.shape)
    new_shape[dim_index] = new_shape[dim_index] + 2 * HALO
    result = jnp.zeros(tuple(new_shape), blocks.dtype)
    for offset in range(-HALO, HALO + 1):
        widths = [(0, 0)] * blocks.ndim
        widths[dim_index] = (HALO + offset, HALO - offset)
        result = jnp.where(amount == offset, jnp.pad(blocks, widths), result)
    return result


def pick_shifted(windows, amount, dim_index):
    new_shape = list(windows.shape)
    new_shape[dim_index] = STEN
    result = jnp.zeros(tuple(new_shape), windows.dtype)
    for offset in range(-HALO, HALO + 1):
        piece = lax.slice_in_dim(windows, HALO + offset, HALO + offset + STEN, axis=dim_index)
        result = jnp.where(amount == offset, piece, result)
    return result


def intersection_add(framed, dim_index):
    element_count = framed.shape[dim_index]
    window_size = framed.shape[dim_index + 1]
    head_part = lax.slice_in_dim(framed, 0, PITCH, axis=dim_index + 1)
    tail_part = lax.slice_in_dim(framed, PITCH, window_size, axis=dim_index + 1)
    widths = [(0, 0)] * framed.ndim
    widths[dim_index + 1] = (0, 2 * PITCH - window_size)
    tail_part = jnp.pad(tail_part, widths)
    merged = framed.shape[:dim_index] + (element_count * PITCH,) + framed.shape[dim_index + 2 :]
    head_part = head_part.reshape(merged)
    tail_part = tail_part.reshape(merged)
    front_pad = [(0, 0)] * len(merged)
    front_pad[dim_index] = (0, PITCH)
    back_pad = [(0, 0)] * len(merged)
    back_pad[dim_index] = (PITCH, 0)
    summed = jnp.pad(head_part, front_pad) + jnp.pad(tail_part, back_pad)
    return lax.slice_in_dim(summed, 0, element_count * PITCH + 2 * HALO, axis=dim_index)


def cut_windows(field, dim_index):
    element_count = (field.shape[dim_index] - 2 * HALO) // PITCH
    widths = [(0, 0)] * field.ndim
    widths[dim_index] = (0, PITCH - 2 * HALO)
    extended = jnp.pad(field, widths)
    split_shape = field.shape[:dim_index] + (element_count, PITCH) + field.shape[dim_index + 1 :]
    head_part = lax.slice_in_dim(extended, 0, element_count * PITCH, axis=dim_index).reshape(
        split_shape
    )
    tail_part = lax.slice_in_dim(
        extended, PITCH, PITCH + element_count * PITCH, axis=dim_index
    ).reshape(split_shape)
    tail_part = lax.slice_in_dim(tail_part, 0, 2 * HALO, axis=dim_index + 1)
    return jnp.concatenate([head_part, tail_part], axis=dim_index + 1)


def fold_margin(padded, dim_index):
    full_size = padded.shape[dim_index]
    inner_size = full_size - 4 * HALO
    core_part = lax.slice_in_dim(padded, 2 * HALO, 2 * HALO + inner_size, axis=dim_index)
    upper_part = lax.slice_in_dim(padded, 0, HALO, axis=dim_index)
    lower_part = lax.slice_in_dim(padded, full_size - HALO, full_size, axis=dim_index)
    upper_pad = [(0, 0)] * padded.ndim
    upper_pad[dim_index] = (0, inner_size - HALO)
    lower_pad = [(0, 0)] * padded.ndim
    lower_pad[dim_index] = (inner_size - HALO, 0)
    return core_part + jnp.pad(upper_part, upper_pad) + jnp.pad(lower_part, lower_pad)


def shards_general(currents, projection, near_blocks, partners, shifts, green):
    row_count = lax.axis_size("row")
    col_count = lax.axis_size("col")
    device_count = row_count * col_count
    elements = ER * EC
    cur_half = currents.astype(jnp.bfloat16)
    spread = extended_2(cur_half.reshape(RHS, BASIS, ER, EC), (("row", 2), ("col", 3)), 1)
    views = []
    for symbol in range(9):
        row_start = symbol // 3
        col_start = symbol % 3
        views.append(
            spread[:, :, row_start : row_start + ER, col_start : col_start + EC].reshape(
                RHS, BASIS, elements
            )
        )
    picked = []
    for neighbour_slot in range(NEIGH):
        chosen = jnp.zeros((RHS, BASIS, elements), jnp.bfloat16)
        for symbol in range(9):
            chosen = jnp.where(partners[neighbour_slot] == symbol, views[symbol], chosen)
        picked.append(chosen)
    near_term = jnp.einsum(
        "kabn,kqbn->qan", near_blocks, jnp.stack(picked), preferred_element_type=jnp.float32
    )
    stencil = jnp.einsum("sbn,qbn->qsn", projection, cur_half, preferred_element_type=jnp.float32)
    blocks = stencil.reshape(RHS, STEN, STEN, elements)
    framed = place_shifted(place_shifted(blocks, shifts[0], 1), shifts[1], 2)
    window_size = STEN + 2 * HALO
    framed = framed.reshape(RHS, window_size, window_size, ER, EC).transpose(0, 3, 1, 4, 2)
    extended = intersection_add(intersection_add(framed, 1), 2)
    padded = extended_2(extended, (("row", 1), ("col", 2)), HALO)
    charges = fold_margin(fold_margin(padded, 1), 2)
    slab = lax.all_to_all(charges, "col", split_axis=1, concat_axis=2, tiled=True)
    slab_rows = slab.shape[1]
    width_cols = slab.shape[2]
    length_cols = 2 * width_cols
    block_cols = length_cols // device_count
    grid_rows = slab_rows * device_count
    length_rows = 2 * grid_rows
    fwd_real, fwd_imag = transform_last(slab, None, length_cols, width_cols, length_cols, -1.0)
    out_real = fwd_real.reshape(RHS, slab_rows, device_count, block_cols)
    out_imag = fwd_imag.reshape(RHS, slab_rows, device_count, block_cols)
    arrived = (
        lax.all_to_all(out_real, ("row", "col"), split_axis=2, concat_axis=2, tiled=True),
        lax.all_to_all(out_imag, ("row", "col"), split_axis=2, concat_axis=2, tiled=True),
    )
    col_real = arrived[0].transpose(0, 3, 2, 1).reshape(RHS, block_cols, grid_rows)
    col_imag = arrived[1].transpose(0, 3, 2, 1).reshape(RHS, block_cols, grid_rows)
    spec_real, spec_imag = transform_last(
        col_real, col_imag, length_rows, grid_rows, length_rows, -1.0
    )
    spec_real = spec_real * green
    spec_imag = spec_imag * green
    back_real, back_imag = transform_last(
        spec_real, spec_imag, length_rows, length_rows, grid_rows, 1.0
    )
    send_real = back_real.reshape(RHS, block_cols, device_count, slab_rows)
    send_imag = back_imag.reshape(RHS, block_cols, device_count, slab_rows)
    returned = (
        lax.all_to_all(send_real, ("row", "col"), split_axis=2, concat_axis=2, tiled=True),
        lax.all_to_all(send_imag, ("row", "col"), split_axis=2, concat_axis=2, tiled=True),
    )
    rows_real = returned[0].transpose(0, 3, 2, 1).reshape(RHS, slab_rows, length_cols)
    rows_imag = returned[1].transpose(0, 3, 2, 1).reshape(RHS, slab_rows, length_cols)
    final_real, final_imag = transform_last(
        rows_real, rows_imag, length_cols, length_cols, width_cols, 1.0
    )
    potential_slab = final_real * (1.0 / (length_rows * length_cols))
    potential = lax.all_to_all(potential_slab, "col", split_axis=2, concat_axis=1, tiled=True)
    rimmed = extended_2(potential, (("row", 1), ("col", 2)), HALO)
    windows = cut_windows(cut_windows(rimmed, 1), 3)
    windows = windows.transpose(0, 2, 4, 1, 3).reshape(RHS, window_size, window_size, elements)
    samples = pick_shifted(pick_shifted(windows, shifts[0], 1), shifts[1], 2).reshape(
        RHS, STEN * STEN, elements
    )
    sample_high = samples.astype(jnp.bfloat16)
    sample_low = (samples - sample_high.astype(jnp.float32)).astype(jnp.bfloat16)
    far_term = jnp.einsum(
        "sbn,qsn->qbn", projection, sample_high, preferred_element_type=jnp.float32
    )
    far_term = far_term + jnp.einsum(
        "sbn,qsn->qbn", projection, sample_low, preferred_element_type=jnp.float32
    )
    return far_term + near_term


LANES = 128
SUB = 8
TILES = 4
GROUPS = 9
PARITY_ORDER = (0, 2, 4, 6, 1, 3, 5, 7)


def roll(value, amount, dim):
    return pltpu.roll(value, amount % value.shape[dim], dim)


def lane_index(shape):
    return lax.broadcasted_iota(jnp.int32, shape, len(shape) - 1)


def sub_index(shape):
    return lax.broadcasted_iota(jnp.int32, shape, len(shape) - 2)


def sum_rows(parts):
    sub = sub_index(parts[0].shape)
    top = sub < 4
    level = []
    for i in range(4):
        a, b = parts[i], parts[i + 4]
        level.append(jnp.where(top, a, b) + roll(jnp.where(top, b, a), 4, 0))
    mask = (sub & 2) == 0
    level = [
        jnp.where(mask, level[i], level[i + 2])
        + jnp.where(mask, roll(level[i], -2, 0), roll(level[i + 2], 2, 0))
        for i in range(2)
    ]
    mask = (sub & 1) == 0
    a, b = level
    return jnp.where(mask, a, b) + jnp.where(mask, roll(a, -1, 0), roll(b, 1, 0))


def next_row(value):
    lane = lane_index(value.shape)
    sub = sub_index(value.shape)
    turned = roll(value, EC, 1)
    carried = jnp.where((sub & 3) == 0, 0.0, roll(turned, 1, 0))
    return jnp.where(lane < EC, carried, turned)


def previous_row(value):
    lane = lane_index(value.shape)
    sub = sub_index(value.shape)
    turned = roll(value, -EC, 1)
    carried = jnp.where((sub & 3) == 3, 0.0, roll(turned, -1, 0))
    return jnp.where(lane >= LANES - EC, carried, turned)


def place_charges(stencil, row_shift, col_shift):
    shape = row_shift.shape
    lane = lane_index(shape)
    sub = sub_index(shape)
    window = STEN + 2 * HALO
    row_mask = {o: row_shift == o for o in range(-HALO, HALO + 1)}
    col_mask = {o: col_shift == o for o in range(-HALO, HALO + 1)}
    first = []
    for rr in range(window):
        line = []
        for c in range(STEN):
            value = jnp.zeros(shape, jnp.float32)
            for o in range(-HALO, HALO + 1):
                source = rr - HALO - o
                if 0 <= source < STEN:
                    value = jnp.where(row_mask[o], stencil(source * STEN + c), value)
            line.append(value)
        first.append(line)
    framed = []
    for rr in range(window):
        line = []
        for cc in range(window):
            value = jnp.zeros(shape, jnp.float32)
            for o in range(-HALO, HALO + 1):
                source = cc - HALO - o
                if 0 <= source < STEN:
                    value = jnp.where(col_mask[o], first[rr][source], value)
            line.append(value)
        framed.append(line)
    grid = []
    for r in range(PITCH):
        line = []
        for cc in range(window):
            value = framed[r + HALO][cc]
            if r < HALO:
                value = value + next_row(framed[r + HALO + PITCH][cc])
            if r >= PITCH - HALO:
                value = value + previous_row(framed[r + HALO - PITCH][cc])
            line.append(value)
        grid.append(line)
    slot = sub & 3
    low_lanes = lane < EC
    high_lanes = lane >= LANES - EC
    line = []
    for cc in range(window):
        value = jnp.where(low_lanes & (slot == 0), roll(roll(framed[10][cc], EC, 1), -3, 0), 0.0)
        value = jnp.where(low_lanes & (slot == 1), roll(roll(framed[11][cc], EC, 1), -2, 0), value)
        value = jnp.where(high_lanes & (slot == 3), roll(roll(framed[0][cc], -EC, 1), 3, 0), value)
        value = jnp.where(high_lanes & (slot == 2), roll(roll(framed[1][cc], -EC, 1), 2, 0), value)
        line.append(value)
    grid.append(line)
    elem_col = lane & (EC - 1)
    parts = [[] for _ in range(SUB)]
    edges = [jnp.zeros(shape, jnp.float32) for _ in range(SUB)]
    for r in range(GROUPS):
        cells = []
        for c in range(PITCH):
            value = grid[r][c + HALO]
            if c < HALO:
                value = value + jnp.where(elem_col == 0, 0.0, roll(grid[r][c + HALO + PITCH], 1, 1))
            if c >= PITCH - HALO:
                value = value + jnp.where(
                    elem_col == EC - 1, 0.0, roll(grid[r][c + HALO - PITCH], -1, 1)
                )
            cells.append(value)
        turned = transpose_blocks([cells[c] for c in PARITY_ORDER], lane)
        for e in range(SUB):
            parts[e].append(turned[e])
            start = EC * e
            edge = edges[e]
            edge = jnp.where(lane == r, roll(grid[r][10], r - start - (EC - 1), 1), edge)
            edge = jnp.where(lane == 64 + r, roll(grid[r][11], 64 + r - start - (EC - 1), 1), edge)
            edge = jnp.where(lane == 63 - r, roll(grid[r][0], 63 - r - start, 1), edge)
            edge = jnp.where(lane == 127 - r, roll(grid[r][1], 127 - r - start, 1), edge)
            edges[e] = edge
    return [parts[e] + [edges[e]] for e in range(SUB)]


def transpose_blocks(values, lane):
    block = lane // EC
    for step in (4, 2, 1):
        mask = (block & step) == 0
        result = list(values)
        for i in range(SUB):
            if i & step:
                continue
            a, b = values[i], values[i + step]
            result[i] = jnp.where(mask, a, roll(b, EC * step, 1))
            result[i + step] = jnp.where(mask, roll(a, -EC * step, 1), b)
        values = result
    return values


def halves(a, b):
    low = lane_index(a.shape) < 64
    return jnp.where(low, a, roll(b, 64, 1)), jnp.where(low, roll(a, 64, 1), b)


def half_rows(a, b):
    top = sub_index(a.shape) < 4
    return jnp.where(top, a, roll(b, 4, 0)), jnp.where(top, roll(a, 4, 0), b)


def gather_rows(part, edge, count):
    sample = edge(0)
    lane = lane_index(sample.shape)
    from_low = (lane == 0) | (lane == 64)
    from_high = (lane == 63) | (lane == 127)
    rows = []
    for j in range(count):
        groups = []
        for r in range(GROUPS):
            value = part(j, r)
            if j > 0:
                value = value + jnp.where(from_low, roll(edge(j - 1), -r, 1), 0.0)
            if j < count - 1:
                value = value + jnp.where(from_high, roll(edge(j + 1), r, 1), 0.0)
            groups.append(value)
        first, second = [], []
        for parity in range(2):
            for b in range(2):
                low, high = half_rows(groups[parity + 4 * b], groups[parity + 4 * b + 2])
                first.append(low)
                second.append(high)
        low, high = half_rows(groups[8], groups[8])
        first.append(low)
        second.append(high)
        rows.append(jnp.concatenate(first + second, axis=0))
    even, odd = [], []
    for j in range(0, count, 2):
        low, high = halves(rows[j], rows[j + 1])
        even.append(low)
        odd.append(high)
    return jnp.concatenate(even, axis=1), jnp.concatenate(odd, axis=1)


def scatter_rows(even, odd, count, put):
    rows = []
    for j in range(0, count, 2):
        tile = slice(64 * j, 64 * j + LANES)
        rows.extend(halves(even[:, tile], odd[:, tile]))
    blocks = []
    for j in range(count):
        first = [rows[j][8 * i : 8 * i + 8] for i in range(5)]
        second = [rows[j][40 + 8 * i : 48 + 8 * i] for i in range(5)]
        groups = [None] * GROUPS
        for parity in range(2):
            for b in range(2):
                low, high = half_rows(first[2 * parity + b], second[2 * parity + b])
                groups[parity + 4 * b] = low
                groups[parity + 4 * b + 2] = high
        sub = sub_index(first[4].shape)
        tail = jnp.where(sub < 4, roll(first[4], 4, 0), second[4])
        head = jnp.where(sub < 4, first[4], roll(second[4], 4, 0))
        groups[8] = jnp.where((sub & 2) == 0, head, tail)
        blocks.append(groups)
    lane = lane_index(blocks[0][0].shape)
    for j in range(count):
        edge = jnp.zeros(blocks[0][0].shape, jnp.float32)
        for r in range(GROUPS):
            if j < count - 1:
                edge = jnp.where(
                    (lane == r) | (lane == 64 + r), roll(blocks[j + 1][r], r, 1), edge
                )
            if j > 0:
                edge = jnp.where(
                    (lane == 63 - r) | (lane == 127 - r), roll(blocks[j - 1][r], -r, 1), edge
                )
        put(j, blocks[j] + [edge])


def read_samples(part, edge, row_shift, col_shift, put):
    shape = row_shift.shape
    lane = lane_index(shape)
    sub = sub_index(shape)
    elem_col = lane & (EC - 1)
    window = STEN + 2 * HALO
    grid = []
    for r in range(GROUPS):
        turned = transpose_blocks([part(e, r) for e in range(SUB)], lane)
        cells = [None] * PITCH
        for place, c in enumerate(PARITY_ORDER):
            cells[c] = turned[place]
        line = [None] * window
        for c in range(PITCH):
            line[c + HALO] = cells[c]
        after = [roll(cells[c], -1, 1) for c in range(HALO)]
        before = [roll(cells[PITCH - HALO + c], 1, 1) for c in range(HALO)]
        for e in range(SUB):
            start = EC * e
            last = lane == start + EC - 1
            zero = lane == start
            after[0] = jnp.where(last, roll(edge(e), start + EC - 1 - r, 1), after[0])
            after[1] = jnp.where(last, roll(edge(e), start + EC - 1 - 64 - r, 1), after[1])
            before[0] = jnp.where(zero, roll(edge(e), start - 63 + r, 1), before[0])
            before[1] = jnp.where(zero, roll(edge(e), start - 127 + r, 1), before[1])
        line[0], line[1] = before
        line[10], line[11] = after
        grid.append(line)
    slot = sub & 3
    first_row = (slot == 0) & (lane < EC)
    last_row = (slot == 3) & (lane >= LANES - EC)
    framed = [[None] * window for _ in range(window)]
    for cc in range(window):
        for r in range(PITCH):
            framed[r + HALO][cc] = grid[r][cc]
        outer = grid[8][cc]
        below = roll(outer, -EC, 1)
        above = roll(outer, EC, 1)
        framed[10][cc] = jnp.where(last_row, roll(below, 3, 0), previous_row(grid[0][cc]))
        framed[11][cc] = jnp.where(last_row, roll(below, 2, 0), previous_row(grid[1][cc]))
        framed[0][cc] = jnp.where(first_row, roll(above, -3, 0), next_row(grid[6][cc]))
        framed[1][cc] = jnp.where(first_row, roll(above, -2, 0), next_row(grid[7][cc]))
    for a in range(STEN):
        line = []
        for cc in range(window):
            value = framed[a + HALO][cc]
            for o in range(-HALO, HALO + 1):
                if o:
                    value = jnp.where(row_shift == o, framed[a + HALO + o][cc], value)
            line.append(value)
        for b in range(STEN):
            value = line[b + HALO]
            for o in range(-HALO, HALO + 1):
                if o:
                    value = jnp.where(col_shift == o, line[b + HALO + o], value)
            put(a * STEN + b, value)


def add_outer_rows(chunk, row_count, col_count):
    sub = sub_index((SUB, LANES))
    even, odd = [], []
    for i in range(row_count):
        for j in range(col_count):
            rows = [chunk(i, j)[8 * k : 8 * k + 8] for k in range(4)]
            if j == 0 and i > 0:
                outer = chunk(i - 1, 0)[32:40]
                rows[0] = rows[0] + jnp.where(sub == 0, outer, 0.0)
                rows[2] = rows[2] + jnp.where(sub == 0, roll(outer, -1, 0), 0.0)
            if j == col_count - 1 and i < row_count - 1:
                outer = chunk(i + 1, j)[32:40]
                rows[1] = rows[1] + jnp.where(sub == 7, outer, 0.0)
                rows[3] = rows[3] + jnp.where(sub == 7, roll(outer, 1, 0), 0.0)
            even.extend(rows[:2])
            odd.extend(rows[2:])
    return jnp.concatenate(even, axis=0), jnp.concatenate(odd, axis=0)


def spread_outer_rows(even, odd, row_count, col_count, put):
    sub = sub_index((SUB, LANES))

    def block(i, j):
        start = 16 * (i * col_count + j)
        return [even[start : start + 8], even[start + 8 : start + 16],
                odd[start : start + 8], odd[start + 8 : start + 16]]

    for i in range(row_count):
        for j in range(col_count):
            outer = jnp.zeros((SUB, LANES), jnp.float32)
            if j == 0 and i < row_count - 1:
                rows = block(i + 1, 0)
                outer = jnp.where(sub == 0, rows[0], jnp.where(sub == 1, roll(rows[2], 1, 0), outer))
            if j == col_count - 1 and i > 0:
                rows = block(i - 1, j)
                outer = jnp.where(sub == 7, rows[1], jnp.where(sub == 6, roll(rows[3], -1, 0), outer))
            put(i, j, block(i, j) + [outer])


def two_terms(value):
    high = value.astype(jnp.bfloat16)
    return high, (value - high.astype(jnp.float32)).astype(jnp.bfloat16)


def dot(left, right, dims=((1,), (0,))):
    return lax.dot_general(left, right, (dims, ((), ())), preferred_element_type=jnp.float32)


def even_positions(row_count, col_count):
    j, c, e = np.meshgrid(np.arange(col_count), np.arange(4), np.arange(EC), indexing="ij")
    columns = (LANES * j + PITCH * e + 2 * c).reshape(-1)
    i, j, b, h, t = np.meshgrid(
        np.arange(row_count), np.arange(col_count), np.arange(2), np.arange(2), np.arange(TILES),
        indexing="ij",
    )
    rows = (ER * PITCH * i + SUB * PITCH * t + PITCH * j + 2 * h + 4 * b).reshape(-1)
    return columns, rows


def angle_pair(left, right, length):
    angles = 2.0 * np.pi * (np.asarray(left)[:, None] * np.asarray(right)[None, :] % length) / length
    return np.asarray(np.cos(angles), np.float32), np.asarray(np.sin(angles), np.float32)


def position_bases(positions, length):
    orders = np.arange(length // 4)
    grouped = positions.reshape(-1, SUB)
    offsets = grouped[0] - grouped[0, 0]
    assert (grouped == grouped[:, :1] + offsets[None, :]).all()
    return (
        *angle_pair(grouped[:, 0], orders, length),
        *angle_pair(offsets, orders, length),
        *angle_pair(offsets + 1, orders, length),
    )


def order_bases(positions, length):
    bases = np.arange(0, length // 4, SUB)
    result = []
    for parity in range(2):
        result.extend(angle_pair(bases, positions + parity, length))
        result.extend(angle_pair(np.arange(SUB), positions + parity, length))
    return tuple(result)


def fill_by_position(sign_of, bases, out_refs):
    base_cos, base_sin, even_cos, even_sin, odd_cos, odd_sin = bases
    ec, es, oc, os = (ref[...] for ref in (even_cos, even_sin, odd_cos, odd_sin))
    start = lane_index(ec.shape) == 0

    def pair(i, carry):
        parts = [[], [], []]
        for h in range(2):
            row = 2 * i + h
            bc, bs = base_cos[pl.ds(row, 1), :], base_sin[pl.ds(row, 1), :]
            parts[0].append(bc * ec - bs * es)
            parts[1].append(jnp.where(start, 1.0, -(bs * ec + bc * es)) * sign_of(row))
            parts[2].append(bc * oc - bs * os)
        rows = pl.ds(pl.multiple_of(16 * i, 16), 16)
        for ref, part in zip(out_refs, parts):
            ref[rows, :] = jnp.concatenate(part, axis=0).astype(ref.dtype)
        return carry

    lax.fori_loop(0, base_cos.shape[0] // 2, pair, 0)


def column_table_kernel(*refs):
    fill_by_position(lambda row: (1 - 2 * ((row // 2) & 1)).astype(jnp.float32), refs[:6], refs[6:])


def row_table_kernel(green_ref, *refs):
    position, order, outs = refs[:6], refs[6:14], refs[14:]
    quarter = position[0].shape[1]
    tiles = quarter // LANES
    sub = sub_index((SUB, quarter))
    flip = jnp.where(sub < 4, 1.0, -1.0)
    fill_by_position(lambda row: flip, position, outs[3:6])
    ebc, ebs, ec, es, obc, obs, oc, os = order
    ec, es, oc, os = (ref[...] for ref in (ec, es, oc, os))
    lanes = jnp.where((lane_index((SUB, quarter)) & 4) == 0, 1.0, -1.0)

    def pair(i, carry):
        parts = [[], [], []]
        for h in range(2):
            row = 2 * i + h
            one = (pl.ds(row, 1), slice(None))
            bc, bs = ebc[one], ebs[one]
            parts[0].append(bc * ec - bs * es)
            first = (sub + row) == 0
            parts[1].append(jnp.where(first, 1.0, -(bs * ec + bc * es)) * lanes)
            parts[2].append(obc[one] * oc - obs[one] * os)
        rows = pl.ds(pl.multiple_of(16 * i, 16), 16)
        for ref, part in zip(outs[:3], parts):
            ref[rows, :] = jnp.concatenate(part, axis=0).astype(ref.dtype)
        return carry

    lax.fori_loop(0, ebc.shape[0] // 2, pair, 0)

    depth = green_ref.shape[0]
    device = lax.axis_index("row") * lax.axis_size("col") + lax.axis_index("col")
    number = sub_index((depth, LANES)) + device * depth
    length = 4 * quarter
    weight = jnp.where(number % quarter == 0, 1.0, 2.0) * (1.0 / (length * length))
    lane = lane_index((depth, LANES))

    def scaled(tile):
        value = green_ref[:, LANES * tile : LANES * (tile + 1)] * weight
        if tile % tiles == 0:
            value = value * jnp.where(lane == 0, 1.0, 2.0)
        else:
            value = value * 2.0
        return jnp.concatenate([value, value], axis=0)

    for t in range(tiles):
        cos_plus, cos_minus = scaled(t), scaled(2 * tiles + t)
        sin_minus, sin_plus = scaled(tiles + t), scaled(3 * tiles + t)
        first = slice(LANES * t, LANES * (t + 1))
        second = slice(quarter + LANES * t, quarter + LANES * (t + 1))
        outs[6][first, :] = (cos_plus + cos_minus).T
        outs[7][first, :] = (cos_plus - cos_minus).T
        outs[6][second, :] = (sin_plus + sin_minus).T
        outs[7][second, :] = (sin_plus - sin_minus).T


def tiled_shifts(shifts_ref, which):
    rows = [shifts_ref[which : which + 1, LANES * t : LANES * (t + 1)] for t in range(TILES)]
    return jnp.concatenate(rows * RHS, axis=0)


def charge_kernel(
    currents_ref, projection_ref, shifts_ref, out_ref, weights, raw, shifts, current, partial, stencil, sems
):
    copies = [
        pltpu.make_async_copy(currents_ref, raw, sems.at[STEN]),
        pltpu.make_async_copy(shifts_ref, shifts, sems.at[STEN + 1]),
    ]

    def weight_copy(step):
        rows = pl.ds(step * STEN, STEN)
        return pltpu.make_async_copy(projection_ref.at[rows], weights.at[rows], sems.at[step])

    copies[0].start()
    for step in range(STEN):
        weight_copy(step).start()
    copies[1].start()
    copies[0].wait()
    current[...] = raw[...].astype(jnp.bfloat16).astype(jnp.float32)

    def one_row(step, carry):
        weight_copy(step).wait()
        for t in range(TILES):
            lanes = slice(LANES * t, LANES * (t + 1))
            totals = [[None] * RHS for _ in range(STEN)]
            for b in range(0, BASIS, 16):
                values = [
                    [current[q, b + 8 * h : b + 8 * h + 8, lanes] for h in range(2)]
                    for q in range(RHS)
                ]
                for s in range(STEN):
                    weight = weights[step * STEN + s, b : b + 16, lanes].astype(jnp.float32)
                    for q in range(RHS):
                        term = weight[:8] * values[q][0] + weight[8:] * values[q][1]
                        totals[s][q] = term if totals[s][q] is None else totals[s][q] + term
            for s in range(STEN):
                for q in range(RHS):
                    partial[s, q * TILES + t] = totals[s][q]
        for s in range(STEN):
            stencil[step * STEN + s] = sum_rows([partial[s, i] for i in range(SUB)])
        return carry

    lax.fori_loop(0, STEN, one_row, 0)
    copies[1].wait()
    chunks = place_charges(
        lambda s: stencil[s], tiled_shifts(shifts, 0), tiled_shifts(shifts, 1)
    )
    to_next, to_previous, to_rows = pack_currents(
        lambda q, t: current[q, :, LANES * t : LANES * (t + 1)]
    )
    mine = lax.axis_index("col")
    block = lane_index((SUB, LANES)) // EC
    middle = ((block & 3) == 1) | ((block & 3) == 2)
    for e in range(SUB):
        after = (mine == e - 1).astype(jnp.float32)
        before = (mine == e + 1).astype(jnp.float32)
        edge = jnp.where(middle, to_rows[e], chunks[e][GROUPS])
        rows = chunks[e][:GROUPS] + [edge, to_next * after + to_previous * before]
        out_ref[e] = jnp.concatenate(rows, axis=0).astype(out_ref.dtype)


def pack_currents(tile):
    half = BASIS // 2
    lane = lane_index((half, LANES))
    elem_col = lane & (EC - 1)
    to_next = jnp.zeros((half, LANES), jnp.float32)
    to_previous = jnp.zeros((half, LANES), jnp.float32)
    for q in range(RHS):
        for t in range(TILES):
            value = tile(q, t)
            for h in range(2):
                place = q * TILES + t + SUB * h
                part = value[half * h : half * (h + 1)]
                here = elem_col == place
                to_next = jnp.where(here, roll(part, place - (EC - 1), 1), to_next)
                to_previous = jnp.where(here, roll(part, place, 1), to_previous)
    lane = lane_index((SUB, LANES))
    to_rows = []
    for e in range(SUB):
        rows = jnp.zeros((SUB, LANES), jnp.float32)
        for q in range(RHS):
            span = slice(SUB * e, SUB * (e + 1))
            last = roll(tile(q, TILES - 1)[span], EC + EC * q - (LANES - EC), 1)
            first = roll(tile(q, 0)[span], 64 + EC + EC * q, 1)
            rows = jnp.where(lane // EC == 1 + q, last, jnp.where(lane // EC == 5 + q, first, rows))
        to_rows.append(rows)
    return to_next, to_previous, to_rows


def forward_rows(edge_row, j, count, which):
    lane = lane_index((SUB, LANES))
    start = EC + 64 * which
    value = roll(edge_row(j), -start, 1)
    for q in range(RHS):
        place = 2 * EC + 2 * q
        if j > 0:
            corner = roll(edge_row(j - 1), place - start - EC * q - (EC - 1), 1)
            value = jnp.where(lane == place, corner, value)
        if j < count - 1:
            corner = roll(edge_row(j + 1), place + 1 - start - EC * q, 1)
            value = jnp.where(lane == place + 1, corner, value)
    return jnp.where(lane < 64, roll(value, 2, 0), roll(roll(value, 64, 1), -2, 0))


def column_sign(shape):
    return jnp.where((lane_index(shape) & EC) == 0, 1.0, -1.0)


def column_kernel(count, rows_ref, even_cos, even_sin, odd_cos, out_ref):
    def part(j, r):
        return rows_ref[j, 8 * r : 8 * r + 8, :].astype(jnp.float32)

    even, odd = gather_rows(part, lambda j: part(j, GROUPS), count)
    both = jnp.concatenate([odd, odd * column_sign(odd.shape)], axis=0).astype(jnp.bfloat16)
    even = even.astype(jnp.bfloat16)
    ec, es = dot(even, even_cos[...]), dot(even, even_sin[...])
    both = dot(both, odd_cos[...])
    oc, os = both[: odd.shape[0]], both[odd.shape[0] :]
    half = out_ref.shape[1]
    mine = lax.axis_index("row")
    ends = [
        [forward_rows(lambda k: part(k, GROUPS), j, count, which) for which in range(2)]
        for j in range(count)
    ]
    sub = sub_index((SUB, LANES))
    middle = (sub >= 2) & (sub < 6)
    device = 0
    for block in (ec + oc, es - os, ec - oc, es + os):
        for t in range(0, block.shape[1], LANES):
            for chunk in halves(block[:half, t : t + LANES], block[half:, t : t + LANES]):
                i, j = device // count, device % count
                below = (mine == i - 1).astype(jnp.float32)
                above = (mine == i + 1).astype(jnp.float32)
                tail = jnp.where(
                    middle, ends[j][0] * below + ends[j][1] * above, chunk[half - SUB :]
                )
                chunk = jnp.concatenate([chunk[: half - SUB], tail], axis=0)
                out_ref[device] = chunk.astype(out_ref.dtype)
                device += 1


def row_kernel(row_count, col_count, in_ref, *refs):
    sources, out_ref, held, sems = refs[:8], refs[8], refs[9:17], refs[17]
    loads = [
        pltpu.make_async_copy(source, target, sems.at[n])
        for n, (source, target) in enumerate(zip(sources, held))
    ]
    for load in loads:
        load.start()
    even_cos, even_sin, odd_cos, back_cos, back_sin, back_odd, sum_ref, diff_ref = held
    even, odd = add_outer_rows(
        lambda i, j: in_ref[i * col_count + j].astype(jnp.float32), row_count, col_count
    )
    flip = jnp.where((sub_index(odd.shape) & 4) == 0, 1.0, -1.0)
    both = jnp.concatenate([odd, odd * flip], axis=1).astype(jnp.bfloat16)
    even = even.astype(jnp.bfloat16)
    for n in range(3):
        loads[n].wait()
    a = [dot(even_cos[...], even), dot(even_sin[...], even)]
    both = dot(odd_cos[...], both)
    b = [both[:, :LANES], both[:, LANES:]]
    quarter = odd.shape[0]
    for n in range(3, 8):
        loads[n].wait()

    def pieces(left, right):
        for k in range(2):
            span = slice(quarter * k, quarter * (k + 1))
            yield two_terms(left[k] * sum_ref[span, :] + right[k] * diff_ref[span, :])

    def fold(value):
        return value[:, :LANES] + value[:, LANES:]

    (ch, cl), (sh, sl) = pieces(a, b)
    even = fold(
        dot(back_cos[...], jnp.concatenate([ch, cl], axis=1))
        + dot(back_sin[...], jnp.concatenate([sh, sl], axis=1))
    )
    (ch, cl), (sh, sl) = pieces(b, a)
    both = dot(back_odd[...], jnp.concatenate([ch, cl, sh, sl], axis=1))
    odd = fold(both[:, : 2 * LANES]) + fold(both[:, 2 * LANES :]) * flip

    def put(i, j, parts):
        out_ref[i * col_count + j] = jnp.concatenate(parts, axis=0).astype(out_ref.dtype)

    spread_outer_rows(even, odd, row_count, col_count, put)


def grid_kernel(count, in_ref, even_cos, even_sin, odd_cos, out_ref):
    devices = in_ref.shape[0]
    first, second = [], []
    for d in range(0, devices, 2):
        low, high = halves(in_ref[d].astype(jnp.float32), in_ref[d + 1].astype(jnp.float32))
        first.append(low)
        second.append(high)
    per_block = devices // 8
    blocks = []
    for k in range(4):
        span = slice(per_block * k, per_block * (k + 1))
        blocks.append(
            jnp.concatenate(
                [jnp.concatenate(first[span], axis=1), jnp.concatenate(second[span], axis=1)], axis=0
            )
        )
    cos_plus, sin_minus, cos_minus, sin_plus = blocks
    half = cos_plus.shape[0]

    def back(values, table):
        terms = [term for value in values for term in two_terms(value)]
        result = dot(jnp.concatenate(terms, axis=0), table[...], ((1,), (1,)))
        return [
            result[2 * half * i : 2 * half * i + half] + result[2 * half * i + half : 2 * half * (i + 1)]
            for i in range(len(values))
        ]

    even = back([cos_plus + cos_minus], even_cos)[0] + back([sin_plus + sin_minus], even_sin)[0]
    odd, turned = back([cos_plus - cos_minus, sin_plus - sin_minus], odd_cos)
    odd = odd + turned * column_sign(odd.shape)

    def put(j, parts):
        out_ref[j] = jnp.concatenate(parts, axis=0).astype(out_ref.dtype)

    scatter_rows(even, odd, count, put)


def far_kernel(grid_ref, projection_ref, shifts_ref, near_ref, out_ref, weights, samples, shifts, totals_ref, sems):
    depth = 16
    count = BASIS // depth

    def load(i):
        rows = pl.ds(i * depth, depth)
        return pltpu.make_async_copy(
            projection_ref.at[:, rows], weights.at[:, rows], sems.at[1 + count + i]
        )

    load_shifts = pltpu.make_async_copy(shifts_ref, shifts, sems.at[0])
    load_shifts.start()
    for i in range(count):
        load(i).start()

    def part(e, r):
        return grid_ref[e, 8 * r : 8 * r + 8, :].astype(jnp.float32)

    def put(s, value):
        samples[s] = value

    load_shifts.wait()
    read_samples(
        part, lambda e: part(e, GROUPS), tiled_shifts(shifts, 0), tiled_shifts(shifts, 1), put
    )
    def store(i):
        rows = pl.ds(i * depth, depth)
        return pltpu.make_async_copy(totals_ref.at[:, rows], out_ref.at[:, rows], sems.at[1 + i])

    for i in range(count):
        span = slice(i * depth, (i + 1) * depth)
        load(i).wait()

        def add_row(a, totals):
            totals = list(totals)
            for b in range(STEN):
                s = a * STEN + b
                for t in range(TILES):
                    weight = weights[s, span, LANES * t : LANES * (t + 1)].astype(jnp.float32)
                    for q in range(RHS):
                        index = q * TILES + t
                        totals[index] = totals[index] + weight * samples[s, index : index + 1, :]
            return tuple(totals)

        start = tuple(
            near_ref[q, span, LANES * t : LANES * (t + 1)] for q in range(RHS) for t in range(TILES)
        )
        totals = lax.fori_loop(0, STEN, add_row, start)
        for q in range(RHS):
            for t in range(TILES):
                totals_ref[q, span, LANES * t : LANES * (t + 1)] = totals[q * TILES + t]
        store(i).start()
    for i in range(count):
        store(i).wait()


def pick_kernel(currents_ref, slab_ref, arrived_ref, partners_ref, out_ref):
    lane = lane_index((BASIS, LANES))
    elem_col = lane & (EC - 1)
    row, col = lax.axis_index("row"), lax.axis_index("col")
    col_count = lax.axis_size("col")
    devices = arrived_ref.shape[0]

    def column_edge(source):
        source = jnp.clip(source, 0, col_count - 1)
        return slab_ref[source, 80:112, :].astype(jnp.float32)

    from_left, from_right = column_edge(col - 1), column_edge(col + 1)

    def beside(edge, q, t, end):
        place = q * TILES + t
        return jnp.concatenate([roll(edge, end - place, 1), roll(edge, end - place - SUB, 1)], axis=0)

    def three(own, left, right):
        return (
            jnp.where(elem_col == 0, left, roll(own, 1, 1)),
            own,
            jnp.where(elem_col == EC - 1, right, roll(own, -1, 1)),
        )

    sub = sub_index((SUB, LANES))

    def outer_row(source):
        parts = []
        for j in range(col_count):
            index = jnp.clip(source * col_count + j, 0, devices - 1)
            value = arrived_ref[index, 32:40, :].astype(jnp.float32)
            parts.append(jnp.where(sub < 4, roll(value, -2, 0), roll(roll(value, 2, 0), -64, 1)))
        return jnp.concatenate(parts, axis=0)

    rows = outer_row(row - 1), outer_row(row + 1)

    def outer_three(value, q, start):
        own = roll(value, start - EC * q, 1)
        left = roll(value, start - 2 * EC - 2 * q, 1)
        right = roll(value, start + EC - 1 - 2 * EC - 2 * q - 1, 1)
        return three(own, left, right)

    for q in range(RHS):
        tiles = []
        for t in range(TILES):
            own = currents_ref[q, :, LANES * t : LANES * (t + 1)]
            own = own.astype(jnp.bfloat16).astype(jnp.float32)
            tiles.append(three(own, beside(from_left, q, t, 0), beside(from_right, q, t, EC - 1)))
        above = outer_three(rows[0], q, 0)
        below = outer_three(rows[1], q, LANES - EC)
        for t in range(TILES):
            lanes = slice(LANES * t, LANES * (t + 1))
            codes = [partners_ref[k : k + 1, lanes] for k in range(1, NEIGH)]
            chosen = [tiles[t][1]] * (NEIGH - 1)
            for c in range(3):
                here = tiles[t][c]
                before = roll(tiles[t - 1][c], EC, 1) if t else above[c]
                after = roll(tiles[t + 1][c], -EC, 1) if t < TILES - 1 else below[c]
                views = (
                    jnp.where(lane < EC, before, roll(here, EC, 1)),
                    here,
                    jnp.where(lane >= LANES - EC, after, roll(here, -EC, 1)),
                )
                for r in range(3):
                    if r == 1 and c == 1:
                        continue
                    for k in range(NEIGH - 1):
                        chosen[k] = jnp.where(codes[k] == 3 * r + c, views[r], chosen[k])
            for k in range(NEIGH - 1):
                out_ref[k, q, :, lanes] = chosen[k].astype(out_ref.dtype)


def near_kernel(has_total, slots, start, stop, *refs):
    values_ref, refs = refs[0], refs[1:]
    total_ref = None
    if has_total:
        total_ref, refs = refs[0], refs[1:]
    blocks_ref, out_ref, blocks, picked, sems = refs
    chunks = (stop - start) // SUB

    def load(chunk, k):
        rows = pl.ds(start + chunk * SUB, SUB)
        return pltpu.make_async_copy(
            blocks_ref.at[slots[k], rows], blocks.at[chunk, k], sems.at[chunk, k]
        )

    for chunk in range(chunks):
        for k in range(len(slots)):
            load(chunk, k).start()
    picked[...] = values_ref[...].astype(jnp.bfloat16).astype(jnp.float32).reshape(picked.shape)
    if has_total:
        out_ref[...] = total_ref[...]

    def one_chunk(chunk, carry):
        for k in range(len(slots)):
            load(chunk, k).wait()
        rows = pl.ds(pl.multiple_of(start + chunk * SUB, SUB), SUB)
        for t in range(TILES):
            lanes = slice(t * LANES, (t + 1) * LANES)
            totals = [[None] * RHS for _ in range(SUB)]
            for k in range(len(slots)):
                for b in range(0, BASIS, 16):
                    values = [
                        [picked[k, q, b + 8 * h : b + 8 * h + 8, lanes] for h in range(2)]
                        for q in range(RHS)
                    ]
                    for a in range(SUB):
                        weight = blocks[chunk, k, a, b : b + 16, lanes].astype(jnp.float32)
                        for q in range(RHS):
                            term = weight[:8] * values[q][0] + weight[8:] * values[q][1]
                            totals[a][q] = term if totals[a][q] is None else totals[a][q] + term
            for q in range(RHS):
                value = sum_rows([totals[a][q] for a in range(SUB)])
                if has_total:
                    value = value + total_ref[q, rows, lanes]
                out_ref[q, rows, lanes] = value
        return carry

    lax.fori_loop(0, chunks, one_chunk, 0)


def near_call(values, total, near_blocks, slots, start, stop):
    elements = near_blocks.shape[3]
    chunks = (stop - start) // SUB
    return pl.pallas_call(
        functools.partial(near_kernel, total is not None, slots, start, stop),
        in_specs=[ON_CHIP] * (1 if total is None else 2) + [IN_PLACE],
        out_specs=ON_CHIP,
        out_shape=jax.ShapeDtypeStruct((RHS, BASIS, elements), jnp.float32),
        scratch_shapes=[
            pltpu.VMEM((chunks, len(slots), SUB, BASIS, elements), jnp.bfloat16),
            pltpu.VMEM((len(slots), RHS, BASIS, elements), jnp.float32),
            pltpu.SemaphoreType.DMA((chunks, len(slots))),
        ],
        compiler_params=NEAR_PARAMS,
        name="near",
    )(*([values] if total is None else [values, total]), near_blocks)


ON_CHIP = pl.BlockSpec(memory_space=pltpu.VMEM)
IN_PLACE = pl.BlockSpec(memory_space=pltpu.HBM)
PARAMS = pltpu.CompilerParams(vmem_limit_bytes=48 << 20)
CHARGE_PARAMS = pltpu.CompilerParams(vmem_limit_bytes=60 << 20)
FULL_PARAMS = pltpu.CompilerParams(vmem_limit_bytes=60 << 20)
NEAR_PARAMS = pltpu.CompilerParams(vmem_limit_bytes=48 << 20)


def whole(shape):
    return pl.BlockSpec(shape, lambda *_: (0,) * len(shape))


def shards_real(currents, projection, near_blocks, partners, shifts, green):
    row_count = lax.axis_size("row")
    col_count = lax.axis_size("col")
    elements = currents.shape[2]
    width = col_count * LANES
    length = 2 * width
    quarter = length // 4
    f32, b16 = jnp.float32, jnp.bfloat16
    struct = jax.ShapeDtypeStruct
    devices = row_count * col_count

    charges = pl.pallas_call(
        charge_kernel,
        in_specs=[IN_PLACE] * 3,
        out_specs=ON_CHIP,
        out_shape=struct((SUB, 112, LANES), b16),
        scratch_shapes=[
            pltpu.VMEM(projection.shape, b16),
            pltpu.VMEM((RHS, BASIS, elements), f32),
            pltpu.VMEM((2, elements), jnp.int32),
            pltpu.VMEM((RHS, BASIS, elements), f32),
            pltpu.VMEM((STEN, SUB, SUB, LANES), f32),
            pltpu.VMEM((STEN * STEN, SUB, LANES), f32),
            pltpu.SemaphoreType.DMA((STEN + 2,)),
        ],
        compiler_params=CHARGE_PARAMS,
        name="charges",
    )(currents, projection, shifts)
    slab = lax.all_to_all(charges, "col", 0, 0, tiled=True)

    columns, rows = even_positions(row_count, col_count)
    table = struct((quarter, quarter), b16)
    col_tables = pl.pallas_call(
        column_table_kernel,
        out_specs=[ON_CHIP] * 3,
        out_shape=[table] * 3,
        compiler_params=PARAMS,
        name="column_tables",
    )(*position_bases(columns, length))
    spread = struct((2 * quarter, LANES), f32)
    row_tables = pl.pallas_call(
        row_table_kernel,
        out_shape=[table] * 6 + [spread] * 2,
        compiler_params=FULL_PARAMS,
        name="row_tables",
    )(green, *position_bases(rows, length), *order_bases(rows, length))
    slab, *row_tables = lax.optimization_barrier((slab, *row_tables))

    spectrum = pl.pallas_call(
        functools.partial(column_kernel, col_count),
        out_shape=struct((devices, 40, LANES), b16),
        in_specs=[ON_CHIP] * 4,
        out_specs=ON_CHIP,
        compiler_params=PARAMS,
        name="columns",
    )(slab, *col_tables)
    spectrum, held = lax.optimization_barrier((spectrum, currents))
    arrived = lax.all_to_all(spectrum, ("row", "col"), 0, 0, tiled=True)
    near = near_call(held, None, near_blocks, (0,), 0, BASIS)
    arrived, near = lax.optimization_barrier((arrived, near))
    rows_back = pl.pallas_call(
        functools.partial(row_kernel, row_count, col_count),
        out_shape=struct((devices, 40, LANES), b16),
        in_specs=[ON_CHIP] + [IN_PLACE] * 8,
        out_specs=ON_CHIP,
        scratch_shapes=[pltpu.VMEM((quarter, quarter), b16)] * 6
        + [pltpu.VMEM((2 * quarter, LANES), f32)] * 2
        + [pltpu.SemaphoreType.DMA((8,))],
        compiler_params=FULL_PARAMS,
        name="rows",
    )(arrived, *row_tables)
    rows_back, ready = lax.optimization_barrier((rows_back, arrived))
    returned = lax.all_to_all(rows_back, ("row", "col"), 0, 0, tiled=True)
    picked = pl.pallas_call(
        pick_kernel,
        in_specs=[whole(currents.shape), ON_CHIP, ON_CHIP, whole(partners.shape)],
        out_specs=ON_CHIP,
        out_shape=struct((NEIGH - 1, RHS, BASIS, elements), b16),
        compiler_params=PARAMS,
        name="pick",
    )(held, slab, ready, partners)
    others = tuple(range(1, NEIGH))
    near = near_call(picked, near, near_blocks, others, 0, BASIS // 2)
    returned, near, picked = lax.optimization_barrier((returned, near, picked))
    potential = pl.pallas_call(
        functools.partial(grid_kernel, col_count),
        out_shape=struct((SUB, 80, LANES), b16),
        in_specs=[ON_CHIP] * 4,
        out_specs=ON_CHIP,
        compiler_params=PARAMS,
        name="grid",
    )(returned, *col_tables)
    potential, near, picked = lax.optimization_barrier((potential, near, picked))
    pieces = lax.all_to_all(potential, "col", 0, 0, tiled=True)
    near = near_call(picked, near, near_blocks, others, BASIS // 2, BASIS)

    return pl.pallas_call(
        far_kernel,
        in_specs=[ON_CHIP, IN_PLACE, IN_PLACE, ON_CHIP],
        out_specs=IN_PLACE,
        out_shape=struct((RHS, BASIS, elements), f32),
        scratch_shapes=[
            pltpu.VMEM(projection.shape, b16),
            pltpu.VMEM((STEN * STEN, SUB, LANES), f32),
            pltpu.VMEM((2, elements), jnp.int32),
            pltpu.VMEM((RHS, BASIS, elements), f32),
            pltpu.SemaphoreType.DMA((9,)),
        ],
        compiler_params=FULL_PARAMS,
        name="far",
    )(pieces, projection, shifts, near)


def shards(currents, projection, near_blocks, partners, shifts, green):
    row_count = lax.axis_size("row")
    col_count = lax.axis_size("col")
    fits = col_count == SUB and green.shape[0] == 64 and 2 * row_count * col_count == green.shape[0]
    if fits and currents.shape[2] == TILES * LANES and row_count * ER == col_count * EC:
        return shards_real(currents, projection, near_blocks, partners, shifts, green)
    return shards_general(currents, projection, near_blocks, partners, shifts, green)


def solution(mesh):
    in_specs = (
        P(None, None, ("row", "col")),
        P(None, None, ("row", "col")),
        P(None, None, None, ("row", "col")),
        P(None, ("row", "col")),
        P(None, ("row", "col")),
        P(("row", "col"), None),
    )
    out_specs = P(None, None, ("row", "col"))
    return jax.shard_map(shards, mesh=mesh, in_specs=in_specs, out_specs=out_specs, check_vma=False)
```

```python
import functools
import math

import jax
import jax.numpy as jnp
import numpy as np
from jax import lax
from jax.experimental import pallas as pl
from jax.experimental.pallas import tpu as pltpu
from jax.sharding import PartitionSpec as P

BASIS = 64
STEN = 8
PITCH = 8
HALO = 2
NEIGH = 4
RHS = 2
ER = 32
EC = 16


def extended_2(block, sides, width):
    for axis, dim in sides:
        count = lax.axis_size(axis)
        forward = [(i, i + 1) for i in range(count - 1)]
        backward = [(target, source) for source, target in forward]
        low = lax.ppermute(
            lax.slice_in_dim(block, block.shape[dim] - width, None, axis=dim), axis, forward
        )
        high = lax.ppermute(lax.slice_in_dim(block, 0, width, axis=dim), axis, backward)
        block = jnp.concatenate([low, block, high], axis=dim)
    return block


def angle_table(first_size, second_size, modulus, direction):
    left_index = jnp.arange(first_size, dtype=jnp.int32)
    right_index = jnp.arange(second_size, dtype=jnp.int32)
    turn_count = left_index[:, None] * right_index[None, :] % modulus
    angles = turn_count.astype(jnp.float32) * (2.0 * math.pi / modulus)
    return (jnp.cos(angles), direction * jnp.sin(angles))


def complex_apply(real_part, imag_part, cosine, sine_table, pattern):
    highest = lax.Precision.HIGHEST
    out_real = jnp.einsum(pattern, real_part, cosine, precision=highest)
    out_imag = jnp.einsum(pattern, real_part, sine_table, precision=highest)
    if imag_part is not None:
        out_real = out_real - jnp.einsum(pattern, imag_part, sine_table, precision=highest)
        out_imag = out_imag + jnp.einsum(pattern, imag_part, cosine, precision=highest)
    return (out_real, out_imag)


def transform_last(real_part, imag_part, length, count_in, count_out, direction):
    leading = real_part.shape[:-1]
    inner_size = 128
    outer_size = length // inner_size
    rows_in = count_in // inner_size
    kept_count = count_out // outer_size
    shaped_real = real_part.reshape(leading + (rows_in, inner_size))
    shaped_imag = None
    if imag_part is not None:
        shaped_imag = imag_part.reshape(leading + (rows_in, inner_size))
    cosine, sine_table = angle_table(rows_in, outer_size, outer_size, direction)
    first_real, first_imag = complex_apply(
        shaped_real, shaped_imag, cosine, sine_table, "...ab,ak->...kb"
    )
    twist_cos, twist_sin = angle_table(outer_size, inner_size, length, direction)
    turned_real = first_real * twist_cos - first_imag * twist_sin
    turned_imag = first_real * twist_sin + first_imag * twist_cos
    cosine, sine_table = angle_table(inner_size, kept_count, inner_size, direction)
    last_real, last_imag = complex_apply(
        turned_real, turned_imag, cosine, sine_table, "...kb,bj->...jk"
    )
    out_shape = leading + (kept_count * outer_size,)
    return (last_real.reshape(out_shape), last_imag.reshape(out_shape))


def place_shifted(blocks, amount, dim_index):
    new_shape = list(blocks.shape)
    new_shape[dim_index] = new_shape[dim_index] + 2 * HALO
    result = jnp.zeros(tuple(new_shape), blocks.dtype)
    for offset in range(-HALO, HALO + 1):
        widths = [(0, 0)] * blocks.ndim
        widths[dim_index] = (HALO + offset, HALO - offset)
        result = jnp.where(amount == offset, jnp.pad(blocks, widths), result)
    return result


def pick_shifted(windows, amount, dim_index):
    new_shape = list(windows.shape)
    new_shape[dim_index] = STEN
    result = jnp.zeros(tuple(new_shape), windows.dtype)
    for offset in range(-HALO, HALO + 1):
        piece = lax.slice_in_dim(windows, HALO + offset, HALO + offset + STEN, axis=dim_index)
        result = jnp.where(amount == offset, piece, result)
    return result


def intersection_add(framed, dim_index):
    element_count = framed.shape[dim_index]
    window_size = framed.shape[dim_index + 1]
    head_part = lax.slice_in_dim(framed, 0, PITCH, axis=dim_index + 1)
    tail_part = lax.slice_in_dim(framed, PITCH, window_size, axis=dim_index + 1)
    widths = [(0, 0)] * framed.ndim
    widths[dim_index + 1] = (0, 2 * PITCH - window_size)
    tail_part = jnp.pad(tail_part, widths)
    merged = framed.shape[:dim_index] + (element_count * PITCH,) + framed.shape[dim_index + 2 :]
    head_part = head_part.reshape(merged)
    tail_part = tail_part.reshape(merged)
    front_pad = [(0, 0)] * len(merged)
    front_pad[dim_index] = (0, PITCH)
    back_pad = [(0, 0)] * len(merged)
    back_pad[dim_index] = (PITCH, 0)
    summed = jnp.pad(head_part, front_pad) + jnp.pad(tail_part, back_pad)
    return lax.slice_in_dim(summed, 0, element_count * PITCH + 2 * HALO, axis=dim_index)


def cut_windows(field, dim_index):
    element_count = (field.shape[dim_index] - 2 * HALO) // PITCH
    widths = [(0, 0)] * field.ndim
    widths[dim_index] = (0, PITCH - 2 * HALO)
    extended = jnp.pad(field, widths)
    split_shape = field.shape[:dim_index] + (element_count, PITCH) + field.shape[dim_index + 1 :]
    head_part = lax.slice_in_dim(extended, 0, element_count * PITCH, axis=dim_index).reshape(
        split_shape
    )
    tail_part = lax.slice_in_dim(
        extended, PITCH, PITCH + element_count * PITCH, axis=dim_index
    ).reshape(split_shape)
    tail_part = lax.slice_in_dim(tail_part, 0, 2 * HALO, axis=dim_index + 1)
    return jnp.concatenate([head_part, tail_part], axis=dim_index + 1)


def fold_margin(padded, dim_index):
    full_size = padded.shape[dim_index]
    inner_size = full_size - 4 * HALO
    core_part = lax.slice_in_dim(padded, 2 * HALO, 2 * HALO + inner_size, axis=dim_index)
    upper_part = lax.slice_in_dim(padded, 0, HALO, axis=dim_index)
    lower_part = lax.slice_in_dim(padded, full_size - HALO, full_size, axis=dim_index)
    upper_pad = [(0, 0)] * padded.ndim
    upper_pad[dim_index] = (0, inner_size - HALO)
    lower_pad = [(0, 0)] * padded.ndim
    lower_pad[dim_index] = (inner_size - HALO, 0)
    return core_part + jnp.pad(upper_part, upper_pad) + jnp.pad(lower_part, lower_pad)


def shards_general(currents, projection, near_blocks, partners, shifts, green):
    row_count = lax.axis_size("row")
    col_count = lax.axis_size("col")
    device_count = row_count * col_count
    elements = ER * EC
    cur_half = currents.astype(jnp.bfloat16)
    spread = extended_2(cur_half.reshape(RHS, BASIS, ER, EC), (("row", 2), ("col", 3)), 1)
    views = []
    for symbol in range(9):
        row_start = symbol // 3
        col_start = symbol % 3
        views.append(
            spread[:, :, row_start : row_start + ER, col_start : col_start + EC].reshape(
                RHS, BASIS, elements
            )
        )
    picked = []
    for neighbour_slot in range(NEIGH):
        chosen = jnp.zeros((RHS, BASIS, elements), jnp.bfloat16)
        for symbol in range(9):
            chosen = jnp.where(partners[neighbour_slot] == symbol, views[symbol], chosen)
        picked.append(chosen)
    near_term = jnp.einsum(
        "kabn,kqbn->qan", near_blocks, jnp.stack(picked), preferred_element_type=jnp.float32
    )
    stencil = jnp.einsum("sbn,qbn->qsn", projection, cur_half, preferred_element_type=jnp.float32)
    blocks = stencil.reshape(RHS, STEN, STEN, elements)
    framed = place_shifted(place_shifted(blocks, shifts[0], 1), shifts[1], 2)
    window_size = STEN + 2 * HALO
    framed = framed.reshape(RHS, window_size, window_size, ER, EC).transpose(0, 3, 1, 4, 2)
    extended = intersection_add(intersection_add(framed, 1), 2)
    padded = extended_2(extended, (("row", 1), ("col", 2)), HALO)
    charges = fold_margin(fold_margin(padded, 1), 2)
    slab = lax.all_to_all(charges, "col", split_axis=1, concat_axis=2, tiled=True)
    slab_rows = slab.shape[1]
    width_cols = slab.shape[2]
    length_cols = 2 * width_cols
    block_cols = length_cols // device_count
    grid_rows = slab_rows * device_count
    length_rows = 2 * grid_rows
    fwd_real, fwd_imag = transform_last(slab, None, length_cols, width_cols, length_cols, -1.0)
    out_real = fwd_real.reshape(RHS, slab_rows, device_count, block_cols)
    out_imag = fwd_imag.reshape(RHS, slab_rows, device_count, block_cols)
    arrived = (
        lax.all_to_all(out_real, ("row", "col"), split_axis=2, concat_axis=2, tiled=True),
        lax.all_to_all(out_imag, ("row", "col"), split_axis=2, concat_axis=2, tiled=True),
    )
    col_real = arrived[0].transpose(0, 3, 2, 1).reshape(RHS, block_cols, grid_rows)
    col_imag = arrived[1].transpose(0, 3, 2, 1).reshape(RHS, block_cols, grid_rows)
    spec_real, spec_imag = transform_last(
        col_real, col_imag, length_rows, grid_rows, length_rows, -1.0
    )
    spec_real = spec_real * green
    spec_imag = spec_imag * green
    back_real, back_imag = transform_last(
        spec_real, spec_imag, length_rows, length_rows, grid_rows, 1.0
    )
    send_real = back_real.reshape(RHS, block_cols, device_count, slab_rows)
    send_imag = back_imag.reshape(RHS, block_cols, device_count, slab_rows)
    returned = (
        lax.all_to_all(send_real, ("row", "col"), split_axis=2, concat_axis=2, tiled=True),
        lax.all_to_all(send_imag, ("row", "col"), split_axis=2, concat_axis=2, tiled=True),
    )
    rows_real = returned[0].transpose(0, 3, 2, 1).reshape(RHS, slab_rows, length_cols)
    rows_imag = returned[1].transpose(0, 3, 2, 1).reshape(RHS, slab_rows, length_cols)
    final_real, final_imag = transform_last(
        rows_real, rows_imag, length_cols, length_cols, width_cols, 1.0
    )
    potential_slab = final_real * (1.0 / (length_rows * length_cols))
    potential = lax.all_to_all(potential_slab, "col", split_axis=2, concat_axis=1, tiled=True)
    rimmed = extended_2(potential, (("row", 1), ("col", 2)), HALO)
    windows = cut_windows(cut_windows(rimmed, 1), 3)
    windows = windows.transpose(0, 2, 4, 1, 3).reshape(RHS, window_size, window_size, elements)
    samples = pick_shifted(pick_shifted(windows, shifts[0], 1), shifts[1], 2).reshape(
        RHS, STEN * STEN, elements
    )
    sample_high = samples.astype(jnp.bfloat16)
    sample_low = (samples - sample_high.astype(jnp.float32)).astype(jnp.bfloat16)
    far_term = jnp.einsum(
        "sbn,qsn->qbn", projection, sample_high, preferred_element_type=jnp.float32
    )
    far_term = far_term + jnp.einsum(
        "sbn,qsn->qbn", projection, sample_low, preferred_element_type=jnp.float32
    )
    return far_term + near_term


LANES = 128
SUB = 8
TILES = 4
GROUPS = 9
PARITY_ORDER = (0, 2, 4, 6, 1, 3, 5, 7)


def roll(value, amount, dim):
    return pltpu.roll(value, amount % value.shape[dim], dim)


def lane_index(shape):
    return lax.broadcasted_iota(jnp.int32, shape, len(shape) - 1)


def sub_index(shape):
    return lax.broadcasted_iota(jnp.int32, shape, len(shape) - 2)


def sum_rows(parts):
    sub = sub_index(parts[0].shape)
    top = sub < 4
    level = []
    for i in range(4):
        a, b = parts[i], parts[i + 4]
        level.append(jnp.where(top, a, b) + roll(jnp.where(top, b, a), 4, 0))
    mask = (sub & 2) == 0
    level = [
        jnp.where(mask, level[i], level[i + 2])
        + jnp.where(mask, roll(level[i], -2, 0), roll(level[i + 2], 2, 0))
        for i in range(2)
    ]
    mask = (sub & 1) == 0
    a, b = level
    return jnp.where(mask, a, b) + jnp.where(mask, roll(a, -1, 0), roll(b, 1, 0))


def next_row(value):
    lane = lane_index(value.shape)
    sub = sub_index(value.shape)
    turned = roll(value, EC, 1)
    carried = jnp.where((sub & 3) == 0, 0.0, roll(turned, 1, 0))
    return jnp.where(lane < EC, carried, turned)


def previous_row(value):
    lane = lane_index(value.shape)
    sub = sub_index(value.shape)
    turned = roll(value, -EC, 1)
    carried = jnp.where((sub & 3) == 3, 0.0, roll(turned, -1, 0))
    return jnp.where(lane >= LANES - EC, carried, turned)


def place_charges(stencil, row_shift, col_shift):
    shape = row_shift.shape
    lane = lane_index(shape)
    sub = sub_index(shape)
    window = STEN + 2 * HALO
    row_mask = {o: row_shift == o for o in range(-HALO, HALO + 1)}
    col_mask = {o: col_shift == o for o in range(-HALO, HALO + 1)}
    first = []
    for rr in range(window):
        line = []
        for c in range(STEN):
            value = jnp.zeros(shape, jnp.float32)
            for o in range(-HALO, HALO + 1):
                source = rr - HALO - o
                if 0 <= source < STEN:
                    value = jnp.where(row_mask[o], stencil(source * STEN + c), value)
            line.append(value)
        first.append(line)
    framed = []
    for rr in range(window):
        line = []
        for cc in range(window):
            value = jnp.zeros(shape, jnp.float32)
            for o in range(-HALO, HALO + 1):
                source = cc - HALO - o
                if 0 <= source < STEN:
                    value = jnp.where(col_mask[o], first[rr][source], value)
            line.append(value)
        framed.append(line)
    grid = []
    for r in range(PITCH):
        line = []
        for cc in range(window):
            value = framed[r + HALO][cc]
            if r < HALO:
                value = value + next_row(framed[r + HALO + PITCH][cc])
            if r >= PITCH - HALO:
                value = value + previous_row(framed[r + HALO - PITCH][cc])
            line.append(value)
        grid.append(line)
    slot = sub & 3
    low_lanes = lane < EC
    high_lanes = lane >= LANES - EC
    line = []
    for cc in range(window):
        value = jnp.where(low_lanes & (slot == 0), roll(roll(framed[10][cc], EC, 1), -3, 0), 0.0)
        value = jnp.where(low_lanes & (slot == 1), roll(roll(framed[11][cc], EC, 1), -2, 0), value)
        value = jnp.where(high_lanes & (slot == 3), roll(roll(framed[0][cc], -EC, 1), 3, 0), value)
        value = jnp.where(high_lanes & (slot == 2), roll(roll(framed[1][cc], -EC, 1), 2, 0), value)
        line.append(value)
    grid.append(line)
    elem_col = lane & (EC - 1)
    parts = [[] for _ in range(SUB)]
    edges = [jnp.zeros(shape, jnp.float32) for _ in range(SUB)]
    for r in range(GROUPS):
        cells = []
        for c in range(PITCH):
            value = grid[r][c + HALO]
            if c < HALO:
                value = value + jnp.where(elem_col == 0, 0.0, roll(grid[r][c + HALO + PITCH], 1, 1))
            if c >= PITCH - HALO:
                value = value + jnp.where(
                    elem_col == EC - 1, 0.0, roll(grid[r][c + HALO - PITCH], -1, 1)
                )
            cells.append(value)
        turned = transpose_blocks([cells[c] for c in PARITY_ORDER], lane)
        for e in range(SUB):
            parts[e].append(turned[e])
            start = EC * e
            edge = edges[e]
            edge = jnp.where(lane == r, roll(grid[r][10], r - start - (EC - 1), 1), edge)
            edge = jnp.where(lane == 64 + r, roll(grid[r][11], 64 + r - start - (EC - 1), 1), edge)
            edge = jnp.where(lane == 63 - r, roll(grid[r][0], 63 - r - start, 1), edge)
            edge = jnp.where(lane == 127 - r, roll(grid[r][1], 127 - r - start, 1), edge)
            edges[e] = edge
    return [parts[e] + [edges[e]] for e in range(SUB)]


def transpose_blocks(values, lane):
    block = lane // EC
    for step in (4, 2, 1):
        mask = (block & step) == 0
        result = list(values)
        for i in range(SUB):
            if i & step:
                continue
            a, b = values[i], values[i + step]
            result[i] = jnp.where(mask, a, roll(b, EC * step, 1))
            result[i + step] = jnp.where(mask, roll(a, -EC * step, 1), b)
        values = result
    return values


def halves(a, b):
    low = lane_index(a.shape) < 64
    return jnp.where(low, a, roll(b, 64, 1)), jnp.where(low, roll(a, 64, 1), b)


def half_rows(a, b):
    top = sub_index(a.shape) < 4
    return jnp.where(top, a, roll(b, 4, 0)), jnp.where(top, roll(a, 4, 0), b)


def gather_rows(part, edge, count):
    sample = edge(0)
    lane = lane_index(sample.shape)
    from_low = (lane == 0) | (lane == 64)
    from_high = (lane == 63) | (lane == 127)
    rows = []
    for j in range(count):
        groups = []
        for r in range(GROUPS):
            value = part(j, r)
            if j > 0:
                value = value + jnp.where(from_low, roll(edge(j - 1), -r, 1), 0.0)
            if j < count - 1:
                value = value + jnp.where(from_high, roll(edge(j + 1), r, 1), 0.0)
            groups.append(value)
        first, second = [], []
        for parity in range(2):
            for b in range(2):
                low, high = half_rows(groups[parity + 4 * b], groups[parity + 4 * b + 2])
                first.append(low)
                second.append(high)
        low, high = half_rows(groups[8], groups[8])
        first.append(low)
        second.append(high)
        rows.append(jnp.concatenate(first + second, axis=0))
    even, odd = [], []
    for j in range(0, count, 2):
        low, high = halves(rows[j], rows[j + 1])
        even.append(low)
        odd.append(high)
    return jnp.concatenate(even, axis=1), jnp.concatenate(odd, axis=1)


def scatter_rows(even, odd, count, put):
    rows = []
    for j in range(0, count, 2):
        tile = slice(64 * j, 64 * j + LANES)
        rows.extend(halves(even[:, tile], odd[:, tile]))
    blocks = []
    for j in range(count):
        first = [rows[j][8 * i : 8 * i + 8] for i in range(5)]
        second = [rows[j][40 + 8 * i : 48 + 8 * i] for i in range(5)]
        groups = [None] * GROUPS
        for parity in range(2):
            for b in range(2):
                low, high = half_rows(first[2 * parity + b], second[2 * parity + b])
                groups[parity + 4 * b] = low
                groups[parity + 4 * b + 2] = high
        sub = sub_index(first[4].shape)
        tail = jnp.where(sub < 4, roll(first[4], 4, 0), second[4])
        head = jnp.where(sub < 4, first[4], roll(second[4], 4, 0))
        groups[8] = jnp.where((sub & 2) == 0, head, tail)
        blocks.append(groups)
    lane = lane_index(blocks[0][0].shape)
    for j in range(count):
        edge = jnp.zeros(blocks[0][0].shape, jnp.float32)
        for r in range(GROUPS):
            if j < count - 1:
                edge = jnp.where(
                    (lane == r) | (lane == 64 + r), roll(blocks[j + 1][r], r, 1), edge
                )
            if j > 0:
                edge = jnp.where(
                    (lane == 63 - r) | (lane == 127 - r), roll(blocks[j - 1][r], -r, 1), edge
                )
        put(j, blocks[j] + [edge])


def read_samples(part, edge, row_shift, col_shift, put):
    shape = row_shift.shape
    lane = lane_index(shape)
    sub = sub_index(shape)
    elem_col = lane & (EC - 1)
    window = STEN + 2 * HALO
    grid = []
    for r in range(GROUPS):
        turned = transpose_blocks([part(e, r) for e in range(SUB)], lane)
        cells = [None] * PITCH
        for place, c in enumerate(PARITY_ORDER):
            cells[c] = turned[place]
        line = [None] * window
        for c in range(PITCH):
            line[c + HALO] = cells[c]
        after = [roll(cells[c], -1, 1) for c in range(HALO)]
        before = [roll(cells[PITCH - HALO + c], 1, 1) for c in range(HALO)]
        for e in range(SUB):
            start = EC * e
            last = lane == start + EC - 1
            zero = lane == start
            after[0] = jnp.where(last, roll(edge(e), start + EC - 1 - r, 1), after[0])
            after[1] = jnp.where(last, roll(edge(e), start + EC - 1 - 64 - r, 1), after[1])
            before[0] = jnp.where(zero, roll(edge(e), start - 63 + r, 1), before[0])
            before[1] = jnp.where(zero, roll(edge(e), start - 127 + r, 1), before[1])
        line[0], line[1] = before
        line[10], line[11] = after
        grid.append(line)
    slot = sub & 3
    first_row = (slot == 0) & (lane < EC)
    last_row = (slot == 3) & (lane >= LANES - EC)
    framed = [[None] * window for _ in range(window)]
    for cc in range(window):
        for r in range(PITCH):
            framed[r + HALO][cc] = grid[r][cc]
        outer = grid[8][cc]
        below = roll(outer, -EC, 1)
        above = roll(outer, EC, 1)
        framed[10][cc] = jnp.where(last_row, roll(below, 3, 0), previous_row(grid[0][cc]))
        framed[11][cc] = jnp.where(last_row, roll(below, 2, 0), previous_row(grid[1][cc]))
        framed[0][cc] = jnp.where(first_row, roll(above, -3, 0), next_row(grid[6][cc]))
        framed[1][cc] = jnp.where(first_row, roll(above, -2, 0), next_row(grid[7][cc]))
    for a in range(STEN):
        line = []
        for cc in range(window):
            value = framed[a + HALO][cc]
            for o in range(-HALO, HALO + 1):
                if o:
                    value = jnp.where(row_shift == o, framed[a + HALO + o][cc], value)
            line.append(value)
        for b in range(STEN):
            value = line[b + HALO]
            for o in range(-HALO, HALO + 1):
                if o:
                    value = jnp.where(col_shift == o, line[b + HALO + o], value)
            put(a * STEN + b, value)


def add_outer_rows(chunk, row_count, col_count):
    sub = sub_index((SUB, LANES))
    even, odd = [], []
    for i in range(row_count):
        for j in range(col_count):
            rows = [chunk(i, j)[8 * k : 8 * k + 8] for k in range(4)]
            if j == 0 and i > 0:
                outer = chunk(i - 1, 0)[32:40]
                rows[0] = rows[0] + jnp.where(sub == 0, outer, 0.0)
                rows[2] = rows[2] + jnp.where(sub == 0, roll(outer, -1, 0), 0.0)
            if j == col_count - 1 and i < row_count - 1:
                outer = chunk(i + 1, j)[32:40]
                rows[1] = rows[1] + jnp.where(sub == 7, outer, 0.0)
                rows[3] = rows[3] + jnp.where(sub == 7, roll(outer, 1, 0), 0.0)
            even.extend(rows[:2])
            odd.extend(rows[2:])
    return jnp.concatenate(even, axis=0), jnp.concatenate(odd, axis=0)


def spread_outer_rows(even, odd, row_count, col_count, put):
    sub = sub_index((SUB, LANES))

    def block(i, j):
        start = 16 * (i * col_count + j)
        return [even[start : start + 8], even[start + 8 : start + 16],
                odd[start : start + 8], odd[start + 8 : start + 16]]

    for i in range(row_count):
        for j in range(col_count):
            outer = jnp.zeros((SUB, LANES), jnp.float32)
            if j == 0 and i < row_count - 1:
                rows = block(i + 1, 0)
                outer = jnp.where(sub == 0, rows[0], jnp.where(sub == 1, roll(rows[2], 1, 0), outer))
            if j == col_count - 1 and i > 0:
                rows = block(i - 1, j)
                outer = jnp.where(sub == 7, rows[1], jnp.where(sub == 6, roll(rows[3], -1, 0), outer))
            put(i, j, block(i, j) + [outer])


def two_terms(value):
    high = value.astype(jnp.bfloat16)
    return high, (value - high.astype(jnp.float32)).astype(jnp.bfloat16)


def dot(left, right, dims=((1,), (0,))):
    return lax.dot_general(left, right, (dims, ((), ())), preferred_element_type=jnp.float32)


def even_positions(row_count, col_count):
    j, c, e = np.meshgrid(np.arange(col_count), np.arange(4), np.arange(EC), indexing="ij")
    columns = (LANES * j + PITCH * e + 2 * c).reshape(-1)
    i, j, b, h, t = np.meshgrid(
        np.arange(row_count), np.arange(col_count), np.arange(2), np.arange(2), np.arange(TILES),
        indexing="ij",
    )
    rows = (ER * PITCH * i + SUB * PITCH * t + PITCH * j + 2 * h + 4 * b).reshape(-1)
    return columns, rows


def angle_pair(left, right, length):
    angles = 2.0 * np.pi * (np.asarray(left)[:, None] * np.asarray(right)[None, :] % length) / length
    return np.asarray(np.cos(angles), np.float32), np.asarray(np.sin(angles), np.float32)


def position_bases(positions, length):
    orders = np.arange(length // 4)
    grouped = positions.reshape(-1, SUB)
    offsets = grouped[0] - grouped[0, 0]
    assert (grouped == grouped[:, :1] + offsets[None, :]).all()
    return np.concatenate(
        [
            *angle_pair(grouped[:, 0], orders, length),
            *angle_pair(offsets, orders, length),
            *angle_pair(offsets + 1, orders, length),
        ]
    )


def split_rows(ref, *counts):
    start, parts = 0, []
    for count in counts:
        parts.append(ref.at[start : start + count])
        start += count
    return parts


def order_bases(positions, length):
    bases = np.arange(0, length // 4, SUB)
    result = []
    for parity in range(2):
        result.extend(angle_pair(bases, positions + parity, length))
        result.extend(angle_pair(np.arange(SUB), positions + parity, length))
    return np.concatenate(result)


def fill_by_position(sign_of, bases, out_refs):
    base_cos, base_sin, even_cos, even_sin, odd_cos, odd_sin = bases
    ec, es, oc, os = (ref[...] for ref in (even_cos, even_sin, odd_cos, odd_sin))
    start = lane_index(ec.shape) == 0

    def pair(i, carry):
        parts = [[], [], []]
        for h in range(2):
            row = 2 * i + h
            bc, bs = base_cos[pl.ds(row, 1), :], base_sin[pl.ds(row, 1), :]
            parts[0].append(bc * ec - bs * es)
            parts[1].append(jnp.where(start, 1.0, -(bs * ec + bc * es)) * sign_of(row))
            parts[2].append(bc * oc - bs * os)
        rows = pl.ds(pl.multiple_of(16 * i, 16), 16)
        for ref, part in zip(out_refs, parts):
            ref[rows, :] = jnp.concatenate(part, axis=0).astype(ref.dtype)
        return carry

    lax.fori_loop(0, base_cos.shape[0] // 2, pair, 0)


def column_table_kernel(bases_ref, *outs):
    count = (bases_ref.shape[0] - 4 * SUB) // 2
    bases = split_rows(bases_ref, count, count, SUB, SUB, SUB, SUB)
    fill_by_position(lambda row: (1 - 2 * ((row // 2) & 1)).astype(jnp.float32), bases, outs)


def row_table_kernel(green_ref, position_ref, order_ref, *outs):
    count = (position_ref.shape[0] - 4 * SUB) // 2
    position = split_rows(position_ref, count, count, SUB, SUB, SUB, SUB)
    order = split_rows(order_ref, count, count, SUB, SUB, count, count, SUB, SUB)
    quarter = position[0].shape[1]
    tiles = quarter // LANES
    sub = sub_index((SUB, quarter))
    flip = jnp.where(sub < 4, 1.0, -1.0)
    fill_by_position(lambda row: flip, position, outs[3:6])
    ebc, ebs, ec, es, obc, obs, oc, os = order
    ec, es, oc, os = (ref[...] for ref in (ec, es, oc, os))
    lanes = jnp.where((lane_index((SUB, quarter)) & 4) == 0, 1.0, -1.0)

    def pair(i, carry):
        parts = [[], [], []]
        for h in range(2):
            row = 2 * i + h
            one = (pl.ds(row, 1), slice(None))
            bc, bs = ebc[one], ebs[one]
            parts[0].append(bc * ec - bs * es)
            first = (sub + row) == 0
            parts[1].append(jnp.where(first, 1.0, -(bs * ec + bc * es)) * lanes)
            parts[2].append(obc[one] * oc - obs[one] * os)
        rows = pl.ds(pl.multiple_of(16 * i, 16), 16)
        for ref, part in zip(outs[:3], parts):
            ref[rows, :] = jnp.concatenate(part, axis=0).astype(ref.dtype)
        return carry

    lax.fori_loop(0, ebc.shape[0] // 2, pair, 0)

    depth = green_ref.shape[0]
    device = lax.axis_index("row") * lax.axis_size("col") + lax.axis_index("col")
    number = sub_index((depth, LANES)) + device * depth
    length = 4 * quarter
    weight = jnp.where(number % quarter == 0, 1.0, 2.0) * (1.0 / (length * length))
    lane = lane_index((depth, LANES))

    def scaled(tile):
        value = green_ref[:, LANES * tile : LANES * (tile + 1)] * weight
        if tile % tiles == 0:
            value = value * jnp.where(lane == 0, 1.0, 2.0)
        else:
            value = value * 2.0
        return jnp.concatenate([value, value], axis=0)

    for t in range(tiles):
        cos_plus, cos_minus = scaled(t), scaled(2 * tiles + t)
        sin_minus, sin_plus = scaled(tiles + t), scaled(3 * tiles + t)
        first = slice(LANES * t, LANES * (t + 1))
        second = slice(quarter + LANES * t, quarter + LANES * (t + 1))
        outs[6][first, :] = (cos_plus + cos_minus).T
        outs[7][first, :] = (cos_plus - cos_minus).T
        outs[6][second, :] = (sin_plus + sin_minus).T
        outs[7][second, :] = (sin_plus - sin_minus).T


def tiled_shifts(shifts_ref, which):
    rows = [shifts_ref[which : which + 1, LANES * t : LANES * (t + 1)] for t in range(TILES)]
    return jnp.concatenate(rows * RHS, axis=0)


def charge_kernel(
    currents_ref, projection_ref, shifts_ref, out_ref, weights, raw, shifts, current, partial, stencil, sems
):
    copies = [
        pltpu.make_async_copy(currents_ref, raw, sems.at[STEN]),
        pltpu.make_async_copy(shifts_ref, shifts, sems.at[STEN + 1]),
    ]

    def weight_copy(step):
        rows = pl.ds(step * STEN, STEN)
        return pltpu.make_async_copy(projection_ref.at[rows], weights.at[rows], sems.at[step])

    copies[0].start()
    for step in range(STEN):
        weight_copy(step).start()
    copies[1].start()
    copies[0].wait()
    current[...] = raw[...].astype(jnp.bfloat16).astype(jnp.float32)

    def one_row(step, carry):
        weight_copy(step).wait()
        for t in range(TILES):
            lanes = slice(LANES * t, LANES * (t + 1))
            totals = [[None] * RHS for _ in range(STEN)]
            for b in range(0, BASIS, 16):
                values = [
                    [current[q, b + 8 * h : b + 8 * h + 8, lanes] for h in range(2)]
                    for q in range(RHS)
                ]
                for s in range(STEN):
                    weight = weights[step * STEN + s, b : b + 16, lanes].astype(jnp.float32)
                    for q in range(RHS):
                        term = weight[:8] * values[q][0] + weight[8:] * values[q][1]
                        totals[s][q] = term if totals[s][q] is None else totals[s][q] + term
            for s in range(STEN):
                for q in range(RHS):
                    partial[s, q * TILES + t] = totals[s][q]
        for s in range(STEN):
            stencil[step * STEN + s] = sum_rows([partial[s, i] for i in range(SUB)])
        return carry

    lax.fori_loop(0, STEN, one_row, 0)
    copies[1].wait()
    chunks = place_charges(
        lambda s: stencil[s], tiled_shifts(shifts, 0), tiled_shifts(shifts, 1)
    )
    to_next, to_previous, to_rows = pack_currents(
        lambda q, t: current[q, :, LANES * t : LANES * (t + 1)]
    )
    mine = lax.axis_index("col")
    block = lane_index((SUB, LANES)) // EC
    middle = ((block & 3) == 1) | ((block & 3) == 2)
    for e in range(SUB):
        after = (mine == e - 1).astype(jnp.float32)
        before = (mine == e + 1).astype(jnp.float32)
        edge = jnp.where(middle, to_rows[e], chunks[e][GROUPS])
        rows = chunks[e][:GROUPS] + [edge, to_next * after + to_previous * before]
        out_ref[e] = jnp.concatenate(rows, axis=0).astype(out_ref.dtype)


def pack_currents(tile):
    half = BASIS // 2
    lane = lane_index((half, LANES))
    elem_col = lane & (EC - 1)
    to_next = jnp.zeros((half, LANES), jnp.float32)
    to_previous = jnp.zeros((half, LANES), jnp.float32)
    for q in range(RHS):
        for t in range(TILES):
            value = tile(q, t)
            for h in range(2):
                place = q * TILES + t + SUB * h
                part = value[half * h : half * (h + 1)]
                here = elem_col == place
                to_next = jnp.where(here, roll(part, place - (EC - 1), 1), to_next)
                to_previous = jnp.where(here, roll(part, place, 1), to_previous)
    lane = lane_index((SUB, LANES))
    to_rows = []
    for e in range(SUB):
        rows = jnp.zeros((SUB, LANES), jnp.float32)
        for q in range(RHS):
            span = slice(SUB * e, SUB * (e + 1))
            last = roll(tile(q, TILES - 1)[span], EC + EC * q - (LANES - EC), 1)
            first = roll(tile(q, 0)[span], 64 + EC + EC * q, 1)
            rows = jnp.where(lane // EC == 1 + q, last, jnp.where(lane // EC == 5 + q, first, rows))
        to_rows.append(rows)
    return to_next, to_previous, to_rows


def forward_rows(edge_row, j, count, which):
    lane = lane_index((SUB, LANES))
    start = EC + 64 * which
    value = roll(edge_row(j), -start, 1)
    for q in range(RHS):
        place = 2 * EC + 2 * q
        if j > 0:
            corner = roll(edge_row(j - 1), place - start - EC * q - (EC - 1), 1)
            value = jnp.where(lane == place, corner, value)
        if j < count - 1:
            corner = roll(edge_row(j + 1), place + 1 - start - EC * q, 1)
            value = jnp.where(lane == place + 1, corner, value)
    return jnp.where(lane < 64, roll(value, 2, 0), roll(roll(value, 64, 1), -2, 0))


def column_sign(shape):
    return jnp.where((lane_index(shape) & EC) == 0, 1.0, -1.0)


def column_kernel(count, rows_ref, even_cos, even_sin, odd_cos, out_ref):
    def part(j, r):
        return rows_ref[j, 8 * r : 8 * r + 8, :].astype(jnp.float32)

    even, odd = gather_rows(part, lambda j: part(j, GROUPS), count)
    both = jnp.concatenate([odd, odd * column_sign(odd.shape)], axis=0).astype(jnp.bfloat16)
    even = even.astype(jnp.bfloat16)
    ec, es = dot(even, even_cos[...]), dot(even, even_sin[...])
    both = dot(both, odd_cos[...])
    oc, os = both[: odd.shape[0]], both[odd.shape[0] :]
    half = out_ref.shape[1]
    mine = lax.axis_index("row")
    ends = [
        [forward_rows(lambda k: part(k, GROUPS), j, count, which) for which in range(2)]
        for j in range(count)
    ]
    sub = sub_index((SUB, LANES))
    middle = (sub >= 2) & (sub < 6)
    device = 0
    for block in (ec + oc, es - os, ec - oc, es + os):
        for t in range(0, block.shape[1], LANES):
            for chunk in halves(block[:half, t : t + LANES], block[half:, t : t + LANES]):
                i, j = device // count, device % count
                below = (mine == i - 1).astype(jnp.float32)
                above = (mine == i + 1).astype(jnp.float32)
                tail = jnp.where(
                    middle, ends[j][0] * below + ends[j][1] * above, chunk[half - SUB :]
                )
                chunk = jnp.concatenate([chunk[: half - SUB], tail], axis=0)
                out_ref[device] = chunk.astype(out_ref.dtype)
                device += 1


def row_kernel(row_count, col_count, *refs):
    sources, out_ref, held, sems = refs[:9], refs[9], refs[10:19], refs[19]
    loads = [
        pltpu.make_async_copy(source, target, sems.at[n])
        for n, (source, target) in enumerate(zip(sources, held))
    ]
    for load in loads:
        load.start()
    in_ref, even_cos, even_sin, odd_cos, back_cos, back_sin, back_odd, sum_ref, diff_ref = held
    loads[0].wait()
    even, odd = add_outer_rows(
        lambda i, j: in_ref[i * col_count + j].astype(jnp.float32), row_count, col_count
    )
    flip = jnp.where((sub_index(odd.shape) & 4) == 0, 1.0, -1.0)
    both = jnp.concatenate([odd, odd * flip], axis=1).astype(jnp.bfloat16)
    even = even.astype(jnp.bfloat16)
    for n in range(1, 4):
        loads[n].wait()
    a = [dot(even_cos[...], even), dot(even_sin[...], even)]
    both = dot(odd_cos[...], both)
    b = [both[:, :LANES], both[:, LANES:]]
    quarter = odd.shape[0]
    for n in range(4, 9):
        loads[n].wait()

    def pieces(left, right):
        for k in range(2):
            span = slice(quarter * k, quarter * (k + 1))
            yield two_terms(left[k] * sum_ref[span, :] + right[k] * diff_ref[span, :])

    def fold(value):
        return value[:, :LANES] + value[:, LANES:]

    (ch, cl), (sh, sl) = pieces(a, b)
    even = fold(
        dot(back_cos[...], jnp.concatenate([ch, cl], axis=1))
        + dot(back_sin[...], jnp.concatenate([sh, sl], axis=1))
    )
    (ch, cl), (sh, sl) = pieces(b, a)
    both = dot(back_odd[...], jnp.concatenate([ch, cl, sh, sl], axis=1))
    odd = fold(both[:, : 2 * LANES]) + fold(both[:, 2 * LANES :]) * flip

    def put(i, j, parts):
        out_ref[i * col_count + j] = jnp.concatenate(parts, axis=0).astype(out_ref.dtype)

    spread_outer_rows(even, odd, row_count, col_count, put)


def grid_kernel(count, in_ref, even_cos, even_sin, odd_cos, out_ref):
    devices = in_ref.shape[0]
    first, second = [], []
    for d in range(0, devices, 2):
        low, high = halves(in_ref[d].astype(jnp.float32), in_ref[d + 1].astype(jnp.float32))
        first.append(low)
        second.append(high)
    per_block = devices // 8
    blocks = []
    for k in range(4):
        span = slice(per_block * k, per_block * (k + 1))
        blocks.append(
            jnp.concatenate(
                [jnp.concatenate(first[span], axis=1), jnp.concatenate(second[span], axis=1)], axis=0
            )
        )
    cos_plus, sin_minus, cos_minus, sin_plus = blocks
    half = cos_plus.shape[0]

    def back(values, table):
        terms = [term for value in values for term in two_terms(value)]
        result = dot(jnp.concatenate(terms, axis=0), table[...], ((1,), (1,)))
        return [
            result[2 * half * i : 2 * half * i + half] + result[2 * half * i + half : 2 * half * (i + 1)]
            for i in range(len(values))
        ]

    even = back([cos_plus + cos_minus], even_cos)[0] + back([sin_plus + sin_minus], even_sin)[0]
    odd, turned = back([cos_plus - cos_minus, sin_plus - sin_minus], odd_cos)
    odd = odd + turned * column_sign(odd.shape)

    def put(j, parts):
        out_ref[j] = jnp.concatenate(parts, axis=0).astype(out_ref.dtype)

    scatter_rows(even, odd, count, put)


def far_kernel(
    source_ref, projection_ref, shifts_ref, near_ref, out_ref, grid_ref, weights, samples, shifts, totals_ref, sems
):
    depth = 16
    count = BASIS // depth

    def load(i):
        rows = pl.ds(i * depth, depth)
        return pltpu.make_async_copy(
            projection_ref.at[:, rows], weights.at[:, rows], sems.at[1 + count + i]
        )

    load_shifts = pltpu.make_async_copy(shifts_ref, shifts, sems.at[0])
    load_grid = pltpu.make_async_copy(source_ref, grid_ref, sems.at[1 + 2 * count])
    load_near = pltpu.make_async_copy(near_ref, totals_ref, sems.at[2 + 2 * count])
    load_grid.start()
    load_shifts.start()
    load_near.start()
    for i in range(count):
        load(i).start()

    def part(e, r):
        return grid_ref[e, 8 * r : 8 * r + 8, :].astype(jnp.float32)

    def put(s, value):
        samples[s] = value

    load_shifts.wait()
    load_grid.wait()
    read_samples(
        part, lambda e: part(e, GROUPS), tiled_shifts(shifts, 0), tiled_shifts(shifts, 1), put
    )
    load_near.wait()

    def store(i):
        rows = pl.ds(i * depth, depth)
        return pltpu.make_async_copy(totals_ref.at[:, rows], out_ref.at[:, rows], sems.at[1 + i])

    for i in range(count):
        span = slice(i * depth, (i + 1) * depth)
        load(i).wait()

        def add_row(a, totals):
            totals = list(totals)
            for b in range(STEN):
                s = a * STEN + b
                for t in range(TILES):
                    weight = weights[s, span, LANES * t : LANES * (t + 1)].astype(jnp.float32)
                    for q in range(RHS):
                        index = q * TILES + t
                        totals[index] = totals[index] + weight * samples[s, index : index + 1, :]
            return tuple(totals)

        start = tuple(
            totals_ref[q, span, LANES * t : LANES * (t + 1)] for q in range(RHS) for t in range(TILES)
        )
        totals = lax.fori_loop(0, STEN, add_row, start)
        for q in range(RHS):
            for t in range(TILES):
                totals_ref[q, span, LANES * t : LANES * (t + 1)] = totals[q * TILES + t]
        store(i).start()
    for i in range(count):
        store(i).wait()


def pick_kernel(currents_ref, slab_ref, arrived_ref, partners_ref, out_ref):
    lane = lane_index((BASIS, LANES))
    elem_col = lane & (EC - 1)
    row, col = lax.axis_index("row"), lax.axis_index("col")
    col_count = lax.axis_size("col")
    devices = arrived_ref.shape[0]

    def column_edge(source):
        source = jnp.clip(source, 0, col_count - 1)
        return slab_ref[source, 80:112, :].astype(jnp.float32)

    from_left, from_right = column_edge(col - 1), column_edge(col + 1)

    def beside(edge, q, t, end):
        place = q * TILES + t
        return jnp.concatenate([roll(edge, end - place, 1), roll(edge, end - place - SUB, 1)], axis=0)

    def three(own, left, right):
        return (
            jnp.where(elem_col == 0, left, roll(own, 1, 1)),
            own,
            jnp.where(elem_col == EC - 1, right, roll(own, -1, 1)),
        )

    sub = sub_index((SUB, LANES))

    def outer_row(source):
        parts = []
        for j in range(col_count):
            index = jnp.clip(source * col_count + j, 0, devices - 1)
            value = arrived_ref[index, 32:40, :].astype(jnp.float32)
            parts.append(jnp.where(sub < 4, roll(value, -2, 0), roll(roll(value, 2, 0), -64, 1)))
        return jnp.concatenate(parts, axis=0)

    rows = outer_row(row - 1), outer_row(row + 1)

    def outer_three(value, q, start):
        own = roll(value, start - EC * q, 1)
        left = roll(value, start - 2 * EC - 2 * q, 1)
        right = roll(value, start + EC - 1 - 2 * EC - 2 * q - 1, 1)
        return three(own, left, right)

    for q in range(RHS):
        tiles = []
        for t in range(TILES):
            own = currents_ref[q, :, LANES * t : LANES * (t + 1)]
            own = own.astype(jnp.bfloat16).astype(jnp.float32)
            tiles.append(three(own, beside(from_left, q, t, 0), beside(from_right, q, t, EC - 1)))
        above = outer_three(rows[0], q, 0)
        below = outer_three(rows[1], q, LANES - EC)
        for t in range(TILES):
            lanes = slice(LANES * t, LANES * (t + 1))
            codes = [partners_ref[k : k + 1, lanes] for k in range(1, NEIGH)]
            chosen = [tiles[t][1]] * (NEIGH - 1)
            for c in range(3):
                here = tiles[t][c]
                before = roll(tiles[t - 1][c], EC, 1) if t else above[c]
                after = roll(tiles[t + 1][c], -EC, 1) if t < TILES - 1 else below[c]
                views = (
                    jnp.where(lane < EC, before, roll(here, EC, 1)),
                    here,
                    jnp.where(lane >= LANES - EC, after, roll(here, -EC, 1)),
                )
                for r in range(3):
                    if r == 1 and c == 1:
                        continue
                    for k in range(NEIGH - 1):
                        chosen[k] = jnp.where(codes[k] == 3 * r + c, views[r], chosen[k])
            for k in range(NEIGH - 1):
                out_ref[k, q, :, lanes] = chosen[k].astype(out_ref.dtype)


def near_kernel(has_total, slots, start, stop, *refs):
    values_ref, refs = refs[0], refs[1:]
    total_ref = None
    if has_total:
        total_ref, refs = refs[0], refs[1:]
    blocks_ref, out_ref, blocks, picked, sems = refs
    chunks = (stop - start) // SUB

    def load(chunk, k):
        rows = pl.ds(start + chunk * SUB, SUB)
        return pltpu.make_async_copy(
            blocks_ref.at[slots[k], rows], blocks.at[chunk, k], sems.at[chunk, k]
        )

    for chunk in range(chunks):
        for k in range(len(slots)):
            load(chunk, k).start()
    picked[...] = values_ref[...].astype(jnp.bfloat16).astype(jnp.float32).reshape(picked.shape)
    if has_total:
        out_ref[...] = total_ref[...]

    def one_chunk(chunk, carry):
        for k in range(len(slots)):
            load(chunk, k).wait()
        rows = pl.ds(pl.multiple_of(start + chunk * SUB, SUB), SUB)
        for t in range(TILES):
            lanes = slice(t * LANES, (t + 1) * LANES)
            totals = [[None] * RHS for _ in range(SUB)]
            for k in range(len(slots)):
                for b in range(0, BASIS, 16):
                    values = [
                        [picked[k, q, b + 8 * h : b + 8 * h + 8, lanes] for h in range(2)]
                        for q in range(RHS)
                    ]
                    for a in range(SUB):
                        weight = blocks[chunk, k, a, b : b + 16, lanes].astype(jnp.float32)
                        for q in range(RHS):
                            term = weight[:8] * values[q][0] + weight[8:] * values[q][1]
                            totals[a][q] = term if totals[a][q] is None else totals[a][q] + term
            for q in range(RHS):
                value = sum_rows([totals[a][q] for a in range(SUB)])
                if has_total:
                    value = value + total_ref[q, rows, lanes]
                out_ref[q, rows, lanes] = value
        return carry

    lax.fori_loop(0, chunks, one_chunk, 0)


def near_call(values, total, near_blocks, slots, start, stop):
    elements = near_blocks.shape[3]
    chunks = (stop - start) // SUB
    return pl.pallas_call(
        functools.partial(near_kernel, total is not None, slots, start, stop),
        in_specs=[ON_CHIP] * (1 if total is None else 2) + [IN_PLACE],
        out_specs=ON_CHIP,
        out_shape=jax.ShapeDtypeStruct((RHS, BASIS, elements), jnp.float32),
        scratch_shapes=[
            pltpu.VMEM((chunks, len(slots), SUB, BASIS, elements), jnp.bfloat16),
            pltpu.VMEM((len(slots), RHS, BASIS, elements), jnp.float32),
            pltpu.SemaphoreType.DMA((chunks, len(slots))),
        ],
        compiler_params=NEAR_PARAMS,
        name="near",
    )(*([values] if total is None else [values, total]), near_blocks)


ON_CHIP = pl.BlockSpec(memory_space=pltpu.VMEM)
IN_PLACE = pl.BlockSpec(memory_space=pltpu.HBM)
PARAMS = pltpu.CompilerParams(vmem_limit_bytes=48 << 20)
CHARGE_PARAMS = pltpu.CompilerParams(vmem_limit_bytes=60 << 20)
FULL_PARAMS = pltpu.CompilerParams(vmem_limit_bytes=60 << 20)
NEAR_PARAMS = pltpu.CompilerParams(vmem_limit_bytes=48 << 20)


def whole(shape):
    return pl.BlockSpec(shape, lambda *_: (0,) * len(shape))


def shards_real(currents, projection, near_blocks, partners, shifts, green):
    row_count = lax.axis_size("row")
    col_count = lax.axis_size("col")
    elements = currents.shape[2]
    width = col_count * LANES
    length = 2 * width
    quarter = length // 4
    f32, b16 = jnp.float32, jnp.bfloat16
    struct = jax.ShapeDtypeStruct
    devices = row_count * col_count

    charges = pl.pallas_call(
        charge_kernel,
        in_specs=[IN_PLACE] * 3,
        out_specs=ON_CHIP,
        out_shape=struct((SUB, 112, LANES), b16),
        scratch_shapes=[
            pltpu.VMEM(projection.shape, b16),
            pltpu.VMEM((RHS, BASIS, elements), f32),
            pltpu.VMEM((2, elements), jnp.int32),
            pltpu.VMEM((RHS, BASIS, elements), f32),
            pltpu.VMEM((STEN, SUB, SUB, LANES), f32),
            pltpu.VMEM((STEN * STEN, SUB, LANES), f32),
            pltpu.SemaphoreType.DMA((STEN + 2,)),
        ],
        compiler_params=CHARGE_PARAMS,
        name="charges",
    )(currents, projection, shifts)
    slab = lax.all_to_all(charges, "col", 0, 0, tiled=True)

    columns, rows = even_positions(row_count, col_count)
    table = struct((quarter, quarter), b16)
    col_tables = pl.pallas_call(
        column_table_kernel,
        out_specs=[ON_CHIP] * 3,
        out_shape=[table] * 3,
        compiler_params=PARAMS,
        name="column_tables",
    )(jnp.asarray(position_bases(columns, length)))
    spectrum = pl.pallas_call(
        functools.partial(column_kernel, col_count),
        out_shape=struct((devices, 40, LANES), b16),
        in_specs=[ON_CHIP] * 4,
        out_specs=ON_CHIP,
        compiler_params=PARAMS,
        name="columns",
    )(slab, *col_tables)
    spectrum, held, held_green = lax.optimization_barrier((spectrum, currents, green))
    arrived = lax.all_to_all(spectrum, ("row", "col"), 0, 0, tiled=True)
    near = near_call(held, None, near_blocks, (0,), 0, BASIS)
    spread = struct((2 * quarter, LANES), f32)
    row_tables = pl.pallas_call(
        row_table_kernel,
        out_shape=[table] * 6 + [spread] * 2,
        compiler_params=FULL_PARAMS,
        name="row_tables",
    )(held_green, jnp.asarray(position_bases(rows, length)), jnp.asarray(order_bases(rows, length)))
    arrived, near, *row_tables = lax.optimization_barrier((arrived, near, *row_tables))
    rows_back = pl.pallas_call(
        functools.partial(row_kernel, row_count, col_count),
        out_shape=struct((devices, 40, LANES), b16),
        in_specs=[IN_PLACE] * 9,
        out_specs=ON_CHIP,
        scratch_shapes=[pltpu.VMEM((devices, 40, LANES), b16)]
        + [pltpu.VMEM((quarter, quarter), b16)] * 6
        + [pltpu.VMEM((2 * quarter, LANES), f32)] * 2
        + [pltpu.SemaphoreType.DMA((9,))],
        compiler_params=FULL_PARAMS,
        name="rows",
    )(arrived, *row_tables)
    rows_back, ready = lax.optimization_barrier((rows_back, arrived))
    returned = lax.all_to_all(rows_back, ("row", "col"), 0, 0, tiled=True)
    picked = pl.pallas_call(
        pick_kernel,
        in_specs=[whole(currents.shape), ON_CHIP, ON_CHIP, whole(partners.shape)],
        out_specs=ON_CHIP,
        out_shape=struct((NEIGH - 1, RHS, BASIS, elements), b16),
        compiler_params=PARAMS,
        name="pick",
    )(held, slab, ready, partners)
    others = tuple(range(1, NEIGH))
    near = near_call(picked, near, near_blocks, others, 0, BASIS // 2)
    returned, near, picked = lax.optimization_barrier((returned, near, picked))
    potential = pl.pallas_call(
        functools.partial(grid_kernel, col_count),
        out_shape=struct((SUB, 80, LANES), b16),
        in_specs=[ON_CHIP] * 4,
        out_specs=ON_CHIP,
        compiler_params=PARAMS,
        name="grid",
    )(returned, *col_tables)
    potential, near, picked = lax.optimization_barrier((potential, near, picked))
    pieces = lax.all_to_all(potential, "col", 0, 0, tiled=True)
    near = near_call(picked, near, near_blocks, others, BASIS // 2, BASIS)

    return pl.pallas_call(
        far_kernel,
        in_specs=[IN_PLACE] * 4,
        out_specs=IN_PLACE,
        out_shape=struct((RHS, BASIS, elements), f32),
        scratch_shapes=[
            pltpu.VMEM((SUB, 80, LANES), b16),
            pltpu.VMEM(projection.shape, b16),
            pltpu.VMEM((STEN * STEN, SUB, LANES), f32),
            pltpu.VMEM((2, elements), jnp.int32),
            pltpu.VMEM((RHS, BASIS, elements), f32),
            pltpu.SemaphoreType.DMA((11,)),
        ],
        compiler_params=FULL_PARAMS,
        name="far",
    )(pieces, projection, shifts, near)


def shards(currents, projection, near_blocks, partners, shifts, green):
    row_count = lax.axis_size("row")
    col_count = lax.axis_size("col")
    fits = col_count == SUB and green.shape[0] == 64 and 2 * row_count * col_count == green.shape[0]
    if fits and currents.shape[2] == TILES * LANES and row_count * ER == col_count * EC:
        return shards_real(currents, projection, near_blocks, partners, shifts, green)
    return shards_general(currents, projection, near_blocks, partners, shifts, green)


def solution(mesh):
    in_specs = (
        P(None, None, ("row", "col")),
        P(None, None, ("row", "col")),
        P(None, None, None, ("row", "col")),
        P(None, ("row", "col")),
        P(None, ("row", "col")),
        P(("row", "col"), None),
    )
    out_specs = P(None, None, ("row", "col"))
    return jax.shard_map(shards, mesh=mesh, in_specs=in_specs, out_specs=out_specs, check_vma=False)
```

```python
import functools
import math

import jax
import jax.numpy as jnp
import numpy as np
from jax import lax
from jax.experimental import pallas as pl
from jax.experimental.pallas import tpu as pltpu
from jax.sharding import PartitionSpec as P

BASIS = 64
STEN = 8
PITCH = 8
HALO = 2
NEIGH = 4
RHS = 2
ER = 32
EC = 16


def extended_2(block, sides, width):
    for axis, dim in sides:
        count = lax.axis_size(axis)
        forward = [(i, i + 1) for i in range(count - 1)]
        backward = [(target, source) for source, target in forward]
        low = lax.ppermute(
            lax.slice_in_dim(block, block.shape[dim] - width, None, axis=dim), axis, forward
        )
        high = lax.ppermute(lax.slice_in_dim(block, 0, width, axis=dim), axis, backward)
        block = jnp.concatenate([low, block, high], axis=dim)
    return block


def angle_table(first_size, second_size, modulus, direction):
    left_index = jnp.arange(first_size, dtype=jnp.int32)
    right_index = jnp.arange(second_size, dtype=jnp.int32)
    turn_count = left_index[:, None] * right_index[None, :] % modulus
    angles = turn_count.astype(jnp.float32) * (2.0 * math.pi / modulus)
    return (jnp.cos(angles), direction * jnp.sin(angles))


def complex_apply(real_part, imag_part, cosine, sine_table, pattern):
    highest = lax.Precision.HIGHEST
    out_real = jnp.einsum(pattern, real_part, cosine, precision=highest)
    out_imag = jnp.einsum(pattern, real_part, sine_table, precision=highest)
    if imag_part is not None:
        out_real = out_real - jnp.einsum(pattern, imag_part, sine_table, precision=highest)
        out_imag = out_imag + jnp.einsum(pattern, imag_part, cosine, precision=highest)
    return (out_real, out_imag)


def transform_last(real_part, imag_part, length, count_in, count_out, direction):
    leading = real_part.shape[:-1]
    inner_size = 128
    outer_size = length // inner_size
    rows_in = count_in // inner_size
    kept_count = count_out // outer_size
    shaped_real = real_part.reshape(leading + (rows_in, inner_size))
    shaped_imag = None
    if imag_part is not None:
        shaped_imag = imag_part.reshape(leading + (rows_in, inner_size))
    cosine, sine_table = angle_table(rows_in, outer_size, outer_size, direction)
    first_real, first_imag = complex_apply(
        shaped_real, shaped_imag, cosine, sine_table, "...ab,ak->...kb"
    )
    twist_cos, twist_sin = angle_table(outer_size, inner_size, length, direction)
    turned_real = first_real * twist_cos - first_imag * twist_sin
    turned_imag = first_real * twist_sin + first_imag * twist_cos
    cosine, sine_table = angle_table(inner_size, kept_count, inner_size, direction)
    last_real, last_imag = complex_apply(
        turned_real, turned_imag, cosine, sine_table, "...kb,bj->...jk"
    )
    out_shape = leading + (kept_count * outer_size,)
    return (last_real.reshape(out_shape), last_imag.reshape(out_shape))


def place_shifted(blocks, amount, dim_index):
    new_shape = list(blocks.shape)
    new_shape[dim_index] = new_shape[dim_index] + 2 * HALO
    result = jnp.zeros(tuple(new_shape), blocks.dtype)
    for offset in range(-HALO, HALO + 1):
        widths = [(0, 0)] * blocks.ndim
        widths[dim_index] = (HALO + offset, HALO - offset)
        result = jnp.where(amount == offset, jnp.pad(blocks, widths), result)
    return result


def pick_shifted(windows, amount, dim_index):
    new_shape = list(windows.shape)
    new_shape[dim_index] = STEN
    result = jnp.zeros(tuple(new_shape), windows.dtype)
    for offset in range(-HALO, HALO + 1):
        piece = lax.slice_in_dim(windows, HALO + offset, HALO + offset + STEN, axis=dim_index)
        result = jnp.where(amount == offset, piece, result)
    return result


def intersection_add(framed, dim_index):
    element_count = framed.shape[dim_index]
    window_size = framed.shape[dim_index + 1]
    head_part = lax.slice_in_dim(framed, 0, PITCH, axis=dim_index + 1)
    tail_part = lax.slice_in_dim(framed, PITCH, window_size, axis=dim_index + 1)
    widths = [(0, 0)] * framed.ndim
    widths[dim_index + 1] = (0, 2 * PITCH - window_size)
    tail_part = jnp.pad(tail_part, widths)
    merged = framed.shape[:dim_index] + (element_count * PITCH,) + framed.shape[dim_index + 2 :]
    head_part = head_part.reshape(merged)
    tail_part = tail_part.reshape(merged)
    front_pad = [(0, 0)] * len(merged)
    front_pad[dim_index] = (0, PITCH)
    back_pad = [(0, 0)] * len(merged)
    back_pad[dim_index] = (PITCH, 0)
    summed = jnp.pad(head_part, front_pad) + jnp.pad(tail_part, back_pad)
    return lax.slice_in_dim(summed, 0, element_count * PITCH + 2 * HALO, axis=dim_index)


def cut_windows(field, dim_index):
    element_count = (field.shape[dim_index] - 2 * HALO) // PITCH
    widths = [(0, 0)] * field.ndim
    widths[dim_index] = (0, PITCH - 2 * HALO)
    extended = jnp.pad(field, widths)
    split_shape = field.shape[:dim_index] + (element_count, PITCH) + field.shape[dim_index + 1 :]
    head_part = lax.slice_in_dim(extended, 0, element_count * PITCH, axis=dim_index).reshape(
        split_shape
    )
    tail_part = lax.slice_in_dim(
        extended, PITCH, PITCH + element_count * PITCH, axis=dim_index
    ).reshape(split_shape)
    tail_part = lax.slice_in_dim(tail_part, 0, 2 * HALO, axis=dim_index + 1)
    return jnp.concatenate([head_part, tail_part], axis=dim_index + 1)


def fold_margin(padded, dim_index):
    full_size = padded.shape[dim_index]
    inner_size = full_size - 4 * HALO
    core_part = lax.slice_in_dim(padded, 2 * HALO, 2 * HALO + inner_size, axis=dim_index)
    upper_part = lax.slice_in_dim(padded, 0, HALO, axis=dim_index)
    lower_part = lax.slice_in_dim(padded, full_size - HALO, full_size, axis=dim_index)
    upper_pad = [(0, 0)] * padded.ndim
    upper_pad[dim_index] = (0, inner_size - HALO)
    lower_pad = [(0, 0)] * padded.ndim
    lower_pad[dim_index] = (inner_size - HALO, 0)
    return core_part + jnp.pad(upper_part, upper_pad) + jnp.pad(lower_part, lower_pad)


def shards_general(currents, projection, near_blocks, partners, shifts, green):
    row_count = lax.axis_size("row")
    col_count = lax.axis_size("col")
    device_count = row_count * col_count
    elements = ER * EC
    cur_half = currents.astype(jnp.bfloat16)
    spread = extended_2(cur_half.reshape(RHS, BASIS, ER, EC), (("row", 2), ("col", 3)), 1)
    views = []
    for symbol in range(9):
        row_start = symbol // 3
        col_start = symbol % 3
        views.append(
            spread[:, :, row_start : row_start + ER, col_start : col_start + EC].reshape(
                RHS, BASIS, elements
            )
        )
    picked = []
    for neighbour_slot in range(NEIGH):
        chosen = jnp.zeros((RHS, BASIS, elements), jnp.bfloat16)
        for symbol in range(9):
            chosen = jnp.where(partners[neighbour_slot] == symbol, views[symbol], chosen)
        picked.append(chosen)
    near_term = jnp.einsum(
        "kabn,kqbn->qan", near_blocks, jnp.stack(picked), preferred_element_type=jnp.float32
    )
    stencil = jnp.einsum("sbn,qbn->qsn", projection, cur_half, preferred_element_type=jnp.float32)
    blocks = stencil.reshape(RHS, STEN, STEN, elements)
    framed = place_shifted(place_shifted(blocks, shifts[0], 1), shifts[1], 2)
    window_size = STEN + 2 * HALO
    framed = framed.reshape(RHS, window_size, window_size, ER, EC).transpose(0, 3, 1, 4, 2)
    extended = intersection_add(intersection_add(framed, 1), 2)
    padded = extended_2(extended, (("row", 1), ("col", 2)), HALO)
    charges = fold_margin(fold_margin(padded, 1), 2)
    slab = lax.all_to_all(charges, "col", split_axis=1, concat_axis=2, tiled=True)
    slab_rows = slab.shape[1]
    width_cols = slab.shape[2]
    length_cols = 2 * width_cols
    block_cols = length_cols // device_count
    grid_rows = slab_rows * device_count
    length_rows = 2 * grid_rows
    fwd_real, fwd_imag = transform_last(slab, None, length_cols, width_cols, length_cols, -1.0)
    out_real = fwd_real.reshape(RHS, slab_rows, device_count, block_cols)
    out_imag = fwd_imag.reshape(RHS, slab_rows, device_count, block_cols)
    arrived = (
        lax.all_to_all(out_real, ("row", "col"), split_axis=2, concat_axis=2, tiled=True),
        lax.all_to_all(out_imag, ("row", "col"), split_axis=2, concat_axis=2, tiled=True),
    )
    col_real = arrived[0].transpose(0, 3, 2, 1).reshape(RHS, block_cols, grid_rows)
    col_imag = arrived[1].transpose(0, 3, 2, 1).reshape(RHS, block_cols, grid_rows)
    spec_real, spec_imag = transform_last(
        col_real, col_imag, length_rows, grid_rows, length_rows, -1.0
    )
    spec_real = spec_real * green
    spec_imag = spec_imag * green
    back_real, back_imag = transform_last(
        spec_real, spec_imag, length_rows, length_rows, grid_rows, 1.0
    )
    send_real = back_real.reshape(RHS, block_cols, device_count, slab_rows)
    send_imag = back_imag.reshape(RHS, block_cols, device_count, slab_rows)
    returned = (
        lax.all_to_all(send_real, ("row", "col"), split_axis=2, concat_axis=2, tiled=True),
        lax.all_to_all(send_imag, ("row", "col"), split_axis=2, concat_axis=2, tiled=True),
    )
    rows_real = returned[0].transpose(0, 3, 2, 1).reshape(RHS, slab_rows, length_cols)
    rows_imag = returned[1].transpose(0, 3, 2, 1).reshape(RHS, slab_rows, length_cols)
    final_real, final_imag = transform_last(
        rows_real, rows_imag, length_cols, length_cols, width_cols, 1.0
    )
    potential_slab = final_real * (1.0 / (length_rows * length_cols))
    potential = lax.all_to_all(potential_slab, "col", split_axis=2, concat_axis=1, tiled=True)
    rimmed = extended_2(potential, (("row", 1), ("col", 2)), HALO)
    windows = cut_windows(cut_windows(rimmed, 1), 3)
    windows = windows.transpose(0, 2, 4, 1, 3).reshape(RHS, window_size, window_size, elements)
    samples = pick_shifted(pick_shifted(windows, shifts[0], 1), shifts[1], 2).reshape(
        RHS, STEN * STEN, elements
    )
    sample_high = samples.astype(jnp.bfloat16)
    sample_low = (samples - sample_high.astype(jnp.float32)).astype(jnp.bfloat16)
    far_term = jnp.einsum(
        "sbn,qsn->qbn", projection, sample_high, preferred_element_type=jnp.float32
    )
    far_term = far_term + jnp.einsum(
        "sbn,qsn->qbn", projection, sample_low, preferred_element_type=jnp.float32
    )
    return far_term + near_term


LANES = 128
SUB = 8
TILES = 4
GROUPS = 9
PARITY_ORDER = (0, 2, 4, 6, 1, 3, 5, 7)


def roll(value, amount, dim):
    return pltpu.roll(value, amount % value.shape[dim], dim)


def lane_index(shape):
    return lax.broadcasted_iota(jnp.int32, shape, len(shape) - 1)


def sub_index(shape):
    return lax.broadcasted_iota(jnp.int32, shape, len(shape) - 2)


def sum_rows(parts):
    sub = sub_index(parts[0].shape)
    top = sub < 4
    level = []
    for i in range(4):
        a, b = parts[i], parts[i + 4]
        level.append(jnp.where(top, a, b) + roll(jnp.where(top, b, a), 4, 0))
    mask = (sub & 2) == 0
    level = [
        jnp.where(mask, level[i], level[i + 2])
        + jnp.where(mask, roll(level[i], -2, 0), roll(level[i + 2], 2, 0))
        for i in range(2)
    ]
    mask = (sub & 1) == 0
    a, b = level
    return jnp.where(mask, a, b) + jnp.where(mask, roll(a, -1, 0), roll(b, 1, 0))


def next_row(value):
    lane = lane_index(value.shape)
    sub = sub_index(value.shape)
    turned = roll(value, EC, 1)
    carried = jnp.where((sub & 3) == 0, 0.0, roll(turned, 1, 0))
    return jnp.where(lane < EC, carried, turned)


def previous_row(value):
    lane = lane_index(value.shape)
    sub = sub_index(value.shape)
    turned = roll(value, -EC, 1)
    carried = jnp.where((sub & 3) == 3, 0.0, roll(turned, -1, 0))
    return jnp.where(lane >= LANES - EC, carried, turned)


def place_charges(stencil, row_shift, col_shift):
    shape = row_shift.shape
    lane = lane_index(shape)
    sub = sub_index(shape)
    window = STEN + 2 * HALO
    row_mask = {o: row_shift == o for o in range(-HALO, HALO + 1)}
    col_mask = {o: col_shift == o for o in range(-HALO, HALO + 1)}
    first = []
    for rr in range(window):
        line = []
        for c in range(STEN):
            value = jnp.zeros(shape, jnp.float32)
            for o in range(-HALO, HALO + 1):
                source = rr - HALO - o
                if 0 <= source < STEN:
                    value = jnp.where(row_mask[o], stencil(source * STEN + c), value)
            line.append(value)
        first.append(line)
    framed = []
    for rr in range(window):
        line = []
        for cc in range(window):
            value = jnp.zeros(shape, jnp.float32)
            for o in range(-HALO, HALO + 1):
                source = cc - HALO - o
                if 0 <= source < STEN:
                    value = jnp.where(col_mask[o], first[rr][source], value)
            line.append(value)
        framed.append(line)
    grid = []
    for r in range(PITCH):
        line = []
        for cc in range(window):
            value = framed[r + HALO][cc]
            if r < HALO:
                value = value + next_row(framed[r + HALO + PITCH][cc])
            if r >= PITCH - HALO:
                value = value + previous_row(framed[r + HALO - PITCH][cc])
            line.append(value)
        grid.append(line)
    slot = sub & 3
    low_lanes = lane < EC
    high_lanes = lane >= LANES - EC
    line = []
    for cc in range(window):
        value = jnp.where(low_lanes & (slot == 0), roll(roll(framed[10][cc], EC, 1), -3, 0), 0.0)
        value = jnp.where(low_lanes & (slot == 1), roll(roll(framed[11][cc], EC, 1), -2, 0), value)
        value = jnp.where(high_lanes & (slot == 3), roll(roll(framed[0][cc], -EC, 1), 3, 0), value)
        value = jnp.where(high_lanes & (slot == 2), roll(roll(framed[1][cc], -EC, 1), 2, 0), value)
        line.append(value)
    grid.append(line)
    elem_col = lane & (EC - 1)
    parts = [[] for _ in range(SUB)]
    edges = [jnp.zeros(shape, jnp.float32) for _ in range(SUB)]
    for r in range(GROUPS):
        cells = []
        for c in range(PITCH):
            value = grid[r][c + HALO]
            if c < HALO:
                value = value + jnp.where(elem_col == 0, 0.0, roll(grid[r][c + HALO + PITCH], 1, 1))
            if c >= PITCH - HALO:
                value = value + jnp.where(
                    elem_col == EC - 1, 0.0, roll(grid[r][c + HALO - PITCH], -1, 1)
                )
            cells.append(value)
        turned = transpose_blocks([cells[c] for c in PARITY_ORDER], lane)
        for e in range(SUB):
            parts[e].append(turned[e])
            start = EC * e
            edge = edges[e]
            edge = jnp.where(lane == r, roll(grid[r][10], r - start - (EC - 1), 1), edge)
            edge = jnp.where(lane == 64 + r, roll(grid[r][11], 64 + r - start - (EC - 1), 1), edge)
            edge = jnp.where(lane == 63 - r, roll(grid[r][0], 63 - r - start, 1), edge)
            edge = jnp.where(lane == 127 - r, roll(grid[r][1], 127 - r - start, 1), edge)
            edges[e] = edge
    return [parts[e] + [edges[e]] for e in range(SUB)]


def transpose_blocks(values, lane):
    block = lane // EC
    for step in (4, 2, 1):
        mask = (block & step) == 0
        result = list(values)
        for i in range(SUB):
            if i & step:
                continue
            a, b = values[i], values[i + step]
            result[i] = jnp.where(mask, a, roll(b, EC * step, 1))
            result[i + step] = jnp.where(mask, roll(a, -EC * step, 1), b)
        values = result
    return values


def halves(a, b):
    low = lane_index(a.shape) < 64
    return jnp.where(low, a, roll(b, 64, 1)), jnp.where(low, roll(a, 64, 1), b)


def half_rows(a, b):
    top = sub_index(a.shape) < 4
    return jnp.where(top, a, roll(b, 4, 0)), jnp.where(top, roll(a, 4, 0), b)


def gather_rows(part, edge, count):
    sample = edge(0)
    lane = lane_index(sample.shape)
    from_low = (lane == 0) | (lane == 64)
    from_high = (lane == 63) | (lane == 127)
    rows = []
    for j in range(count):
        groups = []
        for r in range(GROUPS):
            value = part(j, r)
            if j > 0:
                value = value + jnp.where(from_low, roll(edge(j - 1), -r, 1), 0.0)
            if j < count - 1:
                value = value + jnp.where(from_high, roll(edge(j + 1), r, 1), 0.0)
            groups.append(value)
        first, second = [], []
        for parity in range(2):
            for b in range(2):
                low, high = half_rows(groups[parity + 4 * b], groups[parity + 4 * b + 2])
                first.append(low)
                second.append(high)
        low, high = half_rows(groups[8], groups[8])
        first.append(low)
        second.append(high)
        rows.append(jnp.concatenate(first + second, axis=0))
    even, odd = [], []
    for j in range(0, count, 2):
        low, high = halves(rows[j], rows[j + 1])
        even.append(low)
        odd.append(high)
    return jnp.concatenate(even, axis=1), jnp.concatenate(odd, axis=1)


def scatter_rows(even, odd, count, put):
    rows = []
    for j in range(0, count, 2):
        tile = slice(64 * j, 64 * j + LANES)
        rows.extend(halves(even[:, tile], odd[:, tile]))
    blocks = []
    for j in range(count):
        first = [rows[j][8 * i : 8 * i + 8] for i in range(5)]
        second = [rows[j][40 + 8 * i : 48 + 8 * i] for i in range(5)]
        groups = [None] * GROUPS
        for parity in range(2):
            for b in range(2):
                low, high = half_rows(first[2 * parity + b], second[2 * parity + b])
                groups[parity + 4 * b] = low
                groups[parity + 4 * b + 2] = high
        sub = sub_index(first[4].shape)
        tail = jnp.where(sub < 4, roll(first[4], 4, 0), second[4])
        head = jnp.where(sub < 4, first[4], roll(second[4], 4, 0))
        groups[8] = jnp.where((sub & 2) == 0, head, tail)
        blocks.append(groups)
    lane = lane_index(blocks[0][0].shape)
    for j in range(count):
        edge = jnp.zeros(blocks[0][0].shape, jnp.float32)
        for r in range(GROUPS):
            if j < count - 1:
                edge = jnp.where(
                    (lane == r) | (lane == 64 + r), roll(blocks[j + 1][r], r, 1), edge
                )
            if j > 0:
                edge = jnp.where(
                    (lane == 63 - r) | (lane == 127 - r), roll(blocks[j - 1][r], -r, 1), edge
                )
        put(j, blocks[j] + [edge])


def read_samples(part, edge, row_shift, col_shift, put):
    shape = row_shift.shape
    lane = lane_index(shape)
    sub = sub_index(shape)
    elem_col = lane & (EC - 1)
    window = STEN + 2 * HALO
    grid = []
    for r in range(GROUPS):
        turned = transpose_blocks([part(e, r) for e in range(SUB)], lane)
        cells = [None] * PITCH
        for place, c in enumerate(PARITY_ORDER):
            cells[c] = turned[place]
        line = [None] * window
        for c in range(PITCH):
            line[c + HALO] = cells[c]
        after = [roll(cells[c], -1, 1) for c in range(HALO)]
        before = [roll(cells[PITCH - HALO + c], 1, 1) for c in range(HALO)]
        for e in range(SUB):
            start = EC * e
            last = lane == start + EC - 1
            zero = lane == start
            after[0] = jnp.where(last, roll(edge(e), start + EC - 1 - r, 1), after[0])
            after[1] = jnp.where(last, roll(edge(e), start + EC - 1 - 64 - r, 1), after[1])
            before[0] = jnp.where(zero, roll(edge(e), start - 63 + r, 1), before[0])
            before[1] = jnp.where(zero, roll(edge(e), start - 127 + r, 1), before[1])
        line[0], line[1] = before
        line[10], line[11] = after
        grid.append(line)
    slot = sub & 3
    first_row = (slot == 0) & (lane < EC)
    last_row = (slot == 3) & (lane >= LANES - EC)
    framed = [[None] * window for _ in range(window)]
    for cc in range(window):
        for r in range(PITCH):
            framed[r + HALO][cc] = grid[r][cc]
        outer = grid[8][cc]
        below = roll(outer, -EC, 1)
        above = roll(outer, EC, 1)
        framed[10][cc] = jnp.where(last_row, roll(below, 3, 0), previous_row(grid[0][cc]))
        framed[11][cc] = jnp.where(last_row, roll(below, 2, 0), previous_row(grid[1][cc]))
        framed[0][cc] = jnp.where(first_row, roll(above, -3, 0), next_row(grid[6][cc]))
        framed[1][cc] = jnp.where(first_row, roll(above, -2, 0), next_row(grid[7][cc]))
    for a in range(STEN):
        line = []
        for cc in range(window):
            value = framed[a + HALO][cc]
            for o in range(-HALO, HALO + 1):
                if o:
                    value = jnp.where(row_shift == o, framed[a + HALO + o][cc], value)
            line.append(value)
        for b in range(STEN):
            value = line[b + HALO]
            for o in range(-HALO, HALO + 1):
                if o:
                    value = jnp.where(col_shift == o, line[b + HALO + o], value)
            put(a * STEN + b, value)


def add_outer_rows(chunk, row_count, col_count):
    sub = sub_index((SUB, LANES))
    even, odd = [], []
    for i in range(row_count):
        for j in range(col_count):
            rows = [chunk(i, j)[8 * k : 8 * k + 8] for k in range(4)]
            if j == 0 and i > 0:
                outer = chunk(i - 1, 0)[32:40]
                rows[0] = rows[0] + jnp.where(sub == 0, outer, 0.0)
                rows[2] = rows[2] + jnp.where(sub == 0, roll(outer, -1, 0), 0.0)
            if j == col_count - 1 and i < row_count - 1:
                outer = chunk(i + 1, j)[32:40]
                rows[1] = rows[1] + jnp.where(sub == 7, outer, 0.0)
                rows[3] = rows[3] + jnp.where(sub == 7, roll(outer, 1, 0), 0.0)
            even.extend(rows[:2])
            odd.extend(rows[2:])
    return jnp.concatenate(even, axis=0), jnp.concatenate(odd, axis=0)


def spread_outer_rows(even, odd, row_count, col_count, put):
    sub = sub_index((SUB, LANES))

    def block(i, j):
        start = 16 * (i * col_count + j)
        return [even[start : start + 8], even[start + 8 : start + 16],
                odd[start : start + 8], odd[start + 8 : start + 16]]

    for i in range(row_count):
        for j in range(col_count):
            outer = jnp.zeros((SUB, LANES), jnp.float32)
            if j == 0 and i < row_count - 1:
                rows = block(i + 1, 0)
                outer = jnp.where(sub == 0, rows[0], jnp.where(sub == 1, roll(rows[2], 1, 0), outer))
            if j == col_count - 1 and i > 0:
                rows = block(i - 1, j)
                outer = jnp.where(sub == 7, rows[1], jnp.where(sub == 6, roll(rows[3], -1, 0), outer))
            put(i, j, block(i, j) + [outer])


def two_terms(value):
    high = value.astype(jnp.bfloat16)
    return high, (value - high.astype(jnp.float32)).astype(jnp.bfloat16)


def dot(left, right, dims=((1,), (0,))):
    return lax.dot_general(left, right, (dims, ((), ())), preferred_element_type=jnp.float32)


def even_positions(row_count, col_count):
    j, c, e = np.meshgrid(np.arange(col_count), np.arange(4), np.arange(EC), indexing="ij")
    columns = (LANES * j + PITCH * e + 2 * c).reshape(-1)
    i, j, b, h, t = np.meshgrid(
        np.arange(row_count), np.arange(col_count), np.arange(2), np.arange(2), np.arange(TILES),
        indexing="ij",
    )
    rows = (ER * PITCH * i + SUB * PITCH * t + PITCH * j + 2 * h + 4 * b).reshape(-1)
    return columns, rows


def angle_pair(left, right, length):
    angles = 2.0 * np.pi * (np.asarray(left)[:, None] * np.asarray(right)[None, :] % length) / length
    return np.asarray(np.cos(angles), np.float32), np.asarray(np.sin(angles), np.float32)


def position_bases(positions, length):
    orders = np.arange(length // 4)
    grouped = positions.reshape(-1, SUB)
    offsets = grouped[0] - grouped[0, 0]
    assert (grouped == grouped[:, :1] + offsets[None, :]).all()
    return np.concatenate(
        [
            *angle_pair(grouped[:, 0], orders, length),
            *angle_pair(offsets, orders, length),
            *angle_pair(offsets + 1, orders, length),
        ]
    )


def split_rows(ref, *counts):
    start, parts = 0, []
    for count in counts:
        parts.append(ref.at[start : start + count])
        start += count
    return parts


def order_bases(positions, length):
    bases = np.arange(0, length // 4, SUB)
    result = []
    for parity in range(2):
        result.extend(angle_pair(bases, positions + parity, length))
        result.extend(angle_pair(np.arange(SUB), positions + parity, length))
    return np.concatenate(result)


def fill_by_position(sign_of, bases, out_refs):
    base_cos, base_sin, even_cos, even_sin, odd_cos, odd_sin = bases
    ec, es, oc, os = (ref[...] for ref in (even_cos, even_sin, odd_cos, odd_sin))
    start = lane_index(ec.shape) == 0

    def pair(i, carry):
        parts = [[], [], []]
        for h in range(2):
            row = 2 * i + h
            bc, bs = base_cos[pl.ds(row, 1), :], base_sin[pl.ds(row, 1), :]
            parts[0].append(bc * ec - bs * es)
            parts[1].append(jnp.where(start, 1.0, -(bs * ec + bc * es)) * sign_of(row))
            parts[2].append(bc * oc - bs * os)
        rows = pl.ds(pl.multiple_of(16 * i, 16), 16)
        for ref, part in zip(out_refs, parts):
            ref[rows, :] = jnp.concatenate(part, axis=0).astype(ref.dtype)
        return carry

    lax.fori_loop(0, base_cos.shape[0] // 2, pair, 0)


def column_table_kernel(bases_ref, *outs):
    count = (bases_ref.shape[0] - 4 * SUB) // 2
    bases = split_rows(bases_ref, count, count, SUB, SUB, SUB, SUB)
    fill_by_position(lambda row: (1 - 2 * ((row // 2) & 1)).astype(jnp.float32), bases, outs)


def row_table_kernel(green_ref, position_ref, order_ref, *outs):
    count = (position_ref.shape[0] - 4 * SUB) // 2
    position = split_rows(position_ref, count, count, SUB, SUB, SUB, SUB)
    order = split_rows(order_ref, count, count, SUB, SUB, count, count, SUB, SUB)
    quarter = position[0].shape[1]
    tiles = quarter // LANES
    sub = sub_index((SUB, quarter))
    flip = jnp.where(sub < 4, 1.0, -1.0)
    fill_by_position(lambda row: flip, position, outs[3:6])
    ebc, ebs, ec, es, obc, obs, oc, os = order
    ec, es, oc, os = (ref[...] for ref in (ec, es, oc, os))
    lanes = jnp.where((lane_index((SUB, quarter)) & 4) == 0, 1.0, -1.0)

    def pair(i, carry):
        parts = [[], [], []]
        for h in range(2):
            row = 2 * i + h
            one = (pl.ds(row, 1), slice(None))
            bc, bs = ebc[one], ebs[one]
            parts[0].append(bc * ec - bs * es)
            first = (sub + row) == 0
            parts[1].append(jnp.where(first, 1.0, -(bs * ec + bc * es)) * lanes)
            parts[2].append(obc[one] * oc - obs[one] * os)
        rows = pl.ds(pl.multiple_of(16 * i, 16), 16)
        for ref, part in zip(outs[:3], parts):
            ref[rows, :] = jnp.concatenate(part, axis=0).astype(ref.dtype)
        return carry

    lax.fori_loop(0, ebc.shape[0] // 2, pair, 0)

    depth = green_ref.shape[0]
    device = lax.axis_index("row") * lax.axis_size("col") + lax.axis_index("col")
    number = sub_index((depth, LANES)) + device * depth
    length = 4 * quarter
    weight = jnp.where(number % quarter == 0, 1.0, 2.0) * (1.0 / (length * length))
    lane = lane_index((depth, LANES))

    def scaled(tile):
        value = green_ref[:, LANES * tile : LANES * (tile + 1)] * weight
        if tile % tiles == 0:
            value = value * jnp.where(lane == 0, 1.0, 2.0)
        else:
            value = value * 2.0
        return jnp.concatenate([value, value], axis=0)

    for t in range(tiles):
        cos_plus, cos_minus = scaled(t), scaled(2 * tiles + t)
        sin_minus, sin_plus = scaled(tiles + t), scaled(3 * tiles + t)
        first = slice(LANES * t, LANES * (t + 1))
        second = slice(quarter + LANES * t, quarter + LANES * (t + 1))
        outs[6][first, :] = (cos_plus + cos_minus).T
        outs[7][first, :] = (cos_plus - cos_minus).T
        outs[6][second, :] = (sin_plus + sin_minus).T
        outs[7][second, :] = (sin_plus - sin_minus).T


def tiled_shifts(shifts_ref, which):
    rows = [shifts_ref[which : which + 1, LANES * t : LANES * (t + 1)] for t in range(TILES)]
    return jnp.concatenate(rows * RHS, axis=0)


def charge_kernel(
    currents_ref, projection_ref, shifts_ref, out_ref, weights, raw, shifts, current, partial, stencil, sems
):
    copies = [
        pltpu.make_async_copy(currents_ref, raw, sems.at[STEN]),
        pltpu.make_async_copy(shifts_ref, shifts, sems.at[STEN + 1]),
    ]

    def weight_copy(step):
        rows = pl.ds(step * STEN, STEN)
        return pltpu.make_async_copy(projection_ref.at[rows], weights.at[rows], sems.at[step])

    copies[0].start()
    for step in range(STEN):
        weight_copy(step).start()
    copies[1].start()
    copies[0].wait()
    current[...] = raw[...].astype(jnp.bfloat16).astype(jnp.float32)

    def one_row(step, carry):
        weight_copy(step).wait()
        for t in range(TILES):
            lanes = slice(LANES * t, LANES * (t + 1))
            totals = [[None] * RHS for _ in range(STEN)]
            for b in range(0, BASIS, 16):
                values = [
                    [current[q, b + 8 * h : b + 8 * h + 8, lanes] for h in range(2)]
                    for q in range(RHS)
                ]
                for s in range(STEN):
                    weight = weights[step * STEN + s, b : b + 16, lanes].astype(jnp.float32)
                    for q in range(RHS):
                        term = weight[:8] * values[q][0] + weight[8:] * values[q][1]
                        totals[s][q] = term if totals[s][q] is None else totals[s][q] + term
            for s in range(STEN):
                for q in range(RHS):
                    partial[s, q * TILES + t] = totals[s][q]
        for s in range(STEN):
            stencil[step * STEN + s] = sum_rows([partial[s, i] for i in range(SUB)])
        return carry

    lax.fori_loop(0, STEN, one_row, 0)
    copies[1].wait()
    chunks = place_charges(
        lambda s: stencil[s], tiled_shifts(shifts, 0), tiled_shifts(shifts, 1)
    )
    to_next, to_previous, to_rows = pack_currents(
        lambda q, t: current[q, :, LANES * t : LANES * (t + 1)]
    )
    mine = lax.axis_index("col")
    block = lane_index((SUB, LANES)) // EC
    middle = ((block & 3) == 1) | ((block & 3) == 2)
    for e in range(SUB):
        after = (mine == e - 1).astype(jnp.float32)
        before = (mine == e + 1).astype(jnp.float32)
        edge = jnp.where(middle, to_rows[e], chunks[e][GROUPS])
        rows = chunks[e][:GROUPS] + [edge, to_next * after + to_previous * before]
        out_ref[e] = jnp.concatenate(rows, axis=0).astype(out_ref.dtype)


def pack_currents(tile):
    half = BASIS // 2
    lane = lane_index((half, LANES))
    elem_col = lane & (EC - 1)
    to_next = jnp.zeros((half, LANES), jnp.float32)
    to_previous = jnp.zeros((half, LANES), jnp.float32)
    for q in range(RHS):
        for t in range(TILES):
            value = tile(q, t)
            for h in range(2):
                place = q * TILES + t + SUB * h
                part = value[half * h : half * (h + 1)]
                here = elem_col == place
                to_next = jnp.where(here, roll(part, place - (EC - 1), 1), to_next)
                to_previous = jnp.where(here, roll(part, place, 1), to_previous)
    lane = lane_index((SUB, LANES))
    to_rows = []
    for e in range(SUB):
        rows = jnp.zeros((SUB, LANES), jnp.float32)
        for q in range(RHS):
            span = slice(SUB * e, SUB * (e + 1))
            last = roll(tile(q, TILES - 1)[span], EC + EC * q - (LANES - EC), 1)
            first = roll(tile(q, 0)[span], 64 + EC + EC * q, 1)
            rows = jnp.where(lane // EC == 1 + q, last, jnp.where(lane // EC == 5 + q, first, rows))
        to_rows.append(rows)
    return to_next, to_previous, to_rows


def forward_rows(edge_row, j, count, which):
    lane = lane_index((SUB, LANES))
    start = EC + 64 * which
    value = roll(edge_row(j), -start, 1)
    for q in range(RHS):
        place = 2 * EC + 2 * q
        if j > 0:
            corner = roll(edge_row(j - 1), place - start - EC * q - (EC - 1), 1)
            value = jnp.where(lane == place, corner, value)
        if j < count - 1:
            corner = roll(edge_row(j + 1), place + 1 - start - EC * q, 1)
            value = jnp.where(lane == place + 1, corner, value)
    return jnp.where(lane < 64, roll(value, 2, 0), roll(roll(value, 64, 1), -2, 0))


def column_sign(shape):
    return jnp.where((lane_index(shape) & EC) == 0, 1.0, -1.0)


def column_kernel(count, rows_ref, even_cos, even_sin, odd_cos, out_ref):
    def part(j, r):
        return rows_ref[j, 8 * r : 8 * r + 8, :].astype(jnp.float32)

    even, odd = gather_rows(part, lambda j: part(j, GROUPS), count)
    both = jnp.concatenate([odd, odd * column_sign(odd.shape)], axis=0).astype(jnp.bfloat16)
    even = even.astype(jnp.bfloat16)
    ec, es = dot(even, even_cos[...]), dot(even, even_sin[...])
    both = dot(both, odd_cos[...])
    oc, os = both[: odd.shape[0]], both[odd.shape[0] :]
    half = out_ref.shape[1]
    mine = lax.axis_index("row")
    ends = [
        [forward_rows(lambda k: part(k, GROUPS), j, count, which) for which in range(2)]
        for j in range(count)
    ]
    sub = sub_index((SUB, LANES))
    middle = (sub >= 2) & (sub < 6)
    device = 0
    for block in (ec + oc, es - os, ec - oc, es + os):
        for t in range(0, block.shape[1], LANES):
            for chunk in halves(block[:half, t : t + LANES], block[half:, t : t + LANES]):
                i, j = device // count, device % count
                below = (mine == i - 1).astype(jnp.float32)
                above = (mine == i + 1).astype(jnp.float32)
                tail = jnp.where(
                    middle, ends[j][0] * below + ends[j][1] * above, chunk[half - SUB :]
                )
                chunk = jnp.concatenate([chunk[: half - SUB], tail], axis=0)
                out_ref[device] = chunk.astype(out_ref.dtype)
                device += 1


def row_kernel(row_count, col_count, *refs):
    sources, out_ref, held, sems = refs[:9], refs[9], refs[10:19], refs[19]
    loads = [
        pltpu.make_async_copy(source, target, sems.at[n])
        for n, (source, target) in enumerate(zip(sources, held))
    ]
    for load in loads:
        load.start()
    in_ref, even_cos, even_sin, odd_cos, back_cos, back_sin, back_odd, sum_ref, diff_ref = held
    loads[0].wait()
    even, odd = add_outer_rows(
        lambda i, j: in_ref[i * col_count + j].astype(jnp.float32), row_count, col_count
    )
    flip = jnp.where((sub_index(odd.shape) & 4) == 0, 1.0, -1.0)
    both = jnp.concatenate([odd, odd * flip], axis=1).astype(jnp.bfloat16)
    even = even.astype(jnp.bfloat16)
    for n in range(1, 4):
        loads[n].wait()
    a = [dot(even_cos[...], even), dot(even_sin[...], even)]
    both = dot(odd_cos[...], both)
    b = [both[:, :LANES], both[:, LANES:]]
    quarter = odd.shape[0]
    for n in range(4, 9):
        loads[n].wait()

    def pieces(left, right):
        for k in range(2):
            span = slice(quarter * k, quarter * (k + 1))
            yield two_terms(left[k] * sum_ref[span, :] + right[k] * diff_ref[span, :])

    def fold(value):
        return value[:, :LANES] + value[:, LANES:]

    (ch, cl), (sh, sl) = pieces(a, b)
    even = fold(
        dot(back_cos[...], jnp.concatenate([ch, cl], axis=1))
        + dot(back_sin[...], jnp.concatenate([sh, sl], axis=1))
    )
    (ch, cl), (sh, sl) = pieces(b, a)
    both = dot(back_odd[...], jnp.concatenate([ch, cl, sh, sl], axis=1))
    odd = fold(both[:, : 2 * LANES]) + fold(both[:, 2 * LANES :]) * flip

    def put(i, j, parts):
        out_ref[i * col_count + j] = jnp.concatenate(parts, axis=0).astype(out_ref.dtype)

    spread_outer_rows(even, odd, row_count, col_count, put)


def grid_kernel(count, in_ref, even_cos, even_sin, odd_cos, out_ref):
    devices = in_ref.shape[0]
    first, second = [], []
    for d in range(0, devices, 2):
        low, high = halves(in_ref[d].astype(jnp.float32), in_ref[d + 1].astype(jnp.float32))
        first.append(low)
        second.append(high)
    per_block = devices // 8
    blocks = []
    for k in range(4):
        span = slice(per_block * k, per_block * (k + 1))
        blocks.append(
            jnp.concatenate(
                [jnp.concatenate(first[span], axis=1), jnp.concatenate(second[span], axis=1)], axis=0
            )
        )
    cos_plus, sin_minus, cos_minus, sin_plus = blocks
    half = cos_plus.shape[0]

    def back(values, table):
        terms = [term for value in values for term in two_terms(value)]
        result = dot(jnp.concatenate(terms, axis=0), table[...], ((1,), (1,)))
        return [
            result[2 * half * i : 2 * half * i + half] + result[2 * half * i + half : 2 * half * (i + 1)]
            for i in range(len(values))
        ]

    even = back([cos_plus + cos_minus], even_cos)[0] + back([sin_plus + sin_minus], even_sin)[0]
    odd, turned = back([cos_plus - cos_minus, sin_plus - sin_minus], odd_cos)
    odd = odd + turned * column_sign(odd.shape)

    def put(j, parts):
        out_ref[j] = jnp.concatenate(parts, axis=0).astype(out_ref.dtype)

    scatter_rows(even, odd, count, put)


def far_kernel(
    source_ref, projection_ref, shifts_ref, near_ref, out_ref, grid_ref, weights, samples, shifts, totals_ref, sems
):
    depth = 16
    count = BASIS // depth

    def load(i):
        rows = pl.ds(i * depth, depth)
        return pltpu.make_async_copy(
            projection_ref.at[:, rows], weights.at[:, rows], sems.at[1 + count + i]
        )

    load_shifts = pltpu.make_async_copy(shifts_ref, shifts, sems.at[0])
    load_grid = pltpu.make_async_copy(source_ref, grid_ref, sems.at[1 + 2 * count])
    load_near = pltpu.make_async_copy(near_ref, totals_ref, sems.at[2 + 2 * count])
    load_grid.start()
    load_shifts.start()
    load_near.start()
    for i in range(count):
        load(i).start()

    def part(e, r):
        return grid_ref[e, 8 * r : 8 * r + 8, :].astype(jnp.float32)

    def put(s, value):
        samples[s] = value

    load_shifts.wait()
    load_grid.wait()
    read_samples(
        part, lambda e: part(e, GROUPS), tiled_shifts(shifts, 0), tiled_shifts(shifts, 1), put
    )
    load_near.wait()

    def store(i):
        rows = pl.ds(i * depth, depth)
        return pltpu.make_async_copy(totals_ref.at[:, rows], out_ref.at[:, rows], sems.at[1 + i])

    for i in range(count):
        span = slice(i * depth, (i + 1) * depth)
        load(i).wait()

        def add_row(a, totals):
            totals = list(totals)
            for b in range(STEN):
                s = a * STEN + b
                for t in range(TILES):
                    weight = weights[s, span, LANES * t : LANES * (t + 1)].astype(jnp.float32)
                    for q in range(RHS):
                        index = q * TILES + t
                        totals[index] = totals[index] + weight * samples[s, index : index + 1, :]
            return tuple(totals)

        start = tuple(
            totals_ref[q, span, LANES * t : LANES * (t + 1)] for q in range(RHS) for t in range(TILES)
        )
        totals = lax.fori_loop(0, STEN, add_row, start)
        for q in range(RHS):
            for t in range(TILES):
                totals_ref[q, span, LANES * t : LANES * (t + 1)] = totals[q * TILES + t]
        store(i).start()
    for i in range(count):
        store(i).wait()


def pick_kernel(currents_ref, slab_ref, arrived_ref, partners_ref, out_ref):
    lane = lane_index((BASIS, LANES))
    elem_col = lane & (EC - 1)
    row, col = lax.axis_index("row"), lax.axis_index("col")
    col_count = lax.axis_size("col")
    devices = arrived_ref.shape[0]

    def column_edge(source):
        source = jnp.clip(source, 0, col_count - 1)
        return slab_ref[source, 80:112, :].astype(jnp.float32)

    from_left, from_right = column_edge(col - 1), column_edge(col + 1)

    def beside(edge, q, t, end):
        place = q * TILES + t
        return jnp.concatenate([roll(edge, end - place, 1), roll(edge, end - place - SUB, 1)], axis=0)

    def three(own, left, right):
        return (
            jnp.where(elem_col == 0, left, roll(own, 1, 1)),
            own,
            jnp.where(elem_col == EC - 1, right, roll(own, -1, 1)),
        )

    sub = sub_index((SUB, LANES))

    def outer_row(source):
        parts = []
        for j in range(col_count):
            index = jnp.clip(source * col_count + j, 0, devices - 1)
            value = arrived_ref[index, 32:40, :].astype(jnp.float32)
            parts.append(jnp.where(sub < 4, roll(value, -2, 0), roll(roll(value, 2, 0), -64, 1)))
        return jnp.concatenate(parts, axis=0)

    rows = outer_row(row - 1), outer_row(row + 1)

    def outer_three(value, q, start):
        own = roll(value, start - EC * q, 1)
        left = roll(value, start - 2 * EC - 2 * q, 1)
        right = roll(value, start + EC - 1 - 2 * EC - 2 * q - 1, 1)
        return three(own, left, right)

    for q in range(RHS):
        tiles = []
        for t in range(TILES):
            own = currents_ref[q, :, LANES * t : LANES * (t + 1)]
            own = own.astype(jnp.bfloat16).astype(jnp.float32)
            tiles.append(three(own, beside(from_left, q, t, 0), beside(from_right, q, t, EC - 1)))
        above = outer_three(rows[0], q, 0)
        below = outer_three(rows[1], q, LANES - EC)
        for t in range(TILES):
            lanes = slice(LANES * t, LANES * (t + 1))
            codes = [partners_ref[k : k + 1, lanes] for k in range(1, NEIGH)]
            chosen = [tiles[t][1]] * (NEIGH - 1)
            for c in range(3):
                here = tiles[t][c]
                before = roll(tiles[t - 1][c], EC, 1) if t else above[c]
                after = roll(tiles[t + 1][c], -EC, 1) if t < TILES - 1 else below[c]
                views = (
                    jnp.where(lane < EC, before, roll(here, EC, 1)),
                    here,
                    jnp.where(lane >= LANES - EC, after, roll(here, -EC, 1)),
                )
                for r in range(3):
                    if r == 1 and c == 1:
                        continue
                    for k in range(NEIGH - 1):
                        chosen[k] = jnp.where(codes[k] == 3 * r + c, views[r], chosen[k])
            for k in range(NEIGH - 1):
                out_ref[k, q, :, lanes] = chosen[k].astype(out_ref.dtype)


def near_kernel(has_total, slots, start, stop, *refs):
    values_ref, refs = refs[0], refs[1:]
    total_ref = None
    if has_total:
        total_ref, refs = refs[0], refs[1:]
    blocks_ref, out_ref, blocks, picked, sems = refs
    chunks = (stop - start) // SUB

    def load(chunk, k):
        rows = pl.ds(start + chunk * SUB, SUB)
        return pltpu.make_async_copy(
            blocks_ref.at[slots[k], rows], blocks.at[chunk, k], sems.at[chunk, k]
        )

    for chunk in range(chunks):
        for k in range(len(slots)):
            load(chunk, k).start()
    picked[...] = values_ref[...].astype(jnp.bfloat16).astype(jnp.float32).reshape(picked.shape)
    if has_total:
        out_ref[...] = total_ref[...]

    def one_chunk(chunk, carry):
        for k in range(len(slots)):
            load(chunk, k).wait()
        rows = pl.ds(pl.multiple_of(start + chunk * SUB, SUB), SUB)
        for t in range(TILES):
            lanes = slice(t * LANES, (t + 1) * LANES)
            totals = [[None] * RHS for _ in range(SUB)]
            for k in range(len(slots)):
                for b in range(0, BASIS, 16):
                    values = [
                        [picked[k, q, b + 8 * h : b + 8 * h + 8, lanes] for h in range(2)]
                        for q in range(RHS)
                    ]
                    for a in range(SUB):
                        weight = blocks[chunk, k, a, b : b + 16, lanes].astype(jnp.float32)
                        for q in range(RHS):
                            term = weight[:8] * values[q][0] + weight[8:] * values[q][1]
                            totals[a][q] = term if totals[a][q] is None else totals[a][q] + term
            for q in range(RHS):
                value = sum_rows([totals[a][q] for a in range(SUB)])
                if has_total:
                    value = value + total_ref[q, rows, lanes]
                out_ref[q, rows, lanes] = value
        return carry

    lax.fori_loop(0, chunks, one_chunk, 0)


def near_call(values, total, near_blocks, slots, start, stop):
    elements = near_blocks.shape[3]
    chunks = (stop - start) // SUB
    return pl.pallas_call(
        functools.partial(near_kernel, total is not None, slots, start, stop),
        in_specs=[ON_CHIP] * (1 if total is None else 2) + [IN_PLACE],
        out_specs=ON_CHIP,
        out_shape=jax.ShapeDtypeStruct((RHS, BASIS, elements), jnp.float32),
        scratch_shapes=[
            pltpu.VMEM((chunks, len(slots), SUB, BASIS, elements), jnp.bfloat16),
            pltpu.VMEM((len(slots), RHS, BASIS, elements), jnp.float32),
            pltpu.SemaphoreType.DMA((chunks, len(slots))),
        ],
        compiler_params=NEAR_PARAMS,
        name="near",
    )(*([values] if total is None else [values, total]), near_blocks)


ON_CHIP = pl.BlockSpec(memory_space=pltpu.VMEM)
IN_PLACE = pl.BlockSpec(memory_space=pltpu.HBM)
PARAMS = pltpu.CompilerParams(vmem_limit_bytes=48 << 20)
CHARGE_PARAMS = pltpu.CompilerParams(vmem_limit_bytes=60 << 20)
FULL_PARAMS = pltpu.CompilerParams(vmem_limit_bytes=53 << 20)
NEAR_PARAMS = pltpu.CompilerParams(vmem_limit_bytes=48 << 20)


def whole(shape):
    return pl.BlockSpec(shape, lambda *_: (0,) * len(shape))


def shards_real(currents, projection, near_blocks, partners, shifts, green):
    row_count = lax.axis_size("row")
    col_count = lax.axis_size("col")
    elements = currents.shape[2]
    width = col_count * LANES
    length = 2 * width
    quarter = length // 4
    f32, b16 = jnp.float32, jnp.bfloat16
    struct = jax.ShapeDtypeStruct
    devices = row_count * col_count

    charges = pl.pallas_call(
        charge_kernel,
        in_specs=[IN_PLACE] * 3,
        out_specs=ON_CHIP,
        out_shape=struct((SUB, 112, LANES), b16),
        scratch_shapes=[
            pltpu.VMEM(projection.shape, b16),
            pltpu.VMEM((RHS, BASIS, elements), f32),
            pltpu.VMEM((2, elements), jnp.int32),
            pltpu.VMEM((RHS, BASIS, elements), f32),
            pltpu.VMEM((STEN, SUB, SUB, LANES), f32),
            pltpu.VMEM((STEN * STEN, SUB, LANES), f32),
            pltpu.SemaphoreType.DMA((STEN + 2,)),
        ],
        compiler_params=CHARGE_PARAMS,
        name="charges",
    )(currents, projection, shifts)
    slab = lax.all_to_all(charges, "col", 0, 0, tiled=True)

    columns, rows = even_positions(row_count, col_count)
    table = struct((quarter, quarter), b16)
    col_tables = pl.pallas_call(
        column_table_kernel,
        out_specs=[ON_CHIP] * 3,
        out_shape=[table] * 3,
        compiler_params=PARAMS,
        name="column_tables",
    )(jnp.asarray(position_bases(columns, length)))
    spectrum = pl.pallas_call(
        functools.partial(column_kernel, col_count),
        out_shape=struct((devices, 40, LANES), b16),
        in_specs=[ON_CHIP] * 4,
        out_specs=ON_CHIP,
        compiler_params=PARAMS,
        name="columns",
    )(slab, *col_tables)
    spectrum, held, held_green = lax.optimization_barrier((spectrum, currents, green))
    arrived = lax.all_to_all(spectrum, ("row", "col"), 0, 0, tiled=True)
    near = near_call(held, None, near_blocks, (0,), 0, BASIS)
    spread = struct((2 * quarter, LANES), f32)
    row_tables = pl.pallas_call(
        row_table_kernel,
        out_shape=[table] * 6 + [spread] * 2,
        compiler_params=FULL_PARAMS,
        name="row_tables",
    )(held_green, jnp.asarray(position_bases(rows, length)), jnp.asarray(order_bases(rows, length)))
    arrived, near, *row_tables = lax.optimization_barrier((arrived, near, *row_tables))
    rows_back = pl.pallas_call(
        functools.partial(row_kernel, row_count, col_count),
        out_shape=struct((devices, 40, LANES), b16),
        in_specs=[ON_CHIP] + [IN_PLACE] * 8,
        out_specs=ON_CHIP,
        scratch_shapes=[pltpu.VMEM((devices, 40, LANES), b16)]
        + [pltpu.VMEM((quarter, quarter), b16)] * 6
        + [pltpu.VMEM((2 * quarter, LANES), f32)] * 2
        + [pltpu.SemaphoreType.DMA((9,))],
        compiler_params=FULL_PARAMS,
        name="rows",
    )(arrived, *row_tables)
    rows_back, ready = lax.optimization_barrier((rows_back, arrived))
    returned = lax.all_to_all(rows_back, ("row", "col"), 0, 0, tiled=True)
    picked = pl.pallas_call(
        pick_kernel,
        in_specs=[whole(currents.shape), ON_CHIP, ON_CHIP, whole(partners.shape)],
        out_specs=ON_CHIP,
        out_shape=struct((NEIGH - 1, RHS, BASIS, elements), b16),
        compiler_params=PARAMS,
        name="pick",
    )(held, slab, ready, partners)
    others = tuple(range(1, NEIGH))
    near = near_call(picked, near, near_blocks, others, 0, BASIS // 2)
    returned, near, picked = lax.optimization_barrier((returned, near, picked))
    potential = pl.pallas_call(
        functools.partial(grid_kernel, col_count),
        out_shape=struct((SUB, 80, LANES), b16),
        in_specs=[ON_CHIP] * 4,
        out_specs=ON_CHIP,
        compiler_params=PARAMS,
        name="grid",
    )(returned, *col_tables)
    potential, near, picked = lax.optimization_barrier((potential, near, picked))
    pieces = lax.all_to_all(potential, "col", 0, 0, tiled=True)
    near = near_call(picked, near, near_blocks, others, BASIS // 2, BASIS)

    return pl.pallas_call(
        far_kernel,
        in_specs=[ON_CHIP, IN_PLACE, IN_PLACE, ON_CHIP],
        out_specs=IN_PLACE,
        out_shape=struct((RHS, BASIS, elements), f32),
        scratch_shapes=[
            pltpu.VMEM((SUB, 80, LANES), b16),
            pltpu.VMEM(projection.shape, b16),
            pltpu.VMEM((STEN * STEN, SUB, LANES), f32),
            pltpu.VMEM((2, elements), jnp.int32),
            pltpu.VMEM((RHS, BASIS, elements), f32),
            pltpu.SemaphoreType.DMA((11,)),
        ],
        compiler_params=FULL_PARAMS,
        name="far",
    )(pieces, projection, shifts, near)


def shards(currents, projection, near_blocks, partners, shifts, green):
    row_count = lax.axis_size("row")
    col_count = lax.axis_size("col")
    fits = col_count == SUB and green.shape[0] == 64 and 2 * row_count * col_count == green.shape[0]
    if fits and currents.shape[2] == TILES * LANES and row_count * ER == col_count * EC:
        return shards_real(currents, projection, near_blocks, partners, shifts, green)
    return shards_general(currents, projection, near_blocks, partners, shifts, green)


def solution(mesh):
    in_specs = (
        P(None, None, ("row", "col")),
        P(None, None, ("row", "col")),
        P(None, None, None, ("row", "col")),
        P(None, ("row", "col")),
        P(None, ("row", "col")),
        P(("row", "col"), None),
    )
    out_specs = P(None, None, ("row", "col"))
    return jax.shard_map(shards, mesh=mesh, in_specs=in_specs, out_specs=out_specs, check_vma=False)
```

```python
import functools
import math

import jax
import jax.numpy as jnp
import numpy as np
from jax import lax
from jax.experimental import pallas as pl
from jax.experimental.pallas import tpu as pltpu
from jax.sharding import PartitionSpec as P

BASIS = 64
STEN = 8
PITCH = 8
HALO = 2
NEIGH = 4
RHS = 2
ER = 32
EC = 16


def extended_2(block, sides, width):
    for axis, dim in sides:
        count = lax.axis_size(axis)
        forward = [(i, i + 1) for i in range(count - 1)]
        backward = [(target, source) for source, target in forward]
        low = lax.ppermute(
            lax.slice_in_dim(block, block.shape[dim] - width, None, axis=dim), axis, forward
        )
        high = lax.ppermute(lax.slice_in_dim(block, 0, width, axis=dim), axis, backward)
        block = jnp.concatenate([low, block, high], axis=dim)
    return block


def angle_table(first_size, second_size, modulus, direction):
    left_index = jnp.arange(first_size, dtype=jnp.int32)
    right_index = jnp.arange(second_size, dtype=jnp.int32)
    turn_count = left_index[:, None] * right_index[None, :] % modulus
    angles = turn_count.astype(jnp.float32) * (2.0 * math.pi / modulus)
    return (jnp.cos(angles), direction * jnp.sin(angles))


def complex_apply(real_part, imag_part, cosine, sine_table, pattern):
    highest = lax.Precision.HIGHEST
    out_real = jnp.einsum(pattern, real_part, cosine, precision=highest)
    out_imag = jnp.einsum(pattern, real_part, sine_table, precision=highest)
    if imag_part is not None:
        out_real = out_real - jnp.einsum(pattern, imag_part, sine_table, precision=highest)
        out_imag = out_imag + jnp.einsum(pattern, imag_part, cosine, precision=highest)
    return (out_real, out_imag)


def transform_last(real_part, imag_part, length, count_in, count_out, direction):
    leading = real_part.shape[:-1]
    inner_size = 128
    outer_size = length // inner_size
    rows_in = count_in // inner_size
    kept_count = count_out // outer_size
    shaped_real = real_part.reshape(leading + (rows_in, inner_size))
    shaped_imag = None
    if imag_part is not None:
        shaped_imag = imag_part.reshape(leading + (rows_in, inner_size))
    cosine, sine_table = angle_table(rows_in, outer_size, outer_size, direction)
    first_real, first_imag = complex_apply(
        shaped_real, shaped_imag, cosine, sine_table, "...ab,ak->...kb"
    )
    twist_cos, twist_sin = angle_table(outer_size, inner_size, length, direction)
    turned_real = first_real * twist_cos - first_imag * twist_sin
    turned_imag = first_real * twist_sin + first_imag * twist_cos
    cosine, sine_table = angle_table(inner_size, kept_count, inner_size, direction)
    last_real, last_imag = complex_apply(
        turned_real, turned_imag, cosine, sine_table, "...kb,bj->...jk"
    )
    out_shape = leading + (kept_count * outer_size,)
    return (last_real.reshape(out_shape), last_imag.reshape(out_shape))


def place_shifted(blocks, amount, dim_index):
    new_shape = list(blocks.shape)
    new_shape[dim_index] = new_shape[dim_index] + 2 * HALO
    result = jnp.zeros(tuple(new_shape), blocks.dtype)
    for offset in range(-HALO, HALO + 1):
        widths = [(0, 0)] * blocks.ndim
        widths[dim_index] = (HALO + offset, HALO - offset)
        result = jnp.where(amount == offset, jnp.pad(blocks, widths), result)
    return result


def pick_shifted(windows, amount, dim_index):
    new_shape = list(windows.shape)
    new_shape[dim_index] = STEN
    result = jnp.zeros(tuple(new_shape), windows.dtype)
    for offset in range(-HALO, HALO + 1):
        piece = lax.slice_in_dim(windows, HALO + offset, HALO + offset + STEN, axis=dim_index)
        result = jnp.where(amount == offset, piece, result)
    return result


def intersection_add(framed, dim_index):
    element_count = framed.shape[dim_index]
    window_size = framed.shape[dim_index + 1]
    head_part = lax.slice_in_dim(framed, 0, PITCH, axis=dim_index + 1)
    tail_part = lax.slice_in_dim(framed, PITCH, window_size, axis=dim_index + 1)
    widths = [(0, 0)] * framed.ndim
    widths[dim_index + 1] = (0, 2 * PITCH - window_size)
    tail_part = jnp.pad(tail_part, widths)
    merged = framed.shape[:dim_index] + (element_count * PITCH,) + framed.shape[dim_index + 2 :]
    head_part = head_part.reshape(merged)
    tail_part = tail_part.reshape(merged)
    front_pad = [(0, 0)] * len(merged)
    front_pad[dim_index] = (0, PITCH)
    back_pad = [(0, 0)] * len(merged)
    back_pad[dim_index] = (PITCH, 0)
    summed = jnp.pad(head_part, front_pad) + jnp.pad(tail_part, back_pad)
    return lax.slice_in_dim(summed, 0, element_count * PITCH + 2 * HALO, axis=dim_index)


def cut_windows(field, dim_index):
    element_count = (field.shape[dim_index] - 2 * HALO) // PITCH
    widths = [(0, 0)] * field.ndim
    widths[dim_index] = (0, PITCH - 2 * HALO)
    extended = jnp.pad(field, widths)
    split_shape = field.shape[:dim_index] + (element_count, PITCH) + field.shape[dim_index + 1 :]
    head_part = lax.slice_in_dim(extended, 0, element_count * PITCH, axis=dim_index).reshape(
        split_shape
    )
    tail_part = lax.slice_in_dim(
        extended, PITCH, PITCH + element_count * PITCH, axis=dim_index
    ).reshape(split_shape)
    tail_part = lax.slice_in_dim(tail_part, 0, 2 * HALO, axis=dim_index + 1)
    return jnp.concatenate([head_part, tail_part], axis=dim_index + 1)


def fold_margin(padded, dim_index):
    full_size = padded.shape[dim_index]
    inner_size = full_size - 4 * HALO
    core_part = lax.slice_in_dim(padded, 2 * HALO, 2 * HALO + inner_size, axis=dim_index)
    upper_part = lax.slice_in_dim(padded, 0, HALO, axis=dim_index)
    lower_part = lax.slice_in_dim(padded, full_size - HALO, full_size, axis=dim_index)
    upper_pad = [(0, 0)] * padded.ndim
    upper_pad[dim_index] = (0, inner_size - HALO)
    lower_pad = [(0, 0)] * padded.ndim
    lower_pad[dim_index] = (inner_size - HALO, 0)
    return core_part + jnp.pad(upper_part, upper_pad) + jnp.pad(lower_part, lower_pad)


def shards_general(currents, projection, near_blocks, partners, shifts, green):
    row_count = lax.axis_size("row")
    col_count = lax.axis_size("col")
    device_count = row_count * col_count
    elements = ER * EC
    cur_half = currents.astype(jnp.bfloat16)
    spread = extended_2(cur_half.reshape(RHS, BASIS, ER, EC), (("row", 2), ("col", 3)), 1)
    views = []
    for symbol in range(9):
        row_start = symbol // 3
        col_start = symbol % 3
        views.append(
            spread[:, :, row_start : row_start + ER, col_start : col_start + EC].reshape(
                RHS, BASIS, elements
            )
        )
    picked = []
    for neighbour_slot in range(NEIGH):
        chosen = jnp.zeros((RHS, BASIS, elements), jnp.bfloat16)
        for symbol in range(9):
            chosen = jnp.where(partners[neighbour_slot] == symbol, views[symbol], chosen)
        picked.append(chosen)
    near_term = jnp.einsum(
        "kabn,kqbn->qan", near_blocks, jnp.stack(picked), preferred_element_type=jnp.float32
    )
    stencil = jnp.einsum("sbn,qbn->qsn", projection, cur_half, preferred_element_type=jnp.float32)
    blocks = stencil.reshape(RHS, STEN, STEN, elements)
    framed = place_shifted(place_shifted(blocks, shifts[0], 1), shifts[1], 2)
    window_size = STEN + 2 * HALO
    framed = framed.reshape(RHS, window_size, window_size, ER, EC).transpose(0, 3, 1, 4, 2)
    extended = intersection_add(intersection_add(framed, 1), 2)
    padded = extended_2(extended, (("row", 1), ("col", 2)), HALO)
    charges = fold_margin(fold_margin(padded, 1), 2)
    slab = lax.all_to_all(charges, "col", split_axis=1, concat_axis=2, tiled=True)
    slab_rows = slab.shape[1]
    width_cols = slab.shape[2]
    length_cols = 2 * width_cols
    block_cols = length_cols // device_count
    grid_rows = slab_rows * device_count
    length_rows = 2 * grid_rows
    fwd_real, fwd_imag = transform_last(slab, None, length_cols, width_cols, length_cols, -1.0)
    out_real = fwd_real.reshape(RHS, slab_rows, device_count, block_cols)
    out_imag = fwd_imag.reshape(RHS, slab_rows, device_count, block_cols)
    arrived = (
        lax.all_to_all(out_real, ("row", "col"), split_axis=2, concat_axis=2, tiled=True),
        lax.all_to_all(out_imag, ("row", "col"), split_axis=2, concat_axis=2, tiled=True),
    )
    col_real = arrived[0].transpose(0, 3, 2, 1).reshape(RHS, block_cols, grid_rows)
    col_imag = arrived[1].transpose(0, 3, 2, 1).reshape(RHS, block_cols, grid_rows)
    spec_real, spec_imag = transform_last(
        col_real, col_imag, length_rows, grid_rows, length_rows, -1.0
    )
    spec_real = spec_real * green
    spec_imag = spec_imag * green
    back_real, back_imag = transform_last(
        spec_real, spec_imag, length_rows, length_rows, grid_rows, 1.0
    )
    send_real = back_real.reshape(RHS, block_cols, device_count, slab_rows)
    send_imag = back_imag.reshape(RHS, block_cols, device_count, slab_rows)
    returned = (
        lax.all_to_all(send_real, ("row", "col"), split_axis=2, concat_axis=2, tiled=True),
        lax.all_to_all(send_imag, ("row", "col"), split_axis=2, concat_axis=2, tiled=True),
    )
    rows_real = returned[0].transpose(0, 3, 2, 1).reshape(RHS, slab_rows, length_cols)
    rows_imag = returned[1].transpose(0, 3, 2, 1).reshape(RHS, slab_rows, length_cols)
    final_real, final_imag = transform_last(
        rows_real, rows_imag, length_cols, length_cols, width_cols, 1.0
    )
    potential_slab = final_real * (1.0 / (length_rows * length_cols))
    potential = lax.all_to_all(potential_slab, "col", split_axis=2, concat_axis=1, tiled=True)
    rimmed = extended_2(potential, (("row", 1), ("col", 2)), HALO)
    windows = cut_windows(cut_windows(rimmed, 1), 3)
    windows = windows.transpose(0, 2, 4, 1, 3).reshape(RHS, window_size, window_size, elements)
    samples = pick_shifted(pick_shifted(windows, shifts[0], 1), shifts[1], 2).reshape(
        RHS, STEN * STEN, elements
    )
    sample_high = samples.astype(jnp.bfloat16)
    sample_low = (samples - sample_high.astype(jnp.float32)).astype(jnp.bfloat16)
    far_term = jnp.einsum(
        "sbn,qsn->qbn", projection, sample_high, preferred_element_type=jnp.float32
    )
    far_term = far_term + jnp.einsum(
        "sbn,qsn->qbn", projection, sample_low, preferred_element_type=jnp.float32
    )
    return far_term + near_term


LANES = 128
SUB = 8
TILES = 4
GROUPS = 9
PARITY_ORDER = (0, 2, 4, 6, 1, 3, 5, 7)


def roll(value, amount, dim):
    return pltpu.roll(value, amount % value.shape[dim], dim)


def lane_index(shape):
    return lax.broadcasted_iota(jnp.int32, shape, len(shape) - 1)


def sub_index(shape):
    return lax.broadcasted_iota(jnp.int32, shape, len(shape) - 2)


def sum_rows(parts):
    sub = sub_index(parts[0].shape)
    top = sub < 4
    level = []
    for i in range(4):
        a, b = parts[i], parts[i + 4]
        level.append(jnp.where(top, a, b) + roll(jnp.where(top, b, a), 4, 0))
    mask = (sub & 2) == 0
    level = [
        jnp.where(mask, level[i], level[i + 2])
        + jnp.where(mask, roll(level[i], -2, 0), roll(level[i + 2], 2, 0))
        for i in range(2)
    ]
    mask = (sub & 1) == 0
    a, b = level
    return jnp.where(mask, a, b) + jnp.where(mask, roll(a, -1, 0), roll(b, 1, 0))


def next_row(value):
    lane = lane_index(value.shape)
    sub = sub_index(value.shape)
    turned = roll(value, EC, 1)
    carried = jnp.where((sub & 3) == 0, 0.0, roll(turned, 1, 0))
    return jnp.where(lane < EC, carried, turned)


def previous_row(value):
    lane = lane_index(value.shape)
    sub = sub_index(value.shape)
    turned = roll(value, -EC, 1)
    carried = jnp.where((sub & 3) == 3, 0.0, roll(turned, -1, 0))
    return jnp.where(lane >= LANES - EC, carried, turned)


def place_charges(stencil, row_shift, col_shift):
    shape = row_shift.shape
    lane = lane_index(shape)
    sub = sub_index(shape)
    window = STEN + 2 * HALO
    row_mask = {o: row_shift == o for o in range(-HALO, HALO + 1)}
    col_mask = {o: col_shift == o for o in range(-HALO, HALO + 1)}
    first = []
    for rr in range(window):
        line = []
        for c in range(STEN):
            value = jnp.zeros(shape, jnp.float32)
            for o in range(-HALO, HALO + 1):
                source = rr - HALO - o
                if 0 <= source < STEN:
                    value = jnp.where(row_mask[o], stencil(source * STEN + c), value)
            line.append(value)
        first.append(line)
    framed = []
    for rr in range(window):
        line = []
        for cc in range(window):
            value = jnp.zeros(shape, jnp.float32)
            for o in range(-HALO, HALO + 1):
                source = cc - HALO - o
                if 0 <= source < STEN:
                    value = jnp.where(col_mask[o], first[rr][source], value)
            line.append(value)
        framed.append(line)
    grid = []
    for r in range(PITCH):
        line = []
        for cc in range(window):
            value = framed[r + HALO][cc]
            if r < HALO:
                value = value + next_row(framed[r + HALO + PITCH][cc])
            if r >= PITCH - HALO:
                value = value + previous_row(framed[r + HALO - PITCH][cc])
            line.append(value)
        grid.append(line)
    slot = sub & 3
    low_lanes = lane < EC
    high_lanes = lane >= LANES - EC
    line = []
    for cc in range(window):
        value = jnp.where(low_lanes & (slot == 0), roll(roll(framed[10][cc], EC, 1), -3, 0), 0.0)
        value = jnp.where(low_lanes & (slot == 1), roll(roll(framed[11][cc], EC, 1), -2, 0), value)
        value = jnp.where(high_lanes & (slot == 3), roll(roll(framed[0][cc], -EC, 1), 3, 0), value)
        value = jnp.where(high_lanes & (slot == 2), roll(roll(framed[1][cc], -EC, 1), 2, 0), value)
        line.append(value)
    grid.append(line)
    elem_col = lane & (EC - 1)
    parts = [[] for _ in range(SUB)]
    edges = [jnp.zeros(shape, jnp.float32) for _ in range(SUB)]
    for r in range(GROUPS):
        cells = []
        for c in range(PITCH):
            value = grid[r][c + HALO]
            if c < HALO:
                value = value + jnp.where(elem_col == 0, 0.0, roll(grid[r][c + HALO + PITCH], 1, 1))
            if c >= PITCH - HALO:
                value = value + jnp.where(
                    elem_col == EC - 1, 0.0, roll(grid[r][c + HALO - PITCH], -1, 1)
                )
            cells.append(value)
        turned = transpose_blocks([cells[c] for c in PARITY_ORDER], lane)
        for e in range(SUB):
            parts[e].append(turned[e])
            start = EC * e
            edge = edges[e]
            edge = jnp.where(lane == r, roll(grid[r][10], r - start - (EC - 1), 1), edge)
            edge = jnp.where(lane == 64 + r, roll(grid[r][11], 64 + r - start - (EC - 1), 1), edge)
            edge = jnp.where(lane == 63 - r, roll(grid[r][0], 63 - r - start, 1), edge)
            edge = jnp.where(lane == 127 - r, roll(grid[r][1], 127 - r - start, 1), edge)
            edges[e] = edge
    return [parts[e] + [edges[e]] for e in range(SUB)]


def transpose_blocks(values, lane):
    block = lane // EC
    for step in (4, 2, 1):
        mask = (block & step) == 0
        result = list(values)
        for i in range(SUB):
            if i & step:
                continue
            a, b = values[i], values[i + step]
            result[i] = jnp.where(mask, a, roll(b, EC * step, 1))
            result[i + step] = jnp.where(mask, roll(a, -EC * step, 1), b)
        values = result
    return values


def halves(a, b):
    low = lane_index(a.shape) < 64
    return jnp.where(low, a, roll(b, 64, 1)), jnp.where(low, roll(a, 64, 1), b)


def half_rows(a, b):
    top = sub_index(a.shape) < 4
    return jnp.where(top, a, roll(b, 4, 0)), jnp.where(top, roll(a, 4, 0), b)


def gather_rows(part, edge, count):
    sample = edge(0)
    lane = lane_index(sample.shape)
    from_low = (lane == 0) | (lane == 64)
    from_high = (lane == 63) | (lane == 127)
    rows = []
    for j in range(count):
        groups = []
        for r in range(GROUPS):
            value = part(j, r)
            if j > 0:
                value = value + jnp.where(from_low, roll(edge(j - 1), -r, 1), 0.0)
            if j < count - 1:
                value = value + jnp.where(from_high, roll(edge(j + 1), r, 1), 0.0)
            groups.append(value)
        first, second = [], []
        for parity in range(2):
            for b in range(2):
                low, high = half_rows(groups[parity + 4 * b], groups[parity + 4 * b + 2])
                first.append(low)
                second.append(high)
        low, high = half_rows(groups[8], groups[8])
        first.append(low)
        second.append(high)
        rows.append(jnp.concatenate(first + second, axis=0))
    even, odd = [], []
    for j in range(0, count, 2):
        low, high = halves(rows[j], rows[j + 1])
        even.append(low)
        odd.append(high)
    return jnp.concatenate(even, axis=1), jnp.concatenate(odd, axis=1)


def scatter_rows(even, odd, count, put):
    rows = []
    for j in range(0, count, 2):
        tile = slice(64 * j, 64 * j + LANES)
        rows.extend(halves(even[:, tile], odd[:, tile]))
    blocks = []
    for j in range(count):
        first = [rows[j][8 * i : 8 * i + 8] for i in range(5)]
        second = [rows[j][40 + 8 * i : 48 + 8 * i] for i in range(5)]
        groups = [None] * GROUPS
        for parity in range(2):
            for b in range(2):
                low, high = half_rows(first[2 * parity + b], second[2 * parity + b])
                groups[parity + 4 * b] = low
                groups[parity + 4 * b + 2] = high
        sub = sub_index(first[4].shape)
        tail = jnp.where(sub < 4, roll(first[4], 4, 0), second[4])
        head = jnp.where(sub < 4, first[4], roll(second[4], 4, 0))
        groups[8] = jnp.where((sub & 2) == 0, head, tail)
        blocks.append(groups)
    lane = lane_index(blocks[0][0].shape)
    for j in range(count):
        edge = jnp.zeros(blocks[0][0].shape, jnp.float32)
        for r in range(GROUPS):
            if j < count - 1:
                edge = jnp.where(
                    (lane == r) | (lane == 64 + r), roll(blocks[j + 1][r], r, 1), edge
                )
            if j > 0:
                edge = jnp.where(
                    (lane == 63 - r) | (lane == 127 - r), roll(blocks[j - 1][r], -r, 1), edge
                )
        put(j, blocks[j] + [edge])


def read_samples(part, edge, row_shift, col_shift, put):
    shape = row_shift.shape
    lane = lane_index(shape)
    sub = sub_index(shape)
    elem_col = lane & (EC - 1)
    window = STEN + 2 * HALO
    grid = []
    for r in range(GROUPS):
        turned = transpose_blocks([part(e, r) for e in range(SUB)], lane)
        cells = [None] * PITCH
        for place, c in enumerate(PARITY_ORDER):
            cells[c] = turned[place]
        line = [None] * window
        for c in range(PITCH):
            line[c + HALO] = cells[c]
        after = [roll(cells[c], -1, 1) for c in range(HALO)]
        before = [roll(cells[PITCH - HALO + c], 1, 1) for c in range(HALO)]
        for e in range(SUB):
            start = EC * e
            last = lane == start + EC - 1
            zero = lane == start
            after[0] = jnp.where(last, roll(edge(e), start + EC - 1 - r, 1), after[0])
            after[1] = jnp.where(last, roll(edge(e), start + EC - 1 - 64 - r, 1), after[1])
            before[0] = jnp.where(zero, roll(edge(e), start - 63 + r, 1), before[0])
            before[1] = jnp.where(zero, roll(edge(e), start - 127 + r, 1), before[1])
        line[0], line[1] = before
        line[10], line[11] = after
        grid.append(line)
    slot = sub & 3
    first_row = (slot == 0) & (lane < EC)
    last_row = (slot == 3) & (lane >= LANES - EC)
    framed = [[None] * window for _ in range(window)]
    for cc in range(window):
        for r in range(PITCH):
            framed[r + HALO][cc] = grid[r][cc]
        outer = grid[8][cc]
        below = roll(outer, -EC, 1)
        above = roll(outer, EC, 1)
        framed[10][cc] = jnp.where(last_row, roll(below, 3, 0), previous_row(grid[0][cc]))
        framed[11][cc] = jnp.where(last_row, roll(below, 2, 0), previous_row(grid[1][cc]))
        framed[0][cc] = jnp.where(first_row, roll(above, -3, 0), next_row(grid[6][cc]))
        framed[1][cc] = jnp.where(first_row, roll(above, -2, 0), next_row(grid[7][cc]))
    for a in range(STEN):
        line = []
        for cc in range(window):
            value = framed[a + HALO][cc]
            for o in range(-HALO, HALO + 1):
                if o:
                    value = jnp.where(row_shift == o, framed[a + HALO + o][cc], value)
            line.append(value)
        for b in range(STEN):
            value = line[b + HALO]
            for o in range(-HALO, HALO + 1):
                if o:
                    value = jnp.where(col_shift == o, line[b + HALO + o], value)
            put(a * STEN + b, value)


def add_outer_rows(chunk, row_count, col_count):
    sub = sub_index((SUB, LANES))
    even, odd = [], []
    for i in range(row_count):
        for j in range(col_count):
            rows = [chunk(i, j)[8 * k : 8 * k + 8] for k in range(4)]
            if j == 0 and i > 0:
                outer = chunk(i - 1, 0)[32:40]
                rows[0] = rows[0] + jnp.where(sub == 0, outer, 0.0)
                rows[2] = rows[2] + jnp.where(sub == 0, roll(outer, -1, 0), 0.0)
            if j == col_count - 1 and i < row_count - 1:
                outer = chunk(i + 1, j)[32:40]
                rows[1] = rows[1] + jnp.where(sub == 7, outer, 0.0)
                rows[3] = rows[3] + jnp.where(sub == 7, roll(outer, 1, 0), 0.0)
            even.extend(rows[:2])
            odd.extend(rows[2:])
    return jnp.concatenate(even, axis=0), jnp.concatenate(odd, axis=0)


def spread_outer_rows(even, odd, row_count, col_count, put):
    sub = sub_index((SUB, LANES))

    def block(i, j):
        start = 16 * (i * col_count + j)
        return [even[start : start + 8], even[start + 8 : start + 16],
                odd[start : start + 8], odd[start + 8 : start + 16]]

    for i in range(row_count):
        for j in range(col_count):
            outer = jnp.zeros((SUB, LANES), jnp.float32)
            if j == 0 and i < row_count - 1:
                rows = block(i + 1, 0)
                outer = jnp.where(sub == 0, rows[0], jnp.where(sub == 1, roll(rows[2], 1, 0), outer))
            if j == col_count - 1 and i > 0:
                rows = block(i - 1, j)
                outer = jnp.where(sub == 7, rows[1], jnp.where(sub == 6, roll(rows[3], -1, 0), outer))
            put(i, j, block(i, j) + [outer])


def two_terms(value):
    high = value.astype(jnp.bfloat16)
    return high, (value - high.astype(jnp.float32)).astype(jnp.bfloat16)


def dot(left, right, dims=((1,), (0,))):
    return lax.dot_general(left, right, (dims, ((), ())), preferred_element_type=jnp.float32)


def even_positions(row_count, col_count):
    j, c, e = np.meshgrid(np.arange(col_count), np.arange(4), np.arange(EC), indexing="ij")
    columns = (LANES * j + PITCH * e + 2 * c).reshape(-1)
    i, j, b, h, t = np.meshgrid(
        np.arange(row_count), np.arange(col_count), np.arange(2), np.arange(2), np.arange(TILES),
        indexing="ij",
    )
    rows = (ER * PITCH * i + SUB * PITCH * t + PITCH * j + 2 * h + 4 * b).reshape(-1)
    return columns, rows


def angle_pair(left, right, length):
    angles = 2.0 * np.pi * (np.asarray(left)[:, None] * np.asarray(right)[None, :] % length) / length
    return np.asarray(np.cos(angles), np.float32), np.asarray(np.sin(angles), np.float32)


def position_bases(positions, length):
    orders = np.arange(length // 4)
    grouped = positions.reshape(-1, SUB)
    offsets = grouped[0] - grouped[0, 0]
    assert (grouped == grouped[:, :1] + offsets[None, :]).all()
    return np.concatenate(
        [
            *angle_pair(grouped[:, 0], orders, length),
            *angle_pair(offsets, orders, length),
            *angle_pair(offsets + 1, orders, length),
        ]
    )


def split_rows(ref, *counts):
    start, parts = 0, []
    for count in counts:
        parts.append(ref.at[start : start + count])
        start += count
    return parts


def order_bases(positions, length):
    bases = np.arange(0, length // 4, SUB)
    result = []
    for parity in range(2):
        result.extend(angle_pair(bases, positions + parity, length))
        result.extend(angle_pair(np.arange(SUB), positions + parity, length))
    return np.concatenate(result)


def fill_by_position(sign_of, bases, out_refs):
    base_cos, base_sin, even_cos, even_sin, odd_cos, odd_sin = bases
    ec, es, oc, os = (ref[...] for ref in (even_cos, even_sin, odd_cos, odd_sin))
    start = lane_index(ec.shape) == 0

    def pair(i, carry):
        parts = [[], [], []]
        for h in range(2):
            row = 2 * i + h
            bc, bs = base_cos[pl.ds(row, 1), :], base_sin[pl.ds(row, 1), :]
            parts[0].append(bc * ec - bs * es)
            parts[1].append(jnp.where(start, 1.0, -(bs * ec + bc * es)) * sign_of(row))
            parts[2].append(bc * oc - bs * os)
        rows = pl.ds(pl.multiple_of(16 * i, 16), 16)
        for ref, part in zip(out_refs, parts):
            ref[rows, :] = jnp.concatenate(part, axis=0).astype(ref.dtype)
        return carry

    lax.fori_loop(0, base_cos.shape[0] // 2, pair, 0)


def column_table_kernel(bases_ref, *outs):
    count = (bases_ref.shape[0] - 4 * SUB) // 2
    bases = split_rows(bases_ref, count, count, SUB, SUB, SUB, SUB)
    fill_by_position(lambda row: (1 - 2 * ((row // 2) & 1)).astype(jnp.float32), bases, outs)


def row_table_kernel(green_ref, position_ref, order_ref, *outs):
    count = (position_ref.shape[0] - 4 * SUB) // 2
    position = split_rows(position_ref, count, count, SUB, SUB, SUB, SUB)
    order = split_rows(order_ref, count, count, SUB, SUB, count, count, SUB, SUB)
    quarter = position[0].shape[1]
    tiles = quarter // LANES
    sub = sub_index((SUB, quarter))
    flip = jnp.where(sub < 4, 1.0, -1.0)
    fill_by_position(lambda row: flip, position, outs[3:6])
    ebc, ebs, ec, es, obc, obs, oc, os = order
    ec, es, oc, os = (ref[...] for ref in (ec, es, oc, os))
    lanes = jnp.where((lane_index((SUB, quarter)) & 4) == 0, 1.0, -1.0)

    def pair(i, carry):
        parts = [[], [], []]
        for h in range(2):
            row = 2 * i + h
            one = (pl.ds(row, 1), slice(None))
            bc, bs = ebc[one], ebs[one]
            parts[0].append(bc * ec - bs * es)
            first = (sub + row) == 0
            parts[1].append(jnp.where(first, 1.0, -(bs * ec + bc * es)) * lanes)
            parts[2].append(obc[one] * oc - obs[one] * os)
        rows = pl.ds(pl.multiple_of(16 * i, 16), 16)
        for ref, part in zip(outs[:3], parts):
            ref[rows, :] = jnp.concatenate(part, axis=0).astype(ref.dtype)
        return carry

    lax.fori_loop(0, ebc.shape[0] // 2, pair, 0)

    depth = green_ref.shape[0]
    device = lax.axis_index("row") * lax.axis_size("col") + lax.axis_index("col")
    number = sub_index((depth, LANES)) + device * depth
    length = 4 * quarter
    weight = jnp.where(number % quarter == 0, 1.0, 2.0) * (1.0 / (length * length))
    lane = lane_index((depth, LANES))

    def scaled(tile):
        value = green_ref[:, LANES * tile : LANES * (tile + 1)] * weight
        if tile % tiles == 0:
            value = value * jnp.where(lane == 0, 1.0, 2.0)
        else:
            value = value * 2.0
        return jnp.concatenate([value, value], axis=0)

    for t in range(tiles):
        cos_plus, cos_minus = scaled(t), scaled(2 * tiles + t)
        sin_minus, sin_plus = scaled(tiles + t), scaled(3 * tiles + t)
        first = slice(LANES * t, LANES * (t + 1))
        second = slice(quarter + LANES * t, quarter + LANES * (t + 1))
        outs[6][first, :] = (cos_plus + cos_minus).T
        outs[7][first, :] = (cos_plus - cos_minus).T
        outs[6][second, :] = (sin_plus + sin_minus).T
        outs[7][second, :] = (sin_plus - sin_minus).T


def tiled_shifts(shifts_ref, which):
    rows = [shifts_ref[which : which + 1, LANES * t : LANES * (t + 1)] for t in range(TILES)]
    return jnp.concatenate(rows * RHS, axis=0)


def charge_kernel(
    currents_ref, projection_ref, shifts_ref, out_ref, weights, raw, shifts, current, half, stencil, sems
):
    copies = [
        pltpu.make_async_copy(currents_ref, raw, sems.at[STEN]),
        pltpu.make_async_copy(shifts_ref, shifts, sems.at[STEN + 1]),
    ]

    def weight_copy(step):
        rows = pl.ds(step * STEN, STEN)
        return pltpu.make_async_copy(projection_ref.at[rows], weights.at[rows], sems.at[step])

    copies[0].start()
    for step in range(STEN):
        weight_copy(step).start()
    copies[1].start()
    copies[0].wait()
    half[...] = raw[...].astype(jnp.bfloat16)
    current[...] = half[...].astype(jnp.float32)
    groups = lane_index((SUB, SUB * BASIS)) // BASIS
    adder = jnp.where(groups == sub_index(groups.shape), 1.0, 0.0).astype(jnp.bfloat16)

    def one_row(step, carry):
        weight_copy(step).wait()
        for s in range(0, STEN, 2):
            columns = []
            for h in range(2):
                weight = weights[step * STEN + s + h]
                products = [weight * half[q] for q in range(RHS)]
                columns.append(
                    jnp.concatenate(
                        [
                            products[q][:, LANES * t : LANES * (t + 1)]
                            for q in range(RHS)
                            for t in range(TILES)
                        ],
                        axis=0,
                    )
                )
            sums = dot(adder, jnp.concatenate(columns, axis=1))
            stencil[step * STEN + s] = sums[:, :LANES]
            stencil[step * STEN + s + 1] = sums[:, LANES:]
        return carry

    lax.fori_loop(0, STEN, one_row, 0)
    copies[1].wait()
    chunks = place_charges(
        lambda s: stencil[s], tiled_shifts(shifts, 0), tiled_shifts(shifts, 1)
    )
    to_next, to_previous, to_rows = pack_currents(
        lambda q, t: current[q, :, LANES * t : LANES * (t + 1)]
    )
    mine = lax.axis_index("col")
    block = lane_index((SUB, LANES)) // EC
    middle = ((block & 3) == 1) | ((block & 3) == 2)
    for e in range(SUB):
        after = (mine == e - 1).astype(jnp.float32)
        before = (mine == e + 1).astype(jnp.float32)
        edge = jnp.where(middle, to_rows[e], chunks[e][GROUPS])
        rows = chunks[e][:GROUPS] + [edge, to_next * after + to_previous * before]
        out_ref[e] = jnp.concatenate(rows, axis=0).astype(out_ref.dtype)


def pack_currents(tile):
    half = BASIS // 2
    lane = lane_index((half, LANES))
    elem_col = lane & (EC - 1)
    to_next = jnp.zeros((half, LANES), jnp.float32)
    to_previous = jnp.zeros((half, LANES), jnp.float32)
    for q in range(RHS):
        for t in range(TILES):
            value = tile(q, t)
            for h in range(2):
                place = q * TILES + t + SUB * h
                part = value[half * h : half * (h + 1)]
                here = elem_col == place
                to_next = jnp.where(here, roll(part, place - (EC - 1), 1), to_next)
                to_previous = jnp.where(here, roll(part, place, 1), to_previous)
    lane = lane_index((SUB, LANES))
    to_rows = []
    for e in range(SUB):
        rows = jnp.zeros((SUB, LANES), jnp.float32)
        for q in range(RHS):
            span = slice(SUB * e, SUB * (e + 1))
            last = roll(tile(q, TILES - 1)[span], EC + EC * q - (LANES - EC), 1)
            first = roll(tile(q, 0)[span], 64 + EC + EC * q, 1)
            rows = jnp.where(lane // EC == 1 + q, last, jnp.where(lane // EC == 5 + q, first, rows))
        to_rows.append(rows)
    return to_next, to_previous, to_rows


def forward_rows(edge_row, j, count, which):
    lane = lane_index((SUB, LANES))
    start = EC + 64 * which
    value = roll(edge_row(j), -start, 1)
    for q in range(RHS):
        place = 2 * EC + 2 * q
        if j > 0:
            corner = roll(edge_row(j - 1), place - start - EC * q - (EC - 1), 1)
            value = jnp.where(lane == place, corner, value)
        if j < count - 1:
            corner = roll(edge_row(j + 1), place + 1 - start - EC * q, 1)
            value = jnp.where(lane == place + 1, corner, value)
    return jnp.where(lane < 64, roll(value, 2, 0), roll(roll(value, 64, 1), -2, 0))


def column_sign(shape):
    return jnp.where((lane_index(shape) & EC) == 0, 1.0, -1.0)


def column_kernel(count, rows_ref, even_cos, even_sin, odd_cos, out_ref):
    def part(j, r):
        return rows_ref[j, 8 * r : 8 * r + 8, :].astype(jnp.float32)

    even, odd = gather_rows(part, lambda j: part(j, GROUPS), count)
    both = jnp.concatenate([odd, odd * column_sign(odd.shape)], axis=0).astype(jnp.bfloat16)
    even = even.astype(jnp.bfloat16)
    ec, es = dot(even, even_cos[...]), dot(even, even_sin[...])
    both = dot(both, odd_cos[...])
    oc, os = both[: odd.shape[0]], both[odd.shape[0] :]
    half = out_ref.shape[1]
    mine = lax.axis_index("row")
    ends = [
        [forward_rows(lambda k: part(k, GROUPS), j, count, which) for which in range(2)]
        for j in range(count)
    ]
    sub = sub_index((SUB, LANES))
    middle = (sub >= 2) & (sub < 6)
    device = 0
    for block in (ec + oc, es - os, ec - oc, es + os):
        for t in range(0, block.shape[1], LANES):
            for chunk in halves(block[:half, t : t + LANES], block[half:, t : t + LANES]):
                i, j = device // count, device % count
                below = (mine == i - 1).astype(jnp.float32)
                above = (mine == i + 1).astype(jnp.float32)
                tail = jnp.where(
                    middle, ends[j][0] * below + ends[j][1] * above, chunk[half - SUB :]
                )
                chunk = jnp.concatenate([chunk[: half - SUB], tail], axis=0)
                out_ref[device] = chunk.astype(out_ref.dtype)
                device += 1


def row_kernel(row_count, col_count, *refs):
    sources, out_ref, held, sems = refs[:9], refs[9], refs[10:19], refs[19]
    loads = [
        pltpu.make_async_copy(source, target, sems.at[n])
        for n, (source, target) in enumerate(zip(sources, held))
    ]
    for load in loads:
        load.start()
    in_ref, even_cos, even_sin, odd_cos, back_cos, back_sin, back_odd, sum_ref, diff_ref = held
    loads[0].wait()
    even, odd = add_outer_rows(
        lambda i, j: in_ref[i * col_count + j].astype(jnp.float32), row_count, col_count
    )
    flip = jnp.where((sub_index(odd.shape) & 4) == 0, 1.0, -1.0)
    both = jnp.concatenate([odd, odd * flip], axis=1).astype(jnp.bfloat16)
    even = even.astype(jnp.bfloat16)
    for n in range(1, 4):
        loads[n].wait()
    a = [dot(even_cos[...], even), dot(even_sin[...], even)]
    both = dot(odd_cos[...], both)
    b = [both[:, :LANES], both[:, LANES:]]
    quarter = odd.shape[0]
    for n in range(4, 9):
        loads[n].wait()

    def pieces(left, right):
        for k in range(2):
            span = slice(quarter * k, quarter * (k + 1))
            yield two_terms(left[k] * sum_ref[span, :] + right[k] * diff_ref[span, :])

    def fold(value):
        return value[:, :LANES] + value[:, LANES:]

    (ch, cl), (sh, sl) = pieces(a, b)
    even = fold(
        dot(back_cos[...], jnp.concatenate([ch, cl], axis=1))
        + dot(back_sin[...], jnp.concatenate([sh, sl], axis=1))
    )
    (ch, cl), (sh, sl) = pieces(b, a)
    both = dot(back_odd[...], jnp.concatenate([ch, cl, sh, sl], axis=1))
    odd = fold(both[:, : 2 * LANES]) + fold(both[:, 2 * LANES :]) * flip

    def put(i, j, parts):
        out_ref[i * col_count + j] = jnp.concatenate(parts, axis=0).astype(out_ref.dtype)

    spread_outer_rows(even, odd, row_count, col_count, put)


def grid_kernel(count, in_ref, even_cos, even_sin, odd_cos, out_ref):
    devices = in_ref.shape[0]
    first, second = [], []
    for d in range(0, devices, 2):
        low, high = halves(in_ref[d].astype(jnp.float32), in_ref[d + 1].astype(jnp.float32))
        first.append(low)
        second.append(high)
    per_block = devices // 8
    blocks = []
    for k in range(4):
        span = slice(per_block * k, per_block * (k + 1))
        blocks.append(
            jnp.concatenate(
                [jnp.concatenate(first[span], axis=1), jnp.concatenate(second[span], axis=1)], axis=0
            )
        )
    cos_plus, sin_minus, cos_minus, sin_plus = blocks
    half = cos_plus.shape[0]

    def back(values, table):
        terms = [term for value in values for term in two_terms(value)]
        result = dot(jnp.concatenate(terms, axis=0), table[...], ((1,), (1,)))
        return [
            result[2 * half * i : 2 * half * i + half] + result[2 * half * i + half : 2 * half * (i + 1)]
            for i in range(len(values))
        ]

    even = back([cos_plus + cos_minus], even_cos)[0] + back([sin_plus + sin_minus], even_sin)[0]
    odd, turned = back([cos_plus - cos_minus, sin_plus - sin_minus], odd_cos)
    odd = odd + turned * column_sign(odd.shape)

    def put(j, parts):
        out_ref[j] = jnp.concatenate(parts, axis=0).astype(out_ref.dtype)

    scatter_rows(even, odd, count, put)


def far_kernel(
    source_ref, projection_ref, shifts_ref, near_ref, out_ref, grid_ref, weights, samples, shifts, totals_ref, sems
):
    depth = 16
    count = BASIS // depth

    def load(i):
        rows = pl.ds(i * depth, depth)
        return pltpu.make_async_copy(
            projection_ref.at[:, rows], weights.at[:, rows], sems.at[1 + count + i]
        )

    load_shifts = pltpu.make_async_copy(shifts_ref, shifts, sems.at[0])
    load_grid = pltpu.make_async_copy(source_ref, grid_ref, sems.at[1 + 2 * count])
    load_near = pltpu.make_async_copy(near_ref, totals_ref, sems.at[2 + 2 * count])
    load_grid.start()
    load_shifts.start()
    load_near.start()
    for i in range(count):
        load(i).start()

    def part(e, r):
        return grid_ref[e, 8 * r : 8 * r + 8, :].astype(jnp.float32)

    def put(s, value):
        samples[s] = value

    load_shifts.wait()
    load_grid.wait()
    read_samples(
        part, lambda e: part(e, GROUPS), tiled_shifts(shifts, 0), tiled_shifts(shifts, 1), put
    )
    load_near.wait()

    def store(i):
        rows = pl.ds(i * depth, depth)
        return pltpu.make_async_copy(totals_ref.at[:, rows], out_ref.at[:, rows], sems.at[1 + i])

    for i in range(count):
        span = slice(i * depth, (i + 1) * depth)
        load(i).wait()

        def add_row(a, totals):
            totals = list(totals)
            for b in range(STEN):
                s = a * STEN + b
                for t in range(TILES):
                    weight = weights[s, span, LANES * t : LANES * (t + 1)].astype(jnp.float32)
                    for q in range(RHS):
                        index = q * TILES + t
                        totals[index] = totals[index] + weight * samples[s, index : index + 1, :]
            return tuple(totals)

        start = tuple(
            totals_ref[q, span, LANES * t : LANES * (t + 1)] for q in range(RHS) for t in range(TILES)
        )
        totals = lax.fori_loop(0, STEN, add_row, start)
        for q in range(RHS):
            for t in range(TILES):
                totals_ref[q, span, LANES * t : LANES * (t + 1)] = totals[q * TILES + t]
        store(i).start()
    for i in range(count):
        store(i).wait()


def pick_kernel(currents_ref, slab_ref, arrived_ref, partners_ref, out_ref):
    lane = lane_index((BASIS, LANES))
    elem_col = lane & (EC - 1)
    row, col = lax.axis_index("row"), lax.axis_index("col")
    col_count = lax.axis_size("col")
    devices = arrived_ref.shape[0]

    def column_edge(source):
        source = jnp.clip(source, 0, col_count - 1)
        return slab_ref[source, 80:112, :].astype(jnp.float32)

    from_left, from_right = column_edge(col - 1), column_edge(col + 1)

    def beside(edge, q, t, end):
        place = q * TILES + t
        return jnp.concatenate([roll(edge, end - place, 1), roll(edge, end - place - SUB, 1)], axis=0)

    def three(own, left, right):
        return (
            jnp.where(elem_col == 0, left, roll(own, 1, 1)),
            own,
            jnp.where(elem_col == EC - 1, right, roll(own, -1, 1)),
        )

    sub = sub_index((SUB, LANES))

    def outer_row(source):
        parts = []
        for j in range(col_count):
            index = jnp.clip(source * col_count + j, 0, devices - 1)
            value = arrived_ref[index, 32:40, :].astype(jnp.float32)
            parts.append(jnp.where(sub < 4, roll(value, -2, 0), roll(roll(value, 2, 0), -64, 1)))
        return jnp.concatenate(parts, axis=0)

    rows = outer_row(row - 1), outer_row(row + 1)

    def outer_three(value, q, start):
        own = roll(value, start - EC * q, 1)
        left = roll(value, start - 2 * EC - 2 * q, 1)
        right = roll(value, start + EC - 1 - 2 * EC - 2 * q - 1, 1)
        return three(own, left, right)

    for q in range(RHS):
        tiles = []
        for t in range(TILES):
            own = currents_ref[q, :, LANES * t : LANES * (t + 1)]
            own = own.astype(jnp.bfloat16).astype(jnp.float32)
            tiles.append(three(own, beside(from_left, q, t, 0), beside(from_right, q, t, EC - 1)))
        above = outer_three(rows[0], q, 0)
        below = outer_three(rows[1], q, LANES - EC)
        for t in range(TILES):
            lanes = slice(LANES * t, LANES * (t + 1))
            codes = [partners_ref[k : k + 1, lanes] for k in range(1, NEIGH)]
            chosen = [tiles[t][1]] * (NEIGH - 1)
            for c in range(3):
                here = tiles[t][c]
                before = roll(tiles[t - 1][c], EC, 1) if t else above[c]
                after = roll(tiles[t + 1][c], -EC, 1) if t < TILES - 1 else below[c]
                views = (
                    jnp.where(lane < EC, before, roll(here, EC, 1)),
                    here,
                    jnp.where(lane >= LANES - EC, after, roll(here, -EC, 1)),
                )
                for r in range(3):
                    if r == 1 and c == 1:
                        continue
                    for k in range(NEIGH - 1):
                        chosen[k] = jnp.where(codes[k] == 3 * r + c, views[r], chosen[k])
            for k in range(NEIGH - 1):
                out_ref[k, q, :, lanes] = chosen[k].astype(out_ref.dtype)


def near_kernel(has_total, slots, start, stop, *refs):
    values_ref, refs = refs[0], refs[1:]
    total_ref = None
    if has_total:
        total_ref, refs = refs[0], refs[1:]
    blocks_ref, out_ref, blocks, picked, sems = refs
    chunks = (stop - start) // SUB

    def load(chunk, k):
        rows = pl.ds(start + chunk * SUB, SUB)
        return pltpu.make_async_copy(
            blocks_ref.at[slots[k], rows], blocks.at[chunk, k], sems.at[chunk, k]
        )

    for chunk in range(chunks):
        for k in range(len(slots)):
            load(chunk, k).start()
    picked[...] = values_ref[...].astype(jnp.bfloat16).astype(jnp.float32).reshape(picked.shape)
    if has_total:
        out_ref[...] = total_ref[...]

    def one_chunk(chunk, carry):
        for k in range(len(slots)):
            load(chunk, k).wait()
        rows = pl.ds(pl.multiple_of(start + chunk * SUB, SUB), SUB)
        for t in range(TILES):
            lanes = slice(t * LANES, (t + 1) * LANES)
            totals = [[None] * RHS for _ in range(SUB)]
            for k in range(len(slots)):
                for b in range(0, BASIS, 16):
                    values = [
                        [picked[k, q, b + 8 * h : b + 8 * h + 8, lanes] for h in range(2)]
                        for q in range(RHS)
                    ]
                    for a in range(SUB):
                        weight = blocks[chunk, k, a, b : b + 16, lanes].astype(jnp.float32)
                        for q in range(RHS):
                            term = weight[:8] * values[q][0] + weight[8:] * values[q][1]
                            totals[a][q] = term if totals[a][q] is None else totals[a][q] + term
            for q in range(RHS):
                value = sum_rows([totals[a][q] for a in range(SUB)])
                if has_total:
                    value = value + total_ref[q, rows, lanes]
                out_ref[q, rows, lanes] = value
        return carry

    lax.fori_loop(0, chunks, one_chunk, 0)


def near_call(values, total, near_blocks, slots, start, stop):
    elements = near_blocks.shape[3]
    chunks = (stop - start) // SUB
    return pl.pallas_call(
        functools.partial(near_kernel, total is not None, slots, start, stop),
        in_specs=[ON_CHIP] * (1 if total is None else 2) + [IN_PLACE],
        out_specs=ON_CHIP,
        out_shape=jax.ShapeDtypeStruct((RHS, BASIS, elements), jnp.float32),
        scratch_shapes=[
            pltpu.VMEM((chunks, len(slots), SUB, BASIS, elements), jnp.bfloat16),
            pltpu.VMEM((len(slots), RHS, BASIS, elements), jnp.float32),
            pltpu.SemaphoreType.DMA((chunks, len(slots))),
        ],
        compiler_params=NEAR_PARAMS,
        name="near",
    )(*([values] if total is None else [values, total]), near_blocks)


ON_CHIP = pl.BlockSpec(memory_space=pltpu.VMEM)
IN_PLACE = pl.BlockSpec(memory_space=pltpu.HBM)
PARAMS = pltpu.CompilerParams(vmem_limit_bytes=48 << 20)
CHARGE_PARAMS = pltpu.CompilerParams(vmem_limit_bytes=60 << 20)
FULL_PARAMS = pltpu.CompilerParams(vmem_limit_bytes=53 << 20)
NEAR_PARAMS = pltpu.CompilerParams(vmem_limit_bytes=48 << 20)


def whole(shape):
    return pl.BlockSpec(shape, lambda *_: (0,) * len(shape))


def shards_real(currents, projection, near_blocks, partners, shifts, green):
    row_count = lax.axis_size("row")
    col_count = lax.axis_size("col")
    elements = currents.shape[2]
    width = col_count * LANES
    length = 2 * width
    quarter = length // 4
    f32, b16 = jnp.float32, jnp.bfloat16
    struct = jax.ShapeDtypeStruct
    devices = row_count * col_count

    charges = pl.pallas_call(
        charge_kernel,
        in_specs=[IN_PLACE] * 3,
        out_specs=ON_CHIP,
        out_shape=struct((SUB, 112, LANES), b16),
        scratch_shapes=[
            pltpu.VMEM(projection.shape, b16),
            pltpu.VMEM((RHS, BASIS, elements), f32),
            pltpu.VMEM((2, elements), jnp.int32),
            pltpu.VMEM((RHS, BASIS, elements), f32),
            pltpu.VMEM((RHS, BASIS, elements), b16),
            pltpu.VMEM((STEN * STEN, SUB, LANES), f32),
            pltpu.SemaphoreType.DMA((STEN + 2,)),
        ],
        compiler_params=CHARGE_PARAMS,
        name="charges",
    )(currents, projection, shifts)
    slab = lax.all_to_all(charges, "col", 0, 0, tiled=True)

    columns, rows = even_positions(row_count, col_count)
    table = struct((quarter, quarter), b16)
    col_tables = pl.pallas_call(
        column_table_kernel,
        out_specs=[ON_CHIP] * 3,
        out_shape=[table] * 3,
        compiler_params=PARAMS,
        name="column_tables",
    )(jnp.asarray(position_bases(columns, length)))
    spectrum = pl.pallas_call(
        functools.partial(column_kernel, col_count),
        out_shape=struct((devices, 40, LANES), b16),
        in_specs=[ON_CHIP] * 4,
        out_specs=ON_CHIP,
        compiler_params=PARAMS,
        name="columns",
    )(slab, *col_tables)
    spectrum, held, held_green = lax.optimization_barrier((spectrum, currents, green))
    arrived = lax.all_to_all(spectrum, ("row", "col"), 0, 0, tiled=True)
    near = near_call(held, None, near_blocks, (0,), 0, BASIS)
    spread = struct((2 * quarter, LANES), f32)
    row_tables = pl.pallas_call(
        row_table_kernel,
        out_shape=[table] * 6 + [spread] * 2,
        compiler_params=FULL_PARAMS,
        name="row_tables",
    )(held_green, jnp.asarray(position_bases(rows, length)), jnp.asarray(order_bases(rows, length)))
    arrived, near, *row_tables = lax.optimization_barrier((arrived, near, *row_tables))
    rows_back = pl.pallas_call(
        functools.partial(row_kernel, row_count, col_count),
        out_shape=struct((devices, 40, LANES), b16),
        in_specs=[ON_CHIP] + [IN_PLACE] * 8,
        out_specs=ON_CHIP,
        scratch_shapes=[pltpu.VMEM((devices, 40, LANES), b16)]
        + [pltpu.VMEM((quarter, quarter), b16)] * 6
        + [pltpu.VMEM((2 * quarter, LANES), f32)] * 2
        + [pltpu.SemaphoreType.DMA((9,))],
        compiler_params=FULL_PARAMS,
        name="rows",
    )(arrived, *row_tables)
    rows_back, ready = lax.optimization_barrier((rows_back, arrived))
    returned = lax.all_to_all(rows_back, ("row", "col"), 0, 0, tiled=True)
    picked = pl.pallas_call(
        pick_kernel,
        in_specs=[whole(currents.shape), ON_CHIP, ON_CHIP, whole(partners.shape)],
        out_specs=ON_CHIP,
        out_shape=struct((NEIGH - 1, RHS, BASIS, elements), b16),
        compiler_params=PARAMS,
        name="pick",
    )(held, slab, ready, partners)
    others = tuple(range(1, NEIGH))
    near = near_call(picked, near, near_blocks, others, 0, BASIS // 2)
    returned, near, picked = lax.optimization_barrier((returned, near, picked))
    potential = pl.pallas_call(
        functools.partial(grid_kernel, col_count),
        out_shape=struct((SUB, 80, LANES), b16),
        in_specs=[ON_CHIP] * 4,
        out_specs=ON_CHIP,
        compiler_params=PARAMS,
        name="grid",
    )(returned, *col_tables)
    potential, near, picked = lax.optimization_barrier((potential, near, picked))
    pieces = lax.all_to_all(potential, "col", 0, 0, tiled=True)
    near = near_call(picked, near, near_blocks, others, BASIS // 2, BASIS)

    return pl.pallas_call(
        far_kernel,
        in_specs=[ON_CHIP, IN_PLACE, IN_PLACE, ON_CHIP],
        out_specs=IN_PLACE,
        out_shape=struct((RHS, BASIS, elements), f32),
        scratch_shapes=[
            pltpu.VMEM((SUB, 80, LANES), b16),
            pltpu.VMEM(projection.shape, b16),
            pltpu.VMEM((STEN * STEN, SUB, LANES), f32),
            pltpu.VMEM((2, elements), jnp.int32),
            pltpu.VMEM((RHS, BASIS, elements), f32),
            pltpu.SemaphoreType.DMA((11,)),
        ],
        compiler_params=FULL_PARAMS,
        name="far",
    )(pieces, projection, shifts, near)


def shards(currents, projection, near_blocks, partners, shifts, green):
    row_count = lax.axis_size("row")
    col_count = lax.axis_size("col")
    fits = col_count == SUB and green.shape[0] == 64 and 2 * row_count * col_count == green.shape[0]
    if fits and currents.shape[2] == TILES * LANES and row_count * ER == col_count * EC:
        return shards_real(currents, projection, near_blocks, partners, shifts, green)
    return shards_general(currents, projection, near_blocks, partners, shifts, green)


def solution(mesh):
    in_specs = (
        P(None, None, ("row", "col")),
        P(None, None, ("row", "col")),
        P(None, None, None, ("row", "col")),
        P(None, ("row", "col")),
        P(None, ("row", "col")),
        P(("row", "col"), None),
    )
    out_specs = P(None, None, ("row", "col"))
    return jax.shard_map(shards, mesh=mesh, in_specs=in_specs, out_specs=out_specs, check_vma=False)
```

```python
import functools
import math

import jax
import jax.numpy as jnp
import numpy as np
from jax import lax
from jax.experimental import pallas as pl
from jax.experimental.pallas import tpu as pltpu
from jax.sharding import PartitionSpec as P

BASIS = 64
STEN = 8
PITCH = 8
HALO = 2
NEIGH = 4
RHS = 2
ER = 32
EC = 16


def extended_2(block, sides, width):
    for axis, dim in sides:
        count = lax.axis_size(axis)
        forward = [(i, i + 1) for i in range(count - 1)]
        backward = [(target, source) for source, target in forward]
        low = lax.ppermute(
            lax.slice_in_dim(block, block.shape[dim] - width, None, axis=dim), axis, forward
        )
        high = lax.ppermute(lax.slice_in_dim(block, 0, width, axis=dim), axis, backward)
        block = jnp.concatenate([low, block, high], axis=dim)
    return block


def angle_table(first_size, second_size, modulus, direction):
    left_index = jnp.arange(first_size, dtype=jnp.int32)
    right_index = jnp.arange(second_size, dtype=jnp.int32)
    turn_count = left_index[:, None] * right_index[None, :] % modulus
    angles = turn_count.astype(jnp.float32) * (2.0 * math.pi / modulus)
    return (jnp.cos(angles), direction * jnp.sin(angles))


def complex_apply(real_part, imag_part, cosine, sine_table, pattern):
    highest = lax.Precision.HIGHEST
    out_real = jnp.einsum(pattern, real_part, cosine, precision=highest)
    out_imag = jnp.einsum(pattern, real_part, sine_table, precision=highest)
    if imag_part is not None:
        out_real = out_real - jnp.einsum(pattern, imag_part, sine_table, precision=highest)
        out_imag = out_imag + jnp.einsum(pattern, imag_part, cosine, precision=highest)
    return (out_real, out_imag)


def transform_last(real_part, imag_part, length, count_in, count_out, direction):
    leading = real_part.shape[:-1]
    inner_size = 128
    outer_size = length // inner_size
    rows_in = count_in // inner_size
    kept_count = count_out // outer_size
    shaped_real = real_part.reshape(leading + (rows_in, inner_size))
    shaped_imag = None
    if imag_part is not None:
        shaped_imag = imag_part.reshape(leading + (rows_in, inner_size))
    cosine, sine_table = angle_table(rows_in, outer_size, outer_size, direction)
    first_real, first_imag = complex_apply(
        shaped_real, shaped_imag, cosine, sine_table, "...ab,ak->...kb"
    )
    twist_cos, twist_sin = angle_table(outer_size, inner_size, length, direction)
    turned_real = first_real * twist_cos - first_imag * twist_sin
    turned_imag = first_real * twist_sin + first_imag * twist_cos
    cosine, sine_table = angle_table(inner_size, kept_count, inner_size, direction)
    last_real, last_imag = complex_apply(
        turned_real, turned_imag, cosine, sine_table, "...kb,bj->...jk"
    )
    out_shape = leading + (kept_count * outer_size,)
    return (last_real.reshape(out_shape), last_imag.reshape(out_shape))


def place_shifted(blocks, amount, dim_index):
    new_shape = list(blocks.shape)
    new_shape[dim_index] = new_shape[dim_index] + 2 * HALO
    result = jnp.zeros(tuple(new_shape), blocks.dtype)
    for offset in range(-HALO, HALO + 1):
        widths = [(0, 0)] * blocks.ndim
        widths[dim_index] = (HALO + offset, HALO - offset)
        result = jnp.where(amount == offset, jnp.pad(blocks, widths), result)
    return result


def pick_shifted(windows, amount, dim_index):
    new_shape = list(windows.shape)
    new_shape[dim_index] = STEN
    result = jnp.zeros(tuple(new_shape), windows.dtype)
    for offset in range(-HALO, HALO + 1):
        piece = lax.slice_in_dim(windows, HALO + offset, HALO + offset + STEN, axis=dim_index)
        result = jnp.where(amount == offset, piece, result)
    return result


def intersection_add(framed, dim_index):
    element_count = framed.shape[dim_index]
    window_size = framed.shape[dim_index + 1]
    head_part = lax.slice_in_dim(framed, 0, PITCH, axis=dim_index + 1)
    tail_part = lax.slice_in_dim(framed, PITCH, window_size, axis=dim_index + 1)
    widths = [(0, 0)] * framed.ndim
    widths[dim_index + 1] = (0, 2 * PITCH - window_size)
    tail_part = jnp.pad(tail_part, widths)
    merged = framed.shape[:dim_index] + (element_count * PITCH,) + framed.shape[dim_index + 2 :]
    head_part = head_part.reshape(merged)
    tail_part = tail_part.reshape(merged)
    front_pad = [(0, 0)] * len(merged)
    front_pad[dim_index] = (0, PITCH)
    back_pad = [(0, 0)] * len(merged)
    back_pad[dim_index] = (PITCH, 0)
    summed = jnp.pad(head_part, front_pad) + jnp.pad(tail_part, back_pad)
    return lax.slice_in_dim(summed, 0, element_count * PITCH + 2 * HALO, axis=dim_index)


def cut_windows(field, dim_index):
    element_count = (field.shape[dim_index] - 2 * HALO) // PITCH
    widths = [(0, 0)] * field.ndim
    widths[dim_index] = (0, PITCH - 2 * HALO)
    extended = jnp.pad(field, widths)
    split_shape = field.shape[:dim_index] + (element_count, PITCH) + field.shape[dim_index + 1 :]
    head_part = lax.slice_in_dim(extended, 0, element_count * PITCH, axis=dim_index).reshape(
        split_shape
    )
    tail_part = lax.slice_in_dim(
        extended, PITCH, PITCH + element_count * PITCH, axis=dim_index
    ).reshape(split_shape)
    tail_part = lax.slice_in_dim(tail_part, 0, 2 * HALO, axis=dim_index + 1)
    return jnp.concatenate([head_part, tail_part], axis=dim_index + 1)


def fold_margin(padded, dim_index):
    full_size = padded.shape[dim_index]
    inner_size = full_size - 4 * HALO
    core_part = lax.slice_in_dim(padded, 2 * HALO, 2 * HALO + inner_size, axis=dim_index)
    upper_part = lax.slice_in_dim(padded, 0, HALO, axis=dim_index)
    lower_part = lax.slice_in_dim(padded, full_size - HALO, full_size, axis=dim_index)
    upper_pad = [(0, 0)] * padded.ndim
    upper_pad[dim_index] = (0, inner_size - HALO)
    lower_pad = [(0, 0)] * padded.ndim
    lower_pad[dim_index] = (inner_size - HALO, 0)
    return core_part + jnp.pad(upper_part, upper_pad) + jnp.pad(lower_part, lower_pad)


def shards_general(currents, projection, near_blocks, partners, shifts, green):
    row_count = lax.axis_size("row")
    col_count = lax.axis_size("col")
    device_count = row_count * col_count
    elements = ER * EC
    cur_half = currents.astype(jnp.bfloat16)
    spread = extended_2(cur_half.reshape(RHS, BASIS, ER, EC), (("row", 2), ("col", 3)), 1)
    views = []
    for symbol in range(9):
        row_start = symbol // 3
        col_start = symbol % 3
        views.append(
            spread[:, :, row_start : row_start + ER, col_start : col_start + EC].reshape(
                RHS, BASIS, elements
            )
        )
    picked = []
    for neighbour_slot in range(NEIGH):
        chosen = jnp.zeros((RHS, BASIS, elements), jnp.bfloat16)
        for symbol in range(9):
            chosen = jnp.where(partners[neighbour_slot] == symbol, views[symbol], chosen)
        picked.append(chosen)
    near_term = jnp.einsum(
        "kabn,kqbn->qan", near_blocks, jnp.stack(picked), preferred_element_type=jnp.float32
    )
    stencil = jnp.einsum("sbn,qbn->qsn", projection, cur_half, preferred_element_type=jnp.float32)
    blocks = stencil.reshape(RHS, STEN, STEN, elements)
    framed = place_shifted(place_shifted(blocks, shifts[0], 1), shifts[1], 2)
    window_size = STEN + 2 * HALO
    framed = framed.reshape(RHS, window_size, window_size, ER, EC).transpose(0, 3, 1, 4, 2)
    extended = intersection_add(intersection_add(framed, 1), 2)
    padded = extended_2(extended, (("row", 1), ("col", 2)), HALO)
    charges = fold_margin(fold_margin(padded, 1), 2)
    slab = lax.all_to_all(charges, "col", split_axis=1, concat_axis=2, tiled=True)
    slab_rows = slab.shape[1]
    width_cols = slab.shape[2]
    length_cols = 2 * width_cols
    block_cols = length_cols // device_count
    grid_rows = slab_rows * device_count
    length_rows = 2 * grid_rows
    fwd_real, fwd_imag = transform_last(slab, None, length_cols, width_cols, length_cols, -1.0)
    out_real = fwd_real.reshape(RHS, slab_rows, device_count, block_cols)
    out_imag = fwd_imag.reshape(RHS, slab_rows, device_count, block_cols)
    arrived = (
        lax.all_to_all(out_real, ("row", "col"), split_axis=2, concat_axis=2, tiled=True),
        lax.all_to_all(out_imag, ("row", "col"), split_axis=2, concat_axis=2, tiled=True),
    )
    col_real = arrived[0].transpose(0, 3, 2, 1).reshape(RHS, block_cols, grid_rows)
    col_imag = arrived[1].transpose(0, 3, 2, 1).reshape(RHS, block_cols, grid_rows)
    spec_real, spec_imag = transform_last(
        col_real, col_imag, length_rows, grid_rows, length_rows, -1.0
    )
    spec_real = spec_real * green
    spec_imag = spec_imag * green
    back_real, back_imag = transform_last(
        spec_real, spec_imag, length_rows, length_rows, grid_rows, 1.0
    )
    send_real = back_real.reshape(RHS, block_cols, device_count, slab_rows)
    send_imag = back_imag.reshape(RHS, block_cols, device_count, slab_rows)
    returned = (
        lax.all_to_all(send_real, ("row", "col"), split_axis=2, concat_axis=2, tiled=True),
        lax.all_to_all(send_imag, ("row", "col"), split_axis=2, concat_axis=2, tiled=True),
    )
    rows_real = returned[0].transpose(0, 3, 2, 1).reshape(RHS, slab_rows, length_cols)
    rows_imag = returned[1].transpose(0, 3, 2, 1).reshape(RHS, slab_rows, length_cols)
    final_real, final_imag = transform_last(
        rows_real, rows_imag, length_cols, length_cols, width_cols, 1.0
    )
    potential_slab = final_real * (1.0 / (length_rows * length_cols))
    potential = lax.all_to_all(potential_slab, "col", split_axis=2, concat_axis=1, tiled=True)
    rimmed = extended_2(potential, (("row", 1), ("col", 2)), HALO)
    windows = cut_windows(cut_windows(rimmed, 1), 3)
    windows = windows.transpose(0, 2, 4, 1, 3).reshape(RHS, window_size, window_size, elements)
    samples = pick_shifted(pick_shifted(windows, shifts[0], 1), shifts[1], 2).reshape(
        RHS, STEN * STEN, elements
    )
    sample_high = samples.astype(jnp.bfloat16)
    sample_low = (samples - sample_high.astype(jnp.float32)).astype(jnp.bfloat16)
    far_term = jnp.einsum(
        "sbn,qsn->qbn", projection, sample_high, preferred_element_type=jnp.float32
    )
    far_term = far_term + jnp.einsum(
        "sbn,qsn->qbn", projection, sample_low, preferred_element_type=jnp.float32
    )
    return far_term + near_term


LANES = 128
SUB = 8
TILES = 4
GROUPS = 9
PARITY_ORDER = (0, 2, 4, 6, 1, 3, 5, 7)


def roll(value, amount, dim):
    return pltpu.roll(value, amount % value.shape[dim], dim)


def lane_index(shape):
    return lax.broadcasted_iota(jnp.int32, shape, len(shape) - 1)


def sub_index(shape):
    return lax.broadcasted_iota(jnp.int32, shape, len(shape) - 2)


def sum_rows(parts):
    sub = sub_index(parts[0].shape)
    top = sub < 4
    level = []
    for i in range(4):
        a, b = parts[i], parts[i + 4]
        level.append(jnp.where(top, a, b) + roll(jnp.where(top, b, a), 4, 0))
    mask = (sub & 2) == 0
    level = [
        jnp.where(mask, level[i], level[i + 2])
        + jnp.where(mask, roll(level[i], -2, 0), roll(level[i + 2], 2, 0))
        for i in range(2)
    ]
    mask = (sub & 1) == 0
    a, b = level
    return jnp.where(mask, a, b) + jnp.where(mask, roll(a, -1, 0), roll(b, 1, 0))


def next_row(value):
    lane = lane_index(value.shape)
    sub = sub_index(value.shape)
    turned = roll(value, EC, 1)
    carried = jnp.where((sub & 3) == 0, 0.0, roll(turned, 1, 0))
    return jnp.where(lane < EC, carried, turned)


def previous_row(value):
    lane = lane_index(value.shape)
    sub = sub_index(value.shape)
    turned = roll(value, -EC, 1)
    carried = jnp.where((sub & 3) == 3, 0.0, roll(turned, -1, 0))
    return jnp.where(lane >= LANES - EC, carried, turned)


def place_charges(stencil, row_shift, col_shift):
    shape = row_shift.shape
    lane = lane_index(shape)
    sub = sub_index(shape)
    window = STEN + 2 * HALO
    row_mask = {o: row_shift == o for o in range(-HALO, HALO + 1)}
    col_mask = {o: col_shift == o for o in range(-HALO, HALO + 1)}
    first = []
    for rr in range(window):
        line = []
        for c in range(STEN):
            value = jnp.zeros(shape, jnp.float32)
            for o in range(-HALO, HALO + 1):
                source = rr - HALO - o
                if 0 <= source < STEN:
                    value = jnp.where(row_mask[o], stencil(source * STEN + c), value)
            line.append(value)
        first.append(line)
    framed = []
    for rr in range(window):
        line = []
        for cc in range(window):
            value = jnp.zeros(shape, jnp.float32)
            for o in range(-HALO, HALO + 1):
                source = cc - HALO - o
                if 0 <= source < STEN:
                    value = jnp.where(col_mask[o], first[rr][source], value)
            line.append(value)
        framed.append(line)
    grid = []
    for r in range(PITCH):
        line = []
        for cc in range(window):
            value = framed[r + HALO][cc]
            if r < HALO:
                value = value + next_row(framed[r + HALO + PITCH][cc])
            if r >= PITCH - HALO:
                value = value + previous_row(framed[r + HALO - PITCH][cc])
            line.append(value)
        grid.append(line)
    slot = sub & 3
    low_lanes = lane < EC
    high_lanes = lane >= LANES - EC
    line = []
    for cc in range(window):
        value = jnp.where(low_lanes & (slot == 0), roll(roll(framed[10][cc], EC, 1), -3, 0), 0.0)
        value = jnp.where(low_lanes & (slot == 1), roll(roll(framed[11][cc], EC, 1), -2, 0), value)
        value = jnp.where(high_lanes & (slot == 3), roll(roll(framed[0][cc], -EC, 1), 3, 0), value)
        value = jnp.where(high_lanes & (slot == 2), roll(roll(framed[1][cc], -EC, 1), 2, 0), value)
        line.append(value)
    grid.append(line)
    elem_col = lane & (EC - 1)
    parts = [[] for _ in range(SUB)]
    edges = [jnp.zeros(shape, jnp.float32) for _ in range(SUB)]
    for r in range(GROUPS):
        cells = []
        for c in range(PITCH):
            value = grid[r][c + HALO]
            if c < HALO:
                value = value + jnp.where(elem_col == 0, 0.0, roll(grid[r][c + HALO + PITCH], 1, 1))
            if c >= PITCH - HALO:
                value = value + jnp.where(
                    elem_col == EC - 1, 0.0, roll(grid[r][c + HALO - PITCH], -1, 1)
                )
            cells.append(value)
        turned = transpose_blocks([cells[c] for c in PARITY_ORDER], lane)
        for e in range(SUB):
            parts[e].append(turned[e])
            start = EC * e
            edge = edges[e]
            edge = jnp.where(lane == r, roll(grid[r][10], r - start - (EC - 1), 1), edge)
            edge = jnp.where(lane == 64 + r, roll(grid[r][11], 64 + r - start - (EC - 1), 1), edge)
            edge = jnp.where(lane == 63 - r, roll(grid[r][0], 63 - r - start, 1), edge)
            edge = jnp.where(lane == 127 - r, roll(grid[r][1], 127 - r - start, 1), edge)
            edges[e] = edge
    return [parts[e] + [edges[e]] for e in range(SUB)]


def transpose_blocks(values, lane):
    block = lane // EC
    for step in (4, 2, 1):
        mask = (block & step) == 0
        result = list(values)
        for i in range(SUB):
            if i & step:
                continue
            a, b = values[i], values[i + step]
            result[i] = jnp.where(mask, a, roll(b, EC * step, 1))
            result[i + step] = jnp.where(mask, roll(a, -EC * step, 1), b)
        values = result
    return values


def halves(a, b):
    low = lane_index(a.shape) < 64
    return jnp.where(low, a, roll(b, 64, 1)), jnp.where(low, roll(a, 64, 1), b)


def half_rows(a, b):
    top = sub_index(a.shape) < 4
    return jnp.where(top, a, roll(b, 4, 0)), jnp.where(top, roll(a, 4, 0), b)


def gather_rows(part, edge, count):
    sample = edge(0)
    lane = lane_index(sample.shape)
    from_low = (lane == 0) | (lane == 64)
    from_high = (lane == 63) | (lane == 127)
    rows = []
    for j in range(count):
        groups = []
        for r in range(GROUPS):
            value = part(j, r)
            if j > 0:
                value = value + jnp.where(from_low, roll(edge(j - 1), -r, 1), 0.0)
            if j < count - 1:
                value = value + jnp.where(from_high, roll(edge(j + 1), r, 1), 0.0)
            groups.append(value)
        first, second = [], []
        for parity in range(2):
            for b in range(2):
                low, high = half_rows(groups[parity + 4 * b], groups[parity + 4 * b + 2])
                first.append(low)
                second.append(high)
        low, high = half_rows(groups[8], groups[8])
        first.append(low)
        second.append(high)
        rows.append(jnp.concatenate(first + second, axis=0))
    even, odd = [], []
    for j in range(0, count, 2):
        low, high = halves(rows[j], rows[j + 1])
        even.append(low)
        odd.append(high)
    return jnp.concatenate(even, axis=1), jnp.concatenate(odd, axis=1)


def scatter_rows(even, odd, count, put):
    rows = []
    for j in range(0, count, 2):
        tile = slice(64 * j, 64 * j + LANES)
        rows.extend(halves(even[:, tile], odd[:, tile]))
    blocks = []
    for j in range(count):
        first = [rows[j][8 * i : 8 * i + 8] for i in range(5)]
        second = [rows[j][40 + 8 * i : 48 + 8 * i] for i in range(5)]
        groups = [None] * GROUPS
        for parity in range(2):
            for b in range(2):
                low, high = half_rows(first[2 * parity + b], second[2 * parity + b])
                groups[parity + 4 * b] = low
                groups[parity + 4 * b + 2] = high
        sub = sub_index(first[4].shape)
        tail = jnp.where(sub < 4, roll(first[4], 4, 0), second[4])
        head = jnp.where(sub < 4, first[4], roll(second[4], 4, 0))
        groups[8] = jnp.where((sub & 2) == 0, head, tail)
        blocks.append(groups)
    lane = lane_index(blocks[0][0].shape)
    for j in range(count):
        edge = jnp.zeros(blocks[0][0].shape, jnp.float32)
        for r in range(GROUPS):
            if j < count - 1:
                edge = jnp.where(
                    (lane == r) | (lane == 64 + r), roll(blocks[j + 1][r], r, 1), edge
                )
            if j > 0:
                edge = jnp.where(
                    (lane == 63 - r) | (lane == 127 - r), roll(blocks[j - 1][r], -r, 1), edge
                )
        put(j, blocks[j] + [edge])


def read_samples(part, edge, row_shift, col_shift, put):
    shape = row_shift.shape
    lane = lane_index(shape)
    sub = sub_index(shape)
    elem_col = lane & (EC - 1)
    window = STEN + 2 * HALO
    grid = []
    for r in range(GROUPS):
        turned = transpose_blocks([part(e, r) for e in range(SUB)], lane)
        cells = [None] * PITCH
        for place, c in enumerate(PARITY_ORDER):
            cells[c] = turned[place]
        line = [None] * window
        for c in range(PITCH):
            line[c + HALO] = cells[c]
        after = [roll(cells[c], -1, 1) for c in range(HALO)]
        before = [roll(cells[PITCH - HALO + c], 1, 1) for c in range(HALO)]
        for e in range(SUB):
            start = EC * e
            last = lane == start + EC - 1
            zero = lane == start
            after[0] = jnp.where(last, roll(edge(e), start + EC - 1 - r, 1), after[0])
            after[1] = jnp.where(last, roll(edge(e), start + EC - 1 - 64 - r, 1), after[1])
            before[0] = jnp.where(zero, roll(edge(e), start - 63 + r, 1), before[0])
            before[1] = jnp.where(zero, roll(edge(e), start - 127 + r, 1), before[1])
        line[0], line[1] = before
        line[10], line[11] = after
        grid.append(line)
    slot = sub & 3
    first_row = (slot == 0) & (lane < EC)
    last_row = (slot == 3) & (lane >= LANES - EC)
    framed = [[None] * window for _ in range(window)]
    for cc in range(window):
        for r in range(PITCH):
            framed[r + HALO][cc] = grid[r][cc]
        outer = grid[8][cc]
        below = roll(outer, -EC, 1)
        above = roll(outer, EC, 1)
        framed[10][cc] = jnp.where(last_row, roll(below, 3, 0), previous_row(grid[0][cc]))
        framed[11][cc] = jnp.where(last_row, roll(below, 2, 0), previous_row(grid[1][cc]))
        framed[0][cc] = jnp.where(first_row, roll(above, -3, 0), next_row(grid[6][cc]))
        framed[1][cc] = jnp.where(first_row, roll(above, -2, 0), next_row(grid[7][cc]))
    for a in range(STEN):
        line = []
        for cc in range(window):
            value = framed[a + HALO][cc]
            for o in range(-HALO, HALO + 1):
                if o:
                    value = jnp.where(row_shift == o, framed[a + HALO + o][cc], value)
            line.append(value)
        for b in range(STEN):
            value = line[b + HALO]
            for o in range(-HALO, HALO + 1):
                if o:
                    value = jnp.where(col_shift == o, line[b + HALO + o], value)
            put(a * STEN + b, value)


def add_outer_rows(chunk, row_count, col_count):
    sub = sub_index((SUB, LANES))
    even, odd = [], []
    for i in range(row_count):
        for j in range(col_count):
            rows = [chunk(i, j)[8 * k : 8 * k + 8] for k in range(4)]
            if j == 0 and i > 0:
                outer = chunk(i - 1, 0)[32:40]
                rows[0] = rows[0] + jnp.where(sub == 0, outer, 0.0)
                rows[2] = rows[2] + jnp.where(sub == 0, roll(outer, -1, 0), 0.0)
            if j == col_count - 1 and i < row_count - 1:
                outer = chunk(i + 1, j)[32:40]
                rows[1] = rows[1] + jnp.where(sub == 7, outer, 0.0)
                rows[3] = rows[3] + jnp.where(sub == 7, roll(outer, 1, 0), 0.0)
            even.extend(rows[:2])
            odd.extend(rows[2:])
    return jnp.concatenate(even, axis=0), jnp.concatenate(odd, axis=0)


def spread_outer_rows(even, odd, row_count, col_count, put):
    sub = sub_index((SUB, LANES))

    def block(i, j):
        start = 16 * (i * col_count + j)
        return [even[start : start + 8], even[start + 8 : start + 16],
                odd[start : start + 8], odd[start + 8 : start + 16]]

    for i in range(row_count):
        for j in range(col_count):
            outer = jnp.zeros((SUB, LANES), jnp.float32)
            if j == 0 and i < row_count - 1:
                rows = block(i + 1, 0)
                outer = jnp.where(sub == 0, rows[0], jnp.where(sub == 1, roll(rows[2], 1, 0), outer))
            if j == col_count - 1 and i > 0:
                rows = block(i - 1, j)
                outer = jnp.where(sub == 7, rows[1], jnp.where(sub == 6, roll(rows[3], -1, 0), outer))
            put(i, j, block(i, j) + [outer])


def two_terms(value):
    high = value.astype(jnp.bfloat16)
    return high, (value - high.astype(jnp.float32)).astype(jnp.bfloat16)


def dot(left, right, dims=((1,), (0,))):
    return lax.dot_general(left, right, (dims, ((), ())), preferred_element_type=jnp.float32)


def even_positions(row_count, col_count):
    j, c, e = np.meshgrid(np.arange(col_count), np.arange(4), np.arange(EC), indexing="ij")
    columns = (LANES * j + PITCH * e + 2 * c).reshape(-1)
    i, j, b, h, t = np.meshgrid(
        np.arange(row_count), np.arange(col_count), np.arange(2), np.arange(2), np.arange(TILES),
        indexing="ij",
    )
    rows = (ER * PITCH * i + SUB * PITCH * t + PITCH * j + 2 * h + 4 * b).reshape(-1)
    return columns, rows


def angle_pair(left, right, length):
    angles = 2.0 * np.pi * (np.asarray(left)[:, None] * np.asarray(right)[None, :] % length) / length
    return np.asarray(np.cos(angles), np.float32), np.asarray(np.sin(angles), np.float32)


def position_bases(positions, length):
    orders = np.arange(length // 4)
    grouped = positions.reshape(-1, SUB)
    offsets = grouped[0] - grouped[0, 0]
    assert (grouped == grouped[:, :1] + offsets[None, :]).all()
    return np.concatenate(
        [
            *angle_pair(grouped[:, 0], orders, length),
            *angle_pair(offsets, orders, length),
            *angle_pair(offsets + 1, orders, length),
        ]
    )


def split_rows(ref, *counts):
    start, parts = 0, []
    for count in counts:
        parts.append(ref.at[start : start + count])
        start += count
    return parts


def order_bases(positions, length):
    bases = np.arange(0, length // 4, SUB)
    result = []
    for parity in range(2):
        result.extend(angle_pair(bases, positions + parity, length))
        result.extend(angle_pair(np.arange(SUB), positions + parity, length))
    return np.concatenate(result)


def fill_by_position(sign_of, bases, out_refs):
    base_cos, base_sin, even_cos, even_sin, odd_cos, odd_sin = bases
    ec, es, oc, os = (ref[...] for ref in (even_cos, even_sin, odd_cos, odd_sin))
    start = lane_index(ec.shape) == 0

    def pair(i, carry):
        parts = [[], [], []]
        for h in range(2):
            row = 2 * i + h
            bc, bs = base_cos[pl.ds(row, 1), :], base_sin[pl.ds(row, 1), :]
            parts[0].append(bc * ec - bs * es)
            parts[1].append(jnp.where(start, 1.0, -(bs * ec + bc * es)) * sign_of(row))
            parts[2].append(bc * oc - bs * os)
        rows = pl.ds(pl.multiple_of(16 * i, 16), 16)
        for ref, part in zip(out_refs, parts):
            ref[rows, :] = jnp.concatenate(part, axis=0).astype(ref.dtype)
        return carry

    lax.fori_loop(0, base_cos.shape[0] // 2, pair, 0)


def column_table_kernel(bases_ref, *outs):
    count = (bases_ref.shape[0] - 4 * SUB) // 2
    bases = split_rows(bases_ref, count, count, SUB, SUB, SUB, SUB)
    fill_by_position(lambda row: (1 - 2 * ((row // 2) & 1)).astype(jnp.float32), bases, outs)


def row_table_kernel(green_ref, position_ref, order_ref, *outs):
    count = (position_ref.shape[0] - 4 * SUB) // 2
    position = split_rows(position_ref, count, count, SUB, SUB, SUB, SUB)
    order = split_rows(order_ref, count, count, SUB, SUB, count, count, SUB, SUB)
    quarter = position[0].shape[1]
    tiles = quarter // LANES
    sub = sub_index((SUB, quarter))
    flip = jnp.where(sub < 4, 1.0, -1.0)
    fill_by_position(lambda row: flip, position, outs[3:6])
    ebc, ebs, ec, es, obc, obs, oc, os = order
    ec, es, oc, os = (ref[...] for ref in (ec, es, oc, os))
    lanes = jnp.where((lane_index((SUB, quarter)) & 4) == 0, 1.0, -1.0)

    def pair(i, carry):
        parts = [[], [], []]
        for h in range(2):
            row = 2 * i + h
            one = (pl.ds(row, 1), slice(None))
            bc, bs = ebc[one], ebs[one]
            parts[0].append(bc * ec - bs * es)
            first = (sub + row) == 0
            parts[1].append(jnp.where(first, 1.0, -(bs * ec + bc * es)) * lanes)
            parts[2].append(obc[one] * oc - obs[one] * os)
        rows = pl.ds(pl.multiple_of(16 * i, 16), 16)
        for ref, part in zip(outs[:3], parts):
            ref[rows, :] = jnp.concatenate(part, axis=0).astype(ref.dtype)
        return carry

    lax.fori_loop(0, ebc.shape[0] // 2, pair, 0)

    depth = green_ref.shape[0]
    device = lax.axis_index("row") * lax.axis_size("col") + lax.axis_index("col")
    number = sub_index((depth, LANES)) + device * depth
    length = 4 * quarter
    weight = jnp.where(number % quarter == 0, 1.0, 2.0) * (1.0 / (length * length))
    lane = lane_index((depth, LANES))

    def scaled(tile):
        value = green_ref[:, LANES * tile : LANES * (tile + 1)] * weight
        if tile % tiles == 0:
            value = value * jnp.where(lane == 0, 1.0, 2.0)
        else:
            value = value * 2.0
        return jnp.concatenate([value, value], axis=0)

    for t in range(tiles):
        cos_plus, cos_minus = scaled(t), scaled(2 * tiles + t)
        sin_minus, sin_plus = scaled(tiles + t), scaled(3 * tiles + t)
        first = slice(LANES * t, LANES * (t + 1))
        second = slice(quarter + LANES * t, quarter + LANES * (t + 1))
        outs[6][first, :] = (cos_plus + cos_minus).T
        outs[7][first, :] = (cos_plus - cos_minus).T
        outs[6][second, :] = (sin_plus + sin_minus).T
        outs[7][second, :] = (sin_plus - sin_minus).T


def tiled_shifts(shifts_ref, which):
    rows = [shifts_ref[which : which + 1, LANES * t : LANES * (t + 1)] for t in range(TILES)]
    return jnp.concatenate(rows * RHS, axis=0)


def charge_kernel(
    currents_ref, projection_ref, shifts_ref, out_ref, weights, raw, shifts, current, partial, stencil, sems
):
    copies = [
        pltpu.make_async_copy(currents_ref, raw, sems.at[STEN]),
        pltpu.make_async_copy(shifts_ref, shifts, sems.at[STEN + 1]),
    ]

    def weight_copy(step):
        rows = pl.ds(step * STEN, STEN)
        return pltpu.make_async_copy(projection_ref.at[rows], weights.at[rows], sems.at[step])

    copies[0].start()
    for step in range(STEN):
        weight_copy(step).start()
    copies[1].start()
    copies[0].wait()
    current[...] = raw[...].astype(jnp.bfloat16).astype(jnp.float32)

    def one_row(step, carry):
        weight_copy(step).wait()
        for t in range(TILES):
            lanes = slice(LANES * t, LANES * (t + 1))
            totals = [[None] * RHS for _ in range(STEN)]
            for b in range(0, BASIS, 16):
                values = [
                    [current[q, b + 8 * h : b + 8 * h + 8, lanes] for h in range(2)]
                    for q in range(RHS)
                ]
                for s in range(STEN):
                    weight = weights[step * STEN + s, b : b + 16, lanes].astype(jnp.float32)
                    for q in range(RHS):
                        term = weight[:8] * values[q][0] + weight[8:] * values[q][1]
                        totals[s][q] = term if totals[s][q] is None else totals[s][q] + term
            for s in range(STEN):
                for q in range(RHS):
                    partial[s, q * TILES + t] = totals[s][q]
        for s in range(STEN):
            stencil[step * STEN + s] = sum_rows([partial[s, i] for i in range(SUB)])
        return carry

    lax.fori_loop(0, STEN, one_row, 0)
    copies[1].wait()
    chunks = place_charges(
        lambda s: stencil[s], tiled_shifts(shifts, 0), tiled_shifts(shifts, 1)
    )
    to_next, to_previous, to_rows = pack_currents(
        lambda q, t: current[q, :, LANES * t : LANES * (t + 1)]
    )
    mine = lax.axis_index("col")
    block = lane_index((SUB, LANES)) // EC
    middle = ((block & 3) == 1) | ((block & 3) == 2)
    for e in range(SUB):
        after = (mine == e - 1).astype(jnp.float32)
        before = (mine == e + 1).astype(jnp.float32)
        edge = jnp.where(middle, to_rows[e], chunks[e][GROUPS])
        rows = chunks[e][:GROUPS] + [edge, to_next * after + to_previous * before]
        out_ref[e] = jnp.concatenate(rows, axis=0).astype(out_ref.dtype)


def pack_currents(tile):
    half = BASIS // 2
    lane = lane_index((half, LANES))
    elem_col = lane & (EC - 1)
    to_next = jnp.zeros((half, LANES), jnp.float32)
    to_previous = jnp.zeros((half, LANES), jnp.float32)
    for q in range(RHS):
        for t in range(TILES):
            value = tile(q, t)
            for h in range(2):
                place = q * TILES + t + SUB * h
                part = value[half * h : half * (h + 1)]
                here = elem_col == place
                to_next = jnp.where(here, roll(part, place - (EC - 1), 1), to_next)
                to_previous = jnp.where(here, roll(part, place, 1), to_previous)
    lane = lane_index((SUB, LANES))
    to_rows = []
    for e in range(SUB):
        rows = jnp.zeros((SUB, LANES), jnp.float32)
        for q in range(RHS):
            span = slice(SUB * e, SUB * (e + 1))
            last = roll(tile(q, TILES - 1)[span], EC + EC * q - (LANES - EC), 1)
            first = roll(tile(q, 0)[span], 64 + EC + EC * q, 1)
            rows = jnp.where(lane // EC == 1 + q, last, jnp.where(lane // EC == 5 + q, first, rows))
        to_rows.append(rows)
    return to_next, to_previous, to_rows


def forward_rows(edge_row, j, count, which):
    lane = lane_index((SUB, LANES))
    start = EC + 64 * which
    value = roll(edge_row(j), -start, 1)
    for q in range(RHS):
        place = 2 * EC + 2 * q
        if j > 0:
            corner = roll(edge_row(j - 1), place - start - EC * q - (EC - 1), 1)
            value = jnp.where(lane == place, corner, value)
        if j < count - 1:
            corner = roll(edge_row(j + 1), place + 1 - start - EC * q, 1)
            value = jnp.where(lane == place + 1, corner, value)
    return jnp.where(lane < 64, roll(value, 2, 0), roll(roll(value, 64, 1), -2, 0))


def column_sign(shape):
    return jnp.where((lane_index(shape) & EC) == 0, 1.0, -1.0)


def column_kernel(count, rows_ref, even_cos, even_sin, odd_cos, out_ref):
    def part(j, r):
        return rows_ref[j, 8 * r : 8 * r + 8, :].astype(jnp.float32)

    even, odd = gather_rows(part, lambda j: part(j, GROUPS), count)
    both = jnp.concatenate([odd, odd * column_sign(odd.shape)], axis=0).astype(jnp.bfloat16)
    even = even.astype(jnp.bfloat16)
    ec, es = dot(even, even_cos[...]), dot(even, even_sin[...])
    both = dot(both, odd_cos[...])
    oc, os = both[: odd.shape[0]], both[odd.shape[0] :]
    half = out_ref.shape[1]
    mine = lax.axis_index("row")
    ends = [
        [forward_rows(lambda k: part(k, GROUPS), j, count, which) for which in range(2)]
        for j in range(count)
    ]
    sub = sub_index((SUB, LANES))
    middle = (sub >= 2) & (sub < 6)
    device = 0
    for block in (ec + oc, es - os, ec - oc, es + os):
        for t in range(0, block.shape[1], LANES):
            for chunk in halves(block[:half, t : t + LANES], block[half:, t : t + LANES]):
                i, j = device // count, device % count
                below = (mine == i - 1).astype(jnp.float32)
                above = (mine == i + 1).astype(jnp.float32)
                tail = jnp.where(
                    middle, ends[j][0] * below + ends[j][1] * above, chunk[half - SUB :]
                )
                chunk = jnp.concatenate([chunk[: half - SUB], tail], axis=0)
                out_ref[device] = chunk.astype(out_ref.dtype)
                device += 1


def row_kernel(row_count, col_count, in_ref, even_cos, even_sin, odd_cos, back_cos, back_sin, back_odd,
               sum_ref, diff_ref, out_ref):
    even, odd = add_outer_rows(
        lambda i, j: in_ref[i * col_count + j].astype(jnp.float32), row_count, col_count
    )
    flip = jnp.where((sub_index(odd.shape) & 4) == 0, 1.0, -1.0)
    both = jnp.concatenate([odd, odd * flip], axis=1).astype(jnp.bfloat16)
    even = even.astype(jnp.bfloat16)
    a = [dot(even_cos[...], even), dot(even_sin[...], even)]
    both = dot(odd_cos[...], both)
    b = [both[:, :LANES], both[:, LANES:]]
    quarter = odd.shape[0]

    def pieces(left, right):
        for k in range(2):
            span = slice(quarter * k, quarter * (k + 1))
            yield two_terms(left[k] * sum_ref[span, :] + right[k] * diff_ref[span, :])

    def fold(value):
        return value[:, :LANES] + value[:, LANES:]

    (ch, cl), (sh, sl) = pieces(a, b)
    even = fold(
        dot(back_cos[...], jnp.concatenate([ch, cl], axis=1))
        + dot(back_sin[...], jnp.concatenate([sh, sl], axis=1))
    )
    (ch, cl), (sh, sl) = pieces(b, a)
    both = dot(back_odd[...], jnp.concatenate([ch, cl, sh, sl], axis=1))
    odd = fold(both[:, : 2 * LANES]) + fold(both[:, 2 * LANES :]) * flip

    def put(i, j, parts):
        out_ref[i * col_count + j] = jnp.concatenate(parts, axis=0).astype(out_ref.dtype)

    spread_outer_rows(even, odd, row_count, col_count, put)


def grid_kernel(count, in_ref, even_cos, even_sin, odd_cos, out_ref):
    devices = in_ref.shape[0]
    first, second = [], []
    for d in range(0, devices, 2):
        low, high = halves(in_ref[d].astype(jnp.float32), in_ref[d + 1].astype(jnp.float32))
        first.append(low)
        second.append(high)
    per_block = devices // 8
    blocks = []
    for k in range(4):
        span = slice(per_block * k, per_block * (k + 1))
        blocks.append(
            jnp.concatenate(
                [jnp.concatenate(first[span], axis=1), jnp.concatenate(second[span], axis=1)], axis=0
            )
        )
    cos_plus, sin_minus, cos_minus, sin_plus = blocks
    half = cos_plus.shape[0]

    def back(values, table):
        terms = [term for value in values for term in two_terms(value)]
        result = dot(jnp.concatenate(terms, axis=0), table[...], ((1,), (1,)))
        return [
            result[2 * half * i : 2 * half * i + half] + result[2 * half * i + half : 2 * half * (i + 1)]
            for i in range(len(values))
        ]

    even = back([cos_plus + cos_minus], even_cos)[0] + back([sin_plus + sin_minus], even_sin)[0]
    odd, turned = back([cos_plus - cos_minus, sin_plus - sin_minus], odd_cos)
    odd = odd + turned * column_sign(odd.shape)

    def put(j, parts):
        out_ref[j] = jnp.concatenate(parts, axis=0).astype(out_ref.dtype)

    scatter_rows(even, odd, count, put)


def far_kernel(
    source_ref, projection_ref, shifts_ref, near_ref, out_ref, grid_ref, weights, samples, shifts, totals_ref, sems
):
    depth = 16
    count = BASIS // depth

    def load(i):
        rows = pl.ds(i * depth, depth)
        return pltpu.make_async_copy(
            projection_ref.at[:, rows], weights.at[:, rows], sems.at[1 + count + i]
        )

    load_shifts = pltpu.make_async_copy(shifts_ref, shifts, sems.at[0])
    load_grid = pltpu.make_async_copy(source_ref, grid_ref, sems.at[1 + 2 * count])
    load_near = pltpu.make_async_copy(near_ref, totals_ref, sems.at[2 + 2 * count])
    load_grid.start()
    load_shifts.start()
    load_near.start()
    for i in range(count):
        load(i).start()

    def part(e, r):
        return grid_ref[e, 8 * r : 8 * r + 8, :].astype(jnp.float32)

    def put(s, value):
        samples[s] = value

    load_shifts.wait()
    load_grid.wait()
    read_samples(
        part, lambda e: part(e, GROUPS), tiled_shifts(shifts, 0), tiled_shifts(shifts, 1), put
    )
    load_near.wait()

    def store(i):
        rows = pl.ds(i * depth, depth)
        return pltpu.make_async_copy(totals_ref.at[:, rows], out_ref.at[:, rows], sems.at[1 + i])

    for i in range(count):
        span = slice(i * depth, (i + 1) * depth)
        load(i).wait()

        def add_row(a, totals):
            totals = list(totals)
            for b in range(STEN):
                s = a * STEN + b
                for t in range(TILES):
                    weight = weights[s, span, LANES * t : LANES * (t + 1)].astype(jnp.float32)
                    for q in range(RHS):
                        index = q * TILES + t
                        totals[index] = totals[index] + weight * samples[s, index : index + 1, :]
            return tuple(totals)

        start = tuple(
            totals_ref[q, span, LANES * t : LANES * (t + 1)] for q in range(RHS) for t in range(TILES)
        )
        totals = lax.fori_loop(0, STEN, add_row, start)
        for q in range(RHS):
            for t in range(TILES):
                totals_ref[q, span, LANES * t : LANES * (t + 1)] = totals[q * TILES + t]
        store(i).start()
    for i in range(count):
        store(i).wait()


def pick_kernel(currents_ref, slab_ref, arrived_ref, partners_ref, out_ref):
    lane = lane_index((BASIS, LANES))
    elem_col = lane & (EC - 1)
    row, col = lax.axis_index("row"), lax.axis_index("col")
    col_count = lax.axis_size("col")
    devices = arrived_ref.shape[0]

    def column_edge(source):
        source = jnp.clip(source, 0, col_count - 1)
        return slab_ref[source, 80:112, :].astype(jnp.float32)

    from_left, from_right = column_edge(col - 1), column_edge(col + 1)

    def beside(edge, q, t, end):
        place = q * TILES + t
        return jnp.concatenate([roll(edge, end - place, 1), roll(edge, end - place - SUB, 1)], axis=0)

    def three(own, left, right):
        return (
            jnp.where(elem_col == 0, left, roll(own, 1, 1)),
            own,
            jnp.where(elem_col == EC - 1, right, roll(own, -1, 1)),
        )

    sub = sub_index((SUB, LANES))

    def outer_row(source):
        parts = []
        for j in range(col_count):
            index = jnp.clip(source * col_count + j, 0, devices - 1)
            value = arrived_ref[index, 32:40, :].astype(jnp.float32)
            parts.append(jnp.where(sub < 4, roll(value, -2, 0), roll(roll(value, 2, 0), -64, 1)))
        return jnp.concatenate(parts, axis=0)

    rows = outer_row(row - 1), outer_row(row + 1)

    def outer_three(value, q, start):
        own = roll(value, start - EC * q, 1)
        left = roll(value, start - 2 * EC - 2 * q, 1)
        right = roll(value, start + EC - 1 - 2 * EC - 2 * q - 1, 1)
        return three(own, left, right)

    for q in range(RHS):
        tiles = []
        for t in range(TILES):
            own = currents_ref[q, :, LANES * t : LANES * (t + 1)]
            own = own.astype(jnp.bfloat16).astype(jnp.float32)
            tiles.append(three(own, beside(from_left, q, t, 0), beside(from_right, q, t, EC - 1)))
        above = outer_three(rows[0], q, 0)
        below = outer_three(rows[1], q, LANES - EC)
        for t in range(TILES):
            lanes = slice(LANES * t, LANES * (t + 1))
            codes = [partners_ref[k : k + 1, lanes] for k in range(1, NEIGH)]
            chosen = [tiles[t][1]] * (NEIGH - 1)
            for c in range(3):
                here = tiles[t][c]
                before = roll(tiles[t - 1][c], EC, 1) if t else above[c]
                after = roll(tiles[t + 1][c], -EC, 1) if t < TILES - 1 else below[c]
                views = (
                    jnp.where(lane < EC, before, roll(here, EC, 1)),
                    here,
                    jnp.where(lane >= LANES - EC, after, roll(here, -EC, 1)),
                )
                for r in range(3):
                    if r == 1 and c == 1:
                        continue
                    for k in range(NEIGH - 1):
                        chosen[k] = jnp.where(codes[k] == 3 * r + c, views[r], chosen[k])
            for k in range(NEIGH - 1):
                out_ref[k, q, :, lanes] = chosen[k].astype(out_ref.dtype)


def near_kernel(has_total, slots, start, stop, *refs):
    values_ref, refs = refs[0], refs[1:]
    total_ref = None
    if has_total:
        total_ref, refs = refs[0], refs[1:]
    blocks_ref, out_ref, blocks, picked, sems = refs
    chunks = (stop - start) // SUB

    def load(chunk, k):
        rows = pl.ds(start + chunk * SUB, SUB)
        return pltpu.make_async_copy(
            blocks_ref.at[slots[k], rows], blocks.at[chunk, k], sems.at[chunk, k]
        )

    for chunk in range(chunks):
        for k in range(len(slots)):
            load(chunk, k).start()
    picked[...] = values_ref[...].astype(jnp.bfloat16).astype(jnp.float32).reshape(picked.shape)
    if has_total:
        out_ref[...] = total_ref[...]

    def one_chunk(chunk, carry):
        for k in range(len(slots)):
            load(chunk, k).wait()
        rows = pl.ds(pl.multiple_of(start + chunk * SUB, SUB), SUB)
        for t in range(TILES):
            lanes = slice(t * LANES, (t + 1) * LANES)
            totals = [[None] * RHS for _ in range(SUB)]
            for k in range(len(slots)):
                for b in range(0, BASIS, 16):
                    values = [
                        [picked[k, q, b + 8 * h : b + 8 * h + 8, lanes] for h in range(2)]
                        for q in range(RHS)
                    ]
                    for a in range(SUB):
                        weight = blocks[chunk, k, a, b : b + 16, lanes].astype(jnp.float32)
                        for q in range(RHS):
                            term = weight[:8] * values[q][0] + weight[8:] * values[q][1]
                            totals[a][q] = term if totals[a][q] is None else totals[a][q] + term
            for q in range(RHS):
                value = sum_rows([totals[a][q] for a in range(SUB)])
                if has_total:
                    value = value + total_ref[q, rows, lanes]
                out_ref[q, rows, lanes] = value
        return carry

    lax.fori_loop(0, chunks, one_chunk, 0)


def near_call(values, total, near_blocks, slots, start, stop):
    elements = near_blocks.shape[3]
    chunks = (stop - start) // SUB
    return pl.pallas_call(
        functools.partial(near_kernel, total is not None, slots, start, stop),
        in_specs=[ON_CHIP] * (1 if total is None else 2) + [IN_PLACE],
        out_specs=ON_CHIP,
        out_shape=jax.ShapeDtypeStruct((RHS, BASIS, elements), jnp.float32),
        scratch_shapes=[
            pltpu.VMEM((chunks, len(slots), SUB, BASIS, elements), jnp.bfloat16),
            pltpu.VMEM((len(slots), RHS, BASIS, elements), jnp.float32),
            pltpu.SemaphoreType.DMA((chunks, len(slots))),
        ],
        compiler_params=NEAR_PARAMS,
        name="near",
    )(*([values] if total is None else [values, total]), near_blocks)


ON_CHIP = pl.BlockSpec(memory_space=pltpu.VMEM)
IN_PLACE = pl.BlockSpec(memory_space=pltpu.HBM)
PARAMS = pltpu.CompilerParams(vmem_limit_bytes=48 << 20)
CHARGE_PARAMS = pltpu.CompilerParams(vmem_limit_bytes=60 << 20)
FULL_PARAMS = pltpu.CompilerParams(vmem_limit_bytes=53 << 20)
NEAR_PARAMS = pltpu.CompilerParams(vmem_limit_bytes=48 << 20)


def whole(shape):
    return pl.BlockSpec(shape, lambda *_: (0,) * len(shape))


def shards_real(currents, projection, near_blocks, partners, shifts, green):
    row_count = lax.axis_size("row")
    col_count = lax.axis_size("col")
    elements = currents.shape[2]
    width = col_count * LANES
    length = 2 * width
    quarter = length // 4
    f32, b16 = jnp.float32, jnp.bfloat16
    struct = jax.ShapeDtypeStruct
    devices = row_count * col_count

    charges = pl.pallas_call(
        charge_kernel,
        in_specs=[IN_PLACE] * 3,
        out_specs=ON_CHIP,
        out_shape=struct((SUB, 112, LANES), b16),
        scratch_shapes=[
            pltpu.VMEM(projection.shape, b16),
            pltpu.VMEM((RHS, BASIS, elements), f32),
            pltpu.VMEM((2, elements), jnp.int32),
            pltpu.VMEM((RHS, BASIS, elements), f32),
            pltpu.VMEM((STEN, SUB, SUB, LANES), f32),
            pltpu.VMEM((STEN * STEN, SUB, LANES), f32),
            pltpu.SemaphoreType.DMA((STEN + 2,)),
        ],
        compiler_params=CHARGE_PARAMS,
        name="charges",
    )(currents, projection, shifts)
    slab = lax.all_to_all(charges, "col", 0, 0, tiled=True)

    columns, rows = even_positions(row_count, col_count)
    table = struct((quarter, quarter), b16)
    col_tables = pl.pallas_call(
        column_table_kernel,
        out_specs=[ON_CHIP] * 3,
        out_shape=[table] * 3,
        compiler_params=PARAMS,
        name="column_tables",
    )(jnp.asarray(position_bases(columns, length)))
    spectrum = pl.pallas_call(
        functools.partial(column_kernel, col_count),
        out_shape=struct((devices, 40, LANES), b16),
        in_specs=[ON_CHIP] * 4,
        out_specs=ON_CHIP,
        compiler_params=PARAMS,
        name="columns",
    )(slab, *col_tables)
    spectrum, held, held_green = lax.optimization_barrier((spectrum, currents, green))
    arrived = lax.all_to_all(spectrum, ("row", "col"), 0, 0, tiled=True)
    near = near_call(held, None, near_blocks, (0,), 0, BASIS)
    spread = struct((2 * quarter, LANES), f32)
    row_tables = pl.pallas_call(
        row_table_kernel,
        out_shape=[table] * 6 + [spread] * 2,
        compiler_params=FULL_PARAMS,
        name="row_tables",
    )(held_green, jnp.asarray(position_bases(rows, length)), jnp.asarray(order_bases(rows, length)))
    arrived, near, *row_tables = lax.optimization_barrier((arrived, near, *row_tables))
    rows_back = pl.pallas_call(
        functools.partial(row_kernel, row_count, col_count),
        out_shape=struct((devices, 40, LANES), b16),
        in_specs=[ON_CHIP] * 9,
        out_specs=ON_CHIP,
        compiler_params=FULL_PARAMS,
        name="rows",
    )(arrived, *row_tables)
    rows_back, ready = lax.optimization_barrier((rows_back, arrived))
    returned = lax.all_to_all(rows_back, ("row", "col"), 0, 0, tiled=True)
    picked = pl.pallas_call(
        pick_kernel,
        in_specs=[whole(currents.shape), ON_CHIP, ON_CHIP, whole(partners.shape)],
        out_specs=ON_CHIP,
        out_shape=struct((NEIGH - 1, RHS, BASIS, elements), b16),
        compiler_params=PARAMS,
        name="pick",
    )(held, slab, ready, partners)
    others = tuple(range(1, NEIGH))
    near = near_call(picked, near, near_blocks, others, 0, BASIS // 2)
    returned, near, picked = lax.optimization_barrier((returned, near, picked))
    potential = pl.pallas_call(
        functools.partial(grid_kernel, col_count),
        out_shape=struct((SUB, 80, LANES), b16),
        in_specs=[ON_CHIP] * 4,
        out_specs=ON_CHIP,
        compiler_params=PARAMS,
        name="grid",
    )(returned, *col_tables)
    potential, near, picked = lax.optimization_barrier((potential, near, picked))
    pieces = lax.all_to_all(potential, "col", 0, 0, tiled=True)
    near = near_call(picked, near, near_blocks, others, BASIS // 2, BASIS)

    return pl.pallas_call(
        far_kernel,
        in_specs=[ON_CHIP, IN_PLACE, IN_PLACE, ON_CHIP],
        out_specs=IN_PLACE,
        out_shape=struct((RHS, BASIS, elements), f32),
        scratch_shapes=[
            pltpu.VMEM((SUB, 80, LANES), b16),
            pltpu.VMEM(projection.shape, b16),
            pltpu.VMEM((STEN * STEN, SUB, LANES), f32),
            pltpu.VMEM((2, elements), jnp.int32),
            pltpu.VMEM((RHS, BASIS, elements), f32),
            pltpu.SemaphoreType.DMA((11,)),
        ],
        compiler_params=FULL_PARAMS,
        name="far",
    )(pieces, projection, shifts, near)


def shards(currents, projection, near_blocks, partners, shifts, green):
    row_count = lax.axis_size("row")
    col_count = lax.axis_size("col")
    fits = col_count == SUB and green.shape[0] == 64 and 2 * row_count * col_count == green.shape[0]
    if fits and currents.shape[2] == TILES * LANES and row_count * ER == col_count * EC:
        return shards_real(currents, projection, near_blocks, partners, shifts, green)
    return shards_general(currents, projection, near_blocks, partners, shifts, green)


def solution(mesh):
    in_specs = (
        P(None, None, ("row", "col")),
        P(None, None, ("row", "col")),
        P(None, None, None, ("row", "col")),
        P(None, ("row", "col")),
        P(None, ("row", "col")),
        P(("row", "col"), None),
    )
    out_specs = P(None, None, ("row", "col"))
    return jax.shard_map(shards, mesh=mesh, in_specs=in_specs, out_specs=out_specs, check_vma=False)
```
